256 devices in a mesh: section: 2 (over core), grp: 4 (over x), dev: 32 (over y, z).
Axes of the slice: x: 4, y: 4, z: 8, core: 2. Of those that a mesh axis runs over, the one named last changes fastest.
Arguments:
- frames: bfloat16 [4, 512, 512, 256], P('grp', 'dev', 'section'), may hold values from -6 to 6
- templates: bfloat16 [8192, 256], P('dev'), may hold values from -0.375 to 0.375
- pair_block: int32 [2, 4, 256], P('section', 'grp', 'dev'), may hold values from 0 to 63
- pair_tile: int32 [2, 4, 256], P('section', 'grp', 'dev'), may hold values from 0 to 3
- pair_count: int32 [2, 4, 32], P('section', 'grp', 'dev'), may hold values from 1 to 8, 128 in all within a row
- owner_order: int32 [8192], replicated, may hold values from 0 to 8191, each once
Outputs:
- quantities: float32 [4, 8192], P('grp', 'dev')
The draws below stay inside these ranges and needn't reach their ends.
Inputs may be any that keep to these rules, and one draw needn't show every extreme that they name: `pair_count`: each device's count of live slots; the counts of one section half and run sum to half of all slots there, and one of them is 8. `owner_order`: A permutation of the precursors.
All inputs are finite; a program needn't handle non-finite values.
Results may differ from the reference program's by a relative error of at most 0.00037.
Values may be sent and summed in bfloat16 or wider, within the bound.
A program may use at most 64 MiB of HBM per device.

```python
import math
import jax
import jax.numpy as jnp
import numpy as np
from jax import lax

CH = 256
MOB = 512
SCALES = 6
RAD = 4
TM = 64
PB = 128
PREC = 8192
F_DEV = 16
SLOTS = 8
RUNS = 4
FRAMES = 512
NB = 64
NT = 4
N_SECTION = 2
N_DEV = 32


def set_ends(result, rng, low, largest):
    longest = result.shape.index(max(result.shape))
    spots = []
    for shift in (0, 1):
        where = [jax.random.randint(jax.random.fold_in(rng, axis), (), 0, length) for axis, length in enumerate(result.shape)]
        where[longest] = (where[longest] + shift) % result.shape[longest]
        spots.append(tuple(where))
    return result.at[spots[0]].set(low).at[spots[1]].set(largest)


def level_of(stream_key, shape, shards, least, largest):
    def one(axis_at, shards_of):
        draws = jax.random.uniform(jax.random.fold_in(jax.random.fold_in(stream_key, 6), axis_at), (shards_of,), jnp.float32, least / len(shards), largest / len(shards))
        return jnp.repeat(jnp.exp(draws), shape[axis_at] // shards_of).reshape((-1,) + (1,) * (len(shape) - axis_at - 1))

    factor_of = one(*shards[0])
    for cut in shards[1:]:
        factor_of = factor_of * one(*cut)
    return factor_of


def profile(number_of, total, most, lean):
    weights = [(1 << 20) // math.isqrt(rank ** lean) + 1 for rank in range(2, number_of + 1)]
    surplus, counts = total - most - (number_of - 1), [1] * (number_of - 1)
    while surplus > 0:
        movable = [i for i in range(number_of - 1) if counts[i] < most]
        pool, left = sum([weights[i] for i in movable]), surplus
        for i in movable:
            extra = min(most - counts[i], max(1, left * weights[i] // pool), surplus)
            counts[i] = counts[i] + extra
            surplus = surplus - extra
    return np.array([most] + counts)


def ragged(stream_key, amount, total, most, lean):
    if amount == 2:
        one = jax.random.randint(stream_key, (), max(1, total - most), min(most, total - 1) + 1)
        return jnp.stack([one, total - one])
    lengths = jnp.asarray(profile(amount, total, most, lean), jnp.int32)
    couples = (amount - 1) // 2
    source_of, sink = lengths[1:1 + 2 * couples:2], lengths[2:2 + 2 * couples:2]
    margin = jnp.minimum(source_of - 1, most - sink)
    passed = jax.random.randint(jax.random.fold_in(stream_key, 1), (couples,), 0, 1 << 20) % (margin + 1)
    lengths = lengths.at[1:1 + 2 * couples:2].set(source_of - passed).at[2:2 + 2 * couples:2].set(sink + passed)
    return lengths[jax.random.permutation(jax.random.fold_in(stream_key, 2), amount)]


def scatter_about(own_key, shape, width, limit, shards=(), kind=jnp.bfloat16):
    array = jax.random.normal(own_key, shape, jnp.float32) * width
    if len(shards) > 0:
        array = level_of(own_key, shape, shards, -0.22, 0.18) * array
    return jnp.clip(array, min=-limit, max=limit).astype(kind)


def setup_inputs(seed: int = 0) -> dict:
    seeds = jax.random.split(jax.random.key(seed), 7)
    return {
        "frames": scatter_about(seeds[0], (RUNS, FRAMES, MOB, CH), 1.0, 6.0, ((0, 4), (1, 32), (2, 2))),
        "templates": scatter_about(seeds[1], (PREC, CH), CH ** -0.5, 0.375, ((0, 32),)),
        "pair_block": set_ends(jax.random.randint(seeds[2], (N_SECTION, RUNS, N_DEV * SLOTS), 0, NB), jax.random.fold_in(seeds[2], 1), 0, NB - 1).astype(jnp.int32),
        "pair_tile": set_ends(jax.random.randint(seeds[3], (N_SECTION, RUNS, N_DEV * SLOTS), 0, NT), jax.random.fold_in(seeds[3], 1), 0, NT - 1).astype(jnp.int32),
        "pair_count": jax.vmap(lambda own: ragged(own, N_DEV, N_DEV * SLOTS // 2, SLOTS, 2))(jax.random.split(seeds[4], N_SECTION * RUNS)).reshape((N_SECTION, RUNS, N_DEV)).astype(jnp.int32),
        "owner_order": jax.random.permutation(seeds[5], PREC).astype(jnp.int32),
    }


retention_spread = 2.0

def retention_weights():
    bell_values = [math.exp(-0.5 * (offset / retention_spread) ** 2) for offset in range(-RAD, RAD + 1)]
    bell_total = sum(bell_values)
    return [weight_value / bell_total for weight_value in bell_values]

def mobility_kernels(row_start, row_count):
    row_place = (row_start + jnp.arange(row_count, dtype=jnp.int32)).astype(jnp.float32)
    col_place = jnp.arange(MOB, dtype=jnp.int32).astype(jnp.float32)
    distance = row_place[:, None] - col_place[None, :]
    tables = []
    for level in range(SCALES):
        spread_scans = 2.0 ** level
        scaled = distance / spread_scans
        tables.append((1.0 - scaled * scaled) * jnp.exp(-0.5 * scaled * scaled) / math.sqrt(0.75 * math.sqrt(math.pi) * spread_scans))
    return jnp.stack(tables).astype(jnp.bfloat16)

def smooth_frames(frames_run):
    weights = retention_weights()
    count_frames = frames_run.shape[0]
    padded = jnp.pad(frames_run.astype(jnp.float32), ((RAD, RAD), (0, 0), (0, 0)))
    smoothed = weights[0] * padded[0:count_frames]
    for offset in range(1, 2 * RAD + 1):
        smoothed = smoothed + weights[offset] * padded[offset:offset + count_frames]
    return smoothed.astype(jnp.bfloat16)

def run_quantities(frames_run, blocks_run, tiles_run, counts_run, templates):
    smoothed = smooth_frames(frames_run)
    columns = jnp.moveaxis(smoothed, 1, 0).reshape(MOB, FRAMES * CH)
    kernels = mobility_kernels(0, MOB)
    levels = []
    for level in range(SCALES):
        levels.append(jnp.dot(kernels[level], columns, preferred_element_type=jnp.float32).astype(jnp.bfloat16))
    wavelet_stack = jnp.stack(levels).reshape(SCALES, MOB, FRAMES, CH)
    mob_local = MOB // N_SECTION
    flat_blocks = blocks_run.reshape(-1)
    flat_tiles = tiles_run.reshape(-1)

    def visit_pair(totals, slot_index):
        half_index = slot_index // (N_DEV * SLOTS)
        device = slot_index // SLOTS % N_DEV
        within = slot_index % SLOTS
        live_pairs = counts_run[half_index, device]
        block_id = flat_blocks[slot_index]
        tile_id = flat_tiles[slot_index]
        mob_start = (half_index * mob_local + tile_id * TM).astype(jnp.int32)
        frame_start = (device * F_DEV).astype(jnp.int32)
        tile_cells = lax.dynamic_slice(wavelet_stack, (jnp.int32(0), mob_start, frame_start, jnp.int32(0)), (SCALES, TM, F_DEV, CH)).reshape(-1, CH)
        block_rows = lax.dynamic_slice_in_dim(templates, (block_id * PB).astype(jnp.int32), PB, 0)
        scores = jnp.dot(tile_cells, block_rows.T, preferred_element_type=jnp.float32)
        response = lax.optimization_barrier(jnp.mean(jnp.maximum(scores, 0.0), axis=0)) * (within < live_pairs).astype(jnp.float32)
        block_hit = (jnp.arange(NB, dtype=jnp.int32) == block_id).astype(jnp.float32)
        return (totals + block_hit[:, None] * response[None, :], None)
    totals = lax.scan(visit_pair, jnp.zeros((NB, PB), jnp.float32), jnp.arange(N_SECTION * N_DEV * SLOTS, dtype=jnp.int32))[0]
    return totals.reshape(PREC)

def reference(frames, templates, pair_block, pair_tile, pair_count, owner_order):
    rows_list = []
    for run_index in range(RUNS):
        quantity = run_quantities(frames[run_index], pair_block[:, run_index], pair_tile[:, run_index], pair_count[:, run_index], templates)
        rows_list.append(jnp.zeros((PREC,), jnp.float32).at[owner_order].set(quantity))
    placed = jnp.stack(rows_list)
    run_total = lax.optimization_barrier(jnp.sum(placed, axis=1))
    factor = jnp.mean(run_total) / run_total
    return placed * factor[:, None]
```

```python
import math

import jax
import jax.numpy as jnp
from jax import lax
from jax.experimental import pallas as pl
from jax.experimental.pallas import tpu as pltpu
from jax.sharding import PartitionSpec as P

MOB = 512
SCALES = 6
RAD = 4
TM = 64
PB = 128
PREC = 8192


retention_spread = 2.0


def extended(cells, sides, width):
    for axis, dim in sides:
        count = lax.axis_size(axis)
        ends = count - 1
        head = lax.slice_in_dim(cells, 0, width, axis=dim)
        tail = lax.slice_in_dim(cells, cells.shape[dim] - width, cells.shape[dim], axis=dim)
        cells = jnp.concatenate(
            [
                lax.ppermute(tail, axis, [(i, (i + 1) % count) for i in range(ends)]),
                cells,
                lax.ppermute(head, axis, [((i + 1) % count, i) for i in range(ends)]),
            ],
            axis=dim,
        )
    return cells


def retention_weights():
    bell_values = [
        math.exp(-0.5 * (offset / retention_spread) ** 2) for offset in range(-RAD, RAD + 1)
    ]
    bell_total = sum(bell_values)
    return [weight_value / bell_total for weight_value in bell_values]


def mobility_kernels(row_start, row_count):
    row_place = (row_start + jnp.arange(row_count, dtype=jnp.int32)).astype(jnp.float32)
    col_place = jnp.arange(MOB, dtype=jnp.int32).astype(jnp.float32)
    distance = row_place[:, None] - col_place[None, :]
    tables = []
    for level in range(SCALES):
        spread_scans = 2.0**level
        scaled = distance / spread_scans
        tables.append(
            (1.0 - scaled * scaled)
            * jnp.exp(-0.5 * scaled * scaled)
            / math.sqrt(0.75 * math.sqrt(math.pi) * spread_scans)
        )
    return jnp.stack(tables).astype(jnp.bfloat16)


def on_device(frames, templates, pair_block, pair_tile, pair_count, owner_order):
    section_index = lax.axis_index("section")
    weights = retention_weights()
    count_frames = frames.shape[1]
    mob_local = frames.shape[2]
    channels = frames.shape[3]
    framed = extended(frames, (("dev", 1),), RAD)
    padded = framed.astype(jnp.float32)
    smoothed = weights[0] * padded[:, 0:count_frames]
    for offset in range(1, 2 * RAD + 1):
        smoothed = smoothed + weights[offset] * padded[:, offset : offset + count_frames]
    smoothed = smoothed.astype(jnp.bfloat16)
    gathered = lax.all_gather(smoothed, "section", axis=2, tiled=True)
    kernels = mobility_kernels(section_index * mob_local, mob_local)
    wavelet_stack = jnp.einsum(
        "smn,fnc->sfmc", kernels, gathered[0], preferred_element_type=jnp.float32
    ).astype(jnp.bfloat16)
    template_panel = lax.all_gather(templates, "dev", axis=0, tiled=True)
    slots = pair_block.shape[2]
    live_pairs = pair_count[0, 0, 0]
    block_ids = pair_block[0, 0]
    tile_ids = pair_tile[0, 0]
    responses = score_pairs(wavelet_stack, template_panel, tile_ids, block_ids, live_pairs)
    precursors = block_ids[:, None] * PB + jnp.arange(PB, dtype=jnp.int32)[None, :]
    positions = owner_order[precursors]
    placed = jnp.zeros((PREC,), jnp.float32).at[positions.reshape(-1)].add(responses.reshape(-1))
    dev_count = lax.axis_size("dev")
    local_total = jnp.sum(responses)
    payload = jnp.concatenate(
        [
            placed.reshape(dev_count, PREC // dev_count),
            jnp.broadcast_to(local_total, (dev_count, 128)),
        ],
        axis=1,
    )
    reduced = lax.psum_scatter(payload, "dev", scatter_dimension=0, tiled=True)
    reduced = lax.psum(reduced, "section")
    owned = reduced[:, : PREC // dev_count]
    own_total = reduced[0, PREC // dev_count]
    run_totals = lax.all_gather(own_total, "grp")
    factor = jnp.mean(run_totals) / own_total
    return owned * factor


def score_kernel(tile_ref, block_ref, count_ref, wave_ref, rows_ref, out_ref):
    slot = pl.program_id(0)
    live = slot < count_ref[0]

    @pl.when(live)
    def _():
        rows = rows_ref[...]
        acc = jnp.zeros((1, PB), jnp.float32)
        for level in range(SCALES):
            cells = wave_ref[level].reshape(-1, rows.shape[1])
            scores = lax.dot_general(
                cells, rows, (((1,), (1,)), ((), ())), preferred_element_type=jnp.float32
            )
            acc = acc + jnp.sum(jnp.maximum(scores, 0.0), axis=0, keepdims=True)
        cell_count = SCALES * wave_ref.shape[1] * wave_ref.shape[2]
        out_ref[0] = acc / cell_count

    @pl.when(jnp.logical_not(live))
    def _():
        out_ref[0] = jnp.zeros((1, PB), jnp.float32)


def score_pairs(wavelet_stack, template_panel, tile_ids, block_ids, live_pairs):
    slots = tile_ids.shape[0]
    scales, frames_local, mob_local, channels = wavelet_stack.shape

    def last_live(k, count_ref):
        return jnp.minimum(k, count_ref[0] - 1)

    grid_spec = pltpu.PrefetchScalarGridSpec(
        num_scalar_prefetch=3,
        grid=(slots,),
        in_specs=[
            pl.BlockSpec(
                (scales, frames_local, TM, channels),
                lambda k, t, b, c: (0, 0, t[last_live(k, c)], 0),
            ),
            pl.BlockSpec((PB, channels), lambda k, t, b, c: (b[last_live(k, c)], 0)),
        ],
        out_specs=pl.BlockSpec((1, 1, PB), lambda k, t, b, c: (k, 0, 0)),
    )
    out = pl.pallas_call(
        score_kernel,
        grid_spec=grid_spec,
        out_shape=jax.ShapeDtypeStruct((slots, 1, PB), jnp.float32),
    )(tile_ids, block_ids, live_pairs.reshape(1), wavelet_stack, template_panel)
    return out.reshape(slots, PB)


def solution(mesh):
    placed = (
        P("grp", "dev", "section", None),
        P("dev", None),
        P("section", "grp", "dev"),
        P("section", "grp", "dev"),
        P("section", "grp", "dev"),
        P(),
    )
    return jax.shard_map(
        on_device, mesh=mesh, in_specs=placed, out_specs=P("grp", "dev"), check_vma=False
    )
```

```python
import functools
import math

import jax
import jax.numpy as jnp
from jax import lax
from jax.experimental import pallas as pl
from jax.experimental.pallas import tpu as pltpu
from jax.sharding import PartitionSpec as P

MOB = 512
SCALES = 6
RAD = 4
TM = 64
PB = 128
PREC = 8192


retention_spread = 2.0


def extended(cells, sides, width):
    for axis, dim in sides:
        count = lax.axis_size(axis)
        ends = count - 1
        head = lax.slice_in_dim(cells, 0, width, axis=dim)
        tail = lax.slice_in_dim(cells, cells.shape[dim] - width, cells.shape[dim], axis=dim)
        cells = jnp.concatenate(
            [
                lax.ppermute(tail, axis, [(i, (i + 1) % count) for i in range(ends)]),
                cells,
                lax.ppermute(head, axis, [((i + 1) % count, i) for i in range(ends)]),
            ],
            axis=dim,
        )
    return cells


def retention_weights():
    bell_values = [
        math.exp(-0.5 * (offset / retention_spread) ** 2) for offset in range(-RAD, RAD + 1)
    ]
    bell_total = sum(bell_values)
    return [weight_value / bell_total for weight_value in bell_values]


def mobility_kernels(row_start, row_count):
    row_place = (row_start + jnp.arange(row_count, dtype=jnp.int32)).astype(jnp.float32)
    col_place = jnp.arange(MOB, dtype=jnp.int32).astype(jnp.float32)
    distance = row_place[:, None] - col_place[None, :]
    tables = []
    for level in range(SCALES):
        spread_scans = 2.0**level
        scaled = distance / spread_scans
        tables.append(
            (1.0 - scaled * scaled)
            * jnp.exp(-0.5 * scaled * scaled)
            / math.sqrt(0.75 * math.sqrt(math.pi) * spread_scans)
        )
    return jnp.stack(tables).astype(jnp.bfloat16)


def on_device(frames, templates, pair_block, pair_tile, pair_count, owner_order):
    section_index = lax.axis_index("section")
    weights = retention_weights()
    count_frames = frames.shape[1]
    mob_local = frames.shape[2]
    channels = frames.shape[3]
    framed = extended(frames, (("dev", 1),), RAD)
    padded = framed.astype(jnp.float32)
    smoothed = weights[0] * padded[:, 0:count_frames]
    for offset in range(1, 2 * RAD + 1):
        smoothed = smoothed + weights[offset] * padded[:, offset : offset + count_frames]
    smoothed = smoothed.astype(jnp.bfloat16)
    gathered = lax.all_gather(smoothed, "section", axis=2, tiled=True)
    kernels = mobility_kernels(section_index * mob_local, mob_local)
    wavelet_stack = jnp.einsum(
        "smn,fnc->sfmc", kernels, gathered[0], preferred_element_type=jnp.float32
    ).astype(jnp.bfloat16)
    template_panel = lax.all_gather(templates, "dev", axis=0, tiled=True)
    slots = pair_block.shape[2]
    live_pairs = pair_count[0, 0, 0]
    block_ids = pair_block[0, 0]
    tile_ids = pair_tile[0, 0]
    responses = score_pairs(wavelet_stack, template_panel, tile_ids, block_ids, live_pairs)
    precursors = block_ids[:, None] * PB + jnp.arange(PB, dtype=jnp.int32)[None, :]
    positions = owner_order[precursors]
    placed = jnp.zeros((PREC,), jnp.float32).at[positions.reshape(-1)].add(responses.reshape(-1))
    dev_count = lax.axis_size("dev")
    local_total = jnp.sum(responses)
    payload = jnp.concatenate(
        [
            placed.reshape(dev_count, 1, PREC // dev_count),
            jnp.broadcast_to(local_total, (dev_count, 1, 128)),
        ],
        axis=2,
    )
    return reduce_owned(payload)


def reduce_kernel(sizes, payload_ref, out_ref, gathered, totals, send_sems, recv_sems, total_send, total_recv):
    n_section, n_grp, n_dev = sizes
    section = lax.axis_index("section")
    grp = lax.axis_index("grp")
    dev = lax.axis_index("dev")
    me = section * n_dev + dev
    peers = n_section * n_dev
    owned_width = out_ref.shape[1]

    barrier = pltpu.get_barrier_semaphore()

    def greet(index, carry):
        @pl.when(index != me)
        def _():
            pl.semaphore_signal(
                barrier,
                inc=1,
                device_id=(index // n_dev, grp, index % n_dev),
                device_id_type=pl.DeviceIdType.MESH,
            )

        return carry

    lax.fori_loop(0, peers, greet, 0)
    for step in range(1, n_grp):
        pl.semaphore_signal(
            barrier,
            inc=1,
            device_id=(section, (grp + step) % n_grp, dev),
            device_id_type=pl.DeviceIdType.MESH,
        )
    pl.semaphore_wait(barrier, peers - 1 + n_grp - 1)

    def chunk_copy(index):
        return pltpu.make_async_remote_copy(
            src_ref=payload_ref.at[index % n_dev],
            dst_ref=gathered.at[me],
            send_sem=send_sems.at[index],
            recv_sem=recv_sems.at[me],
            device_id=(index // n_dev, grp, index % n_dev),
            device_id_type=pl.DeviceIdType.MESH,
        )

    def send(index, carry):
        @pl.when(index != me)
        def _():
            chunk_copy(index).start()

        return carry

    lax.fori_loop(0, peers, send, 0)
    gathered[me] = payload_ref[dev]

    def arrive(index, carry):
        @pl.when(index != me)
        def _():
            pltpu.make_async_remote_copy(
                src_ref=payload_ref.at[0],
                dst_ref=gathered.at[index],
                send_sem=send_sems.at[index],
                recv_sem=recv_sems.at[index],
                device_id=(index // n_dev, grp, index % n_dev),
                device_id_type=pl.DeviceIdType.MESH,
            ).wait_recv()
            chunk_copy(index).wait_send()

        return carry

    lax.fori_loop(0, peers, arrive, 0)

    def accumulate(index, acc):
        return acc + gathered[index]

    summed = lax.fori_loop(0, peers, accumulate, jnp.zeros(gathered.shape[1:], jnp.float32))
    totals[grp] = summed[:, owned_width:]

    def total_copy(step):
        target = (grp + step) % n_grp
        return pltpu.make_async_remote_copy(
            src_ref=totals.at[grp],
            dst_ref=totals.at[grp],
            send_sem=total_send.at[target],
            recv_sem=total_recv.at[grp],
            device_id=(section, target, dev),
            device_id_type=pl.DeviceIdType.MESH,
        )

    for step in range(1, n_grp):
        total_copy(step).start()
    for step in range(1, n_grp):
        source = (grp + step) % n_grp
        pltpu.make_async_remote_copy(
            src_ref=totals.at[source],
            dst_ref=totals.at[source],
            send_sem=total_send.at[source],
            recv_sem=total_recv.at[source],
            device_id=(section, source, dev),
            device_id_type=pl.DeviceIdType.MESH,
        ).wait_recv()
        total_copy(step).wait_send()
    run_sum = totals[0]
    for index in range(1, n_grp):
        run_sum = run_sum + totals[index]
    own_total = summed[:, owned_width : owned_width + 1]
    factor = (run_sum[:, 0:1] / n_grp) / own_total
    out_ref[...] = summed[:, :owned_width] * factor


def reduce_owned(payload):
    sizes = (lax.axis_size("section"), lax.axis_size("grp"), lax.axis_size("dev"))
    n_section, n_grp, n_dev = sizes
    peers = n_section * n_dev
    rows, one, width = payload.shape
    owned_width = width - 128
    return pl.pallas_call(
        functools.partial(reduce_kernel, sizes),
        out_shape=jax.ShapeDtypeStruct((1, owned_width), jnp.float32),
        in_specs=[pl.BlockSpec(memory_space=pltpu.VMEM)],
        out_specs=pl.BlockSpec(memory_space=pltpu.VMEM),
        scratch_shapes=[
            pltpu.VMEM((peers, 1, width), jnp.float32),
            pltpu.VMEM((n_grp, 1, 128), jnp.float32),
            pltpu.SemaphoreType.DMA((peers,)),
            pltpu.SemaphoreType.DMA((peers,)),
            pltpu.SemaphoreType.DMA((n_grp,)),
            pltpu.SemaphoreType.DMA((n_grp,)),
        ],
        compiler_params=pltpu.CompilerParams(collective_id=0, has_side_effects=True),
    )(payload)


def score_kernel(tile_ref, block_ref, count_ref, wave_ref, rows_ref, out_ref):
    slot = pl.program_id(0)
    live = slot < count_ref[0]

    @pl.when(live)
    def _():
        rows = rows_ref[...]
        acc = jnp.zeros((1, PB), jnp.float32)
        for level in range(SCALES):
            cells = wave_ref[level].reshape(-1, rows.shape[1])
            scores = lax.dot_general(
                cells, rows, (((1,), (1,)), ((), ())), preferred_element_type=jnp.float32
            )
            acc = acc + jnp.sum(jnp.maximum(scores, 0.0), axis=0, keepdims=True)
        cell_count = SCALES * wave_ref.shape[1] * wave_ref.shape[2]
        out_ref[0] = acc / cell_count

    @pl.when(jnp.logical_not(live))
    def _():
        out_ref[0] = jnp.zeros((1, PB), jnp.float32)


def score_pairs(wavelet_stack, template_panel, tile_ids, block_ids, live_pairs):
    slots = tile_ids.shape[0]
    scales, frames_local, mob_local, channels = wavelet_stack.shape

    def last_live(k, count_ref):
        return jnp.minimum(k, count_ref[0] - 1)

    grid_spec = pltpu.PrefetchScalarGridSpec(
        num_scalar_prefetch=3,
        grid=(slots,),
        in_specs=[
            pl.BlockSpec(
                (scales, frames_local, TM, channels),
                lambda k, t, b, c: (0, 0, t[last_live(k, c)], 0),
            ),
            pl.BlockSpec((PB, channels), lambda k, t, b, c: (b[last_live(k, c)], 0)),
        ],
        out_specs=pl.BlockSpec((1, 1, PB), lambda k, t, b, c: (k, 0, 0)),
    )
    out = pl.pallas_call(
        score_kernel,
        grid_spec=grid_spec,
        out_shape=jax.ShapeDtypeStruct((slots, 1, PB), jnp.float32),
    )(tile_ids, block_ids, live_pairs.reshape(1), wavelet_stack, template_panel)
    return out.reshape(slots, PB)


def solution(mesh):
    placed = (
        P("grp", "dev", "section", None),
        P("dev", None),
        P("section", "grp", "dev"),
        P("section", "grp", "dev"),
        P("section", "grp", "dev"),
        P(),
    )
    return jax.shard_map(
        on_device, mesh=mesh, in_specs=placed, out_specs=P("grp", "dev"), check_vma=False
    )
```

```python
import functools
import math

import jax
import jax.numpy as jnp
from jax import lax
from jax.experimental import pallas as pl
from jax.experimental.pallas import tpu as pltpu
from jax.sharding import PartitionSpec as P

MOB = 512
SCALES = 6
RAD = 4
TM = 64
PB = 128
PREC = 8192


retention_spread = 2.0


def extended(cells, sides, width):
    for axis, dim in sides:
        count = lax.axis_size(axis)
        ends = count - 1
        head = lax.slice_in_dim(cells, 0, width, axis=dim)
        tail = lax.slice_in_dim(cells, cells.shape[dim] - width, cells.shape[dim], axis=dim)
        cells = jnp.concatenate(
            [
                lax.ppermute(tail, axis, [(i, (i + 1) % count) for i in range(ends)]),
                cells,
                lax.ppermute(head, axis, [((i + 1) % count, i) for i in range(ends)]),
            ],
            axis=dim,
        )
    return cells


def retention_weights():
    bell_values = [
        math.exp(-0.5 * (offset / retention_spread) ** 2) for offset in range(-RAD, RAD + 1)
    ]
    bell_total = sum(bell_values)
    return [weight_value / bell_total for weight_value in bell_values]


def mobility_kernels(row_start, row_count):
    row_place = (row_start + jnp.arange(row_count, dtype=jnp.int32)).astype(jnp.float32)
    col_place = jnp.arange(MOB, dtype=jnp.int32).astype(jnp.float32)
    distance = row_place[:, None] - col_place[None, :]
    tables = []
    for level in range(SCALES):
        spread_scans = 2.0**level
        scaled = distance / spread_scans
        tables.append(
            (1.0 - scaled * scaled)
            * jnp.exp(-0.5 * scaled * scaled)
            / math.sqrt(0.75 * math.sqrt(math.pi) * spread_scans)
        )
    return jnp.stack(tables).astype(jnp.bfloat16)


def on_device(frames, templates, pair_block, pair_tile, pair_count, owner_order):
    section_index = lax.axis_index("section")
    weights = retention_weights()
    count_frames = frames.shape[1]
    mob_local = frames.shape[2]
    channels = frames.shape[3]
    framed = extended(frames, (("dev", 1),), RAD)
    padded = framed.astype(jnp.float32)
    smoothed = weights[0] * padded[:, 0:count_frames]
    for offset in range(1, 2 * RAD + 1):
        smoothed = smoothed + weights[offset] * padded[:, offset : offset + count_frames]
    smoothed = smoothed.astype(jnp.bfloat16)
    section_count = lax.axis_size("section")
    partner = lax.ppermute(
        smoothed, "section", [(i, (i + 1) % section_count) for i in range(section_count)]
    )
    gathered = jnp.where(
        section_index == 0,
        jnp.concatenate([smoothed, partner], axis=2),
        jnp.concatenate([partner, smoothed], axis=2),
    )
    kernels = mobility_kernels(section_index * mob_local, mob_local)
    wavelet_stack = jnp.einsum(
        "smn,fnc->sfmc", kernels, gathered[0], preferred_element_type=jnp.float32
    ).astype(jnp.bfloat16)
    half_rows = templates.shape[0] // 2
    my_half = lax.dynamic_slice_in_dim(templates, section_index * half_rows, half_rows, 0)
    my_rows = lax.all_gather(my_half, "dev", axis=0, tiled=True)
    other_rows = lax.ppermute(
        my_rows, "section", [(i, (i + 1) % section_count) for i in range(section_count)]
    )
    slots = pair_block.shape[2]
    live_pairs = pair_count[0, 0, 0]
    block_ids = pair_block[0, 0]
    tile_ids = pair_tile[0, 0]
    responses = score_pairs(
        wavelet_stack, my_rows, other_rows, tile_ids, block_ids, live_pairs, section_index
    )
    precursors = block_ids[:, None] * PB + jnp.arange(PB, dtype=jnp.int32)[None, :]
    positions = owner_order[precursors]
    placed = jnp.zeros((PREC,), jnp.float32).at[positions.reshape(-1)].add(responses.reshape(-1))
    dev_count = lax.axis_size("dev")
    local_total = jnp.sum(responses)
    payload = jnp.concatenate(
        [
            placed.reshape(dev_count, 1, PREC // dev_count),
            jnp.broadcast_to(local_total, (dev_count, 1, 128)),
        ],
        axis=2,
    )
    return reduce_owned(payload)


def reduce_kernel(sizes, payload_ref, out_ref, gathered, totals, send_sems, recv_sems, total_send, total_recv):
    n_section, n_grp, n_dev = sizes
    section = lax.axis_index("section")
    grp = lax.axis_index("grp")
    dev = lax.axis_index("dev")
    me = section * n_dev + dev
    peers = n_section * n_dev
    owned_width = out_ref.shape[1]

    barrier = pltpu.get_barrier_semaphore()

    def greet(index, carry):
        @pl.when(index != me)
        def _():
            pl.semaphore_signal(
                barrier,
                inc=1,
                device_id=(index // n_dev, grp, index % n_dev),
                device_id_type=pl.DeviceIdType.MESH,
            )

        return carry

    lax.fori_loop(0, peers, greet, 0)
    for step in range(1, n_grp):
        pl.semaphore_signal(
            barrier,
            inc=1,
            device_id=(section, (grp + step) % n_grp, dev),
            device_id_type=pl.DeviceIdType.MESH,
        )
    pl.semaphore_wait(barrier, peers - 1 + n_grp - 1)

    def chunk_copy(index):
        return pltpu.make_async_remote_copy(
            src_ref=payload_ref.at[index % n_dev],
            dst_ref=gathered.at[me],
            send_sem=send_sems.at[index],
            recv_sem=recv_sems.at[me],
            device_id=(index // n_dev, grp, index % n_dev),
            device_id_type=pl.DeviceIdType.MESH,
        )

    def send(index, carry):
        @pl.when(index != me)
        def _():
            chunk_copy(index).start()

        return carry

    lax.fori_loop(0, peers, send, 0)
    gathered[me] = payload_ref[dev]

    def arrive(index, carry):
        @pl.when(index != me)
        def _():
            pltpu.make_async_remote_copy(
                src_ref=payload_ref.at[0],
                dst_ref=gathered.at[index],
                send_sem=send_sems.at[index],
                recv_sem=recv_sems.at[index],
                device_id=(index // n_dev, grp, index % n_dev),
                device_id_type=pl.DeviceIdType.MESH,
            ).wait_recv()
            chunk_copy(index).wait_send()

        return carry

    lax.fori_loop(0, peers, arrive, 0)

    def accumulate(index, acc):
        return acc + gathered[index]

    summed = lax.fori_loop(0, peers, accumulate, jnp.zeros(gathered.shape[1:], jnp.float32))
    totals[grp] = summed[:, owned_width:]

    def total_copy(step):
        target = (grp + step) % n_grp
        return pltpu.make_async_remote_copy(
            src_ref=totals.at[grp],
            dst_ref=totals.at[grp],
            send_sem=total_send.at[target],
            recv_sem=total_recv.at[grp],
            device_id=(section, target, dev),
            device_id_type=pl.DeviceIdType.MESH,
        )

    for step in range(1, n_grp):
        total_copy(step).start()
    for step in range(1, n_grp):
        source = (grp + step) % n_grp
        pltpu.make_async_remote_copy(
            src_ref=totals.at[source],
            dst_ref=totals.at[source],
            send_sem=total_send.at[source],
            recv_sem=total_recv.at[source],
            device_id=(section, source, dev),
            device_id_type=pl.DeviceIdType.MESH,
        ).wait_recv()
        total_copy(step).wait_send()
    run_sum = totals[0]
    for index in range(1, n_grp):
        run_sum = run_sum + totals[index]
    own_total = summed[:, owned_width : owned_width + 1]
    factor = (run_sum[:, 0:1] / n_grp) / own_total
    out_ref[...] = summed[:, :owned_width] * factor


def reduce_owned(payload):
    sizes = (lax.axis_size("section"), lax.axis_size("grp"), lax.axis_size("dev"))
    n_section, n_grp, n_dev = sizes
    peers = n_section * n_dev
    rows, one, width = payload.shape
    owned_width = width - 128
    return pl.pallas_call(
        functools.partial(reduce_kernel, sizes),
        out_shape=jax.ShapeDtypeStruct((1, owned_width), jnp.float32),
        in_specs=[pl.BlockSpec(memory_space=pltpu.VMEM)],
        out_specs=pl.BlockSpec(memory_space=pltpu.VMEM),
        scratch_shapes=[
            pltpu.VMEM((peers, 1, width), jnp.float32),
            pltpu.VMEM((n_grp, 1, 128), jnp.float32),
            pltpu.SemaphoreType.DMA((peers,)),
            pltpu.SemaphoreType.DMA((peers,)),
            pltpu.SemaphoreType.DMA((n_grp,)),
            pltpu.SemaphoreType.DMA((n_grp,)),
        ],
        compiler_params=pltpu.CompilerParams(collective_id=0, has_side_effects=True),
    )(payload)


def score_kernel(tile_ref, block_ref, count_ref, section_ref, wave_ref, mine_ref, other_ref, out_ref):
    slot = pl.program_id(0)
    live = slot < count_ref[0]
    mine = block_ref[slot] % 2 == section_ref[0]

    def score(rows_ref):
        rows = rows_ref[...]
        acc = jnp.zeros((1, PB), jnp.float32)
        for level in range(SCALES):
            cells = wave_ref[level].reshape(-1, rows.shape[1])
            scores = lax.dot_general(
                cells, rows, (((1,), (1,)), ((), ())), preferred_element_type=jnp.float32
            )
            acc = acc + jnp.sum(jnp.maximum(scores, 0.0), axis=0, keepdims=True)
        cell_count = SCALES * wave_ref.shape[1] * wave_ref.shape[2]
        out_ref[0] = acc / cell_count

    @pl.when(jnp.logical_and(live, mine))
    def _():
        score(mine_ref)

    @pl.when(jnp.logical_and(live, jnp.logical_not(mine)))
    def _():
        score(other_ref)

    @pl.when(jnp.logical_not(live))
    def _():
        out_ref[0] = jnp.zeros((1, PB), jnp.float32)


def score_pairs(wavelet_stack, my_rows, other_rows, tile_ids, block_ids, live_pairs, section_index):
    slots = tile_ids.shape[0]
    scales, frames_local, mob_local, channels = wavelet_stack.shape

    def last_live(k, count_ref):
        return jnp.minimum(k, count_ref[0] - 1)

    def rows_block(k, t, b, c, s):
        return (b[last_live(k, c)] // 2, 0)

    grid_spec = pltpu.PrefetchScalarGridSpec(
        num_scalar_prefetch=4,
        grid=(slots,),
        in_specs=[
            pl.BlockSpec(
                (scales, frames_local, TM, channels),
                lambda k, t, b, c, s: (0, 0, t[last_live(k, c)], 0),
            ),
            pl.BlockSpec((PB, channels), rows_block),
            pl.BlockSpec((PB, channels), rows_block),
        ],
        out_specs=pl.BlockSpec((1, 1, PB), lambda k, t, b, c, s: (k, 0, 0)),
    )
    out = pl.pallas_call(
        score_kernel,
        grid_spec=grid_spec,
        out_shape=jax.ShapeDtypeStruct((slots, 1, PB), jnp.float32),
    )(
        tile_ids,
        block_ids,
        live_pairs.reshape(1),
        section_index.astype(jnp.int32).reshape(1),
        wavelet_stack,
        my_rows,
        other_rows,
    )
    return out.reshape(slots, PB)


def solution(mesh):
    placed = (
        P("grp", "dev", "section", None),
        P("dev", None),
        P("section", "grp", "dev"),
        P("section", "grp", "dev"),
        P("section", "grp", "dev"),
        P(),
    )
    return jax.shard_map(
        on_device, mesh=mesh, in_specs=placed, out_specs=P("grp", "dev"), check_vma=False
    )
```

```python
import functools
import math

import jax
import jax.numpy as jnp
from jax import lax
from jax.experimental import pallas as pl
from jax.experimental.pallas import tpu as pltpu
from jax.sharding import PartitionSpec as P

MOB = 512
SCALES = 6
RAD = 4
TM = 64
PB = 128
PREC = 8192
DEV = ("dy", "dz")


retention_spread = 2.0


def extended(cells, sides, width):
    for axis, dim in sides:
        count = lax.axis_size(axis)
        ends = count - 1
        head = lax.slice_in_dim(cells, 0, width, axis=dim)
        tail = lax.slice_in_dim(cells, cells.shape[dim] - width, cells.shape[dim], axis=dim)
        cells = jnp.concatenate(
            [
                lax.ppermute(tail, axis, [(i, (i + 1) % count) for i in range(ends)]),
                cells,
                lax.ppermute(head, axis, [((i + 1) % count, i) for i in range(ends)]),
            ],
            axis=dim,
        )
    return cells


def retention_weights():
    bell_values = [
        math.exp(-0.5 * (offset / retention_spread) ** 2) for offset in range(-RAD, RAD + 1)
    ]
    bell_total = sum(bell_values)
    return [weight_value / bell_total for weight_value in bell_values]


def mobility_kernels(row_start, row_count, col_start):
    row_place = (row_start + jnp.arange(row_count, dtype=jnp.int32)).astype(jnp.float32)
    col_place = ((col_start + jnp.arange(MOB, dtype=jnp.int32)) % MOB).astype(jnp.float32)
    distance = row_place[:, None] - col_place[None, :]
    tables = []
    for level in range(SCALES):
        spread_scans = 2.0**level
        scaled = distance / spread_scans
        tables.append(
            (1.0 - scaled * scaled)
            * jnp.exp(-0.5 * scaled * scaled)
            / math.sqrt(0.75 * math.sqrt(math.pi) * spread_scans)
        )
    return jnp.stack(tables).astype(jnp.bfloat16)


def on_device(frames, templates, pair_block, pair_tile, pair_count, owner_order):
    section_index = lax.axis_index("section")
    weights = retention_weights()
    count_frames = frames.shape[1]
    mob_local = frames.shape[2]
    channels = frames.shape[3]
    framed = extended(frames, ((DEV, 1),), RAD)
    padded = framed.astype(jnp.float32)
    smoothed = weights[0] * padded[:, 0:count_frames]
    for offset in range(1, 2 * RAD + 1):
        smoothed = smoothed + weights[offset] * padded[:, offset : offset + count_frames]
    smoothed = smoothed.astype(jnp.bfloat16)
    section_count = lax.axis_size("section")
    partner = lax.ppermute(
        smoothed, "section", [(i, (i + 1) % section_count) for i in range(section_count)]
    )
    gathered = jnp.concatenate([smoothed, partner], axis=2)
    kernels = mobility_kernels(section_index * mob_local, mob_local, section_index * mob_local)
    wavelet_stack = jnp.einsum(
        "smn,fnc->sfmc", kernels, gathered[0], preferred_element_type=jnp.float32
    ).astype(jnp.bfloat16)
    half_rows = templates.shape[0] // 2
    my_half = lax.dynamic_slice_in_dim(templates, section_index * half_rows, half_rows, 0)
    my_rows = lax.all_gather(my_half, "dz", axis=0, tiled=True)
    my_rows = lax.all_gather(my_rows, "dy", axis=0, tiled=True)
    other_rows = lax.ppermute(
        my_rows, "section", [(i, (i + 1) % section_count) for i in range(section_count)]
    )
    slots = pair_block.shape[2]
    live_pairs = pair_count[0, 0, 0]
    block_ids = pair_block[0, 0]
    tile_ids = pair_tile[0, 0]
    responses = score_pairs(
        wavelet_stack, my_rows, other_rows, tile_ids, block_ids, live_pairs, section_index
    )
    precursors = block_ids[:, None] * PB + jnp.arange(PB, dtype=jnp.int32)[None, :]
    positions = owner_order[precursors]
    placed = jnp.zeros((PREC,), jnp.float32).at[positions.reshape(-1)].add(responses.reshape(-1))
    dev_count = lax.axis_size(DEV)
    local_total = jnp.sum(responses)
    payload = jnp.concatenate(
        [
            placed.reshape(dev_count, 1, PREC // dev_count),
            jnp.broadcast_to(local_total, (dev_count, 1, 128)),
        ],
        axis=2,
    )
    return reduce_owned(payload)


def reduce_kernel(sizes, payload_ref, out_ref, gathered, totals, send_sems, recv_sems, total_send, total_recv):
    n_section, n_grp, n_dy, n_dz = sizes
    n_dev = n_dy * n_dz
    section = lax.axis_index("section")
    grp = lax.axis_index("grp")
    dy = lax.axis_index("dy")
    dz = lax.axis_index("dz")
    dev = dy * n_dz + dz
    me = section * n_dev + dev
    peers = n_section * n_dev
    owned_width = out_ref.shape[1]

    barrier = pltpu.get_barrier_semaphore()

    def greet(index, carry):
        @pl.when(index != me)
        def _():
            pl.semaphore_signal(
                barrier,
                inc=1,
                device_id=(index // n_dev, grp, index % n_dev // n_dz, index % n_dz),
                device_id_type=pl.DeviceIdType.MESH,
            )

        return carry

    lax.fori_loop(0, peers, greet, 0)
    for step in range(1, n_grp):
        pl.semaphore_signal(
            barrier,
            inc=1,
            device_id=(section, (grp + step) % n_grp, dy, dz),
            device_id_type=pl.DeviceIdType.MESH,
        )
    pl.semaphore_wait(barrier, peers - 1 + n_grp - 1)

    def chunk_copy(index):
        return pltpu.make_async_remote_copy(
            src_ref=payload_ref.at[index % n_dev],
            dst_ref=gathered.at[me],
            send_sem=send_sems.at[index],
            recv_sem=recv_sems.at[me],
            device_id=(index // n_dev, grp, index % n_dev // n_dz, index % n_dz),
            device_id_type=pl.DeviceIdType.MESH,
        )

    def send(index, carry):
        @pl.when(index != me)
        def _():
            chunk_copy(index).start()

        return carry

    lax.fori_loop(0, peers, send, 0)
    gathered[me] = payload_ref[dev]

    def arrive(index, carry):
        @pl.when(index != me)
        def _():
            pltpu.make_async_remote_copy(
                src_ref=payload_ref.at[0],
                dst_ref=gathered.at[index],
                send_sem=send_sems.at[index],
                recv_sem=recv_sems.at[index],
                device_id=(index // n_dev, grp, index % n_dev // n_dz, index % n_dz),
                device_id_type=pl.DeviceIdType.MESH,
            ).wait_recv()
            chunk_copy(index).wait_send()

        return carry

    lax.fori_loop(0, peers, arrive, 0)

    def accumulate(index, acc):
        return acc + gathered[index]

    summed = lax.fori_loop(0, peers, accumulate, jnp.zeros(gathered.shape[1:], jnp.float32))
    totals[grp] = summed[:, owned_width:]

    def total_copy(step):
        target = (grp + step) % n_grp
        return pltpu.make_async_remote_copy(
            src_ref=totals.at[grp],
            dst_ref=totals.at[grp],
            send_sem=total_send.at[target],
            recv_sem=total_recv.at[grp],
            device_id=(section, target, dy, dz),
            device_id_type=pl.DeviceIdType.MESH,
        )

    for step in range(1, n_grp):
        total_copy(step).start()
    for step in range(1, n_grp):
        source = (grp + step) % n_grp
        pltpu.make_async_remote_copy(
            src_ref=totals.at[source],
            dst_ref=totals.at[source],
            send_sem=total_send.at[source],
            recv_sem=total_recv.at[source],
            device_id=(section, source, dy, dz),
            device_id_type=pl.DeviceIdType.MESH,
        ).wait_recv()
        total_copy(step).wait_send()
    run_sum = totals[0]
    for index in range(1, n_grp):
        run_sum = run_sum + totals[index]
    own_total = summed[:, owned_width : owned_width + 1]
    factor = (run_sum[:, 0:1] / n_grp) / own_total
    out_ref[...] = summed[:, :owned_width] * factor


def reduce_owned(payload):
    sizes = (lax.axis_size("section"), lax.axis_size("grp"), lax.axis_size("dy"), lax.axis_size("dz"))
    n_section, n_grp, n_dy, n_dz = sizes
    peers = n_section * n_dy * n_dz
    rows, one, width = payload.shape
    owned_width = width - 128
    return pl.pallas_call(
        functools.partial(reduce_kernel, sizes),
        out_shape=jax.ShapeDtypeStruct((1, owned_width), jnp.float32),
        in_specs=[pl.BlockSpec(memory_space=pltpu.VMEM)],
        out_specs=pl.BlockSpec(memory_space=pltpu.VMEM),
        scratch_shapes=[
            pltpu.VMEM((peers, 1, width), jnp.float32),
            pltpu.VMEM((n_grp, 1, 128), jnp.float32),
            pltpu.SemaphoreType.DMA((peers,)),
            pltpu.SemaphoreType.DMA((peers,)),
            pltpu.SemaphoreType.DMA((n_grp,)),
            pltpu.SemaphoreType.DMA((n_grp,)),
        ],
        compiler_params=pltpu.CompilerParams(collective_id=0, has_side_effects=True),
    )(payload)


def score_kernel(tile_ref, block_ref, count_ref, section_ref, wave_ref, mine_ref, other_ref, out_ref):
    slot = pl.program_id(0)
    live = slot < count_ref[0]
    mine = block_ref[slot] % 2 == section_ref[0]

    def score(rows_ref):
        rows = rows_ref[...]
        acc = jnp.zeros((1, PB), jnp.float32)
        for level in range(SCALES):
            cells = wave_ref[level].reshape(-1, rows.shape[1])
            scores = lax.dot_general(
                cells, rows, (((1,), (1,)), ((), ())), preferred_element_type=jnp.float32
            )
            acc = acc + jnp.sum(jnp.maximum(scores, 0.0), axis=0, keepdims=True)
        cell_count = SCALES * wave_ref.shape[1] * wave_ref.shape[2]
        out_ref[0] = acc / cell_count

    @pl.when(jnp.logical_and(live, mine))
    def _():
        score(mine_ref)

    @pl.when(jnp.logical_and(live, jnp.logical_not(mine)))
    def _():
        score(other_ref)

    @pl.when(jnp.logical_not(live))
    def _():
        out_ref[0] = jnp.zeros((1, PB), jnp.float32)


def score_pairs(wavelet_stack, my_rows, other_rows, tile_ids, block_ids, live_pairs, section_index):
    slots = tile_ids.shape[0]
    scales, frames_local, mob_local, channels = wavelet_stack.shape

    def last_live(k, count_ref):
        return jnp.minimum(k, count_ref[0] - 1)

    def rows_block(k, t, b, c, s):
        return (b[last_live(k, c)] // 2, 0)

    grid_spec = pltpu.PrefetchScalarGridSpec(
        num_scalar_prefetch=4,
        grid=(slots,),
        in_specs=[
            pl.BlockSpec(
                (scales, frames_local, TM, channels),
                lambda k, t, b, c, s: (0, 0, t[last_live(k, c)], 0),
            ),
            pl.BlockSpec((PB, channels), rows_block),
            pl.BlockSpec((PB, channels), rows_block),
        ],
        out_specs=pl.BlockSpec((1, 1, PB), lambda k, t, b, c, s: (k, 0, 0)),
    )
    out = pl.pallas_call(
        score_kernel,
        grid_spec=grid_spec,
        out_shape=jax.ShapeDtypeStruct((slots, 1, PB), jnp.float32),
    )(
        tile_ids,
        block_ids,
        live_pairs.reshape(1),
        section_index.astype(jnp.int32).reshape(1),
        wavelet_stack,
        my_rows,
        other_rows,
    )
    return out.reshape(slots, PB)


def solution(mesh):
    section_count, grp_count, dev_count = mesh.devices.shape
    dz_count = 8 if dev_count % 8 == 0 else dev_count
    split_mesh = jax.sharding.Mesh(
        mesh.devices.reshape(section_count, grp_count, dev_count // dz_count, dz_count),
        ("section", "grp", "dy", "dz"),
    )
    placed = (
        P("grp", DEV, "section", None),
        P(DEV, None),
        P("section", "grp", DEV),
        P("section", "grp", DEV),
        P("section", "grp", DEV),
        P(),
    )
    return jax.shard_map(
        on_device, mesh=split_mesh, in_specs=placed, out_specs=P("grp", DEV), check_vma=False
    )
```

```python
import functools
import math

import jax
import jax.numpy as jnp
from jax import lax
from jax.experimental import pallas as pl
from jax.experimental.pallas import tpu as pltpu
from jax.sharding import PartitionSpec as P

MOB = 512
SCALES = 6
RAD = 4
TM = 64
PB = 128
PREC = 8192
DEV = ("dy", "dz")


retention_spread = 2.0


def extended(cells, sides, width):
    for axis, dim in sides:
        count = lax.axis_size(axis)
        ends = count - 1
        head = lax.slice_in_dim(cells, 0, width, axis=dim)
        tail = lax.slice_in_dim(cells, cells.shape[dim] - width, cells.shape[dim], axis=dim)
        cells = jnp.concatenate(
            [
                lax.ppermute(tail, axis, [(i, (i + 1) % count) for i in range(ends)]),
                cells,
                lax.ppermute(head, axis, [((i + 1) % count, i) for i in range(ends)]),
            ],
            axis=dim,
        )
    return cells


def retention_weights():
    bell_values = [
        math.exp(-0.5 * (offset / retention_spread) ** 2) for offset in range(-RAD, RAD + 1)
    ]
    bell_total = sum(bell_values)
    return [weight_value / bell_total for weight_value in bell_values]


def mobility_kernels(row_start, row_count, col_start):
    row_place = (row_start + jnp.arange(row_count, dtype=jnp.int32)).astype(jnp.float32)
    col_place = ((col_start + jnp.arange(MOB, dtype=jnp.int32)) % MOB).astype(jnp.float32)
    distance = row_place[:, None] - col_place[None, :]
    tables = []
    for level in range(SCALES):
        spread_scans = 2.0**level
        scaled = distance / spread_scans
        tables.append(
            (1.0 - scaled * scaled)
            * jnp.exp(-0.5 * scaled * scaled)
            / math.sqrt(0.75 * math.sqrt(math.pi) * spread_scans)
        )
    return jnp.stack(tables).astype(jnp.bfloat16)


def on_device(frames, templates, pair_block, pair_tile, pair_count, owner_order):
    section_index = lax.axis_index("section")
    weights = retention_weights()
    count_frames = frames.shape[1]
    mob_local = frames.shape[2]
    channels = frames.shape[3]
    framed = extended(frames, ((DEV, 1),), RAD)
    padded = framed.astype(jnp.float32)
    smoothed = weights[0] * padded[:, 0:count_frames]
    for offset in range(1, 2 * RAD + 1):
        smoothed = smoothed + weights[offset] * padded[:, offset : offset + count_frames]
    smoothed = smoothed.astype(jnp.bfloat16)
    section_count = lax.axis_size("section")
    partner = lax.ppermute(
        smoothed, "section", [(i, (i + 1) % section_count) for i in range(section_count)]
    )
    gathered = jnp.concatenate([smoothed, partner], axis=2)
    kernels = mobility_kernels(section_index * mob_local, mob_local, section_index * mob_local)
    wavelet_stack = jnp.einsum(
        "smn,fnc->sfmc", kernels, gathered[0], preferred_element_type=jnp.float32
    ).astype(jnp.bfloat16)
    half_rows = templates.shape[0] // 2
    my_half = lax.dynamic_slice_in_dim(templates, section_index * half_rows, half_rows, 0)
    my_rows = gather_rows(my_half)
    other_rows = lax.ppermute(
        my_rows, "section", [(i, (i + 1) % section_count) for i in range(section_count)]
    )
    slots = pair_block.shape[2]
    live_pairs = pair_count[0, 0, 0]
    block_ids = pair_block[0, 0]
    tile_ids = pair_tile[0, 0]
    responses = score_pairs(
        wavelet_stack, my_rows, other_rows, tile_ids, block_ids, live_pairs, section_index
    )
    precursors = block_ids[:, None] * PB + jnp.arange(PB, dtype=jnp.int32)[None, :]
    positions = owner_order[precursors]
    placed = jnp.zeros((PREC,), jnp.float32).at[positions.reshape(-1)].add(responses.reshape(-1))
    dev_count = lax.axis_size(DEV)
    local_total = jnp.sum(responses)
    payload = jnp.concatenate(
        [
            placed.reshape(dev_count, 1, PREC // dev_count),
            jnp.broadcast_to(local_total, (dev_count, 1, 128)),
        ],
        axis=2,
    )
    return reduce_owned(payload)


def reduce_kernel(sizes, payload_ref, out_ref, gathered, totals, send_sems, recv_sems, total_send, total_recv):
    n_section, n_grp, n_dy, n_dz = sizes
    n_dev = n_dy * n_dz
    section = lax.axis_index("section")
    grp = lax.axis_index("grp")
    dy = lax.axis_index("dy")
    dz = lax.axis_index("dz")
    dev = dy * n_dz + dz
    me = section * n_dev + dev
    peers = n_section * n_dev
    owned_width = out_ref.shape[1]

    barrier = pltpu.get_barrier_semaphore()

    def greet(index, carry):
        @pl.when(index != me)
        def _():
            pl.semaphore_signal(
                barrier,
                inc=1,
                device_id=(index // n_dev, grp, index % n_dev // n_dz, index % n_dz),
                device_id_type=pl.DeviceIdType.MESH,
            )

        return carry

    lax.fori_loop(0, peers, greet, 0)
    for step in range(1, n_grp):
        pl.semaphore_signal(
            barrier,
            inc=1,
            device_id=(section, (grp + step) % n_grp, dy, dz),
            device_id_type=pl.DeviceIdType.MESH,
        )
    pl.semaphore_wait(barrier, peers - 1 + n_grp - 1)

    def chunk_copy(index):
        return pltpu.make_async_remote_copy(
            src_ref=payload_ref.at[index % n_dev],
            dst_ref=gathered.at[me],
            send_sem=send_sems.at[index],
            recv_sem=recv_sems.at[me],
            device_id=(index // n_dev, grp, index % n_dev // n_dz, index % n_dz),
            device_id_type=pl.DeviceIdType.MESH,
        )

    def send(index, carry):
        @pl.when(index != me)
        def _():
            chunk_copy(index).start()

        return carry

    lax.fori_loop(0, peers, send, 0)
    gathered[me] = payload_ref[dev]

    def arrive(index, carry):
        @pl.when(index != me)
        def _():
            pltpu.make_async_remote_copy(
                src_ref=payload_ref.at[0],
                dst_ref=gathered.at[index],
                send_sem=send_sems.at[index],
                recv_sem=recv_sems.at[index],
                device_id=(index // n_dev, grp, index % n_dev // n_dz, index % n_dz),
                device_id_type=pl.DeviceIdType.MESH,
            ).wait_recv()
            chunk_copy(index).wait_send()

        return carry

    lax.fori_loop(0, peers, arrive, 0)

    def accumulate(index, acc):
        return acc + gathered[index]

    summed = lax.fori_loop(0, peers, accumulate, jnp.zeros(gathered.shape[1:], jnp.float32))
    totals[grp] = summed[:, owned_width:]

    def total_copy(step):
        target = (grp + step) % n_grp
        return pltpu.make_async_remote_copy(
            src_ref=totals.at[grp],
            dst_ref=totals.at[grp],
            send_sem=total_send.at[target],
            recv_sem=total_recv.at[grp],
            device_id=(section, target, dy, dz),
            device_id_type=pl.DeviceIdType.MESH,
        )

    for step in range(1, n_grp):
        total_copy(step).start()
    for step in range(1, n_grp):
        source = (grp + step) % n_grp
        pltpu.make_async_remote_copy(
            src_ref=totals.at[source],
            dst_ref=totals.at[source],
            send_sem=total_send.at[source],
            recv_sem=total_recv.at[source],
            device_id=(section, source, dy, dz),
            device_id_type=pl.DeviceIdType.MESH,
        ).wait_recv()
        total_copy(step).wait_send()
    run_sum = totals[0]
    for index in range(1, n_grp):
        run_sum = run_sum + totals[index]
    own_total = summed[:, owned_width : owned_width + 1]
    factor = (run_sum[:, 0:1] / n_grp) / own_total
    out_ref[...] = summed[:, :owned_width] * factor


def reduce_owned(payload):
    sizes = (lax.axis_size("section"), lax.axis_size("grp"), lax.axis_size("dy"), lax.axis_size("dz"))
    n_section, n_grp, n_dy, n_dz = sizes
    peers = n_section * n_dy * n_dz
    rows, one, width = payload.shape
    owned_width = width - 128
    return pl.pallas_call(
        functools.partial(reduce_kernel, sizes),
        out_shape=jax.ShapeDtypeStruct((1, owned_width), jnp.float32),
        in_specs=[pl.BlockSpec(memory_space=pltpu.VMEM)],
        out_specs=pl.BlockSpec(memory_space=pltpu.VMEM),
        scratch_shapes=[
            pltpu.VMEM((peers, 1, width), jnp.float32),
            pltpu.VMEM((n_grp, 1, 128), jnp.float32),
            pltpu.SemaphoreType.DMA((peers,)),
            pltpu.SemaphoreType.DMA((peers,)),
            pltpu.SemaphoreType.DMA((n_grp,)),
            pltpu.SemaphoreType.DMA((n_grp,)),
        ],
        compiler_params=pltpu.CompilerParams(collective_id=0, has_side_effects=True),
    )(payload)


def gather_kernel(sizes, half_ref, out_ref, own_sem, z_send, z_recv, y_send, y_recv):
    n_dy, n_dz = sizes
    section = lax.axis_index("section")
    grp = lax.axis_index("grp")
    dy = lax.axis_index("dy")
    dz = lax.axis_index("dz")
    dev = dy * n_dz + dz

    barrier = pltpu.get_barrier_semaphore()
    for step in range(1, n_dz):
        pl.semaphore_signal(
            barrier,
            inc=1,
            device_id=(section, grp, dy, (dz + step) % n_dz),
            device_id_type=pl.DeviceIdType.MESH,
        )
    for step in range(1, n_dy):
        pl.semaphore_signal(
            barrier,
            inc=1,
            device_id=(section, grp, (dy + step) % n_dy, dz),
            device_id_type=pl.DeviceIdType.MESH,
        )
    pl.semaphore_wait(barrier, n_dz - 1 + n_dy - 1)

    own = pltpu.make_async_copy(half_ref, out_ref.at[dev], own_sem)
    own.start()

    def z_copy(target, source):
        return pltpu.make_async_remote_copy(
            src_ref=half_ref,
            dst_ref=out_ref.at[dy * n_dz + source],
            send_sem=z_send.at[target],
            recv_sem=z_recv.at[source],
            device_id=(section, grp, dy, target),
            device_id_type=pl.DeviceIdType.MESH,
        )

    for step in range(1, n_dz):
        z_copy((dz + step) % n_dz, dz).start()
    own.wait()
    for step in range(1, n_dz):
        source = (dz + n_dz - step) % n_dz
        z_copy(source, source).wait_recv()
    for step in range(1, n_dz):
        z_copy((dz + step) % n_dz, dz).wait_send()

    def y_copy(target, source):
        return pltpu.make_async_remote_copy(
            src_ref=out_ref.at[pl.ds(source * n_dz, n_dz)],
            dst_ref=out_ref.at[pl.ds(source * n_dz, n_dz)],
            send_sem=y_send.at[target],
            recv_sem=y_recv.at[source],
            device_id=(section, grp, target, dz),
            device_id_type=pl.DeviceIdType.MESH,
        )

    for step in range(1, n_dy):
        y_copy((dy + step) % n_dy, dy).start()
    for step in range(1, n_dy):
        source = (dy + n_dy - step) % n_dy
        y_copy(source, source).wait_recv()
    for step in range(1, n_dy):
        y_copy((dy + step) % n_dy, dy).wait_send()


def gather_rows(half):
    sizes = (lax.axis_size("dy"), lax.axis_size("dz"))
    n_dy, n_dz = sizes
    rows, channels = half.shape
    out = pl.pallas_call(
        functools.partial(gather_kernel, sizes),
        out_shape=jax.ShapeDtypeStruct((n_dy * n_dz, rows, channels), half.dtype),
        in_specs=[pl.BlockSpec(memory_space=pltpu.VMEM)],
        out_specs=pl.BlockSpec(memory_space=pltpu.VMEM),
        scratch_shapes=[
            pltpu.SemaphoreType.DMA(()),
            pltpu.SemaphoreType.DMA((n_dz,)),
            pltpu.SemaphoreType.DMA((n_dz,)),
            pltpu.SemaphoreType.DMA((n_dy,)),
            pltpu.SemaphoreType.DMA((n_dy,)),
        ],
        compiler_params=pltpu.CompilerParams(collective_id=1, has_side_effects=True),
    )(half)
    return out.reshape(n_dy * n_dz * rows, channels)


def score_kernel(tile_ref, block_ref, count_ref, section_ref, wave_ref, mine_ref, other_ref, out_ref):
    slot = pl.program_id(0)
    live = slot < count_ref[0]
    mine = block_ref[slot] % 2 == section_ref[0]

    def score(rows_ref):
        rows = rows_ref[...]
        acc = jnp.zeros((1, PB), jnp.float32)
        for level in range(SCALES):
            cells = wave_ref[level].reshape(-1, rows.shape[1])
            scores = lax.dot_general(
                cells, rows, (((1,), (1,)), ((), ())), preferred_element_type=jnp.float32
            )
            acc = acc + jnp.sum(jnp.maximum(scores, 0.0), axis=0, keepdims=True)
        cell_count = SCALES * wave_ref.shape[1] * wave_ref.shape[2]
        out_ref[0] = acc / cell_count

    @pl.when(jnp.logical_and(live, mine))
    def _():
        score(mine_ref)

    @pl.when(jnp.logical_and(live, jnp.logical_not(mine)))
    def _():
        score(other_ref)

    @pl.when(jnp.logical_not(live))
    def _():
        out_ref[0] = jnp.zeros((1, PB), jnp.float32)


def score_pairs(wavelet_stack, my_rows, other_rows, tile_ids, block_ids, live_pairs, section_index):
    slots = tile_ids.shape[0]
    scales, frames_local, mob_local, channels = wavelet_stack.shape

    def last_live(k, count_ref):
        return jnp.minimum(k, count_ref[0] - 1)

    def rows_block(k, t, b, c, s):
        return (b[last_live(k, c)] // 2, 0)

    grid_spec = pltpu.PrefetchScalarGridSpec(
        num_scalar_prefetch=4,
        grid=(slots,),
        in_specs=[
            pl.BlockSpec(
                (scales, frames_local, TM, channels),
                lambda k, t, b, c, s: (0, 0, t[last_live(k, c)], 0),
            ),
            pl.BlockSpec((PB, channels), rows_block),
            pl.BlockSpec((PB, channels), rows_block),
        ],
        out_specs=pl.BlockSpec((1, 1, PB), lambda k, t, b, c, s: (k, 0, 0)),
    )
    out = pl.pallas_call(
        score_kernel,
        grid_spec=grid_spec,
        out_shape=jax.ShapeDtypeStruct((slots, 1, PB), jnp.float32),
    )(
        tile_ids,
        block_ids,
        live_pairs.reshape(1),
        section_index.astype(jnp.int32).reshape(1),
        wavelet_stack,
        my_rows,
        other_rows,
    )
    return out.reshape(slots, PB)


def solution(mesh):
    section_count, grp_count, dev_count = mesh.devices.shape
    dz_count = 8 if dev_count % 8 == 0 else dev_count
    split_mesh = jax.sharding.Mesh(
        mesh.devices.reshape(section_count, grp_count, dev_count // dz_count, dz_count),
        ("section", "grp", "dy", "dz"),
    )
    placed = (
        P("grp", DEV, "section", None),
        P(DEV, None),
        P("section", "grp", DEV),
        P("section", "grp", DEV),
        P("section", "grp", DEV),
        P(),
    )
    return jax.shard_map(
        on_device, mesh=split_mesh, in_specs=placed, out_specs=P("grp", DEV), check_vma=False
    )
```

```python
import functools
import math

import jax
import jax.numpy as jnp
from jax import lax
from jax.experimental import pallas as pl
from jax.experimental.pallas import tpu as pltpu
from jax.sharding import PartitionSpec as P

MOB = 512
SCALES = 6
RAD = 4
TM = 64
PB = 128
PREC = 8192
DEV = ("dy", "dz")


retention_spread = 2.0


def extended(cells, sides, width):
    for axis, dim in sides:
        count = lax.axis_size(axis)
        ends = count - 1
        head = lax.slice_in_dim(cells, 0, width, axis=dim)
        tail = lax.slice_in_dim(cells, cells.shape[dim] - width, cells.shape[dim], axis=dim)
        cells = jnp.concatenate(
            [
                lax.ppermute(tail, axis, [(i, (i + 1) % count) for i in range(ends)]),
                cells,
                lax.ppermute(head, axis, [((i + 1) % count, i) for i in range(ends)]),
            ],
            axis=dim,
        )
    return cells


def retention_weights():
    bell_values = [
        math.exp(-0.5 * (offset / retention_spread) ** 2) for offset in range(-RAD, RAD + 1)
    ]
    bell_total = sum(bell_values)
    return [weight_value / bell_total for weight_value in bell_values]


def mobility_kernels(row_start, row_count, col_start):
    row_place = (row_start + jnp.arange(row_count, dtype=jnp.int32)).astype(jnp.float32)
    col_place = ((col_start + jnp.arange(MOB, dtype=jnp.int32)) % MOB).astype(jnp.float32)
    distance = row_place[:, None] - col_place[None, :]
    tables = []
    for level in range(SCALES):
        spread_scans = 2.0**level
        scaled = distance / spread_scans
        tables.append(
            (1.0 - scaled * scaled)
            * jnp.exp(-0.5 * scaled * scaled)
            / math.sqrt(0.75 * math.sqrt(math.pi) * spread_scans)
        )
    return jnp.stack(tables).astype(jnp.bfloat16)


def on_device(frames, templates, pair_block, pair_tile, pair_count, owner_order):
    section_index = lax.axis_index("section")
    weights = retention_weights()
    count_frames = frames.shape[1]
    mob_local = frames.shape[2]
    channels = frames.shape[3]
    framed = extended(frames, ((DEV, 1),), RAD)
    padded = framed.astype(jnp.float32)
    smoothed = weights[0] * padded[:, 0:count_frames]
    for offset in range(1, 2 * RAD + 1):
        smoothed = smoothed + weights[offset] * padded[:, offset : offset + count_frames]
    smoothed = smoothed.astype(jnp.bfloat16)
    section_count = lax.axis_size("section")
    partner = lax.ppermute(
        smoothed, "section", [(i, (i + 1) % section_count) for i in range(section_count)]
    )
    gathered = jnp.concatenate([smoothed, partner], axis=2)
    kernels = mobility_kernels(section_index * mob_local, mob_local, section_index * mob_local)
    wavelet_stack = jnp.einsum(
        "smn,fnc->sfmc", kernels, gathered[0], preferred_element_type=jnp.float32
    ).astype(jnp.bfloat16)
    half_rows = templates.shape[0] // 2
    my_half = lax.dynamic_slice_in_dim(templates, section_index * half_rows, half_rows, 0)
    my_rows = gather_rows(my_half)
    other_rows = lax.ppermute(
        my_rows, "section", [(i, (i + 1) % section_count) for i in range(section_count)]
    )
    slots = pair_block.shape[2]
    live_pairs = pair_count[0, 0, 0]
    block_ids = pair_block[0, 0]
    tile_ids = pair_tile[0, 0]
    responses = score_pairs(
        wavelet_stack, my_rows, other_rows, tile_ids, block_ids, live_pairs, section_index
    )
    precursors = block_ids[:, None] * PB + jnp.arange(PB, dtype=jnp.int32)[None, :]
    positions = owner_order[precursors]
    placed = jnp.zeros((PREC,), jnp.float32).at[positions.reshape(-1)].add(responses.reshape(-1))
    dev_count = lax.axis_size(DEV)
    local_total = jnp.sum(responses)
    payload = jnp.concatenate(
        [
            placed.reshape(dev_count, 1, PREC // dev_count),
            jnp.broadcast_to(local_total, (dev_count, 1, 128)),
        ],
        axis=2,
    )
    return reduce_owned(payload)


def reduce_kernel(sizes, payload_ref, out_ref, gathered, totals, send_sems, recv_sems, total_send, total_recv):
    n_section, n_grp, n_dy, n_dz = sizes
    n_dev = n_dy * n_dz
    section = lax.axis_index("section")
    grp = lax.axis_index("grp")
    dy = lax.axis_index("dy")
    dz = lax.axis_index("dz")
    dev = dy * n_dz + dz
    me = section * n_dev + dev
    peers = n_section * n_dev
    owned_width = out_ref.shape[1]

    barrier = pltpu.get_barrier_semaphore()

    def greet(index, carry):
        @pl.when(index != me)
        def _():
            pl.semaphore_signal(
                barrier,
                inc=1,
                device_id=(index // n_dev, grp, index % n_dev // n_dz, index % n_dz),
                device_id_type=pl.DeviceIdType.MESH,
            )

        return carry

    lax.fori_loop(0, peers, greet, 0)
    for step in range(1, n_grp):
        pl.semaphore_signal(
            barrier,
            inc=1,
            device_id=(section, (grp + step) % n_grp, dy, dz),
            device_id_type=pl.DeviceIdType.MESH,
        )
    pl.semaphore_wait(barrier, peers - 1 + n_grp - 1)

    def chunk_copy(index):
        return pltpu.make_async_remote_copy(
            src_ref=payload_ref.at[index % n_dev],
            dst_ref=gathered.at[me],
            send_sem=send_sems.at[index],
            recv_sem=recv_sems.at[me],
            device_id=(index // n_dev, grp, index % n_dev // n_dz, index % n_dz),
            device_id_type=pl.DeviceIdType.MESH,
        )

    def send(index, carry):
        @pl.when(index != me)
        def _():
            chunk_copy(index).start()

        return carry

    lax.fori_loop(0, peers, send, 0)
    gathered[me] = payload_ref[dev]

    def arrive(index, carry):
        @pl.when(index != me)
        def _():
            pltpu.make_async_remote_copy(
                src_ref=payload_ref.at[0],
                dst_ref=gathered.at[index],
                send_sem=send_sems.at[index],
                recv_sem=recv_sems.at[index],
                device_id=(index // n_dev, grp, index % n_dev // n_dz, index % n_dz),
                device_id_type=pl.DeviceIdType.MESH,
            ).wait_recv()
            chunk_copy(index).wait_send()

        return carry

    lax.fori_loop(0, peers, arrive, 0)

    def accumulate(index, acc):
        return acc + gathered[index]

    summed = lax.fori_loop(0, peers, accumulate, jnp.zeros(gathered.shape[1:], jnp.float32))
    totals[grp] = summed[:, owned_width:]

    def total_copy(step):
        target = (grp + step) % n_grp
        return pltpu.make_async_remote_copy(
            src_ref=totals.at[grp],
            dst_ref=totals.at[grp],
            send_sem=total_send.at[target],
            recv_sem=total_recv.at[grp],
            device_id=(section, target, dy, dz),
            device_id_type=pl.DeviceIdType.MESH,
        )

    for step in range(1, n_grp):
        total_copy(step).start()
    for step in range(1, n_grp):
        source = (grp + step) % n_grp
        pltpu.make_async_remote_copy(
            src_ref=totals.at[source],
            dst_ref=totals.at[source],
            send_sem=total_send.at[source],
            recv_sem=total_recv.at[source],
            device_id=(section, source, dy, dz),
            device_id_type=pl.DeviceIdType.MESH,
        ).wait_recv()
        total_copy(step).wait_send()
    run_sum = totals[0]
    for index in range(1, n_grp):
        run_sum = run_sum + totals[index]
    own_total = summed[:, owned_width : owned_width + 1]
    factor = (run_sum[:, 0:1] / n_grp) / own_total
    out_ref[...] = summed[:, :owned_width] * factor


def reduce_owned(payload):
    sizes = (lax.axis_size("section"), lax.axis_size("grp"), lax.axis_size("dy"), lax.axis_size("dz"))
    n_section, n_grp, n_dy, n_dz = sizes
    peers = n_section * n_dy * n_dz
    rows, one, width = payload.shape
    owned_width = width - 128
    return pl.pallas_call(
        functools.partial(reduce_kernel, sizes),
        out_shape=jax.ShapeDtypeStruct((1, owned_width), jnp.float32),
        in_specs=[pl.BlockSpec(memory_space=pltpu.VMEM)],
        out_specs=pl.BlockSpec(memory_space=pltpu.VMEM),
        scratch_shapes=[
            pltpu.VMEM((peers, 1, width), jnp.float32),
            pltpu.VMEM((n_grp, 1, 128), jnp.float32),
            pltpu.SemaphoreType.DMA((peers,)),
            pltpu.SemaphoreType.DMA((peers,)),
            pltpu.SemaphoreType.DMA((n_grp,)),
            pltpu.SemaphoreType.DMA((n_grp,)),
        ],
        compiler_params=pltpu.CompilerParams(collective_id=0, has_side_effects=True),
    )(payload)


def gather_kernel(sizes, half_ref, out_ref, own_sem, send_sems, recv_sems):
    n_dy, n_dz = sizes
    n_dev = n_dy * n_dz
    section = lax.axis_index("section")
    grp = lax.axis_index("grp")
    dev = lax.axis_index("dy") * n_dz + lax.axis_index("dz")

    def peer(index):
        return (section, grp, index // n_dz, index % n_dz)

    barrier = pltpu.get_barrier_semaphore()
    for step in range(1, n_dev):
        pl.semaphore_signal(
            barrier,
            inc=1,
            device_id=peer((dev + step) % n_dev),
            device_id_type=pl.DeviceIdType.MESH,
        )
    pl.semaphore_wait(barrier, n_dev - 1)

    own = pltpu.make_async_copy(half_ref, out_ref.at[dev], own_sem)
    own.start()

    def row_copy(target, source):
        return pltpu.make_async_remote_copy(
            src_ref=half_ref,
            dst_ref=out_ref.at[source],
            send_sem=send_sems.at[target],
            recv_sem=recv_sems.at[source],
            device_id=peer(target),
            device_id_type=pl.DeviceIdType.MESH,
        )

    for step in range(1, n_dev):
        row_copy((dev + step) % n_dev, dev).start()
    own.wait()
    for step in range(1, n_dev):
        source = (dev + n_dev - step) % n_dev
        row_copy(source, source).wait_recv()
    for step in range(1, n_dev):
        row_copy((dev + step) % n_dev, dev).wait_send()


def gather_rows(half):
    sizes = (lax.axis_size("dy"), lax.axis_size("dz"))
    n_dy, n_dz = sizes
    rows, channels = half.shape
    out = pl.pallas_call(
        functools.partial(gather_kernel, sizes),
        out_shape=jax.ShapeDtypeStruct((n_dy * n_dz, rows, channels), half.dtype),
        in_specs=[pl.BlockSpec(memory_space=pltpu.VMEM)],
        out_specs=pl.BlockSpec(memory_space=pltpu.VMEM),
        scratch_shapes=[
            pltpu.SemaphoreType.DMA(()),
            pltpu.SemaphoreType.DMA((n_dy * n_dz,)),
            pltpu.SemaphoreType.DMA((n_dy * n_dz,)),
        ],
        compiler_params=pltpu.CompilerParams(collective_id=1, has_side_effects=True),
    )(half)
    return out.reshape(n_dy * n_dz * rows, channels)


def score_kernel(tile_ref, block_ref, count_ref, section_ref, wave_ref, mine_ref, other_ref, out_ref):
    slot = pl.program_id(0)
    live = slot < count_ref[0]
    mine = block_ref[slot] % 2 == section_ref[0]

    def score(rows_ref):
        rows = rows_ref[...]
        acc = jnp.zeros((1, PB), jnp.float32)
        for level in range(SCALES):
            cells = wave_ref[level].reshape(-1, rows.shape[1])
            scores = lax.dot_general(
                cells, rows, (((1,), (1,)), ((), ())), preferred_element_type=jnp.float32
            )
            acc = acc + jnp.sum(jnp.maximum(scores, 0.0), axis=0, keepdims=True)
        cell_count = SCALES * wave_ref.shape[1] * wave_ref.shape[2]
        out_ref[0] = acc / cell_count

    @pl.when(jnp.logical_and(live, mine))
    def _():
        score(mine_ref)

    @pl.when(jnp.logical_and(live, jnp.logical_not(mine)))
    def _():
        score(other_ref)

    @pl.when(jnp.logical_not(live))
    def _():
        out_ref[0] = jnp.zeros((1, PB), jnp.float32)


def score_pairs(wavelet_stack, my_rows, other_rows, tile_ids, block_ids, live_pairs, section_index):
    slots = tile_ids.shape[0]
    scales, frames_local, mob_local, channels = wavelet_stack.shape

    def last_live(k, count_ref):
        return jnp.minimum(k, count_ref[0] - 1)

    def rows_block(k, t, b, c, s):
        return (b[last_live(k, c)] // 2, 0)

    grid_spec = pltpu.PrefetchScalarGridSpec(
        num_scalar_prefetch=4,
        grid=(slots,),
        in_specs=[
            pl.BlockSpec(
                (scales, frames_local, TM, channels),
                lambda k, t, b, c, s: (0, 0, t[last_live(k, c)], 0),
            ),
            pl.BlockSpec((PB, channels), rows_block),
            pl.BlockSpec((PB, channels), rows_block),
        ],
        out_specs=pl.BlockSpec((1, 1, PB), lambda k, t, b, c, s: (k, 0, 0)),
    )
    out = pl.pallas_call(
        score_kernel,
        grid_spec=grid_spec,
        out_shape=jax.ShapeDtypeStruct((slots, 1, PB), jnp.float32),
    )(
        tile_ids,
        block_ids,
        live_pairs.reshape(1),
        section_index.astype(jnp.int32).reshape(1),
        wavelet_stack,
        my_rows,
        other_rows,
    )
    return out.reshape(slots, PB)


def solution(mesh):
    section_count, grp_count, dev_count = mesh.devices.shape
    dz_count = 8 if dev_count % 8 == 0 else dev_count
    split_mesh = jax.sharding.Mesh(
        mesh.devices.reshape(section_count, grp_count, dev_count // dz_count, dz_count),
        ("section", "grp", "dy", "dz"),
    )
    placed = (
        P("grp", DEV, "section", None),
        P(DEV, None),
        P("section", "grp", DEV),
        P("section", "grp", DEV),
        P("section", "grp", DEV),
        P(),
    )
    return jax.shard_map(
        on_device, mesh=split_mesh, in_specs=placed, out_specs=P("grp", DEV), check_vma=False
    )
```

```python
import functools
import math

import jax
import jax.numpy as jnp
from jax import lax
from jax.experimental import pallas as pl
from jax.experimental.pallas import tpu as pltpu
from jax.sharding import PartitionSpec as P

MOB = 512
SCALES = 6
RAD = 4
TM = 64
PB = 128
PREC = 8192
DEV = ("dy", "dz")


retention_spread = 2.0


def extended(cells, sides, width):
    for axis, dim in sides:
        count = lax.axis_size(axis)
        ends = count - 1
        head = lax.slice_in_dim(cells, 0, width, axis=dim)
        tail = lax.slice_in_dim(cells, cells.shape[dim] - width, cells.shape[dim], axis=dim)
        cells = jnp.concatenate(
            [
                lax.ppermute(tail, axis, [(i, (i + 1) % count) for i in range(ends)]),
                cells,
                lax.ppermute(head, axis, [((i + 1) % count, i) for i in range(ends)]),
            ],
            axis=dim,
        )
    return cells


def retention_weights():
    bell_values = [
        math.exp(-0.5 * (offset / retention_spread) ** 2) for offset in range(-RAD, RAD + 1)
    ]
    bell_total = sum(bell_values)
    return [weight_value / bell_total for weight_value in bell_values]


def mobility_kernels(row_start, row_count, col_start):
    row_place = (row_start + jnp.arange(row_count, dtype=jnp.int32)).astype(jnp.float32)
    col_place = ((col_start + jnp.arange(MOB, dtype=jnp.int32)) % MOB).astype(jnp.float32)
    distance = row_place[:, None] - col_place[None, :]
    tables = []
    for level in range(SCALES):
        spread_scans = 2.0**level
        scaled = distance / spread_scans
        tables.append(
            (1.0 - scaled * scaled)
            * jnp.exp(-0.5 * scaled * scaled)
            / math.sqrt(0.75 * math.sqrt(math.pi) * spread_scans)
        )
    return jnp.stack(tables).astype(jnp.bfloat16)


def on_device(frames, templates, pair_block, pair_tile, pair_count, owner_order):
    section_index = lax.axis_index("section")
    mob_local = frames.shape[2]
    section_count = lax.axis_size("section")
    kernels = mobility_kernels(section_index * mob_local, mob_local, section_index * mob_local)
    half_rows = templates.shape[0] // 2
    my_half = lax.dynamic_slice_in_dim(templates, section_index * half_rows, half_rows, 0)
    my_rows, wavelet_stack = frame_work(frames[0], kernels, my_half)
    other_rows = lax.ppermute(
        my_rows, "section", [(i, (i + 1) % section_count) for i in range(section_count)]
    )
    slots = pair_block.shape[2]
    live_pairs = pair_count[0, 0, 0]
    block_ids = pair_block[0, 0]
    tile_ids = pair_tile[0, 0]
    responses = score_pairs(
        wavelet_stack, my_rows, other_rows, tile_ids, block_ids, live_pairs, section_index
    )
    precursors = block_ids[:, None] * PB + jnp.arange(PB, dtype=jnp.int32)[None, :]
    positions = owner_order[precursors]
    placed = jnp.zeros((PREC,), jnp.float32).at[positions.reshape(-1)].add(responses.reshape(-1))
    dev_count = lax.axis_size(DEV)
    local_total = jnp.sum(responses)
    payload = jnp.concatenate(
        [
            placed.reshape(dev_count, 1, PREC // dev_count),
            jnp.broadcast_to(local_total, (dev_count, 1, 128)),
        ],
        axis=2,
    )
    return reduce_owned(payload)


def reduce_kernel(sizes, payload_ref, out_ref, gathered, totals, send_sems, recv_sems, total_send, total_recv):
    n_section, n_grp, n_dy, n_dz = sizes
    n_dev = n_dy * n_dz
    section = lax.axis_index("section")
    grp = lax.axis_index("grp")
    dy = lax.axis_index("dy")
    dz = lax.axis_index("dz")
    dev = dy * n_dz + dz
    me = section * n_dev + dev
    peers = n_section * n_dev
    owned_width = out_ref.shape[1]

    barrier = pltpu.get_barrier_semaphore()

    def greet(index, carry):
        @pl.when(index != me)
        def _():
            pl.semaphore_signal(
                barrier,
                inc=1,
                device_id=(index // n_dev, grp, index % n_dev // n_dz, index % n_dz),
                device_id_type=pl.DeviceIdType.MESH,
            )

        return carry

    lax.fori_loop(0, peers, greet, 0)
    for step in range(1, n_grp):
        pl.semaphore_signal(
            barrier,
            inc=1,
            device_id=(section, (grp + step) % n_grp, dy, dz),
            device_id_type=pl.DeviceIdType.MESH,
        )
    pl.semaphore_wait(barrier, peers - 1 + n_grp - 1)

    def chunk_copy(index):
        return pltpu.make_async_remote_copy(
            src_ref=payload_ref.at[index % n_dev],
            dst_ref=gathered.at[me],
            send_sem=send_sems.at[index],
            recv_sem=recv_sems.at[me],
            device_id=(index // n_dev, grp, index % n_dev // n_dz, index % n_dz),
            device_id_type=pl.DeviceIdType.MESH,
        )

    def send(index, carry):
        @pl.when(index != me)
        def _():
            chunk_copy(index).start()

        return carry

    lax.fori_loop(0, peers, send, 0)
    gathered[me] = payload_ref[dev]

    def arrive(index, carry):
        @pl.when(index != me)
        def _():
            pltpu.make_async_remote_copy(
                src_ref=payload_ref.at[0],
                dst_ref=gathered.at[index],
                send_sem=send_sems.at[index],
                recv_sem=recv_sems.at[index],
                device_id=(index // n_dev, grp, index % n_dev // n_dz, index % n_dz),
                device_id_type=pl.DeviceIdType.MESH,
            ).wait_recv()
            chunk_copy(index).wait_send()

        return carry

    lax.fori_loop(0, peers, arrive, 0)

    def accumulate(index, acc):
        return acc + gathered[index]

    summed = lax.fori_loop(0, peers, accumulate, jnp.zeros(gathered.shape[1:], jnp.float32))
    totals[grp] = summed[:, owned_width:]

    def total_copy(step):
        target = (grp + step) % n_grp
        return pltpu.make_async_remote_copy(
            src_ref=totals.at[grp],
            dst_ref=totals.at[grp],
            send_sem=total_send.at[target],
            recv_sem=total_recv.at[grp],
            device_id=(section, target, dy, dz),
            device_id_type=pl.DeviceIdType.MESH,
        )

    for step in range(1, n_grp):
        total_copy(step).start()
    for step in range(1, n_grp):
        source = (grp + step) % n_grp
        pltpu.make_async_remote_copy(
            src_ref=totals.at[source],
            dst_ref=totals.at[source],
            send_sem=total_send.at[source],
            recv_sem=total_recv.at[source],
            device_id=(section, source, dy, dz),
            device_id_type=pl.DeviceIdType.MESH,
        ).wait_recv()
        total_copy(step).wait_send()
    run_sum = totals[0]
    for index in range(1, n_grp):
        run_sum = run_sum + totals[index]
    own_total = summed[:, owned_width : owned_width + 1]
    factor = (run_sum[:, 0:1] / n_grp) / own_total
    out_ref[...] = summed[:, :owned_width] * factor


def reduce_owned(payload):
    sizes = (lax.axis_size("section"), lax.axis_size("grp"), lax.axis_size("dy"), lax.axis_size("dz"))
    n_section, n_grp, n_dy, n_dz = sizes
    peers = n_section * n_dy * n_dz
    rows, one, width = payload.shape
    owned_width = width - 128
    return pl.pallas_call(
        functools.partial(reduce_kernel, sizes),
        out_shape=jax.ShapeDtypeStruct((1, owned_width), jnp.float32),
        in_specs=[pl.BlockSpec(memory_space=pltpu.VMEM)],
        out_specs=pl.BlockSpec(memory_space=pltpu.VMEM),
        scratch_shapes=[
            pltpu.VMEM((peers, 1, width), jnp.float32),
            pltpu.VMEM((n_grp, 1, 128), jnp.float32),
            pltpu.SemaphoreType.DMA((peers,)),
            pltpu.SemaphoreType.DMA((peers,)),
            pltpu.SemaphoreType.DMA((n_grp,)),
            pltpu.SemaphoreType.DMA((n_grp,)),
        ],
        compiler_params=pltpu.CompilerParams(collective_id=0, has_side_effects=True),
    )(payload)


def frame_kernel(
    sizes,
    frames_ref,
    kernels_ref,
    half_ref,
    out_ref,
    wave_ref,
    halo_left,
    halo_right,
    own_scans,
    partner_scans,
    own_sem,
    z_send,
    z_recv,
    y_send,
    y_recv,
    halo_send,
    halo_recv,
    swap_send,
    swap_recv,
):
    n_section, n_dy, n_dz = sizes
    n_dev = n_dy * n_dz
    section = lax.axis_index("section")
    grp = lax.axis_index("grp")
    dy = lax.axis_index("dy")
    dz = lax.axis_index("dz")
    dev = dy * n_dz + dz
    partner_section = (section + 1) % n_section

    def dev_peer(index):
        return (section, grp, index // n_dz, index % n_dz)

    barrier = pltpu.get_barrier_semaphore()
    for step in range(1, n_dz):
        pl.semaphore_signal(
            barrier,
            inc=1,
            device_id=(section, grp, dy, (dz + step) % n_dz),
            device_id_type=pl.DeviceIdType.MESH,
        )
    for step in range(1, n_dy):
        pl.semaphore_signal(
            barrier,
            inc=1,
            device_id=(section, grp, (dy + step) % n_dy, dz),
            device_id_type=pl.DeviceIdType.MESH,
        )
    pl.semaphore_signal(
        barrier,
        inc=1,
        device_id=(partner_section, grp, dy, dz),
        device_id_type=pl.DeviceIdType.MESH,
    )
    has_left = dev > 0
    has_right = dev < n_dev - 1
    far_left = jnp.logical_and(has_left, dz == 0)
    far_right = jnp.logical_and(has_right, dz == n_dz - 1)

    @pl.when(far_left)
    def _():
        pl.semaphore_signal(
            barrier, inc=1, device_id=dev_peer(dev - 1), device_id_type=pl.DeviceIdType.MESH
        )

    @pl.when(far_right)
    def _():
        pl.semaphore_signal(
            barrier, inc=1, device_id=dev_peer(dev + 1), device_id_type=pl.DeviceIdType.MESH
        )

    extra = far_left.astype(jnp.int32) + far_right.astype(jnp.int32)
    pl.semaphore_wait(barrier, n_dz - 1 + n_dy - 1 + 1 + extra)

    own = pltpu.make_async_copy(half_ref, out_ref.at[dev], own_sem)
    own.start()

    def z_copy(target, source):
        return pltpu.make_async_remote_copy(
            src_ref=half_ref,
            dst_ref=out_ref.at[dy * n_dz + source],
            send_sem=z_send.at[target],
            recv_sem=z_recv.at[source],
            device_id=(section, grp, dy, target),
            device_id_type=pl.DeviceIdType.MESH,
        )

    for step in range(1, n_dz):
        z_copy((dz + step) % n_dz, dz).start()

    count_frames = frames_ref.shape[0]

    def to_left():
        return pltpu.make_async_remote_copy(
            src_ref=frames_ref.at[pl.ds(0, RAD)],
            dst_ref=halo_right,
            send_sem=halo_send.at[0],
            recv_sem=halo_recv.at[1],
            device_id=dev_peer(dev - 1),
            device_id_type=pl.DeviceIdType.MESH,
        )

    def to_right():
        return pltpu.make_async_remote_copy(
            src_ref=frames_ref.at[pl.ds(count_frames - RAD, RAD)],
            dst_ref=halo_left,
            send_sem=halo_send.at[1],
            recv_sem=halo_recv.at[0],
            device_id=dev_peer(dev + 1),
            device_id_type=pl.DeviceIdType.MESH,
        )

    @pl.when(has_left)
    def _():
        to_left().start()

    @pl.when(has_right)
    def _():
        to_right().start()

    @pl.when(jnp.logical_not(has_left))
    def _():
        halo_left[...] = jnp.zeros(halo_left.shape, halo_left.dtype)

    @pl.when(jnp.logical_not(has_right))
    def _():
        halo_right[...] = jnp.zeros(halo_right.shape, halo_right.dtype)

    @pl.when(has_left)
    def _():
        to_right_of_left = pltpu.make_async_remote_copy(
            src_ref=frames_ref.at[pl.ds(0, RAD)],
            dst_ref=halo_left,
            send_sem=halo_send.at[1],
            recv_sem=halo_recv.at[0],
            device_id=dev_peer(dev - 1),
            device_id_type=pl.DeviceIdType.MESH,
        )
        to_right_of_left.wait_recv()
        to_left().wait_send()

    @pl.when(has_right)
    def _():
        to_left_of_right = pltpu.make_async_remote_copy(
            src_ref=frames_ref.at[pl.ds(0, RAD)],
            dst_ref=halo_right,
            send_sem=halo_send.at[0],
            recv_sem=halo_recv.at[1],
            device_id=dev_peer(dev + 1),
            device_id_type=pl.DeviceIdType.MESH,
        )
        to_left_of_right.wait_recv()
        to_right().wait_send()

    weights = retention_weights()

    def padded_frame(place):
        if place < RAD:
            return halo_left[place]
        if place < RAD + count_frames:
            return frames_ref[place - RAD]
        return halo_right[place - RAD - count_frames]

    for frame in range(count_frames):
        total = weights[0] * padded_frame(frame).astype(jnp.float32)
        for offset in range(1, 2 * RAD + 1):
            total = total + weights[offset] * padded_frame(frame + offset).astype(jnp.float32)
        own_scans[frame] = total.astype(own_scans.dtype)

    swap = pltpu.make_async_remote_copy(
        src_ref=own_scans,
        dst_ref=partner_scans,
        send_sem=swap_send,
        recv_sem=swap_recv,
        device_id=(partner_section, grp, dy, dz),
        device_id_type=pl.DeviceIdType.MESH,
    )
    swap.start()
    own.wait()
    for step in range(1, n_dz):
        source = (dz + n_dz - step) % n_dz
        z_copy(source, source).wait_recv()
    for step in range(1, n_dz):
        z_copy((dz + step) % n_dz, dz).wait_send()

    def y_copy(target, source):
        return pltpu.make_async_remote_copy(
            src_ref=out_ref.at[pl.ds(source * n_dz, n_dz)],
            dst_ref=out_ref.at[pl.ds(source * n_dz, n_dz)],
            send_sem=y_send.at[target],
            recv_sem=y_recv.at[source],
            device_id=(section, grp, target, dz),
            device_id_type=pl.DeviceIdType.MESH,
        )

    for step in range(1, n_dy):
        y_copy((dy + step) % n_dy, dy).start()
    swap.wait()

    half = own_scans.shape[1]

    def level_frame(frame, carry):
        for level in range(SCALES):
            table = kernels_ref[level]
            acc = jnp.dot(table[:, :half], own_scans[frame], preferred_element_type=jnp.float32)
            acc = acc + jnp.dot(
                table[:, half:], partner_scans[frame], preferred_element_type=jnp.float32
            )
            wave_ref[level, frame] = acc.astype(wave_ref.dtype)
        return carry

    lax.fori_loop(0, count_frames, level_frame, 0)

    for step in range(1, n_dy):
        source = (dy + n_dy - step) % n_dy
        y_copy(source, source).wait_recv()
    for step in range(1, n_dy):
        y_copy((dy + step) % n_dy, dy).wait_send()


def frame_work(frames, kernels, half):
    sizes = (lax.axis_size("section"), lax.axis_size("dy"), lax.axis_size("dz"))
    n_section, n_dy, n_dz = sizes
    rows, channels = half.shape
    count_frames, mob_local, _ = frames.shape
    rows_out, wave = pl.pallas_call(
        functools.partial(frame_kernel, sizes),
        out_shape=(
            jax.ShapeDtypeStruct((n_dy * n_dz, rows, channels), half.dtype),
            jax.ShapeDtypeStruct((SCALES, count_frames, mob_local, channels), jnp.bfloat16),
        ),
        in_specs=[pl.BlockSpec(memory_space=pltpu.VMEM)] * 3,
        out_specs=(pl.BlockSpec(memory_space=pltpu.VMEM), pl.BlockSpec(memory_space=pltpu.VMEM)),
        scratch_shapes=[
            pltpu.VMEM((RAD, mob_local, channels), frames.dtype),
            pltpu.VMEM((RAD, mob_local, channels), frames.dtype),
            pltpu.VMEM((count_frames, mob_local, channels), jnp.bfloat16),
            pltpu.VMEM((count_frames, mob_local, channels), jnp.bfloat16),
            pltpu.SemaphoreType.DMA(()),
            pltpu.SemaphoreType.DMA((n_dz,)),
            pltpu.SemaphoreType.DMA((n_dz,)),
            pltpu.SemaphoreType.DMA((n_dy,)),
            pltpu.SemaphoreType.DMA((n_dy,)),
            pltpu.SemaphoreType.DMA((2,)),
            pltpu.SemaphoreType.DMA((2,)),
            pltpu.SemaphoreType.DMA(()),
            pltpu.SemaphoreType.DMA(()),
        ],
        compiler_params=pltpu.CompilerParams(
            collective_id=1, has_side_effects=True, vmem_limit_bytes=56 * 1024 * 1024
        ),
    )(frames, kernels, half)
    return rows_out.reshape(n_dy * n_dz * rows, channels), wave


def score_kernel(tile_ref, block_ref, count_ref, section_ref, wave_ref, mine_ref, other_ref, out_ref):
    slot = pl.program_id(0)
    live = slot < count_ref[0]
    mine = block_ref[slot] % 2 == section_ref[0]

    def score(rows_ref):
        rows = rows_ref[...]
        acc = jnp.zeros((1, PB), jnp.float32)
        for level in range(SCALES):
            cells = wave_ref[level].reshape(-1, rows.shape[1])
            scores = lax.dot_general(
                cells, rows, (((1,), (1,)), ((), ())), preferred_element_type=jnp.float32
            )
            acc = acc + jnp.sum(jnp.maximum(scores, 0.0), axis=0, keepdims=True)
        cell_count = SCALES * wave_ref.shape[1] * wave_ref.shape[2]
        out_ref[0] = acc / cell_count

    @pl.when(jnp.logical_and(live, mine))
    def _():
        score(mine_ref)

    @pl.when(jnp.logical_and(live, jnp.logical_not(mine)))
    def _():
        score(other_ref)

    @pl.when(jnp.logical_not(live))
    def _():
        out_ref[0] = jnp.zeros((1, PB), jnp.float32)


def score_pairs(wavelet_stack, my_rows, other_rows, tile_ids, block_ids, live_pairs, section_index):
    slots = tile_ids.shape[0]
    scales, frames_local, mob_local, channels = wavelet_stack.shape

    def last_live(k, count_ref):
        return jnp.minimum(k, count_ref[0] - 1)

    def rows_block(k, t, b, c, s):
        return (b[last_live(k, c)] // 2, 0)

    grid_spec = pltpu.PrefetchScalarGridSpec(
        num_scalar_prefetch=4,
        grid=(slots,),
        in_specs=[
            pl.BlockSpec(
                (scales, frames_local, TM, channels),
                lambda k, t, b, c, s: (0, 0, t[last_live(k, c)], 0),
            ),
            pl.BlockSpec((PB, channels), rows_block),
            pl.BlockSpec((PB, channels), rows_block),
        ],
        out_specs=pl.BlockSpec((1, 1, PB), lambda k, t, b, c, s: (k, 0, 0)),
    )
    out = pl.pallas_call(
        score_kernel,
        grid_spec=grid_spec,
        out_shape=jax.ShapeDtypeStruct((slots, 1, PB), jnp.float32),
    )(
        tile_ids,
        block_ids,
        live_pairs.reshape(1),
        section_index.astype(jnp.int32).reshape(1),
        wavelet_stack,
        my_rows,
        other_rows,
    )
    return out.reshape(slots, PB)


def solution(mesh):
    section_count, grp_count, dev_count = mesh.devices.shape
    dz_count = 8 if dev_count % 8 == 0 else dev_count
    split_mesh = jax.sharding.Mesh(
        mesh.devices.reshape(section_count, grp_count, dev_count // dz_count, dz_count),
        ("section", "grp", "dy", "dz"),
    )
    placed = (
        P("grp", DEV, "section", None),
        P(DEV, None),
        P("section", "grp", DEV),
        P("section", "grp", DEV),
        P("section", "grp", DEV),
        P(),
    )
    return jax.shard_map(
        on_device, mesh=split_mesh, in_specs=placed, out_specs=P("grp", DEV), check_vma=False
    )
```

```python
import functools
import math

import jax
import jax.numpy as jnp
from jax import lax
from jax.experimental import pallas as pl
from jax.experimental.pallas import tpu as pltpu
from jax.sharding import PartitionSpec as P

MOB = 512
SCALES = 6
RAD = 4
TM = 64
PB = 128
PREC = 8192
DEV = ("dy", "dz")


retention_spread = 2.0


def extended(cells, sides, width):
    for axis, dim in sides:
        count = lax.axis_size(axis)
        ends = count - 1
        head = lax.slice_in_dim(cells, 0, width, axis=dim)
        tail = lax.slice_in_dim(cells, cells.shape[dim] - width, cells.shape[dim], axis=dim)
        cells = jnp.concatenate(
            [
                lax.ppermute(tail, axis, [(i, (i + 1) % count) for i in range(ends)]),
                cells,
                lax.ppermute(head, axis, [((i + 1) % count, i) for i in range(ends)]),
            ],
            axis=dim,
        )
    return cells


def retention_weights():
    bell_values = [
        math.exp(-0.5 * (offset / retention_spread) ** 2) for offset in range(-RAD, RAD + 1)
    ]
    bell_total = sum(bell_values)
    return [weight_value / bell_total for weight_value in bell_values]


def mobility_kernels(row_start, row_count, col_start):
    row_place = (row_start + jnp.arange(row_count, dtype=jnp.int32)).astype(jnp.float32)
    col_place = ((col_start + jnp.arange(MOB, dtype=jnp.int32)) % MOB).astype(jnp.float32)
    distance = row_place[:, None] - col_place[None, :]
    tables = []
    for level in range(SCALES):
        spread_scans = 2.0**level
        scaled = distance / spread_scans
        tables.append(
            (1.0 - scaled * scaled)
            * jnp.exp(-0.5 * scaled * scaled)
            / math.sqrt(0.75 * math.sqrt(math.pi) * spread_scans)
        )
    return jnp.stack(tables).astype(jnp.bfloat16)


def on_device(frames, templates, pair_block, pair_tile, pair_count, owner_order):
    section_index = lax.axis_index("section")
    mob_local = frames.shape[2]
    section_count = lax.axis_size("section")
    kernels = mobility_kernels(section_index * mob_local, mob_local, section_index * mob_local)
    half_rows = templates.shape[0] // 2
    my_half = lax.dynamic_slice_in_dim(templates, section_index * half_rows, half_rows, 0)
    my_rows, wavelet_stack = frame_work(frames[0], kernels, my_half)
    other_rows = lax.ppermute(
        my_rows, "section", [(i, (i + 1) % section_count) for i in range(section_count)]
    )
    slots = pair_block.shape[2]
    live_pairs = pair_count[0, 0, 0]
    block_ids = pair_block[0, 0]
    tile_ids = pair_tile[0, 0]
    responses = score_pairs(
        wavelet_stack, my_rows, other_rows, tile_ids, block_ids, live_pairs, section_index
    )
    precursors = block_ids[:, None] * PB + jnp.arange(PB, dtype=jnp.int32)[None, :]
    positions = owner_order[precursors]
    placed = jnp.zeros((PREC,), jnp.float32).at[positions.reshape(-1)].add(responses.reshape(-1))
    dev_count = lax.axis_size(DEV)
    local_total = jnp.sum(responses)
    payload = jnp.concatenate(
        [
            placed.reshape(dev_count, 1, PREC // dev_count),
            jnp.broadcast_to(local_total, (dev_count, 1, 128)),
        ],
        axis=2,
    )
    return reduce_owned(payload)


def reduce_kernel(sizes, payload_ref, out_ref, gathered, totals, send_sems, recv_sems, total_send, total_recv):
    n_section, n_grp, n_dy, n_dz = sizes
    n_dev = n_dy * n_dz
    section = lax.axis_index("section")
    grp = lax.axis_index("grp")
    dy = lax.axis_index("dy")
    dz = lax.axis_index("dz")
    dev = dy * n_dz + dz
    me = section * n_dev + dev
    peers = n_section * n_dev
    owned_width = out_ref.shape[1]

    barrier = pltpu.get_barrier_semaphore()

    def greet(index, carry):
        @pl.when(index != me)
        def _():
            pl.semaphore_signal(
                barrier,
                inc=1,
                device_id=(index // n_dev, grp, index % n_dev // n_dz, index % n_dz),
                device_id_type=pl.DeviceIdType.MESH,
            )

        return carry

    lax.fori_loop(0, peers, greet, 0)
    for step in range(1, n_grp):
        pl.semaphore_signal(
            barrier,
            inc=1,
            device_id=(section, (grp + step) % n_grp, dy, dz),
            device_id_type=pl.DeviceIdType.MESH,
        )
    pl.semaphore_wait(barrier, peers - 1 + n_grp - 1)

    def chunk_copy(index):
        return pltpu.make_async_remote_copy(
            src_ref=payload_ref.at[index % n_dev],
            dst_ref=gathered.at[me],
            send_sem=send_sems.at[index],
            recv_sem=recv_sems.at[me],
            device_id=(index // n_dev, grp, index % n_dev // n_dz, index % n_dz),
            device_id_type=pl.DeviceIdType.MESH,
        )

    def send(index, carry):
        @pl.when(index != me)
        def _():
            chunk_copy(index).start()

        return carry

    lax.fori_loop(0, peers, send, 0)
    gathered[me] = payload_ref[dev]

    def arrive(index, carry):
        @pl.when(index != me)
        def _():
            pltpu.make_async_remote_copy(
                src_ref=payload_ref.at[0],
                dst_ref=gathered.at[index],
                send_sem=send_sems.at[index],
                recv_sem=recv_sems.at[index],
                device_id=(index // n_dev, grp, index % n_dev // n_dz, index % n_dz),
                device_id_type=pl.DeviceIdType.MESH,
            ).wait_recv()
            chunk_copy(index).wait_send()

        return carry

    lax.fori_loop(0, peers, arrive, 0)

    def accumulate(index, acc):
        return acc + gathered[index]

    summed = lax.fori_loop(0, peers, accumulate, jnp.zeros(gathered.shape[1:], jnp.float32))
    totals[grp] = summed[:, owned_width:]

    def total_copy(step):
        target = (grp + step) % n_grp
        return pltpu.make_async_remote_copy(
            src_ref=totals.at[grp],
            dst_ref=totals.at[grp],
            send_sem=total_send.at[target],
            recv_sem=total_recv.at[grp],
            device_id=(section, target, dy, dz),
            device_id_type=pl.DeviceIdType.MESH,
        )

    for step in range(1, n_grp):
        total_copy(step).start()
    for step in range(1, n_grp):
        source = (grp + step) % n_grp
        pltpu.make_async_remote_copy(
            src_ref=totals.at[source],
            dst_ref=totals.at[source],
            send_sem=total_send.at[source],
            recv_sem=total_recv.at[source],
            device_id=(section, source, dy, dz),
            device_id_type=pl.DeviceIdType.MESH,
        ).wait_recv()
        total_copy(step).wait_send()
    run_sum = totals[0]
    for index in range(1, n_grp):
        run_sum = run_sum + totals[index]
    own_total = summed[:, owned_width : owned_width + 1]
    factor = (run_sum[:, 0:1] / n_grp) / own_total
    out_ref[...] = summed[:, :owned_width] * factor


def reduce_owned(payload):
    sizes = (lax.axis_size("section"), lax.axis_size("grp"), lax.axis_size("dy"), lax.axis_size("dz"))
    n_section, n_grp, n_dy, n_dz = sizes
    peers = n_section * n_dy * n_dz
    rows, one, width = payload.shape
    owned_width = width - 128
    return pl.pallas_call(
        functools.partial(reduce_kernel, sizes),
        out_shape=jax.ShapeDtypeStruct((1, owned_width), jnp.float32),
        in_specs=[pl.BlockSpec(memory_space=pltpu.VMEM)],
        out_specs=pl.BlockSpec(memory_space=pltpu.VMEM),
        scratch_shapes=[
            pltpu.VMEM((peers, 1, width), jnp.float32),
            pltpu.VMEM((n_grp, 1, 128), jnp.float32),
            pltpu.SemaphoreType.DMA((peers,)),
            pltpu.SemaphoreType.DMA((peers,)),
            pltpu.SemaphoreType.DMA((n_grp,)),
            pltpu.SemaphoreType.DMA((n_grp,)),
        ],
        compiler_params=pltpu.CompilerParams(collective_id=0, has_side_effects=True),
    )(payload)


def frame_kernel(
    sizes,
    frames_ref,
    kernels_ref,
    half_ref,
    out_ref,
    wave_ref,
    halo_left,
    halo_right,
    own_scans,
    partner_scans,
    own_sem,
    z_send,
    z_recv,
    y_send,
    y_recv,
    halo_send,
    halo_recv,
    swap_send,
    swap_recv,
):
    n_section, n_dy, n_dz = sizes
    n_dev = n_dy * n_dz
    section = lax.axis_index("section")
    grp = lax.axis_index("grp")
    dy = lax.axis_index("dy")
    dz = lax.axis_index("dz")
    dev = dy * n_dz + dz
    partner_section = (section + 1) % n_section

    def dev_peer(index):
        return (section, grp, index // n_dz, index % n_dz)

    barrier = pltpu.get_barrier_semaphore()
    for step in range(1, n_dz):
        pl.semaphore_signal(
            barrier,
            inc=1,
            device_id=(section, grp, dy, (dz + step) % n_dz),
            device_id_type=pl.DeviceIdType.MESH,
        )
    for step in range(1, n_dy):
        pl.semaphore_signal(
            barrier,
            inc=1,
            device_id=(section, grp, (dy + step) % n_dy, dz),
            device_id_type=pl.DeviceIdType.MESH,
        )
    pl.semaphore_signal(
        barrier,
        inc=1,
        device_id=(partner_section, grp, dy, dz),
        device_id_type=pl.DeviceIdType.MESH,
    )
    has_left = dev > 0
    has_right = dev < n_dev - 1
    far_left = jnp.logical_and(has_left, dz == 0)
    far_right = jnp.logical_and(has_right, dz == n_dz - 1)

    @pl.when(far_left)
    def _():
        pl.semaphore_signal(
            barrier, inc=1, device_id=dev_peer(dev - 1), device_id_type=pl.DeviceIdType.MESH
        )

    @pl.when(far_right)
    def _():
        pl.semaphore_signal(
            barrier, inc=1, device_id=dev_peer(dev + 1), device_id_type=pl.DeviceIdType.MESH
        )

    extra = far_left.astype(jnp.int32) + far_right.astype(jnp.int32)
    pl.semaphore_wait(barrier, n_dz - 1 + n_dy - 1 + 1 + extra)

    own = pltpu.make_async_copy(half_ref, out_ref.at[dev], own_sem)
    own.start()

    def z_copy(target, source):
        return pltpu.make_async_remote_copy(
            src_ref=half_ref,
            dst_ref=out_ref.at[dy * n_dz + source],
            send_sem=z_send.at[target],
            recv_sem=z_recv.at[source],
            device_id=(section, grp, dy, target),
            device_id_type=pl.DeviceIdType.MESH,
        )

    for step in range(1, n_dz):
        z_copy((dz + step) % n_dz, dz).start()

    def y_copy(target, source, chunk):
        slot = source * n_dz + chunk
        return pltpu.make_async_remote_copy(
            src_ref=out_ref.at[slot],
            dst_ref=out_ref.at[slot],
            send_sem=y_send.at[target * n_dz + chunk],
            recv_sem=y_recv.at[slot],
            device_id=(section, grp, target, dz),
            device_id_type=pl.DeviceIdType.MESH,
        )

    def y_own(target):
        return pltpu.make_async_remote_copy(
            src_ref=half_ref,
            dst_ref=out_ref.at[dev],
            send_sem=y_send.at[target * n_dz + dz],
            recv_sem=y_recv.at[dev],
            device_id=(section, grp, target, dz),
            device_id_type=pl.DeviceIdType.MESH,
        )

    for step in range(1, n_dy):
        y_own((dy + step) % n_dy).start()
    for step in range(1, n_dz):
        source = (dz + n_dz - step) % n_dz
        z_copy(source, source).wait_recv()
        for hop in range(1, n_dy):
            y_copy((dy + hop) % n_dy, dy, source).start()
    own.wait()
    for step in range(1, n_dz):
        z_copy((dz + step) % n_dz, dz).wait_send()

    count_frames = frames_ref.shape[0]

    def to_left():
        return pltpu.make_async_remote_copy(
            src_ref=frames_ref.at[pl.ds(0, RAD)],
            dst_ref=halo_right,
            send_sem=halo_send.at[0],
            recv_sem=halo_recv.at[1],
            device_id=dev_peer(dev - 1),
            device_id_type=pl.DeviceIdType.MESH,
        )

    def to_right():
        return pltpu.make_async_remote_copy(
            src_ref=frames_ref.at[pl.ds(count_frames - RAD, RAD)],
            dst_ref=halo_left,
            send_sem=halo_send.at[1],
            recv_sem=halo_recv.at[0],
            device_id=dev_peer(dev + 1),
            device_id_type=pl.DeviceIdType.MESH,
        )

    @pl.when(has_left)
    def _():
        to_left().start()

    @pl.when(has_right)
    def _():
        to_right().start()

    @pl.when(jnp.logical_not(has_left))
    def _():
        halo_left[...] = jnp.zeros(halo_left.shape, halo_left.dtype)

    @pl.when(jnp.logical_not(has_right))
    def _():
        halo_right[...] = jnp.zeros(halo_right.shape, halo_right.dtype)

    @pl.when(has_left)
    def _():
        to_right_of_left = pltpu.make_async_remote_copy(
            src_ref=frames_ref.at[pl.ds(0, RAD)],
            dst_ref=halo_left,
            send_sem=halo_send.at[1],
            recv_sem=halo_recv.at[0],
            device_id=dev_peer(dev - 1),
            device_id_type=pl.DeviceIdType.MESH,
        )
        to_right_of_left.wait_recv()
        to_left().wait_send()

    @pl.when(has_right)
    def _():
        to_left_of_right = pltpu.make_async_remote_copy(
            src_ref=frames_ref.at[pl.ds(0, RAD)],
            dst_ref=halo_right,
            send_sem=halo_send.at[0],
            recv_sem=halo_recv.at[1],
            device_id=dev_peer(dev + 1),
            device_id_type=pl.DeviceIdType.MESH,
        )
        to_left_of_right.wait_recv()
        to_right().wait_send()

    weights = retention_weights()

    def padded_frame(place):
        if place < RAD:
            return halo_left[place]
        if place < RAD + count_frames:
            return frames_ref[place - RAD]
        return halo_right[place - RAD - count_frames]

    for frame in range(count_frames):
        total = weights[0] * padded_frame(frame).astype(jnp.float32)
        for offset in range(1, 2 * RAD + 1):
            total = total + weights[offset] * padded_frame(frame + offset).astype(jnp.float32)
        own_scans[frame] = total.astype(own_scans.dtype)

    swap = pltpu.make_async_remote_copy(
        src_ref=own_scans,
        dst_ref=partner_scans,
        send_sem=swap_send,
        recv_sem=swap_recv,
        device_id=(partner_section, grp, dy, dz),
        device_id_type=pl.DeviceIdType.MESH,
    )
    swap.start()
    swap.wait()

    half = own_scans.shape[1]

    def level_frame(frame, carry):
        for level in range(SCALES):
            table = kernels_ref[level]
            acc = jnp.dot(table[:, :half], own_scans[frame], preferred_element_type=jnp.float32)
            acc = acc + jnp.dot(
                table[:, half:], partner_scans[frame], preferred_element_type=jnp.float32
            )
            wave_ref[level, frame] = acc.astype(wave_ref.dtype)
        return carry

    lax.fori_loop(0, count_frames, level_frame, 0)

    for step in range(1, n_dy):
        source = (dy + n_dy - step) % n_dy
        for chunk in range(n_dz):
            y_copy(source, source, chunk).wait_recv()
    for step in range(1, n_dy):
        for chunk in range(n_dz):
            y_copy((dy + step) % n_dy, dy, chunk).wait_send()


def frame_work(frames, kernels, half):
    sizes = (lax.axis_size("section"), lax.axis_size("dy"), lax.axis_size("dz"))
    n_section, n_dy, n_dz = sizes
    rows, channels = half.shape
    count_frames, mob_local, _ = frames.shape
    rows_out, wave = pl.pallas_call(
        functools.partial(frame_kernel, sizes),
        out_shape=(
            jax.ShapeDtypeStruct((n_dy * n_dz, rows, channels), half.dtype),
            jax.ShapeDtypeStruct((SCALES, count_frames, mob_local, channels), jnp.bfloat16),
        ),
        in_specs=[pl.BlockSpec(memory_space=pltpu.VMEM)] * 3,
        out_specs=(pl.BlockSpec(memory_space=pltpu.VMEM), pl.BlockSpec(memory_space=pltpu.VMEM)),
        scratch_shapes=[
            pltpu.VMEM((RAD, mob_local, channels), frames.dtype),
            pltpu.VMEM((RAD, mob_local, channels), frames.dtype),
            pltpu.VMEM((count_frames, mob_local, channels), jnp.bfloat16),
            pltpu.VMEM((count_frames, mob_local, channels), jnp.bfloat16),
            pltpu.SemaphoreType.DMA(()),
            pltpu.SemaphoreType.DMA((n_dz,)),
            pltpu.SemaphoreType.DMA((n_dz,)),
            pltpu.SemaphoreType.DMA((n_dy * n_dz,)),
            pltpu.SemaphoreType.DMA((n_dy * n_dz,)),
            pltpu.SemaphoreType.DMA((2,)),
            pltpu.SemaphoreType.DMA((2,)),
            pltpu.SemaphoreType.DMA(()),
            pltpu.SemaphoreType.DMA(()),
        ],
        compiler_params=pltpu.CompilerParams(
            collective_id=1, has_side_effects=True, vmem_limit_bytes=56 * 1024 * 1024
        ),
    )(frames, kernels, half)
    return rows_out.reshape(n_dy * n_dz * rows, channels), wave


def score_kernel(tile_ref, block_ref, count_ref, section_ref, wave_ref, mine_ref, other_ref, out_ref):
    slot = pl.program_id(0)
    live = slot < count_ref[0]
    mine = block_ref[slot] % 2 == section_ref[0]

    def score(rows_ref):
        rows = rows_ref[...]
        acc = jnp.zeros((1, PB), jnp.float32)
        for level in range(SCALES):
            cells = wave_ref[level].reshape(-1, rows.shape[1])
            scores = lax.dot_general(
                cells, rows, (((1,), (1,)), ((), ())), preferred_element_type=jnp.float32
            )
            acc = acc + jnp.sum(jnp.maximum(scores, 0.0), axis=0, keepdims=True)
        cell_count = SCALES * wave_ref.shape[1] * wave_ref.shape[2]
        out_ref[0] = acc / cell_count

    @pl.when(jnp.logical_and(live, mine))
    def _():
        score(mine_ref)

    @pl.when(jnp.logical_and(live, jnp.logical_not(mine)))
    def _():
        score(other_ref)

    @pl.when(jnp.logical_not(live))
    def _():
        out_ref[0] = jnp.zeros((1, PB), jnp.float32)


def score_pairs(wavelet_stack, my_rows, other_rows, tile_ids, block_ids, live_pairs, section_index):
    slots = tile_ids.shape[0]
    scales, frames_local, mob_local, channels = wavelet_stack.shape

    def last_live(k, count_ref):
        return jnp.minimum(k, count_ref[0] - 1)

    def rows_block(k, t, b, c, s):
        return (b[last_live(k, c)] // 2, 0)

    grid_spec = pltpu.PrefetchScalarGridSpec(
        num_scalar_prefetch=4,
        grid=(slots,),
        in_specs=[
            pl.BlockSpec(
                (scales, frames_local, TM, channels),
                lambda k, t, b, c, s: (0, 0, t[last_live(k, c)], 0),
            ),
            pl.BlockSpec((PB, channels), rows_block),
            pl.BlockSpec((PB, channels), rows_block),
        ],
        out_specs=pl.BlockSpec((1, 1, PB), lambda k, t, b, c, s: (k, 0, 0)),
    )
    out = pl.pallas_call(
        score_kernel,
        grid_spec=grid_spec,
        out_shape=jax.ShapeDtypeStruct((slots, 1, PB), jnp.float32),
    )(
        tile_ids,
        block_ids,
        live_pairs.reshape(1),
        section_index.astype(jnp.int32).reshape(1),
        wavelet_stack,
        my_rows,
        other_rows,
    )
    return out.reshape(slots, PB)


def solution(mesh):
    section_count, grp_count, dev_count = mesh.devices.shape
    dz_count = 8 if dev_count % 8 == 0 else dev_count
    split_mesh = jax.sharding.Mesh(
        mesh.devices.reshape(section_count, grp_count, dev_count // dz_count, dz_count),
        ("section", "grp", "dy", "dz"),
    )
    placed = (
        P("grp", DEV, "section", None),
        P(DEV, None),
        P("section", "grp", DEV),
        P("section", "grp", DEV),
        P("section", "grp", DEV),
        P(),
    )
    return jax.shard_map(
        on_device, mesh=split_mesh, in_specs=placed, out_specs=P("grp", DEV), check_vma=False
    )
```

```python
import functools
import math

import jax
import jax.numpy as jnp
from jax import lax
from jax.experimental import pallas as pl
from jax.experimental.pallas import tpu as pltpu
from jax.sharding import PartitionSpec as P

MOB = 512
SCALES = 6
RAD = 4
TM = 64
PB = 128
PREC = 8192
DEV = ("dy", "dz")


retention_spread = 2.0


def extended(cells, sides, width):
    for axis, dim in sides:
        count = lax.axis_size(axis)
        ends = count - 1
        head = lax.slice_in_dim(cells, 0, width, axis=dim)
        tail = lax.slice_in_dim(cells, cells.shape[dim] - width, cells.shape[dim], axis=dim)
        cells = jnp.concatenate(
            [
                lax.ppermute(tail, axis, [(i, (i + 1) % count) for i in range(ends)]),
                cells,
                lax.ppermute(head, axis, [((i + 1) % count, i) for i in range(ends)]),
            ],
            axis=dim,
        )
    return cells


def retention_weights():
    bell_values = [
        math.exp(-0.5 * (offset / retention_spread) ** 2) for offset in range(-RAD, RAD + 1)
    ]
    bell_total = sum(bell_values)
    return [weight_value / bell_total for weight_value in bell_values]


def mobility_kernels(row_start, row_count, col_start):
    row_place = (row_start + jnp.arange(row_count, dtype=jnp.int32)).astype(jnp.float32)
    col_place = ((col_start + jnp.arange(MOB, dtype=jnp.int32)) % MOB).astype(jnp.float32)
    distance = row_place[:, None] - col_place[None, :]
    tables = []
    for level in range(SCALES):
        spread_scans = 2.0**level
        scaled = distance / spread_scans
        tables.append(
            (1.0 - scaled * scaled)
            * jnp.exp(-0.5 * scaled * scaled)
            / math.sqrt(0.75 * math.sqrt(math.pi) * spread_scans)
        )
    return jnp.stack(tables).astype(jnp.bfloat16)


def on_device(frames, templates, pair_block, pair_tile, pair_count, owner_order):
    section_index = lax.axis_index("section")
    mob_local = frames.shape[2]
    section_count = lax.axis_size("section")
    kernels = mobility_kernels(section_index * mob_local, mob_local, section_index * mob_local)
    half_rows = templates.shape[0] // 2
    my_half = lax.dynamic_slice_in_dim(templates, section_index * half_rows, half_rows, 0)
    my_rows, wavelet_stack = frame_work(frames[0], kernels, my_half)
    other_rows = lax.ppermute(
        my_rows, "section", [(i, (i + 1) % section_count) for i in range(section_count)]
    )
    slots = pair_block.shape[2]
    live_pairs = pair_count[0, 0, 0]
    block_ids = pair_block[0, 0]
    tile_ids = pair_tile[0, 0]
    responses = score_pairs(
        wavelet_stack, my_rows, other_rows, tile_ids, block_ids, live_pairs, section_index
    )
    positions = jnp.take(owner_order.reshape(-1, PB), block_ids, axis=0).reshape(-1)
    groups = PREC // PB
    by_group = jnp.where(
        (positions // PB)[:, None] == jnp.arange(groups, dtype=jnp.int32)[None, :],
        responses.reshape(-1)[:, None],
        0.0,
    )
    by_lane = ((positions % PB)[:, None] == jnp.arange(PB, dtype=jnp.int32)[None, :]).astype(
        jnp.float32
    )
    placed = jnp.einsum(
        "ka,kb->ab",
        by_group,
        by_lane,
        precision=lax.Precision.HIGHEST,
        preferred_element_type=jnp.float32,
    ).reshape(-1)
    dev_count = lax.axis_size(DEV)
    local_total = jnp.sum(responses)
    payload = jnp.concatenate(
        [
            placed.reshape(dev_count, 1, PREC // dev_count),
            jnp.broadcast_to(local_total, (dev_count, 1, 128)),
        ],
        axis=2,
    )
    return reduce_owned(payload)


def reduce_kernel(sizes, payload_ref, out_ref, gathered, totals, send_sems, recv_sems, total_send, total_recv):
    n_section, n_grp, n_dy, n_dz = sizes
    n_dev = n_dy * n_dz
    section = lax.axis_index("section")
    grp = lax.axis_index("grp")
    dy = lax.axis_index("dy")
    dz = lax.axis_index("dz")
    dev = dy * n_dz + dz
    me = section * n_dev + dev
    peers = n_section * n_dev
    owned_width = out_ref.shape[1]

    barrier = pltpu.get_barrier_semaphore()

    def greet(index, carry):
        @pl.when(index != me)
        def _():
            pl.semaphore_signal(
                barrier,
                inc=1,
                device_id=(index // n_dev, grp, index % n_dev // n_dz, index % n_dz),
                device_id_type=pl.DeviceIdType.MESH,
            )

        return carry

    lax.fori_loop(0, peers, greet, 0)
    for step in range(1, n_grp):
        pl.semaphore_signal(
            barrier,
            inc=1,
            device_id=(section, (grp + step) % n_grp, dy, dz),
            device_id_type=pl.DeviceIdType.MESH,
        )
    pl.semaphore_wait(barrier, peers - 1 + n_grp - 1)

    def chunk_copy(index):
        return pltpu.make_async_remote_copy(
            src_ref=payload_ref.at[index % n_dev],
            dst_ref=gathered.at[me],
            send_sem=send_sems.at[index],
            recv_sem=recv_sems.at[me],
            device_id=(index // n_dev, grp, index % n_dev // n_dz, index % n_dz),
            device_id_type=pl.DeviceIdType.MESH,
        )

    def send(index, carry):
        @pl.when(index != me)
        def _():
            chunk_copy(index).start()

        return carry

    lax.fori_loop(0, peers, send, 0)
    gathered[me] = payload_ref[dev]

    def arrive(index, carry):
        @pl.when(index != me)
        def _():
            pltpu.make_async_remote_copy(
                src_ref=payload_ref.at[0],
                dst_ref=gathered.at[index],
                send_sem=send_sems.at[index],
                recv_sem=recv_sems.at[index],
                device_id=(index // n_dev, grp, index % n_dev // n_dz, index % n_dz),
                device_id_type=pl.DeviceIdType.MESH,
            ).wait_recv()
            chunk_copy(index).wait_send()

        return carry

    lax.fori_loop(0, peers, arrive, 0)

    def accumulate(index, acc):
        return acc + gathered[index]

    summed = lax.fori_loop(0, peers, accumulate, jnp.zeros(gathered.shape[1:], jnp.float32))
    totals[grp] = summed[:, owned_width:]

    def total_copy(step):
        target = (grp + step) % n_grp
        return pltpu.make_async_remote_copy(
            src_ref=totals.at[grp],
            dst_ref=totals.at[grp],
            send_sem=total_send.at[target],
            recv_sem=total_recv.at[grp],
            device_id=(section, target, dy, dz),
            device_id_type=pl.DeviceIdType.MESH,
        )

    for step in range(1, n_grp):
        total_copy(step).start()
    for step in range(1, n_grp):
        source = (grp + step) % n_grp
        pltpu.make_async_remote_copy(
            src_ref=totals.at[source],
            dst_ref=totals.at[source],
            send_sem=total_send.at[source],
            recv_sem=total_recv.at[source],
            device_id=(section, source, dy, dz),
            device_id_type=pl.DeviceIdType.MESH,
        ).wait_recv()
        total_copy(step).wait_send()
    run_sum = totals[0]
    for index in range(1, n_grp):
        run_sum = run_sum + totals[index]
    own_total = summed[:, owned_width : owned_width + 1]
    factor = (run_sum[:, 0:1] / n_grp) / own_total
    out_ref[...] = summed[:, :owned_width] * factor


def reduce_owned(payload):
    sizes = (lax.axis_size("section"), lax.axis_size("grp"), lax.axis_size("dy"), lax.axis_size("dz"))
    n_section, n_grp, n_dy, n_dz = sizes
    peers = n_section * n_dy * n_dz
    rows, one, width = payload.shape
    owned_width = width - 128
    return pl.pallas_call(
        functools.partial(reduce_kernel, sizes),
        out_shape=jax.ShapeDtypeStruct((1, owned_width), jnp.float32),
        in_specs=[pl.BlockSpec(memory_space=pltpu.VMEM)],
        out_specs=pl.BlockSpec(memory_space=pltpu.VMEM),
        scratch_shapes=[
            pltpu.VMEM((peers, 1, width), jnp.float32),
            pltpu.VMEM((n_grp, 1, 128), jnp.float32),
            pltpu.SemaphoreType.DMA((peers,)),
            pltpu.SemaphoreType.DMA((peers,)),
            pltpu.SemaphoreType.DMA((n_grp,)),
            pltpu.SemaphoreType.DMA((n_grp,)),
        ],
        compiler_params=pltpu.CompilerParams(collective_id=0, has_side_effects=True),
    )(payload)


def frame_kernel(
    sizes,
    frames_ref,
    kernels_ref,
    half_ref,
    out_ref,
    wave_ref,
    halo_left,
    halo_right,
    own_scans,
    partner_scans,
    own_sem,
    z_send,
    z_recv,
    y_send,
    y_recv,
    halo_send,
    halo_recv,
    swap_send,
    swap_recv,
):
    n_section, n_dy, n_dz = sizes
    n_dev = n_dy * n_dz
    section = lax.axis_index("section")
    grp = lax.axis_index("grp")
    dy = lax.axis_index("dy")
    dz = lax.axis_index("dz")
    dev = dy * n_dz + dz
    partner_section = (section + 1) % n_section

    def dev_peer(index):
        return (section, grp, index // n_dz, index % n_dz)

    barrier = pltpu.get_barrier_semaphore()
    for step in range(1, n_dz):
        pl.semaphore_signal(
            barrier,
            inc=1,
            device_id=(section, grp, dy, (dz + step) % n_dz),
            device_id_type=pl.DeviceIdType.MESH,
        )
    for step in range(1, n_dy):
        pl.semaphore_signal(
            barrier,
            inc=1,
            device_id=(section, grp, (dy + step) % n_dy, dz),
            device_id_type=pl.DeviceIdType.MESH,
        )
    pl.semaphore_signal(
        barrier,
        inc=1,
        device_id=(partner_section, grp, dy, dz),
        device_id_type=pl.DeviceIdType.MESH,
    )
    has_left = dev > 0
    has_right = dev < n_dev - 1
    far_left = jnp.logical_and(has_left, dz == 0)
    far_right = jnp.logical_and(has_right, dz == n_dz - 1)

    @pl.when(far_left)
    def _():
        pl.semaphore_signal(
            barrier, inc=1, device_id=dev_peer(dev - 1), device_id_type=pl.DeviceIdType.MESH
        )

    @pl.when(far_right)
    def _():
        pl.semaphore_signal(
            barrier, inc=1, device_id=dev_peer(dev + 1), device_id_type=pl.DeviceIdType.MESH
        )

    extra = far_left.astype(jnp.int32) + far_right.astype(jnp.int32)
    pl.semaphore_wait(barrier, n_dz - 1 + n_dy - 1 + 1 + extra)

    own = pltpu.make_async_copy(half_ref, out_ref.at[dev], own_sem)
    own.start()

    def z_copy(target, source):
        return pltpu.make_async_remote_copy(
            src_ref=half_ref,
            dst_ref=out_ref.at[dy * n_dz + source],
            send_sem=z_send.at[target],
            recv_sem=z_recv.at[source],
            device_id=(section, grp, dy, target),
            device_id_type=pl.DeviceIdType.MESH,
        )

    for step in range(1, n_dz):
        z_copy((dz + step) % n_dz, dz).start()

    def y_copy(target, source, chunk):
        slot = source * n_dz + chunk
        return pltpu.make_async_remote_copy(
            src_ref=out_ref.at[slot],
            dst_ref=out_ref.at[slot],
            send_sem=y_send.at[target * n_dz + chunk],
            recv_sem=y_recv.at[slot],
            device_id=(section, grp, target, dz),
            device_id_type=pl.DeviceIdType.MESH,
        )

    def y_own(target):
        return pltpu.make_async_remote_copy(
            src_ref=half_ref,
            dst_ref=out_ref.at[dev],
            send_sem=y_send.at[target * n_dz + dz],
            recv_sem=y_recv.at[dev],
            device_id=(section, grp, target, dz),
            device_id_type=pl.DeviceIdType.MESH,
        )

    for step in range(1, n_dy):
        y_own((dy + step) % n_dy).start()
    for step in range(1, n_dz):
        source = (dz + n_dz - step) % n_dz
        z_copy(source, source).wait_recv()
        for hop in range(1, n_dy):
            y_copy((dy + hop) % n_dy, dy, source).start()
    own.wait()
    for step in range(1, n_dz):
        z_copy((dz + step) % n_dz, dz).wait_send()

    count_frames = frames_ref.shape[0]

    def to_left():
        return pltpu.make_async_remote_copy(
            src_ref=frames_ref.at[pl.ds(0, RAD)],
            dst_ref=halo_right,
            send_sem=halo_send.at[0],
            recv_sem=halo_recv.at[1],
            device_id=dev_peer(dev - 1),
            device_id_type=pl.DeviceIdType.MESH,
        )

    def to_right():
        return pltpu.make_async_remote_copy(
            src_ref=frames_ref.at[pl.ds(count_frames - RAD, RAD)],
            dst_ref=halo_left,
            send_sem=halo_send.at[1],
            recv_sem=halo_recv.at[0],
            device_id=dev_peer(dev + 1),
            device_id_type=pl.DeviceIdType.MESH,
        )

    @pl.when(has_left)
    def _():
        to_left().start()

    @pl.when(has_right)
    def _():
        to_right().start()

    @pl.when(jnp.logical_not(has_left))
    def _():
        halo_left[...] = jnp.zeros(halo_left.shape, halo_left.dtype)

    @pl.when(jnp.logical_not(has_right))
    def _():
        halo_right[...] = jnp.zeros(halo_right.shape, halo_right.dtype)

    @pl.when(has_left)
    def _():
        to_right_of_left = pltpu.make_async_remote_copy(
            src_ref=frames_ref.at[pl.ds(0, RAD)],
            dst_ref=halo_left,
            send_sem=halo_send.at[1],
            recv_sem=halo_recv.at[0],
            device_id=dev_peer(dev - 1),
            device_id_type=pl.DeviceIdType.MESH,
        )
        to_right_of_left.wait_recv()
        to_left().wait_send()

    @pl.when(has_right)
    def _():
        to_left_of_right = pltpu.make_async_remote_copy(
            src_ref=frames_ref.at[pl.ds(0, RAD)],
            dst_ref=halo_right,
            send_sem=halo_send.at[0],
            recv_sem=halo_recv.at[1],
            device_id=dev_peer(dev + 1),
            device_id_type=pl.DeviceIdType.MESH,
        )
        to_left_of_right.wait_recv()
        to_right().wait_send()

    weights = retention_weights()

    def padded_frame(place):
        if place < RAD:
            return halo_left[place]
        if place < RAD + count_frames:
            return frames_ref[place - RAD]
        return halo_right[place - RAD - count_frames]

    for frame in range(count_frames):
        total = weights[0] * padded_frame(frame).astype(jnp.float32)
        for offset in range(1, 2 * RAD + 1):
            total = total + weights[offset] * padded_frame(frame + offset).astype(jnp.float32)
        own_scans[frame] = total.astype(own_scans.dtype)

    swap = pltpu.make_async_remote_copy(
        src_ref=own_scans,
        dst_ref=partner_scans,
        send_sem=swap_send,
        recv_sem=swap_recv,
        device_id=(partner_section, grp, dy, dz),
        device_id_type=pl.DeviceIdType.MESH,
    )
    swap.start()
    swap.wait()

    half = own_scans.shape[1]

    def level_frame(frame, carry):
        for level in range(SCALES):
            table = kernels_ref[level]
            acc = jnp.dot(table[:, :half], own_scans[frame], preferred_element_type=jnp.float32)
            acc = acc + jnp.dot(
                table[:, half:], partner_scans[frame], preferred_element_type=jnp.float32
            )
            wave_ref[level, frame] = acc.astype(wave_ref.dtype)
        return carry

    lax.fori_loop(0, count_frames, level_frame, 0)

    for step in range(1, n_dy):
        source = (dy + n_dy - step) % n_dy
        for chunk in range(n_dz):
            y_copy(source, source, chunk).wait_recv()
    for step in range(1, n_dy):
        for chunk in range(n_dz):
            y_copy((dy + step) % n_dy, dy, chunk).wait_send()


def frame_work(frames, kernels, half):
    sizes = (lax.axis_size("section"), lax.axis_size("dy"), lax.axis_size("dz"))
    n_section, n_dy, n_dz = sizes
    rows, channels = half.shape
    count_frames, mob_local, _ = frames.shape
    rows_out, wave = pl.pallas_call(
        functools.partial(frame_kernel, sizes),
        out_shape=(
            jax.ShapeDtypeStruct((n_dy * n_dz, rows, channels), half.dtype),
            jax.ShapeDtypeStruct((SCALES, count_frames, mob_local, channels), jnp.bfloat16),
        ),
        in_specs=[pl.BlockSpec(memory_space=pltpu.VMEM)] * 3,
        out_specs=(pl.BlockSpec(memory_space=pltpu.VMEM), pl.BlockSpec(memory_space=pltpu.VMEM)),
        scratch_shapes=[
            pltpu.VMEM((RAD, mob_local, channels), frames.dtype),
            pltpu.VMEM((RAD, mob_local, channels), frames.dtype),
            pltpu.VMEM((count_frames, mob_local, channels), jnp.bfloat16),
            pltpu.VMEM((count_frames, mob_local, channels), jnp.bfloat16),
            pltpu.SemaphoreType.DMA(()),
            pltpu.SemaphoreType.DMA((n_dz,)),
            pltpu.SemaphoreType.DMA((n_dz,)),
            pltpu.SemaphoreType.DMA((n_dy * n_dz,)),
            pltpu.SemaphoreType.DMA((n_dy * n_dz,)),
            pltpu.SemaphoreType.DMA((2,)),
            pltpu.SemaphoreType.DMA((2,)),
            pltpu.SemaphoreType.DMA(()),
            pltpu.SemaphoreType.DMA(()),
        ],
        compiler_params=pltpu.CompilerParams(
            collective_id=1, has_side_effects=True, vmem_limit_bytes=56 * 1024 * 1024
        ),
    )(frames, kernels, half)
    return rows_out.reshape(n_dy * n_dz * rows, channels), wave


def score_kernel(tile_ref, block_ref, count_ref, section_ref, wave_ref, mine_ref, other_ref, out_ref):
    slot = pl.program_id(0)
    live = slot < count_ref[0]
    mine = block_ref[slot] % 2 == section_ref[0]

    def score(rows_ref):
        rows = rows_ref[...]
        acc = jnp.zeros((1, PB), jnp.float32)
        for level in range(SCALES):
            cells = wave_ref[level].reshape(-1, rows.shape[1])
            scores = lax.dot_general(
                cells, rows, (((1,), (1,)), ((), ())), preferred_element_type=jnp.float32
            )
            acc = acc + jnp.sum(jnp.maximum(scores, 0.0), axis=0, keepdims=True)
        cell_count = SCALES * wave_ref.shape[1] * wave_ref.shape[2]
        out_ref[0] = acc / cell_count

    @pl.when(jnp.logical_and(live, mine))
    def _():
        score(mine_ref)

    @pl.when(jnp.logical_and(live, jnp.logical_not(mine)))
    def _():
        score(other_ref)

    @pl.when(jnp.logical_not(live))
    def _():
        out_ref[0] = jnp.zeros((1, PB), jnp.float32)


def score_pairs(wavelet_stack, my_rows, other_rows, tile_ids, block_ids, live_pairs, section_index):
    slots = tile_ids.shape[0]
    scales, frames_local, mob_local, channels = wavelet_stack.shape

    def last_live(k, count_ref):
        return jnp.minimum(k, count_ref[0] - 1)

    def rows_block(k, t, b, c, s):
        return (b[last_live(k, c)] // 2, 0)

    grid_spec = pltpu.PrefetchScalarGridSpec(
        num_scalar_prefetch=4,
        grid=(slots,),
        in_specs=[
            pl.BlockSpec(
                (scales, frames_local, TM, channels),
                lambda k, t, b, c, s: (0, 0, t[last_live(k, c)], 0),
            ),
            pl.BlockSpec((PB, channels), rows_block),
            pl.BlockSpec((PB, channels), rows_block),
        ],
        out_specs=pl.BlockSpec((1, 1, PB), lambda k, t, b, c, s: (k, 0, 0)),
    )
    out = pl.pallas_call(
        score_kernel,
        grid_spec=grid_spec,
        out_shape=jax.ShapeDtypeStruct((slots, 1, PB), jnp.float32),
    )(
        tile_ids,
        block_ids,
        live_pairs.reshape(1),
        section_index.astype(jnp.int32).reshape(1),
        wavelet_stack,
        my_rows,
        other_rows,
    )
    return out.reshape(slots, PB)


def solution(mesh):
    section_count, grp_count, dev_count = mesh.devices.shape
    dz_count = 8 if dev_count % 8 == 0 else dev_count
    split_mesh = jax.sharding.Mesh(
        mesh.devices.reshape(section_count, grp_count, dev_count // dz_count, dz_count),
        ("section", "grp", "dy", "dz"),
    )
    placed = (
        P("grp", DEV, "section", None),
        P(DEV, None),
        P("section", "grp", DEV),
        P("section", "grp", DEV),
        P("section", "grp", DEV),
        P(),
    )
    return jax.shard_map(
        on_device, mesh=split_mesh, in_specs=placed, out_specs=P("grp", DEV), check_vma=False
    )
```

```python
import functools
import math

import jax
import jax.numpy as jnp
from jax import lax
from jax.experimental import pallas as pl
from jax.experimental.pallas import tpu as pltpu
from jax.sharding import PartitionSpec as P

MOB = 512
SCALES = 6
RAD = 4
TM = 64
PB = 128
PREC = 8192
DEV = ("dy", "dz")


retention_spread = 2.0


def extended(cells, sides, width):
    for axis, dim in sides:
        count = lax.axis_size(axis)
        ends = count - 1
        head = lax.slice_in_dim(cells, 0, width, axis=dim)
        tail = lax.slice_in_dim(cells, cells.shape[dim] - width, cells.shape[dim], axis=dim)
        cells = jnp.concatenate(
            [
                lax.ppermute(tail, axis, [(i, (i + 1) % count) for i in range(ends)]),
                cells,
                lax.ppermute(head, axis, [((i + 1) % count, i) for i in range(ends)]),
            ],
            axis=dim,
        )
    return cells


def retention_weights():
    bell_values = [
        math.exp(-0.5 * (offset / retention_spread) ** 2) for offset in range(-RAD, RAD + 1)
    ]
    bell_total = sum(bell_values)
    return [weight_value / bell_total for weight_value in bell_values]


def mobility_kernels(row_start, row_count, col_start):
    row_place = (row_start + jnp.arange(row_count, dtype=jnp.int32)).astype(jnp.float32)
    col_place = ((col_start + jnp.arange(MOB, dtype=jnp.int32)) % MOB).astype(jnp.float32)
    distance = row_place[:, None] - col_place[None, :]
    tables = []
    for level in range(SCALES):
        spread_scans = 2.0**level
        scaled = distance / spread_scans
        tables.append(
            (1.0 - scaled * scaled)
            * jnp.exp(-0.5 * scaled * scaled)
            / math.sqrt(0.75 * math.sqrt(math.pi) * spread_scans)
        )
    return jnp.stack(tables).astype(jnp.bfloat16)


def on_device(frames, templates, pair_block, pair_tile, pair_count, owner_order):
    section_index = lax.axis_index("section")
    mob_local = frames.shape[2]
    section_count = lax.axis_size("section")
    kernels = mobility_kernels(section_index * mob_local, mob_local, section_index * mob_local)
    half_rows = templates.shape[0] // 2
    my_half = lax.dynamic_slice_in_dim(templates, section_index * half_rows, half_rows, 0)
    my_rows, wavelet_stack = frame_work(frames[0], kernels, my_half)
    other_rows = lax.ppermute(
        my_rows, "section", [(i, (i + 1) % section_count) for i in range(section_count)]
    )
    slots = pair_block.shape[2]
    live_pairs = pair_count[0, 0, 0]
    block_ids = pair_block[0, 0]
    tile_ids = pair_tile[0, 0]
    responses = score_pairs(
        wavelet_stack, my_rows, other_rows, tile_ids, block_ids, live_pairs, section_index
    )
    positions = jnp.take(owner_order.reshape(-1, PB), block_ids, axis=0).reshape(-1)
    groups = PREC // PB
    by_group = jnp.where(
        (positions // PB)[:, None] == jnp.arange(groups, dtype=jnp.int32)[None, :],
        responses.reshape(-1)[:, None],
        0.0,
    )
    by_lane = ((positions % PB)[:, None] == jnp.arange(PB, dtype=jnp.int32)[None, :]).astype(
        jnp.float32
    )
    placed = jnp.einsum(
        "ka,kb->ab",
        by_group,
        by_lane,
        precision=lax.Precision.HIGHEST,
        preferred_element_type=jnp.float32,
    ).reshape(-1)
    dev_count = lax.axis_size(DEV)
    local_total = jnp.sum(responses)
    payload = jnp.concatenate(
        [
            placed.reshape(dev_count, 1, PREC // dev_count),
            jnp.broadcast_to(local_total, (dev_count, 1, 128)),
        ],
        axis=2,
    )
    return reduce_owned(payload)


def reduce_kernel(sizes, payload_ref, out_ref, gathered, totals, send_sems, recv_sems, total_send, total_recv):
    n_section, n_grp, n_dy, n_dz = sizes
    n_dev = n_dy * n_dz
    section = lax.axis_index("section")
    grp = lax.axis_index("grp")
    dy = lax.axis_index("dy")
    dz = lax.axis_index("dz")
    dev = dy * n_dz + dz
    me = section * n_dev + dev
    peers = n_section * n_dev
    owned_width = out_ref.shape[1]

    barrier = pltpu.get_barrier_semaphore()

    def greet(index, carry):
        @pl.when(index != me)
        def _():
            pl.semaphore_signal(
                barrier,
                inc=1,
                device_id=(index // n_dev, grp, index % n_dev // n_dz, index % n_dz),
                device_id_type=pl.DeviceIdType.MESH,
            )

        return carry

    lax.fori_loop(0, peers, greet, 0)
    for step in range(1, n_grp):
        pl.semaphore_signal(
            barrier,
            inc=1,
            device_id=(section, (grp + step) % n_grp, dy, dz),
            device_id_type=pl.DeviceIdType.MESH,
        )
    pl.semaphore_wait(barrier, peers - 1 + n_grp - 1)

    def chunk_copy(index):
        return pltpu.make_async_remote_copy(
            src_ref=payload_ref.at[index % n_dev],
            dst_ref=gathered.at[me],
            send_sem=send_sems.at[index],
            recv_sem=recv_sems.at[me],
            device_id=(index // n_dev, grp, index % n_dev // n_dz, index % n_dz),
            device_id_type=pl.DeviceIdType.MESH,
        )

    def send(index, carry):
        @pl.when(index != me)
        def _():
            chunk_copy(index).start()

        return carry

    lax.fori_loop(0, peers, send, 0)
    gathered[me] = payload_ref[dev]

    def arrive(index, carry):
        @pl.when(index != me)
        def _():
            pltpu.make_async_remote_copy(
                src_ref=payload_ref.at[0],
                dst_ref=gathered.at[index],
                send_sem=send_sems.at[index],
                recv_sem=recv_sems.at[index],
                device_id=(index // n_dev, grp, index % n_dev // n_dz, index % n_dz),
                device_id_type=pl.DeviceIdType.MESH,
            ).wait_recv()
            chunk_copy(index).wait_send()

        return carry

    lax.fori_loop(0, peers, arrive, 0)

    def accumulate(index, acc):
        return acc + gathered[index]

    summed = lax.fori_loop(0, peers, accumulate, jnp.zeros(gathered.shape[1:], jnp.float32))
    totals[grp] = summed[:, owned_width:]

    def total_copy(step):
        target = (grp + step) % n_grp
        return pltpu.make_async_remote_copy(
            src_ref=totals.at[grp],
            dst_ref=totals.at[grp],
            send_sem=total_send.at[target],
            recv_sem=total_recv.at[grp],
            device_id=(section, target, dy, dz),
            device_id_type=pl.DeviceIdType.MESH,
        )

    for step in range(1, n_grp):
        total_copy(step).start()
    for step in range(1, n_grp):
        source = (grp + step) % n_grp
        pltpu.make_async_remote_copy(
            src_ref=totals.at[source],
            dst_ref=totals.at[source],
            send_sem=total_send.at[source],
            recv_sem=total_recv.at[source],
            device_id=(section, source, dy, dz),
            device_id_type=pl.DeviceIdType.MESH,
        ).wait_recv()
        total_copy(step).wait_send()
    run_sum = totals[0]
    for index in range(1, n_grp):
        run_sum = run_sum + totals[index]
    own_total = summed[:, owned_width : owned_width + 1]
    factor = (run_sum[:, 0:1] / n_grp) / own_total
    out_ref[...] = summed[:, :owned_width] * factor


def reduce_owned(payload):
    sizes = (lax.axis_size("section"), lax.axis_size("grp"), lax.axis_size("dy"), lax.axis_size("dz"))
    n_section, n_grp, n_dy, n_dz = sizes
    peers = n_section * n_dy * n_dz
    rows, one, width = payload.shape
    owned_width = width - 128
    return pl.pallas_call(
        functools.partial(reduce_kernel, sizes),
        out_shape=jax.ShapeDtypeStruct((1, owned_width), jnp.float32),
        in_specs=[pl.BlockSpec(memory_space=pltpu.VMEM)],
        out_specs=pl.BlockSpec(memory_space=pltpu.VMEM),
        scratch_shapes=[
            pltpu.VMEM((peers, 1, width), jnp.float32),
            pltpu.VMEM((n_grp, 1, 128), jnp.float32),
            pltpu.SemaphoreType.DMA((peers,)),
            pltpu.SemaphoreType.DMA((peers,)),
            pltpu.SemaphoreType.DMA((n_grp,)),
            pltpu.SemaphoreType.DMA((n_grp,)),
        ],
        compiler_params=pltpu.CompilerParams(collective_id=0, has_side_effects=True),
    )(payload)


def frame_kernel(
    sizes,
    frames_ref,
    kernels_ref,
    half_ref,
    out_ref,
    wave_ref,
    halo_left,
    halo_right,
    own_scans,
    partner_scans,
    own_sem,
    z_send,
    z_recv,
    y_send,
    y_recv,
    halo_send,
    halo_recv,
    swap_send,
    swap_recv,
):
    n_section, n_dy, n_dz = sizes
    n_dev = n_dy * n_dz
    section = lax.axis_index("section")
    grp = lax.axis_index("grp")
    dy = lax.axis_index("dy")
    dz = lax.axis_index("dz")
    dev = dy * n_dz + dz
    partner_section = (section + 1) % n_section

    def dev_peer(index):
        return (section, grp, index // n_dz, index % n_dz)

    barrier = pltpu.get_barrier_semaphore()
    for step in range(1, n_dz):
        pl.semaphore_signal(
            barrier,
            inc=1,
            device_id=(section, grp, dy, (dz + step) % n_dz),
            device_id_type=pl.DeviceIdType.MESH,
        )
    up = (dy + 1) % n_dy
    down = (dy + n_dy - 1) % n_dy
    for row in (up, down):
        pl.semaphore_signal(
            barrier,
            inc=1,
            device_id=(section, grp, row, dz),
            device_id_type=pl.DeviceIdType.MESH,
        )
    pl.semaphore_signal(
        barrier,
        inc=1,
        device_id=(partner_section, grp, dy, dz),
        device_id_type=pl.DeviceIdType.MESH,
    )
    has_left = dev > 0
    has_right = dev < n_dev - 1
    far_left = jnp.logical_and(has_left, dz == 0)
    far_right = jnp.logical_and(has_right, dz == n_dz - 1)

    @pl.when(far_left)
    def _():
        pl.semaphore_signal(
            barrier, inc=1, device_id=dev_peer(dev - 1), device_id_type=pl.DeviceIdType.MESH
        )

    @pl.when(far_right)
    def _():
        pl.semaphore_signal(
            barrier, inc=1, device_id=dev_peer(dev + 1), device_id_type=pl.DeviceIdType.MESH
        )

    extra = far_left.astype(jnp.int32) + far_right.astype(jnp.int32)
    pl.semaphore_wait(barrier, n_dz - 1 + 2 + 1 + extra)

    own = pltpu.make_async_copy(half_ref, out_ref.at[dev], own_sem)
    own.start()

    def z_copy(target, source):
        return pltpu.make_async_remote_copy(
            src_ref=half_ref,
            dst_ref=out_ref.at[dy * n_dz + source],
            send_sem=z_send.at[target],
            recv_sem=z_recv.at[source],
            device_id=(section, grp, dy, target),
            device_id_type=pl.DeviceIdType.MESH,
        )

    for step in range(1, n_dz):
        z_copy((dz + step) % n_dz, dz).start()

    def y_copy(direction, row, chunk):
        slot = row * n_dz + chunk
        target = up if direction == 0 else down
        return pltpu.make_async_remote_copy(
            src_ref=out_ref.at[slot],
            dst_ref=out_ref.at[slot],
            send_sem=y_send.at[direction * n_dy * n_dz + slot],
            recv_sem=y_recv.at[slot],
            device_id=(section, grp, target, dz),
            device_id_type=pl.DeviceIdType.MESH,
        )

    def y_own(direction):
        target = up if direction == 0 else down
        return pltpu.make_async_remote_copy(
            src_ref=half_ref,
            dst_ref=out_ref.at[dev],
            send_sem=y_send.at[direction * n_dy * n_dz + dev],
            recv_sem=y_recv.at[dev],
            device_id=(section, grp, target, dz),
            device_id_type=pl.DeviceIdType.MESH,
        )

    for direction in (0, 1):
        y_own(direction).start()
    for step in range(1, n_dz):
        source = (dz + n_dz - step) % n_dz
        z_copy(source, source).wait_recv()
        for direction in (0, 1):
            y_copy(direction, dy, source).start()
    own.wait()
    for step in range(1, n_dz):
        z_copy((dz + step) % n_dz, dz).wait_send()

    count_frames = frames_ref.shape[0]

    def to_left():
        return pltpu.make_async_remote_copy(
            src_ref=frames_ref.at[pl.ds(0, RAD)],
            dst_ref=halo_right,
            send_sem=halo_send.at[0],
            recv_sem=halo_recv.at[1],
            device_id=dev_peer(dev - 1),
            device_id_type=pl.DeviceIdType.MESH,
        )

    def to_right():
        return pltpu.make_async_remote_copy(
            src_ref=frames_ref.at[pl.ds(count_frames - RAD, RAD)],
            dst_ref=halo_left,
            send_sem=halo_send.at[1],
            recv_sem=halo_recv.at[0],
            device_id=dev_peer(dev + 1),
            device_id_type=pl.DeviceIdType.MESH,
        )

    @pl.when(has_left)
    def _():
        to_left().start()

    @pl.when(has_right)
    def _():
        to_right().start()

    @pl.when(jnp.logical_not(has_left))
    def _():
        halo_left[...] = jnp.zeros(halo_left.shape, halo_left.dtype)

    @pl.when(jnp.logical_not(has_right))
    def _():
        halo_right[...] = jnp.zeros(halo_right.shape, halo_right.dtype)

    @pl.when(has_left)
    def _():
        to_right_of_left = pltpu.make_async_remote_copy(
            src_ref=frames_ref.at[pl.ds(0, RAD)],
            dst_ref=halo_left,
            send_sem=halo_send.at[1],
            recv_sem=halo_recv.at[0],
            device_id=dev_peer(dev - 1),
            device_id_type=pl.DeviceIdType.MESH,
        )
        to_right_of_left.wait_recv()
        to_left().wait_send()

    @pl.when(has_right)
    def _():
        to_left_of_right = pltpu.make_async_remote_copy(
            src_ref=frames_ref.at[pl.ds(0, RAD)],
            dst_ref=halo_right,
            send_sem=halo_send.at[0],
            recv_sem=halo_recv.at[1],
            device_id=dev_peer(dev + 1),
            device_id_type=pl.DeviceIdType.MESH,
        )
        to_left_of_right.wait_recv()
        to_right().wait_send()

    weights = retention_weights()

    def padded_frame(place):
        if place < RAD:
            return halo_left[place]
        if place < RAD + count_frames:
            return frames_ref[place - RAD]
        return halo_right[place - RAD - count_frames]

    for frame in range(count_frames):
        total = weights[0] * padded_frame(frame).astype(jnp.float32)
        for offset in range(1, 2 * RAD + 1):
            total = total + weights[offset] * padded_frame(frame + offset).astype(jnp.float32)
        own_scans[frame] = total.astype(own_scans.dtype)

    swap = pltpu.make_async_remote_copy(
        src_ref=own_scans,
        dst_ref=partner_scans,
        send_sem=swap_send,
        recv_sem=swap_recv,
        device_id=(partner_section, grp, dy, dz),
        device_id_type=pl.DeviceIdType.MESH,
    )
    swap.start()
    relay = n_dz // 2
    for chunk in range(n_dz):
        y_copy(0, down, chunk).wait_recv()
        if chunk < relay:
            y_copy(0, down, chunk).start()
        y_copy(1, up, chunk).wait_recv()
        if chunk >= relay:
            y_copy(1, up, chunk).start()
    swap.wait()

    half = own_scans.shape[1]

    def level_frame(frame, carry):
        for level in range(SCALES):
            table = kernels_ref[level]
            acc = jnp.dot(table[:, :half], own_scans[frame], preferred_element_type=jnp.float32)
            acc = acc + jnp.dot(
                table[:, half:], partner_scans[frame], preferred_element_type=jnp.float32
            )
            wave_ref[level, frame] = acc.astype(wave_ref.dtype)
        return carry

    lax.fori_loop(0, count_frames, level_frame, 0)

    opposite = (dy + 2) % n_dy
    for chunk in range(n_dz):
        y_copy(0, opposite, chunk).wait_recv()
    for direction in (0, 1):
        for chunk in range(n_dz):
            y_copy(direction, dy, chunk).wait_send()
    for chunk in range(relay):
        y_copy(0, down, chunk).wait_send()
    for chunk in range(relay, n_dz):
        y_copy(1, up, chunk).wait_send()


def frame_work(frames, kernels, half):
    sizes = (lax.axis_size("section"), lax.axis_size("dy"), lax.axis_size("dz"))
    n_section, n_dy, n_dz = sizes
    rows, channels = half.shape
    count_frames, mob_local, _ = frames.shape
    rows_out, wave = pl.pallas_call(
        functools.partial(frame_kernel, sizes),
        out_shape=(
            jax.ShapeDtypeStruct((n_dy * n_dz, rows, channels), half.dtype),
            jax.ShapeDtypeStruct((SCALES, count_frames, mob_local, channels), jnp.bfloat16),
        ),
        in_specs=[pl.BlockSpec(memory_space=pltpu.VMEM)] * 3,
        out_specs=(pl.BlockSpec(memory_space=pltpu.VMEM), pl.BlockSpec(memory_space=pltpu.VMEM)),
        scratch_shapes=[
            pltpu.VMEM((RAD, mob_local, channels), frames.dtype),
            pltpu.VMEM((RAD, mob_local, channels), frames.dtype),
            pltpu.VMEM((count_frames, mob_local, channels), jnp.bfloat16),
            pltpu.VMEM((count_frames, mob_local, channels), jnp.bfloat16),
            pltpu.SemaphoreType.DMA(()),
            pltpu.SemaphoreType.DMA((n_dz,)),
            pltpu.SemaphoreType.DMA((n_dz,)),
            pltpu.SemaphoreType.DMA((2 * n_dy * n_dz,)),
            pltpu.SemaphoreType.DMA((n_dy * n_dz,)),
            pltpu.SemaphoreType.DMA((2,)),
            pltpu.SemaphoreType.DMA((2,)),
            pltpu.SemaphoreType.DMA(()),
            pltpu.SemaphoreType.DMA(()),
        ],
        compiler_params=pltpu.CompilerParams(
            collective_id=1, has_side_effects=True, vmem_limit_bytes=56 * 1024 * 1024
        ),
    )(frames, kernels, half)
    return rows_out.reshape(n_dy * n_dz * rows, channels), wave


def score_kernel(tile_ref, block_ref, count_ref, section_ref, wave_ref, mine_ref, other_ref, out_ref):
    slot = pl.program_id(0)
    live = slot < count_ref[0]
    mine = block_ref[slot] % 2 == section_ref[0]

    def score(rows_ref):
        rows = rows_ref[...]
        acc = jnp.zeros((1, PB), jnp.float32)
        for level in range(SCALES):
            cells = wave_ref[level].reshape(-1, rows.shape[1])
            scores = lax.dot_general(
                cells, rows, (((1,), (1,)), ((), ())), preferred_element_type=jnp.float32
            )
            acc = acc + jnp.sum(jnp.maximum(scores, 0.0), axis=0, keepdims=True)
        cell_count = SCALES * wave_ref.shape[1] * wave_ref.shape[2]
        out_ref[0] = acc / cell_count

    @pl.when(jnp.logical_and(live, mine))
    def _():
        score(mine_ref)

    @pl.when(jnp.logical_and(live, jnp.logical_not(mine)))
    def _():
        score(other_ref)

    @pl.when(jnp.logical_not(live))
    def _():
        out_ref[0] = jnp.zeros((1, PB), jnp.float32)


def score_pairs(wavelet_stack, my_rows, other_rows, tile_ids, block_ids, live_pairs, section_index):
    slots = tile_ids.shape[0]
    scales, frames_local, mob_local, channels = wavelet_stack.shape

    def last_live(k, count_ref):
        return jnp.minimum(k, count_ref[0] - 1)

    def rows_block(k, t, b, c, s):
        return (b[last_live(k, c)] // 2, 0)

    grid_spec = pltpu.PrefetchScalarGridSpec(
        num_scalar_prefetch=4,
        grid=(slots,),
        in_specs=[
            pl.BlockSpec(
                (scales, frames_local, TM, channels),
                lambda k, t, b, c, s: (0, 0, t[last_live(k, c)], 0),
            ),
            pl.BlockSpec((PB, channels), rows_block),
            pl.BlockSpec((PB, channels), rows_block),
        ],
        out_specs=pl.BlockSpec((1, 1, PB), lambda k, t, b, c, s: (k, 0, 0)),
    )
    out = pl.pallas_call(
        score_kernel,
        grid_spec=grid_spec,
        out_shape=jax.ShapeDtypeStruct((slots, 1, PB), jnp.float32),
    )(
        tile_ids,
        block_ids,
        live_pairs.reshape(1),
        section_index.astype(jnp.int32).reshape(1),
        wavelet_stack,
        my_rows,
        other_rows,
    )
    return out.reshape(slots, PB)


def solution(mesh):
    section_count, grp_count, dev_count = mesh.devices.shape
    dz_count = 8 if dev_count % 8 == 0 else dev_count
    split_mesh = jax.sharding.Mesh(
        mesh.devices.reshape(section_count, grp_count, dev_count // dz_count, dz_count),
        ("section", "grp", "dy", "dz"),
    )
    placed = (
        P("grp", DEV, "section", None),
        P(DEV, None),
        P("section", "grp", DEV),
        P("section", "grp", DEV),
        P("section", "grp", DEV),
        P(),
    )
    return jax.shard_map(
        on_device, mesh=split_mesh, in_specs=placed, out_specs=P("grp", DEV), check_vma=False
    )
```

```python
import functools
import math

import jax
import jax.numpy as jnp
from jax import lax
from jax.experimental import pallas as pl
from jax.experimental.pallas import tpu as pltpu
from jax.sharding import PartitionSpec as P

MOB = 512
SCALES = 6
RAD = 4
TM = 64
PB = 128
PREC = 8192
DEV = ("dy", "dz")


retention_spread = 2.0


def extended(cells, sides, width):
    for axis, dim in sides:
        count = lax.axis_size(axis)
        ends = count - 1
        head = lax.slice_in_dim(cells, 0, width, axis=dim)
        tail = lax.slice_in_dim(cells, cells.shape[dim] - width, cells.shape[dim], axis=dim)
        cells = jnp.concatenate(
            [
                lax.ppermute(tail, axis, [(i, (i + 1) % count) for i in range(ends)]),
                cells,
                lax.ppermute(head, axis, [((i + 1) % count, i) for i in range(ends)]),
            ],
            axis=dim,
        )
    return cells


def retention_weights():
    bell_values = [
        math.exp(-0.5 * (offset / retention_spread) ** 2) for offset in range(-RAD, RAD + 1)
    ]
    bell_total = sum(bell_values)
    return [weight_value / bell_total for weight_value in bell_values]


def mobility_kernels(row_start, row_count, col_start):
    row_place = (row_start + jnp.arange(row_count, dtype=jnp.int32)).astype(jnp.float32)
    col_place = ((col_start + jnp.arange(MOB, dtype=jnp.int32)) % MOB).astype(jnp.float32)
    distance = row_place[:, None] - col_place[None, :]
    tables = []
    for level in range(SCALES):
        spread_scans = 2.0**level
        scaled = distance / spread_scans
        tables.append(
            (1.0 - scaled * scaled)
            * jnp.exp(-0.5 * scaled * scaled)
            / math.sqrt(0.75 * math.sqrt(math.pi) * spread_scans)
        )
    return jnp.stack(tables).astype(jnp.bfloat16)


def on_device(frames, templates, pair_block, pair_tile, pair_count, owner_order):
    section_index = lax.axis_index("section")
    mob_local = frames.shape[2]
    section_count = lax.axis_size("section")
    kernels = mobility_kernels(section_index * mob_local, mob_local, section_index * mob_local)
    half_rows = templates.shape[0] // 2
    my_half = lax.dynamic_slice_in_dim(templates, section_index * half_rows, half_rows, 0)
    my_rows, wavelet_stack = frame_work(frames[0], kernels, my_half)
    other_rows = lax.ppermute(
        my_rows, "section", [(i, (i + 1) % section_count) for i in range(section_count)]
    )
    slots = pair_block.shape[2]
    live_pairs = pair_count[0, 0, 0]
    block_ids = pair_block[0, 0]
    tile_ids = pair_tile[0, 0]
    responses = score_pairs(
        wavelet_stack, my_rows, other_rows, tile_ids, block_ids, live_pairs, section_index
    )
    positions = jnp.take(owner_order.reshape(-1, PB), block_ids, axis=0).reshape(-1)
    groups = PREC // PB
    by_group = jnp.where(
        (positions // PB)[:, None] == jnp.arange(groups, dtype=jnp.int32)[None, :],
        responses.reshape(-1)[:, None],
        0.0,
    )
    by_lane = ((positions % PB)[:, None] == jnp.arange(PB, dtype=jnp.int32)[None, :]).astype(
        jnp.float32
    )
    placed = jnp.einsum(
        "ka,kb->ab",
        by_group,
        by_lane,
        precision=lax.Precision.HIGHEST,
        preferred_element_type=jnp.float32,
    ).reshape(-1)
    dev_count = lax.axis_size(DEV)
    local_total = jnp.sum(responses)
    payload = jnp.concatenate(
        [
            placed.reshape(dev_count, 1, PREC // dev_count),
            jnp.broadcast_to(local_total, (dev_count, 1, 128)),
        ],
        axis=2,
    )
    return reduce_owned(payload)


def reduce_kernel(sizes, payload_ref, out_ref, gathered, totals, send_sems, recv_sems, total_send, total_recv):
    n_section, n_grp, n_dy, n_dz = sizes
    n_dev = n_dy * n_dz
    section = lax.axis_index("section")
    grp = lax.axis_index("grp")
    dy = lax.axis_index("dy")
    dz = lax.axis_index("dz")
    dev = dy * n_dz + dz
    me = section * n_dev + dev
    peers = n_section * n_dev
    owned_width = out_ref.shape[1]

    barrier = pltpu.get_barrier_semaphore()

    def greet(index, carry):
        @pl.when(index != me)
        def _():
            pl.semaphore_signal(
                barrier,
                inc=1,
                device_id=(index // n_dev, grp, index % n_dev // n_dz, index % n_dz),
                device_id_type=pl.DeviceIdType.MESH,
            )

        return carry

    lax.fori_loop(0, peers, greet, 0)
    for step in range(1, n_grp):
        pl.semaphore_signal(
            barrier,
            inc=1,
            device_id=(section, (grp + step) % n_grp, dy, dz),
            device_id_type=pl.DeviceIdType.MESH,
        )
    pl.semaphore_wait(barrier, peers - 1 + n_grp - 1)

    def chunk_copy(index):
        return pltpu.make_async_remote_copy(
            src_ref=payload_ref.at[index % n_dev],
            dst_ref=gathered.at[me],
            send_sem=send_sems.at[index],
            recv_sem=recv_sems.at[me],
            device_id=(index // n_dev, grp, index % n_dev // n_dz, index % n_dz),
            device_id_type=pl.DeviceIdType.MESH,
        )

    def send(index, carry):
        @pl.when(index != me)
        def _():
            chunk_copy(index).start()

        return carry

    lax.fori_loop(0, peers, send, 0)
    gathered[me] = payload_ref[dev]

    def arrive(index, carry):
        @pl.when(index != me)
        def _():
            pltpu.make_async_remote_copy(
                src_ref=payload_ref.at[0],
                dst_ref=gathered.at[index],
                send_sem=send_sems.at[index],
                recv_sem=recv_sems.at[index],
                device_id=(index // n_dev, grp, index % n_dev // n_dz, index % n_dz),
                device_id_type=pl.DeviceIdType.MESH,
            ).wait_recv()
            chunk_copy(index).wait_send()

        return carry

    lax.fori_loop(0, peers, arrive, 0)

    def accumulate(index, acc):
        return acc + gathered[index]

    summed = lax.fori_loop(0, peers, accumulate, jnp.zeros(gathered.shape[1:], jnp.float32))
    totals[grp] = summed[:, owned_width:]

    def total_copy(step):
        target = (grp + step) % n_grp
        return pltpu.make_async_remote_copy(
            src_ref=totals.at[grp],
            dst_ref=totals.at[grp],
            send_sem=total_send.at[target],
            recv_sem=total_recv.at[grp],
            device_id=(section, target, dy, dz),
            device_id_type=pl.DeviceIdType.MESH,
        )

    for step in range(1, n_grp):
        total_copy(step).start()
    for step in range(1, n_grp):
        source = (grp + step) % n_grp
        pltpu.make_async_remote_copy(
            src_ref=totals.at[source],
            dst_ref=totals.at[source],
            send_sem=total_send.at[source],
            recv_sem=total_recv.at[source],
            device_id=(section, source, dy, dz),
            device_id_type=pl.DeviceIdType.MESH,
        ).wait_recv()
        total_copy(step).wait_send()
    run_sum = totals[0]
    for index in range(1, n_grp):
        run_sum = run_sum + totals[index]
    own_total = summed[:, owned_width : owned_width + 1]
    factor = (run_sum[:, 0:1] / n_grp) / own_total
    out_ref[...] = summed[:, :owned_width] * factor


def reduce_owned(payload):
    sizes = (lax.axis_size("section"), lax.axis_size("grp"), lax.axis_size("dy"), lax.axis_size("dz"))
    n_section, n_grp, n_dy, n_dz = sizes
    peers = n_section * n_dy * n_dz
    rows, one, width = payload.shape
    owned_width = width - 128
    return pl.pallas_call(
        functools.partial(reduce_kernel, sizes),
        out_shape=jax.ShapeDtypeStruct((1, owned_width), jnp.float32),
        in_specs=[pl.BlockSpec(memory_space=pltpu.VMEM)],
        out_specs=pl.BlockSpec(memory_space=pltpu.VMEM),
        scratch_shapes=[
            pltpu.VMEM((peers, 1, width), jnp.float32),
            pltpu.VMEM((n_grp, 1, 128), jnp.float32),
            pltpu.SemaphoreType.DMA((peers,)),
            pltpu.SemaphoreType.DMA((peers,)),
            pltpu.SemaphoreType.DMA((n_grp,)),
            pltpu.SemaphoreType.DMA((n_grp,)),
        ],
        compiler_params=pltpu.CompilerParams(collective_id=0, has_side_effects=True),
    )(payload)


def frame_kernel(
    sizes,
    frames_ref,
    kernels_ref,
    half_ref,
    out_ref,
    wave_ref,
    halo_left,
    halo_right,
    own_scans,
    partner_scans,
    own_sem,
    z_send,
    z_recv,
    y_send,
    y_recv,
    halo_send,
    halo_recv,
    swap_send,
    swap_recv,
):
    n_section, n_dy, n_dz = sizes
    n_dev = n_dy * n_dz
    section = lax.axis_index("section")
    grp = lax.axis_index("grp")
    dy = lax.axis_index("dy")
    dz = lax.axis_index("dz")
    dev = dy * n_dz + dz
    partner_section = (section + 1) % n_section

    def dev_peer(index):
        return (section, grp, index // n_dz, index % n_dz)

    barrier = pltpu.get_barrier_semaphore()
    for step in range(1, n_dz):
        pl.semaphore_signal(
            barrier,
            inc=1,
            device_id=(section, grp, dy, (dz + step) % n_dz),
            device_id_type=pl.DeviceIdType.MESH,
        )
    up = (dy + 1) % n_dy
    down = (dy + n_dy - 1) % n_dy
    for row in (up, down):
        pl.semaphore_signal(
            barrier,
            inc=1,
            device_id=(section, grp, row, dz),
            device_id_type=pl.DeviceIdType.MESH,
        )
    pl.semaphore_signal(
        barrier,
        inc=1,
        device_id=(partner_section, grp, dy, dz),
        device_id_type=pl.DeviceIdType.MESH,
    )
    has_left = dev > 0
    has_right = dev < n_dev - 1
    far_left = jnp.logical_and(has_left, dz == 0)
    far_right = jnp.logical_and(has_right, dz == n_dz - 1)

    @pl.when(far_left)
    def _():
        pl.semaphore_signal(
            barrier, inc=1, device_id=dev_peer(dev - 1), device_id_type=pl.DeviceIdType.MESH
        )

    @pl.when(far_right)
    def _():
        pl.semaphore_signal(
            barrier, inc=1, device_id=dev_peer(dev + 1), device_id_type=pl.DeviceIdType.MESH
        )

    extra = far_left.astype(jnp.int32) + far_right.astype(jnp.int32)
    pl.semaphore_wait(barrier, n_dz - 1 + 2 + 1 + extra)

    own = pltpu.make_async_copy(half_ref, out_ref.at[dev], own_sem)
    own.start()

    def z_copy(target, source):
        return pltpu.make_async_remote_copy(
            src_ref=half_ref,
            dst_ref=out_ref.at[dy * n_dz + source],
            send_sem=z_send.at[target],
            recv_sem=z_recv.at[source],
            device_id=(section, grp, dy, target),
            device_id_type=pl.DeviceIdType.MESH,
        )

    for step in range(1, n_dz):
        z_copy((dz + step) % n_dz, dz).start()

    def y_copy(direction, row, chunk):
        slot = row * n_dz + chunk
        target = up if direction == 0 else down
        return pltpu.make_async_remote_copy(
            src_ref=out_ref.at[slot],
            dst_ref=out_ref.at[slot],
            send_sem=y_send.at[direction * n_dy * n_dz + slot],
            recv_sem=y_recv.at[slot],
            device_id=(section, grp, target, dz),
            device_id_type=pl.DeviceIdType.MESH,
        )

    def y_own(direction):
        target = up if direction == 0 else down
        return pltpu.make_async_remote_copy(
            src_ref=half_ref,
            dst_ref=out_ref.at[dev],
            send_sem=y_send.at[direction * n_dy * n_dz + dev],
            recv_sem=y_recv.at[dev],
            device_id=(section, grp, target, dz),
            device_id_type=pl.DeviceIdType.MESH,
        )

    for direction in (0, 1):
        y_own(direction).start()
    for step in range(1, n_dz):
        source = (dz + n_dz - step) % n_dz
        z_copy(source, source).wait_recv()
        for direction in (0, 1):
            y_copy(direction, dy, source).start()
    own.wait()
    for step in range(1, n_dz):
        z_copy((dz + step) % n_dz, dz).wait_send()

    count_frames = frames_ref.shape[0]

    def to_left():
        return pltpu.make_async_remote_copy(
            src_ref=frames_ref.at[pl.ds(0, RAD)],
            dst_ref=halo_right,
            send_sem=halo_send.at[0],
            recv_sem=halo_recv.at[1],
            device_id=dev_peer(dev - 1),
            device_id_type=pl.DeviceIdType.MESH,
        )

    def to_right():
        return pltpu.make_async_remote_copy(
            src_ref=frames_ref.at[pl.ds(count_frames - RAD, RAD)],
            dst_ref=halo_left,
            send_sem=halo_send.at[1],
            recv_sem=halo_recv.at[0],
            device_id=dev_peer(dev + 1),
            device_id_type=pl.DeviceIdType.MESH,
        )

    @pl.when(has_left)
    def _():
        to_left().start()

    @pl.when(has_right)
    def _():
        to_right().start()

    @pl.when(jnp.logical_not(has_left))
    def _():
        halo_left[...] = jnp.zeros(halo_left.shape, halo_left.dtype)

    @pl.when(jnp.logical_not(has_right))
    def _():
        halo_right[...] = jnp.zeros(halo_right.shape, halo_right.dtype)

    @pl.when(has_left)
    def _():
        to_right_of_left = pltpu.make_async_remote_copy(
            src_ref=frames_ref.at[pl.ds(0, RAD)],
            dst_ref=halo_left,
            send_sem=halo_send.at[1],
            recv_sem=halo_recv.at[0],
            device_id=dev_peer(dev - 1),
            device_id_type=pl.DeviceIdType.MESH,
        )
        to_right_of_left.wait_recv()
        to_left().wait_send()

    @pl.when(has_right)
    def _():
        to_left_of_right = pltpu.make_async_remote_copy(
            src_ref=frames_ref.at[pl.ds(0, RAD)],
            dst_ref=halo_right,
            send_sem=halo_send.at[0],
            recv_sem=halo_recv.at[1],
            device_id=dev_peer(dev + 1),
            device_id_type=pl.DeviceIdType.MESH,
        )
        to_left_of_right.wait_recv()
        to_right().wait_send()

    weights = retention_weights()

    row_block = 32

    def smooth_rows(block, carry):
        rows = pl.ds(pl.multiple_of(block * row_block, row_block), row_block)

        def padded_frame(place):
            if place < RAD:
                return halo_left[place, rows, :]
            if place < RAD + count_frames:
                return frames_ref[place - RAD, rows, :]
            return halo_right[place - RAD - count_frames, rows, :]

        for frame in range(count_frames):
            total = weights[0] * padded_frame(frame).astype(jnp.float32)
            for offset in range(1, 2 * RAD + 1):
                total = total + weights[offset] * padded_frame(frame + offset).astype(jnp.float32)
            own_scans[frame, rows, :] = total.astype(own_scans.dtype)
        return carry

    lax.fori_loop(0, own_scans.shape[1] // row_block, smooth_rows, 0)

    swap = pltpu.make_async_remote_copy(
        src_ref=own_scans,
        dst_ref=partner_scans,
        send_sem=swap_send,
        recv_sem=swap_recv,
        device_id=(partner_section, grp, dy, dz),
        device_id_type=pl.DeviceIdType.MESH,
    )
    swap.start()
    relay = n_dz // 2
    for chunk in range(n_dz):
        y_copy(0, down, chunk).wait_recv()
        if chunk < relay:
            y_copy(0, down, chunk).start()
        y_copy(1, up, chunk).wait_recv()
        if chunk >= relay:
            y_copy(1, up, chunk).start()
    swap.wait()

    half = own_scans.shape[1]

    def level_frame(frame, carry):
        for level in range(SCALES):
            table = kernels_ref[level]
            acc = jnp.dot(table[:, :half], own_scans[frame], preferred_element_type=jnp.float32)
            acc = acc + jnp.dot(
                table[:, half:], partner_scans[frame], preferred_element_type=jnp.float32
            )
            wave_ref[level, frame] = acc.astype(wave_ref.dtype)
        return carry

    lax.fori_loop(0, count_frames, level_frame, 0)

    opposite = (dy + 2) % n_dy
    for chunk in range(n_dz):
        y_copy(0, opposite, chunk).wait_recv()
    for direction in (0, 1):
        for chunk in range(n_dz):
            y_copy(direction, dy, chunk).wait_send()
    for chunk in range(relay):
        y_copy(0, down, chunk).wait_send()
    for chunk in range(relay, n_dz):
        y_copy(1, up, chunk).wait_send()


def frame_work(frames, kernels, half):
    sizes = (lax.axis_size("section"), lax.axis_size("dy"), lax.axis_size("dz"))
    n_section, n_dy, n_dz = sizes
    rows, channels = half.shape
    count_frames, mob_local, _ = frames.shape
    rows_out, wave = pl.pallas_call(
        functools.partial(frame_kernel, sizes),
        out_shape=(
            jax.ShapeDtypeStruct((n_dy * n_dz, rows, channels), half.dtype),
            jax.ShapeDtypeStruct((SCALES, count_frames, mob_local, channels), jnp.bfloat16),
        ),
        in_specs=[pl.BlockSpec(memory_space=pltpu.VMEM)] * 3,
        out_specs=(pl.BlockSpec(memory_space=pltpu.VMEM), pl.BlockSpec(memory_space=pltpu.VMEM)),
        scratch_shapes=[
            pltpu.VMEM((RAD, mob_local, channels), frames.dtype),
            pltpu.VMEM((RAD, mob_local, channels), frames.dtype),
            pltpu.VMEM((count_frames, mob_local, channels), jnp.bfloat16),
            pltpu.VMEM((count_frames, mob_local, channels), jnp.bfloat16),
            pltpu.SemaphoreType.DMA(()),
            pltpu.SemaphoreType.DMA((n_dz,)),
            pltpu.SemaphoreType.DMA((n_dz,)),
            pltpu.SemaphoreType.DMA((2 * n_dy * n_dz,)),
            pltpu.SemaphoreType.DMA((n_dy * n_dz,)),
            pltpu.SemaphoreType.DMA((2,)),
            pltpu.SemaphoreType.DMA((2,)),
            pltpu.SemaphoreType.DMA(()),
            pltpu.SemaphoreType.DMA(()),
        ],
        compiler_params=pltpu.CompilerParams(
            collective_id=1, has_side_effects=True, vmem_limit_bytes=56 * 1024 * 1024
        ),
    )(frames, kernels, half)
    return rows_out.reshape(n_dy * n_dz * rows, channels), wave


def score_kernel(tile_ref, block_ref, count_ref, section_ref, wave_ref, mine_ref, other_ref, out_ref):
    slot = pl.program_id(0)
    live = slot < count_ref[0]
    mine = block_ref[slot] % 2 == section_ref[0]

    def score(rows_ref):
        rows = rows_ref[...]
        acc = jnp.zeros((1, PB), jnp.float32)
        for level in range(SCALES):
            cells = wave_ref[level].reshape(-1, rows.shape[1])
            scores = lax.dot_general(
                cells, rows, (((1,), (1,)), ((), ())), preferred_element_type=jnp.float32
            )
            acc = acc + jnp.sum(jnp.maximum(scores, 0.0), axis=0, keepdims=True)
        cell_count = SCALES * wave_ref.shape[1] * wave_ref.shape[2]
        out_ref[0] = acc / cell_count

    @pl.when(jnp.logical_and(live, mine))
    def _():
        score(mine_ref)

    @pl.when(jnp.logical_and(live, jnp.logical_not(mine)))
    def _():
        score(other_ref)

    @pl.when(jnp.logical_not(live))
    def _():
        out_ref[0] = jnp.zeros((1, PB), jnp.float32)


def score_pairs(wavelet_stack, my_rows, other_rows, tile_ids, block_ids, live_pairs, section_index):
    slots = tile_ids.shape[0]
    scales, frames_local, mob_local, channels = wavelet_stack.shape

    def last_live(k, count_ref):
        return jnp.minimum(k, count_ref[0] - 1)

    def rows_block(k, t, b, c, s):
        return (b[last_live(k, c)] // 2, 0)

    grid_spec = pltpu.PrefetchScalarGridSpec(
        num_scalar_prefetch=4,
        grid=(slots,),
        in_specs=[
            pl.BlockSpec(
                (scales, frames_local, TM, channels),
                lambda k, t, b, c, s: (0, 0, t[last_live(k, c)], 0),
            ),
            pl.BlockSpec((PB, channels), rows_block),
            pl.BlockSpec((PB, channels), rows_block),
        ],
        out_specs=pl.BlockSpec((1, 1, PB), lambda k, t, b, c, s: (k, 0, 0)),
    )
    out = pl.pallas_call(
        score_kernel,
        grid_spec=grid_spec,
        out_shape=jax.ShapeDtypeStruct((slots, 1, PB), jnp.float32),
    )(
        tile_ids,
        block_ids,
        live_pairs.reshape(1),
        section_index.astype(jnp.int32).reshape(1),
        wavelet_stack,
        my_rows,
        other_rows,
    )
    return out.reshape(slots, PB)


def solution(mesh):
    section_count, grp_count, dev_count = mesh.devices.shape
    dz_count = 8 if dev_count % 8 == 0 else dev_count
    split_mesh = jax.sharding.Mesh(
        mesh.devices.reshape(section_count, grp_count, dev_count // dz_count, dz_count),
        ("section", "grp", "dy", "dz"),
    )
    placed = (
        P("grp", DEV, "section", None),
        P(DEV, None),
        P("section", "grp", DEV),
        P("section", "grp", DEV),
        P("section", "grp", DEV),
        P(),
    )
    return jax.shard_map(
        on_device, mesh=split_mesh, in_specs=placed, out_specs=P("grp", DEV), check_vma=False
    )
```

```python
import functools
import math

import jax
import jax.numpy as jnp
from jax import lax
from jax.experimental import pallas as pl
from jax.experimental.pallas import tpu as pltpu
from jax.sharding import PartitionSpec as P

MOB = 512
SCALES = 6
RAD = 4
TM = 64
PB = 128
PREC = 8192
DEV = ("dy", "dz")


retention_spread = 2.0


def extended(cells, sides, width):
    for axis, dim in sides:
        count = lax.axis_size(axis)
        ends = count - 1
        head = lax.slice_in_dim(cells, 0, width, axis=dim)
        tail = lax.slice_in_dim(cells, cells.shape[dim] - width, cells.shape[dim], axis=dim)
        cells = jnp.concatenate(
            [
                lax.ppermute(tail, axis, [(i, (i + 1) % count) for i in range(ends)]),
                cells,
                lax.ppermute(head, axis, [((i + 1) % count, i) for i in range(ends)]),
            ],
            axis=dim,
        )
    return cells


def retention_weights():
    bell_values = [
        math.exp(-0.5 * (offset / retention_spread) ** 2) for offset in range(-RAD, RAD + 1)
    ]
    bell_total = sum(bell_values)
    return [weight_value / bell_total for weight_value in bell_values]


def mobility_kernels(row_start, row_count, col_start):
    row_place = (row_start + jnp.arange(row_count, dtype=jnp.int32)).astype(jnp.float32)
    col_place = ((col_start + jnp.arange(MOB, dtype=jnp.int32)) % MOB).astype(jnp.float32)
    distance = row_place[:, None] - col_place[None, :]
    tables = []
    for level in range(SCALES):
        spread_scans = 2.0**level
        scaled = distance / spread_scans
        tables.append(
            (1.0 - scaled * scaled)
            * jnp.exp(-0.5 * scaled * scaled)
            / math.sqrt(0.75 * math.sqrt(math.pi) * spread_scans)
        )
    return jnp.stack(tables).astype(jnp.bfloat16)


def on_device(frames, templates, pair_block, pair_tile, pair_count, owner_order):
    section_index = lax.axis_index("section")
    mob_local = frames.shape[2]
    section_count = lax.axis_size("section")
    kernels = mobility_kernels(section_index * mob_local, mob_local, section_index * mob_local)
    half_rows = templates.shape[0] // 2
    my_half = lax.dynamic_slice_in_dim(templates, section_index * half_rows, half_rows, 0)
    my_rows, wavelet_stack = frame_work(frames[0], kernels, my_half)
    other_rows = lax.ppermute(
        my_rows, "section", [(i, (i + 1) % section_count) for i in range(section_count)]
    )
    slots = pair_block.shape[2]
    live_pairs = pair_count[0, 0, 0]
    block_ids = pair_block[0, 0]
    tile_ids = pair_tile[0, 0]
    responses = score_pairs(
        wavelet_stack, my_rows, other_rows, tile_ids, block_ids, live_pairs, section_index
    )
    positions = jnp.take(owner_order.reshape(-1, PB), block_ids, axis=0).reshape(-1)
    groups = PREC // PB
    by_group = jnp.where(
        (positions // PB)[:, None] == jnp.arange(groups, dtype=jnp.int32)[None, :],
        responses.reshape(-1)[:, None],
        0.0,
    )
    by_lane = ((positions % PB)[:, None] == jnp.arange(PB, dtype=jnp.int32)[None, :]).astype(
        jnp.float32
    )
    placed = jnp.einsum(
        "ka,kb->ab",
        by_group,
        by_lane,
        precision=lax.Precision.HIGHEST,
        preferred_element_type=jnp.float32,
    ).reshape(-1)
    dev_count = lax.axis_size(DEV)
    local_total = jnp.sum(responses)
    payload = jnp.concatenate(
        [
            placed.reshape(dev_count, 1, PREC // dev_count),
            jnp.broadcast_to(local_total, (dev_count, 1, 128)),
        ],
        axis=2,
    )
    return reduce_owned(payload)


def reduce_kernel(sizes, payload_ref, out_ref, gathered, totals, send_sems, recv_sems, total_send, total_recv):
    n_section, n_grp, n_dy, n_dz = sizes
    n_dev = n_dy * n_dz
    section = lax.axis_index("section")
    grp = lax.axis_index("grp")
    dy = lax.axis_index("dy")
    dz = lax.axis_index("dz")
    dev = dy * n_dz + dz
    me = section * n_dev + dev
    peers = n_section * n_dev
    owned_width = out_ref.shape[1]

    barrier = pltpu.get_barrier_semaphore()

    def greet(index, carry):
        @pl.when(index != me)
        def _():
            pl.semaphore_signal(
                barrier,
                inc=1,
                device_id=(index // n_dev, grp, index % n_dev // n_dz, index % n_dz),
                device_id_type=pl.DeviceIdType.MESH,
            )

        return carry

    lax.fori_loop(0, peers, greet, 0)
    for step in range(1, n_grp):
        pl.semaphore_signal(
            barrier,
            inc=1,
            device_id=(section, (grp + step) % n_grp, dy, dz),
            device_id_type=pl.DeviceIdType.MESH,
        )
    pl.semaphore_wait(barrier, peers - 1 + n_grp - 1)

    def chunk_copy(index):
        return pltpu.make_async_remote_copy(
            src_ref=payload_ref.at[index % n_dev],
            dst_ref=gathered.at[me],
            send_sem=send_sems.at[index],
            recv_sem=recv_sems.at[me],
            device_id=(index // n_dev, grp, index % n_dev // n_dz, index % n_dz),
            device_id_type=pl.DeviceIdType.MESH,
        )

    def send(index, carry):
        @pl.when(index != me)
        def _():
            chunk_copy(index).start()

        return carry

    lax.fori_loop(0, peers, send, 0)
    gathered[me] = payload_ref[dev]

    def arrive(index, carry):
        @pl.when(index != me)
        def _():
            pltpu.make_async_remote_copy(
                src_ref=payload_ref.at[0],
                dst_ref=gathered.at[index],
                send_sem=send_sems.at[index],
                recv_sem=recv_sems.at[index],
                device_id=(index // n_dev, grp, index % n_dev // n_dz, index % n_dz),
                device_id_type=pl.DeviceIdType.MESH,
            ).wait_recv()
            chunk_copy(index).wait_send()

        return carry

    lax.fori_loop(0, peers, arrive, 0)

    def accumulate(index, acc):
        return acc + gathered[index]

    summed = lax.fori_loop(0, peers, accumulate, jnp.zeros(gathered.shape[1:], jnp.float32))
    totals[grp] = summed[:, owned_width:]

    def total_copy(step):
        target = (grp + step) % n_grp
        return pltpu.make_async_remote_copy(
            src_ref=totals.at[grp],
            dst_ref=totals.at[grp],
            send_sem=total_send.at[target],
            recv_sem=total_recv.at[grp],
            device_id=(section, target, dy, dz),
            device_id_type=pl.DeviceIdType.MESH,
        )

    for step in range(1, n_grp):
        total_copy(step).start()
    for step in range(1, n_grp):
        source = (grp + step) % n_grp
        pltpu.make_async_remote_copy(
            src_ref=totals.at[source],
            dst_ref=totals.at[source],
            send_sem=total_send.at[source],
            recv_sem=total_recv.at[source],
            device_id=(section, source, dy, dz),
            device_id_type=pl.DeviceIdType.MESH,
        ).wait_recv()
        total_copy(step).wait_send()
    run_sum = totals[0]
    for index in range(1, n_grp):
        run_sum = run_sum + totals[index]
    own_total = summed[:, owned_width : owned_width + 1]
    factor = (run_sum[:, 0:1] / n_grp) / own_total
    out_ref[...] = summed[:, :owned_width] * factor


def reduce_owned(payload):
    sizes = (lax.axis_size("section"), lax.axis_size("grp"), lax.axis_size("dy"), lax.axis_size("dz"))
    n_section, n_grp, n_dy, n_dz = sizes
    peers = n_section * n_dy * n_dz
    rows, one, width = payload.shape
    owned_width = width - 128
    return pl.pallas_call(
        functools.partial(reduce_kernel, sizes),
        out_shape=jax.ShapeDtypeStruct((1, owned_width), jnp.float32),
        in_specs=[pl.BlockSpec(memory_space=pltpu.VMEM)],
        out_specs=pl.BlockSpec(memory_space=pltpu.VMEM),
        scratch_shapes=[
            pltpu.VMEM((peers, 1, width), jnp.float32),
            pltpu.VMEM((n_grp, 1, 128), jnp.float32),
            pltpu.SemaphoreType.DMA((peers,)),
            pltpu.SemaphoreType.DMA((peers,)),
            pltpu.SemaphoreType.DMA((n_grp,)),
            pltpu.SemaphoreType.DMA((n_grp,)),
        ],
        compiler_params=pltpu.CompilerParams(collective_id=0, has_side_effects=True),
    )(payload)


def frame_kernel(
    sizes,
    frames_ref,
    kernels_ref,
    half_ref,
    out_ref,
    wave_ref,
    halo_left,
    halo_right,
    own_scans,
    partner_scans,
    own_sem,
    z_send,
    z_recv,
    y_send,
    y_recv,
    halo_send,
    halo_recv,
    swap_send,
    swap_recv,
):
    n_section, n_dy, n_dz = sizes
    n_dev = n_dy * n_dz
    section = lax.axis_index("section")
    grp = lax.axis_index("grp")
    dy = lax.axis_index("dy")
    dz = lax.axis_index("dz")
    dev = dy * n_dz + dz
    partner_section = (section + 1) % n_section

    def dev_peer(index):
        return (section, grp, index // n_dz, index % n_dz)

    barrier = pltpu.get_barrier_semaphore()
    for step in range(1, n_dz):
        pl.semaphore_signal(
            barrier,
            inc=1,
            device_id=(section, grp, dy, (dz + step) % n_dz),
            device_id_type=pl.DeviceIdType.MESH,
        )
    up = (dy + 1) % n_dy
    down = (dy + n_dy - 1) % n_dy
    for row in (up, down):
        pl.semaphore_signal(
            barrier,
            inc=1,
            device_id=(section, grp, row, dz),
            device_id_type=pl.DeviceIdType.MESH,
        )
    pl.semaphore_signal(
        barrier,
        inc=1,
        device_id=(partner_section, grp, dy, dz),
        device_id_type=pl.DeviceIdType.MESH,
    )
    has_left = dev > 0
    has_right = dev < n_dev - 1
    far_left = jnp.logical_and(has_left, dz == 0)
    far_right = jnp.logical_and(has_right, dz == n_dz - 1)

    @pl.when(far_left)
    def _():
        pl.semaphore_signal(
            barrier, inc=1, device_id=dev_peer(dev - 1), device_id_type=pl.DeviceIdType.MESH
        )

    @pl.when(far_right)
    def _():
        pl.semaphore_signal(
            barrier, inc=1, device_id=dev_peer(dev + 1), device_id_type=pl.DeviceIdType.MESH
        )

    extra = far_left.astype(jnp.int32) + far_right.astype(jnp.int32)
    pl.semaphore_wait(barrier, n_dz - 1 + 2 + 1 + extra)

    own = pltpu.make_async_copy(half_ref, out_ref.at[dev], own_sem)
    own.start()

    def z_copy(target, source):
        return pltpu.make_async_remote_copy(
            src_ref=half_ref,
            dst_ref=out_ref.at[dy * n_dz + source],
            send_sem=z_send.at[target],
            recv_sem=z_recv.at[source],
            device_id=(section, grp, dy, target),
            device_id_type=pl.DeviceIdType.MESH,
        )

    for step in range(1, n_dz):
        z_copy((dz + step) % n_dz, dz).start()

    def y_copy(direction, row, chunk):
        slot = row * n_dz + chunk
        target = up if direction == 0 else down
        return pltpu.make_async_remote_copy(
            src_ref=out_ref.at[slot],
            dst_ref=out_ref.at[slot],
            send_sem=y_send.at[direction * n_dy * n_dz + slot],
            recv_sem=y_recv.at[slot],
            device_id=(section, grp, target, dz),
            device_id_type=pl.DeviceIdType.MESH,
        )

    def y_own(direction):
        target = up if direction == 0 else down
        return pltpu.make_async_remote_copy(
            src_ref=half_ref,
            dst_ref=out_ref.at[dev],
            send_sem=y_send.at[direction * n_dy * n_dz + dev],
            recv_sem=y_recv.at[dev],
            device_id=(section, grp, target, dz),
            device_id_type=pl.DeviceIdType.MESH,
        )

    for direction in (0, 1):
        y_own(direction).start()
    count_frames = frames_ref.shape[0]

    def to_left():
        return pltpu.make_async_remote_copy(
            src_ref=frames_ref.at[pl.ds(0, RAD)],
            dst_ref=halo_right,
            send_sem=halo_send.at[0],
            recv_sem=halo_recv.at[1],
            device_id=dev_peer(dev - 1),
            device_id_type=pl.DeviceIdType.MESH,
        )

    def to_right():
        return pltpu.make_async_remote_copy(
            src_ref=frames_ref.at[pl.ds(count_frames - RAD, RAD)],
            dst_ref=halo_left,
            send_sem=halo_send.at[1],
            recv_sem=halo_recv.at[0],
            device_id=dev_peer(dev + 1),
            device_id_type=pl.DeviceIdType.MESH,
        )

    @pl.when(has_left)
    def _():
        to_left().start()

    @pl.when(has_right)
    def _():
        to_right().start()

    @pl.when(jnp.logical_not(has_left))
    def _():
        halo_left[...] = jnp.zeros(halo_left.shape, halo_left.dtype)

    @pl.when(jnp.logical_not(has_right))
    def _():
        halo_right[...] = jnp.zeros(halo_right.shape, halo_right.dtype)

    @pl.when(has_left)
    def _():
        to_right_of_left = pltpu.make_async_remote_copy(
            src_ref=frames_ref.at[pl.ds(0, RAD)],
            dst_ref=halo_left,
            send_sem=halo_send.at[1],
            recv_sem=halo_recv.at[0],
            device_id=dev_peer(dev - 1),
            device_id_type=pl.DeviceIdType.MESH,
        )
        to_right_of_left.wait_recv()
        to_left().wait_send()

    @pl.when(has_right)
    def _():
        to_left_of_right = pltpu.make_async_remote_copy(
            src_ref=frames_ref.at[pl.ds(0, RAD)],
            dst_ref=halo_right,
            send_sem=halo_send.at[0],
            recv_sem=halo_recv.at[1],
            device_id=dev_peer(dev + 1),
            device_id_type=pl.DeviceIdType.MESH,
        )
        to_left_of_right.wait_recv()
        to_right().wait_send()

    weights = retention_weights()

    row_block = 32

    def smooth_rows(block, carry):
        rows = pl.ds(pl.multiple_of(block * row_block, row_block), row_block)

        def padded_frame(place):
            if place < RAD:
                return halo_left[place, rows, :]
            if place < RAD + count_frames:
                return frames_ref[place - RAD, rows, :]
            return halo_right[place - RAD - count_frames, rows, :]

        for frame in range(count_frames):
            total = weights[0] * padded_frame(frame).astype(jnp.float32)
            for offset in range(1, 2 * RAD + 1):
                total = total + weights[offset] * padded_frame(frame + offset).astype(jnp.float32)
            own_scans[frame, rows, :] = total.astype(own_scans.dtype)
        return carry

    lax.fori_loop(0, own_scans.shape[1] // row_block, smooth_rows, 0)

    swap = pltpu.make_async_remote_copy(
        src_ref=own_scans,
        dst_ref=partner_scans,
        send_sem=swap_send,
        recv_sem=swap_recv,
        device_id=(partner_section, grp, dy, dz),
        device_id_type=pl.DeviceIdType.MESH,
    )
    swap.start()
    for step in range(1, n_dz):
        source = (dz + n_dz - step) % n_dz
        z_copy(source, source).wait_recv()
        for direction in (0, 1):
            y_copy(direction, dy, source).start()
    own.wait()
    for step in range(1, n_dz):
        z_copy((dz + step) % n_dz, dz).wait_send()

    relay = n_dz // 2
    for chunk in range(n_dz):
        y_copy(0, down, chunk).wait_recv()
        if chunk < relay:
            y_copy(0, down, chunk).start()
        y_copy(1, up, chunk).wait_recv()
        if chunk >= relay:
            y_copy(1, up, chunk).start()
    swap.wait()

    half = own_scans.shape[1]

    def level_frame(frame, carry):
        for level in range(SCALES):
            table = kernels_ref[level]
            acc = jnp.dot(table[:, :half], own_scans[frame], preferred_element_type=jnp.float32)
            acc = acc + jnp.dot(
                table[:, half:], partner_scans[frame], preferred_element_type=jnp.float32
            )
            wave_ref[level, frame] = acc.astype(wave_ref.dtype)
        return carry

    lax.fori_loop(0, count_frames, level_frame, 0)

    opposite = (dy + 2) % n_dy
    for chunk in range(n_dz):
        y_copy(0, opposite, chunk).wait_recv()
    for direction in (0, 1):
        for chunk in range(n_dz):
            y_copy(direction, dy, chunk).wait_send()
    for chunk in range(relay):
        y_copy(0, down, chunk).wait_send()
    for chunk in range(relay, n_dz):
        y_copy(1, up, chunk).wait_send()


def frame_work(frames, kernels, half):
    sizes = (lax.axis_size("section"), lax.axis_size("dy"), lax.axis_size("dz"))
    n_section, n_dy, n_dz = sizes
    rows, channels = half.shape
    count_frames, mob_local, _ = frames.shape
    rows_out, wave = pl.pallas_call(
        functools.partial(frame_kernel, sizes),
        out_shape=(
            jax.ShapeDtypeStruct((n_dy * n_dz, rows, channels), half.dtype),
            jax.ShapeDtypeStruct((SCALES, count_frames, mob_local, channels), jnp.bfloat16),
        ),
        in_specs=[pl.BlockSpec(memory_space=pltpu.VMEM)] * 3,
        out_specs=(pl.BlockSpec(memory_space=pltpu.VMEM), pl.BlockSpec(memory_space=pltpu.VMEM)),
        scratch_shapes=[
            pltpu.VMEM((RAD, mob_local, channels), frames.dtype),
            pltpu.VMEM((RAD, mob_local, channels), frames.dtype),
            pltpu.VMEM((count_frames, mob_local, channels), jnp.bfloat16),
            pltpu.VMEM((count_frames, mob_local, channels), jnp.bfloat16),
            pltpu.SemaphoreType.DMA(()),
            pltpu.SemaphoreType.DMA((n_dz,)),
            pltpu.SemaphoreType.DMA((n_dz,)),
            pltpu.SemaphoreType.DMA((2 * n_dy * n_dz,)),
            pltpu.SemaphoreType.DMA((n_dy * n_dz,)),
            pltpu.SemaphoreType.DMA((2,)),
            pltpu.SemaphoreType.DMA((2,)),
            pltpu.SemaphoreType.DMA(()),
            pltpu.SemaphoreType.DMA(()),
        ],
        compiler_params=pltpu.CompilerParams(
            collective_id=1, has_side_effects=True, vmem_limit_bytes=56 * 1024 * 1024
        ),
    )(frames, kernels, half)
    return rows_out.reshape(n_dy * n_dz * rows, channels), wave


def score_kernel(tile_ref, block_ref, count_ref, section_ref, wave_ref, mine_ref, other_ref, out_ref):
    slot = pl.program_id(0)
    live = slot < count_ref[0]
    mine = block_ref[slot] % 2 == section_ref[0]

    def score(rows_ref):
        rows = rows_ref[...]
        acc = jnp.zeros((1, PB), jnp.float32)
        for level in range(SCALES):
            cells = wave_ref[level].reshape(-1, rows.shape[1])
            scores = lax.dot_general(
                cells, rows, (((1,), (1,)), ((), ())), preferred_element_type=jnp.float32
            )
            acc = acc + jnp.sum(jnp.maximum(scores, 0.0), axis=0, keepdims=True)
        cell_count = SCALES * wave_ref.shape[1] * wave_ref.shape[2]
        out_ref[0] = acc / cell_count

    @pl.when(jnp.logical_and(live, mine))
    def _():
        score(mine_ref)

    @pl.when(jnp.logical_and(live, jnp.logical_not(mine)))
    def _():
        score(other_ref)

    @pl.when(jnp.logical_not(live))
    def _():
        out_ref[0] = jnp.zeros((1, PB), jnp.float32)


def score_pairs(wavelet_stack, my_rows, other_rows, tile_ids, block_ids, live_pairs, section_index):
    slots = tile_ids.shape[0]
    scales, frames_local, mob_local, channels = wavelet_stack.shape

    def last_live(k, count_ref):
        return jnp.minimum(k, count_ref[0] - 1)

    def rows_block(k, t, b, c, s):
        return (b[last_live(k, c)] // 2, 0)

    grid_spec = pltpu.PrefetchScalarGridSpec(
        num_scalar_prefetch=4,
        grid=(slots,),
        in_specs=[
            pl.BlockSpec(
                (scales, frames_local, TM, channels),
                lambda k, t, b, c, s: (0, 0, t[last_live(k, c)], 0),
            ),
            pl.BlockSpec((PB, channels), rows_block),
            pl.BlockSpec((PB, channels), rows_block),
        ],
        out_specs=pl.BlockSpec((1, 1, PB), lambda k, t, b, c, s: (k, 0, 0)),
    )
    out = pl.pallas_call(
        score_kernel,
        grid_spec=grid_spec,
        out_shape=jax.ShapeDtypeStruct((slots, 1, PB), jnp.float32),
    )(
        tile_ids,
        block_ids,
        live_pairs.reshape(1),
        section_index.astype(jnp.int32).reshape(1),
        wavelet_stack,
        my_rows,
        other_rows,
    )
    return out.reshape(slots, PB)


def solution(mesh):
    section_count, grp_count, dev_count = mesh.devices.shape
    dz_count = 8 if dev_count % 8 == 0 else dev_count
    split_mesh = jax.sharding.Mesh(
        mesh.devices.reshape(section_count, grp_count, dev_count // dz_count, dz_count),
        ("section", "grp", "dy", "dz"),
    )
    placed = (
        P("grp", DEV, "section", None),
        P(DEV, None),
        P("section", "grp", DEV),
        P("section", "grp", DEV),
        P("section", "grp", DEV),
        P(),
    )
    return jax.shard_map(
        on_device, mesh=split_mesh, in_specs=placed, out_specs=P("grp", DEV), check_vma=False
    )
```

```python
import functools
import math

import jax
import jax.numpy as jnp
from jax import lax
from jax.experimental import pallas as pl
from jax.experimental.pallas import tpu as pltpu
from jax.sharding import PartitionSpec as P

MOB = 512
SCALES = 6
RAD = 4
TM = 64
PB = 128
PREC = 8192
DEV = ("dy", "dz")


retention_spread = 2.0


def extended(cells, sides, width):
    for axis, dim in sides:
        count = lax.axis_size(axis)
        ends = count - 1
        head = lax.slice_in_dim(cells, 0, width, axis=dim)
        tail = lax.slice_in_dim(cells, cells.shape[dim] - width, cells.shape[dim], axis=dim)
        cells = jnp.concatenate(
            [
                lax.ppermute(tail, axis, [(i, (i + 1) % count) for i in range(ends)]),
                cells,
                lax.ppermute(head, axis, [((i + 1) % count, i) for i in range(ends)]),
            ],
            axis=dim,
        )
    return cells


def retention_weights():
    bell_values = [
        math.exp(-0.5 * (offset / retention_spread) ** 2) for offset in range(-RAD, RAD + 1)
    ]
    bell_total = sum(bell_values)
    return [weight_value / bell_total for weight_value in bell_values]


def mobility_kernels(row_start, row_count, col_start):
    row_place = (row_start + jnp.arange(row_count, dtype=jnp.int32)).astype(jnp.float32)
    col_place = ((col_start + jnp.arange(MOB, dtype=jnp.int32)) % MOB).astype(jnp.float32)
    distance = row_place[:, None] - col_place[None, :]
    tables = []
    for level in range(SCALES):
        spread_scans = 2.0**level
        scaled = distance / spread_scans
        tables.append(
            (1.0 - scaled * scaled)
            * jnp.exp(-0.5 * scaled * scaled)
            / math.sqrt(0.75 * math.sqrt(math.pi) * spread_scans)
        )
    return jnp.stack(tables).astype(jnp.bfloat16)


def on_device(frames, templates, pair_block, pair_tile, pair_count, owner_order):
    section_index = lax.axis_index("section")
    mob_local = frames.shape[2]
    section_count = lax.axis_size("section")
    kernels = mobility_kernels(section_index * mob_local, mob_local, section_index * mob_local)
    half_rows = templates.shape[0] // 2
    my_half = lax.dynamic_slice_in_dim(templates, section_index * half_rows, half_rows, 0)
    my_rows, wavelet_stack = frame_work(frames[0], kernels, my_half)
    other_rows = lax.ppermute(
        my_rows, "section", [(i, (i + 1) % section_count) for i in range(section_count)]
    )
    slots = pair_block.shape[2]
    live_pairs = pair_count[0, 0, 0]
    block_ids = pair_block[0, 0]
    tile_ids = pair_tile[0, 0]
    responses = score_pairs(
        wavelet_stack, my_rows, other_rows, tile_ids, block_ids, live_pairs, section_index
    )
    positions = jnp.take(owner_order.reshape(-1, PB), block_ids, axis=0).reshape(-1)
    groups = PREC // PB
    by_group = jnp.where(
        (positions // PB)[:, None] == jnp.arange(groups, dtype=jnp.int32)[None, :],
        responses.reshape(-1)[:, None],
        0.0,
    )
    by_lane = ((positions % PB)[:, None] == jnp.arange(PB, dtype=jnp.int32)[None, :]).astype(
        jnp.float32
    )
    placed = jnp.einsum(
        "ka,kb->ab",
        by_group,
        by_lane,
        precision=lax.Precision.HIGHEST,
        preferred_element_type=jnp.float32,
    ).reshape(-1)
    dev_count = lax.axis_size(DEV)
    local_total = jnp.sum(responses)
    payload = jnp.concatenate(
        [
            placed.reshape(dev_count, 1, PREC // dev_count),
            jnp.broadcast_to(local_total, (dev_count, 1, 128)),
        ],
        axis=2,
    )
    return reduce_owned(payload)


def reduce_kernel(sizes, payload_ref, out_ref, gathered, totals, send_sems, recv_sems, total_send, total_recv):
    n_section, n_grp, n_dy, n_dz = sizes
    n_dev = n_dy * n_dz
    section = lax.axis_index("section")
    grp = lax.axis_index("grp")
    dy = lax.axis_index("dy")
    dz = lax.axis_index("dz")
    dev = dy * n_dz + dz
    me = section * n_dev + dev
    peers = n_section * n_dev
    owned_width = out_ref.shape[1]

    barrier = pltpu.get_barrier_semaphore()

    def greet(index, carry):
        @pl.when(index != me)
        def _():
            pl.semaphore_signal(
                barrier,
                inc=1,
                device_id=(index // n_dev, grp, index % n_dev // n_dz, index % n_dz),
                device_id_type=pl.DeviceIdType.MESH,
            )

        return carry

    lax.fori_loop(0, peers, greet, 0)
    for step in range(1, n_grp):
        pl.semaphore_signal(
            barrier,
            inc=1,
            device_id=(section, (grp + step) % n_grp, dy, dz),
            device_id_type=pl.DeviceIdType.MESH,
        )
    pl.semaphore_wait(barrier, peers - 1 + n_grp - 1)

    def chunk_copy(index):
        return pltpu.make_async_remote_copy(
            src_ref=payload_ref.at[index % n_dev],
            dst_ref=gathered.at[me],
            send_sem=send_sems.at[index],
            recv_sem=recv_sems.at[me],
            device_id=(index // n_dev, grp, index % n_dev // n_dz, index % n_dz),
            device_id_type=pl.DeviceIdType.MESH,
        )

    def send(index, carry):
        @pl.when(index != me)
        def _():
            chunk_copy(index).start()

        return carry

    lax.fori_loop(0, peers, send, 0)
    gathered[me] = payload_ref[dev]

    def arrive(index, carry):
        @pl.when(index != me)
        def _():
            pltpu.make_async_remote_copy(
                src_ref=payload_ref.at[0],
                dst_ref=gathered.at[index],
                send_sem=send_sems.at[index],
                recv_sem=recv_sems.at[index],
                device_id=(index // n_dev, grp, index % n_dev // n_dz, index % n_dz),
                device_id_type=pl.DeviceIdType.MESH,
            ).wait_recv()
            chunk_copy(index).wait_send()

        return carry

    lax.fori_loop(0, peers, arrive, 0)

    def accumulate(index, acc):
        return acc + gathered[index]

    summed = lax.fori_loop(0, peers, accumulate, jnp.zeros(gathered.shape[1:], jnp.float32))
    totals[grp] = summed[:, owned_width:]

    def total_copy(step):
        target = (grp + step) % n_grp
        return pltpu.make_async_remote_copy(
            src_ref=totals.at[grp],
            dst_ref=totals.at[grp],
            send_sem=total_send.at[target],
            recv_sem=total_recv.at[grp],
            device_id=(section, target, dy, dz),
            device_id_type=pl.DeviceIdType.MESH,
        )

    for step in range(1, n_grp):
        total_copy(step).start()
    for step in range(1, n_grp):
        source = (grp + step) % n_grp
        pltpu.make_async_remote_copy(
            src_ref=totals.at[source],
            dst_ref=totals.at[source],
            send_sem=total_send.at[source],
            recv_sem=total_recv.at[source],
            device_id=(section, source, dy, dz),
            device_id_type=pl.DeviceIdType.MESH,
        ).wait_recv()
        total_copy(step).wait_send()
    run_sum = totals[0]
    for index in range(1, n_grp):
        run_sum = run_sum + totals[index]
    own_total = summed[:, owned_width : owned_width + 1]
    factor = (run_sum[:, 0:1] / n_grp) / own_total
    out_ref[...] = summed[:, :owned_width] * factor


def reduce_owned(payload):
    sizes = (lax.axis_size("section"), lax.axis_size("grp"), lax.axis_size("dy"), lax.axis_size("dz"))
    n_section, n_grp, n_dy, n_dz = sizes
    peers = n_section * n_dy * n_dz
    rows, one, width = payload.shape
    owned_width = width - 128
    return pl.pallas_call(
        functools.partial(reduce_kernel, sizes),
        out_shape=jax.ShapeDtypeStruct((1, owned_width), jnp.float32),
        in_specs=[pl.BlockSpec(memory_space=pltpu.VMEM)],
        out_specs=pl.BlockSpec(memory_space=pltpu.VMEM),
        scratch_shapes=[
            pltpu.VMEM((peers, 1, width), jnp.float32),
            pltpu.VMEM((n_grp, 1, 128), jnp.float32),
            pltpu.SemaphoreType.DMA((peers,)),
            pltpu.SemaphoreType.DMA((peers,)),
            pltpu.SemaphoreType.DMA((n_grp,)),
            pltpu.SemaphoreType.DMA((n_grp,)),
        ],
        compiler_params=pltpu.CompilerParams(collective_id=0, has_side_effects=True),
    )(payload)


def frame_kernel(
    sizes,
    frames_ref,
    kernels_ref,
    half_ref,
    out_ref,
    wave_ref,
    halo_left,
    halo_right,
    own_scans,
    partner_scans,
    own_sem,
    z_send,
    z_recv,
    y_send,
    y_recv,
    halo_send,
    halo_recv,
    swap_send,
    swap_recv,
):
    n_section, n_dy, n_dz = sizes
    n_dev = n_dy * n_dz
    section = lax.axis_index("section")
    grp = lax.axis_index("grp")
    dy = lax.axis_index("dy")
    dz = lax.axis_index("dz")
    dev = dy * n_dz + dz
    partner_section = (section + 1) % n_section

    def dev_peer(index):
        return (section, grp, index // n_dz, index % n_dz)

    barrier = pltpu.get_barrier_semaphore()
    for step in range(1, n_dz):
        pl.semaphore_signal(
            barrier,
            inc=1,
            device_id=(section, grp, dy, (dz + step) % n_dz),
            device_id_type=pl.DeviceIdType.MESH,
        )
    up = (dy + 1) % n_dy
    down = (dy + n_dy - 1) % n_dy
    for row in (up, down):
        pl.semaphore_signal(
            barrier,
            inc=1,
            device_id=(section, grp, row, dz),
            device_id_type=pl.DeviceIdType.MESH,
        )
    pl.semaphore_signal(
        barrier,
        inc=1,
        device_id=(partner_section, grp, dy, dz),
        device_id_type=pl.DeviceIdType.MESH,
    )
    has_left = dev > 0
    has_right = dev < n_dev - 1
    far_left = jnp.logical_and(has_left, dz == 0)
    far_right = jnp.logical_and(has_right, dz == n_dz - 1)

    @pl.when(far_left)
    def _():
        pl.semaphore_signal(
            barrier, inc=1, device_id=dev_peer(dev - 1), device_id_type=pl.DeviceIdType.MESH
        )

    @pl.when(far_right)
    def _():
        pl.semaphore_signal(
            barrier, inc=1, device_id=dev_peer(dev + 1), device_id_type=pl.DeviceIdType.MESH
        )

    extra = far_left.astype(jnp.int32) + far_right.astype(jnp.int32)
    pl.semaphore_wait(barrier, n_dz - 1 + 2 + 1 + extra)

    own = pltpu.make_async_copy(half_ref, out_ref.at[dev], own_sem)
    own.start()

    def z_copy(target, source):
        return pltpu.make_async_remote_copy(
            src_ref=half_ref,
            dst_ref=out_ref.at[dy * n_dz + source],
            send_sem=z_send.at[target],
            recv_sem=z_recv.at[source],
            device_id=(section, grp, dy, target),
            device_id_type=pl.DeviceIdType.MESH,
        )

    for step in range(1, n_dz):
        z_copy((dz + step) % n_dz, dz).start()

    count_frames = frames_ref.shape[0]

    def to_left():
        return pltpu.make_async_remote_copy(
            src_ref=frames_ref.at[pl.ds(0, RAD)],
            dst_ref=halo_right,
            send_sem=halo_send.at[0],
            recv_sem=halo_recv.at[1],
            device_id=dev_peer(dev - 1),
            device_id_type=pl.DeviceIdType.MESH,
        )

    def to_right():
        return pltpu.make_async_remote_copy(
            src_ref=frames_ref.at[pl.ds(count_frames - RAD, RAD)],
            dst_ref=halo_left,
            send_sem=halo_send.at[1],
            recv_sem=halo_recv.at[0],
            device_id=dev_peer(dev + 1),
            device_id_type=pl.DeviceIdType.MESH,
        )

    @pl.when(has_left)
    def _():
        to_left().start()

    @pl.when(has_right)
    def _():
        to_right().start()

    @pl.when(jnp.logical_not(has_left))
    def _():
        halo_left[...] = jnp.zeros(halo_left.shape, halo_left.dtype)

    @pl.when(jnp.logical_not(has_right))
    def _():
        halo_right[...] = jnp.zeros(halo_right.shape, halo_right.dtype)

    def y_copy(direction, row, chunk):
        slot = row * n_dz + chunk
        target = up if direction == 0 else down
        return pltpu.make_async_remote_copy(
            src_ref=out_ref.at[slot],
            dst_ref=out_ref.at[slot],
            send_sem=y_send.at[direction * n_dy * n_dz + slot],
            recv_sem=y_recv.at[slot],
            device_id=(section, grp, target, dz),
            device_id_type=pl.DeviceIdType.MESH,
        )

    def y_own(direction):
        target = up if direction == 0 else down
        return pltpu.make_async_remote_copy(
            src_ref=half_ref,
            dst_ref=out_ref.at[dev],
            send_sem=y_send.at[direction * n_dy * n_dz + dev],
            recv_sem=y_recv.at[dev],
            device_id=(section, grp, target, dz),
            device_id_type=pl.DeviceIdType.MESH,
        )

    for direction in (0, 1):
        y_own(direction).start()
    for step in range(1, n_dz):
        source = (dz + n_dz - step) % n_dz
        z_copy(source, source).wait_recv()
        for direction in (0, 1):
            y_copy(direction, dy, source).start()
    own.wait()
    for step in range(1, n_dz):
        z_copy((dz + step) % n_dz, dz).wait_send()

    @pl.when(has_left)
    def _():
        to_right_of_left = pltpu.make_async_remote_copy(
            src_ref=frames_ref.at[pl.ds(0, RAD)],
            dst_ref=halo_left,
            send_sem=halo_send.at[1],
            recv_sem=halo_recv.at[0],
            device_id=dev_peer(dev - 1),
            device_id_type=pl.DeviceIdType.MESH,
        )
        to_right_of_left.wait_recv()
        to_left().wait_send()

    @pl.when(has_right)
    def _():
        to_left_of_right = pltpu.make_async_remote_copy(
            src_ref=frames_ref.at[pl.ds(0, RAD)],
            dst_ref=halo_right,
            send_sem=halo_send.at[0],
            recv_sem=halo_recv.at[1],
            device_id=dev_peer(dev + 1),
            device_id_type=pl.DeviceIdType.MESH,
        )
        to_left_of_right.wait_recv()
        to_right().wait_send()

    weights = retention_weights()

    row_block = 32

    def smooth_rows(block, carry):
        rows = pl.ds(pl.multiple_of(block * row_block, row_block), row_block)

        def padded_frame(place):
            if place < RAD:
                return halo_left[place, rows, :]
            if place < RAD + count_frames:
                return frames_ref[place - RAD, rows, :]
            return halo_right[place - RAD - count_frames, rows, :]

        for frame in range(count_frames):
            total = weights[0] * padded_frame(frame).astype(jnp.float32)
            for offset in range(1, 2 * RAD + 1):
                total = total + weights[offset] * padded_frame(frame + offset).astype(jnp.float32)
            own_scans[frame, rows, :] = total.astype(own_scans.dtype)
        return carry

    lax.fori_loop(0, own_scans.shape[1] // row_block, smooth_rows, 0)

    swap = pltpu.make_async_remote_copy(
        src_ref=own_scans,
        dst_ref=partner_scans,
        send_sem=swap_send,
        recv_sem=swap_recv,
        device_id=(partner_section, grp, dy, dz),
        device_id_type=pl.DeviceIdType.MESH,
    )
    swap.start()
    relay = n_dz // 2
    for chunk in range(n_dz):
        y_copy(0, down, chunk).wait_recv()
        if chunk < relay:
            y_copy(0, down, chunk).start()
        y_copy(1, up, chunk).wait_recv()
        if chunk >= relay:
            y_copy(1, up, chunk).start()
    swap.wait()

    half = own_scans.shape[1]

    def level_frame(frame, carry):
        for level in range(SCALES):
            table = kernels_ref[level]
            acc = jnp.dot(table[:, :half], own_scans[frame], preferred_element_type=jnp.float32)
            acc = acc + jnp.dot(
                table[:, half:], partner_scans[frame], preferred_element_type=jnp.float32
            )
            wave_ref[level, frame] = acc.astype(wave_ref.dtype)
        return carry

    lax.fori_loop(0, count_frames, level_frame, 0)

    opposite = (dy + 2) % n_dy
    for chunk in range(n_dz):
        y_copy(0, opposite, chunk).wait_recv()
    for direction in (0, 1):
        for chunk in range(n_dz):
            y_copy(direction, dy, chunk).wait_send()
    for chunk in range(relay):
        y_copy(0, down, chunk).wait_send()
    for chunk in range(relay, n_dz):
        y_copy(1, up, chunk).wait_send()


def frame_work(frames, kernels, half):
    sizes = (lax.axis_size("section"), lax.axis_size("dy"), lax.axis_size("dz"))
    n_section, n_dy, n_dz = sizes
    rows, channels = half.shape
    count_frames, mob_local, _ = frames.shape
    rows_out, wave = pl.pallas_call(
        functools.partial(frame_kernel, sizes),
        out_shape=(
            jax.ShapeDtypeStruct((n_dy * n_dz, rows, channels), half.dtype),
            jax.ShapeDtypeStruct((SCALES, count_frames, mob_local, channels), jnp.bfloat16),
        ),
        in_specs=[pl.BlockSpec(memory_space=pltpu.VMEM)] * 3,
        out_specs=(pl.BlockSpec(memory_space=pltpu.VMEM), pl.BlockSpec(memory_space=pltpu.VMEM)),
        scratch_shapes=[
            pltpu.VMEM((RAD, mob_local, channels), frames.dtype),
            pltpu.VMEM((RAD, mob_local, channels), frames.dtype),
            pltpu.VMEM((count_frames, mob_local, channels), jnp.bfloat16),
            pltpu.VMEM((count_frames, mob_local, channels), jnp.bfloat16),
            pltpu.SemaphoreType.DMA(()),
            pltpu.SemaphoreType.DMA((n_dz,)),
            pltpu.SemaphoreType.DMA((n_dz,)),
            pltpu.SemaphoreType.DMA((2 * n_dy * n_dz,)),
            pltpu.SemaphoreType.DMA((n_dy * n_dz,)),
            pltpu.SemaphoreType.DMA((2,)),
            pltpu.SemaphoreType.DMA((2,)),
            pltpu.SemaphoreType.DMA(()),
            pltpu.SemaphoreType.DMA(()),
        ],
        compiler_params=pltpu.CompilerParams(
            collective_id=1, has_side_effects=True, vmem_limit_bytes=56 * 1024 * 1024
        ),
    )(frames, kernels, half)
    return rows_out.reshape(n_dy * n_dz * rows, channels), wave


def score_kernel(tile_ref, block_ref, count_ref, section_ref, wave_ref, mine_ref, other_ref, out_ref):
    slot = pl.program_id(0)
    live = slot < count_ref[0]
    mine = block_ref[slot] % 2 == section_ref[0]

    def score(rows_ref):
        rows = rows_ref[...]
        acc = jnp.zeros((1, PB), jnp.float32)
        for level in range(SCALES):
            cells = wave_ref[level].reshape(-1, rows.shape[1])
            scores = lax.dot_general(
                cells, rows, (((1,), (1,)), ((), ())), preferred_element_type=jnp.float32
            )
            acc = acc + jnp.sum(jnp.maximum(scores, 0.0), axis=0, keepdims=True)
        cell_count = SCALES * wave_ref.shape[1] * wave_ref.shape[2]
        out_ref[0] = acc / cell_count

    @pl.when(jnp.logical_and(live, mine))
    def _():
        score(mine_ref)

    @pl.when(jnp.logical_and(live, jnp.logical_not(mine)))
    def _():
        score(other_ref)

    @pl.when(jnp.logical_not(live))
    def _():
        out_ref[0] = jnp.zeros((1, PB), jnp.float32)


def score_pairs(wavelet_stack, my_rows, other_rows, tile_ids, block_ids, live_pairs, section_index):
    slots = tile_ids.shape[0]
    scales, frames_local, mob_local, channels = wavelet_stack.shape

    def last_live(k, count_ref):
        return jnp.minimum(k, count_ref[0] - 1)

    def rows_block(k, t, b, c, s):
        return (b[last_live(k, c)] // 2, 0)

    grid_spec = pltpu.PrefetchScalarGridSpec(
        num_scalar_prefetch=4,
        grid=(slots,),
        in_specs=[
            pl.BlockSpec(
                (scales, frames_local, TM, channels),
                lambda k, t, b, c, s: (0, 0, t[last_live(k, c)], 0),
            ),
            pl.BlockSpec((PB, channels), rows_block),
            pl.BlockSpec((PB, channels), rows_block),
        ],
        out_specs=pl.BlockSpec((1, 1, PB), lambda k, t, b, c, s: (k, 0, 0)),
    )
    out = pl.pallas_call(
        score_kernel,
        grid_spec=grid_spec,
        out_shape=jax.ShapeDtypeStruct((slots, 1, PB), jnp.float32),
    )(
        tile_ids,
        block_ids,
        live_pairs.reshape(1),
        section_index.astype(jnp.int32).reshape(1),
        wavelet_stack,
        my_rows,
        other_rows,
    )
    return out.reshape(slots, PB)


def solution(mesh):
    section_count, grp_count, dev_count = mesh.devices.shape
    dz_count = 8 if dev_count % 8 == 0 else dev_count
    split_mesh = jax.sharding.Mesh(
        mesh.devices.reshape(section_count, grp_count, dev_count // dz_count, dz_count),
        ("section", "grp", "dy", "dz"),
    )
    placed = (
        P("grp", DEV, "section", None),
        P(DEV, None),
        P("section", "grp", DEV),
        P("section", "grp", DEV),
        P("section", "grp", DEV),
        P(),
    )
    return jax.shard_map(
        on_device, mesh=split_mesh, in_specs=placed, out_specs=P("grp", DEV), check_vma=False
    )
```

```python
import functools
import math

import jax
import jax.numpy as jnp
from jax import lax
from jax.experimental import pallas as pl
from jax.experimental.pallas import tpu as pltpu
from jax.sharding import PartitionSpec as P

MOB = 512
SCALES = 6
RAD = 4
TM = 64
PB = 128
PREC = 8192
DEV = ("dy", "dz")


retention_spread = 2.0


def extended(cells, sides, width):
    for axis, dim in sides:
        count = lax.axis_size(axis)
        ends = count - 1
        head = lax.slice_in_dim(cells, 0, width, axis=dim)
        tail = lax.slice_in_dim(cells, cells.shape[dim] - width, cells.shape[dim], axis=dim)
        cells = jnp.concatenate(
            [
                lax.ppermute(tail, axis, [(i, (i + 1) % count) for i in range(ends)]),
                cells,
                lax.ppermute(head, axis, [((i + 1) % count, i) for i in range(ends)]),
            ],
            axis=dim,
        )
    return cells


def retention_weights():
    bell_values = [
        math.exp(-0.5 * (offset / retention_spread) ** 2) for offset in range(-RAD, RAD + 1)
    ]
    bell_total = sum(bell_values)
    return [weight_value / bell_total for weight_value in bell_values]


def mobility_kernels(row_start, row_count, col_start):
    row_place = (row_start + jnp.arange(row_count, dtype=jnp.int32)).astype(jnp.float32)
    col_place = ((col_start + jnp.arange(MOB, dtype=jnp.int32)) % MOB).astype(jnp.float32)
    distance = row_place[:, None] - col_place[None, :]
    tables = []
    for level in range(SCALES):
        spread_scans = 2.0**level
        scaled = distance / spread_scans
        tables.append(
            (1.0 - scaled * scaled)
            * jnp.exp(-0.5 * scaled * scaled)
            / math.sqrt(0.75 * math.sqrt(math.pi) * spread_scans)
        )
    return jnp.stack(tables).astype(jnp.bfloat16)


def on_device(frames, templates, pair_block, pair_tile, pair_count, owner_order):
    section_index = lax.axis_index("section")
    mob_local = frames.shape[2]
    section_count = lax.axis_size("section")
    kernels = mobility_kernels(section_index * mob_local, mob_local, section_index * mob_local)
    half_rows = templates.shape[0] // 2
    my_half = lax.dynamic_slice_in_dim(templates, section_index * half_rows, half_rows, 0)
    my_rows, wavelet_stack = frame_work(frames[0], kernels, my_half)
    other_rows = lax.ppermute(
        my_rows, "section", [(i, (i + 1) % section_count) for i in range(section_count)]
    )
    slots = pair_block.shape[2]
    live_pairs = pair_count[0, 0, 0]
    block_ids = pair_block[0, 0]
    tile_ids = pair_tile[0, 0]
    responses = score_pairs(
        wavelet_stack, my_rows, other_rows, tile_ids, block_ids, live_pairs, section_index
    )
    positions = jnp.take(owner_order.reshape(-1, PB), block_ids, axis=0).reshape(-1)
    groups = PREC // PB
    by_group = jnp.where(
        (positions // PB)[:, None] == jnp.arange(groups, dtype=jnp.int32)[None, :],
        responses.reshape(-1)[:, None],
        0.0,
    )
    by_lane = ((positions % PB)[:, None] == jnp.arange(PB, dtype=jnp.int32)[None, :]).astype(
        jnp.float32
    )
    placed = jnp.einsum(
        "ka,kb->ab",
        by_group,
        by_lane,
        precision=lax.Precision.HIGHEST,
        preferred_element_type=jnp.float32,
    ).reshape(-1)
    dev_count = lax.axis_size(DEV)
    local_total = jnp.sum(responses)
    payload = jnp.concatenate(
        [
            placed.reshape(dev_count, 1, PREC // dev_count),
            jnp.broadcast_to(local_total, (dev_count, 1, 128)),
        ],
        axis=2,
    )
    return reduce_owned(payload)


def reduce_kernel(sizes, payload_ref, out_ref, gathered, totals, send_sems, recv_sems, total_send, total_recv):
    n_section, n_grp, n_dy, n_dz = sizes
    n_dev = n_dy * n_dz
    section = lax.axis_index("section")
    grp = lax.axis_index("grp")
    dy = lax.axis_index("dy")
    dz = lax.axis_index("dz")
    dev = dy * n_dz + dz
    me = section * n_dev + dev
    peers = n_section * n_dev
    owned_width = out_ref.shape[1]

    barrier = pltpu.get_barrier_semaphore()

    def greet(index, carry):
        @pl.when(index != me)
        def _():
            pl.semaphore_signal(
                barrier,
                inc=1,
                device_id=(index // n_dev, grp, index % n_dev // n_dz, index % n_dz),
                device_id_type=pl.DeviceIdType.MESH,
            )

        return carry

    lax.fori_loop(0, peers, greet, 0)
    for step in range(1, n_grp):
        pl.semaphore_signal(
            barrier,
            inc=1,
            device_id=(section, (grp + step) % n_grp, dy, dz),
            device_id_type=pl.DeviceIdType.MESH,
        )
    pl.semaphore_wait(barrier, peers - 1 + n_grp - 1)

    def chunk_copy(index):
        return pltpu.make_async_remote_copy(
            src_ref=payload_ref.at[index % n_dev],
            dst_ref=gathered.at[me],
            send_sem=send_sems.at[index],
            recv_sem=recv_sems.at[me],
            device_id=(index // n_dev, grp, index % n_dev // n_dz, index % n_dz),
            device_id_type=pl.DeviceIdType.MESH,
        )

    def send(index, carry):
        @pl.when(index != me)
        def _():
            chunk_copy(index).start()

        return carry

    lax.fori_loop(0, peers, send, 0)
    gathered[me] = payload_ref[dev]

    def arrive(index, carry):
        @pl.when(index != me)
        def _():
            pltpu.make_async_remote_copy(
                src_ref=payload_ref.at[0],
                dst_ref=gathered.at[index],
                send_sem=send_sems.at[index],
                recv_sem=recv_sems.at[index],
                device_id=(index // n_dev, grp, index % n_dev // n_dz, index % n_dz),
                device_id_type=pl.DeviceIdType.MESH,
            ).wait_recv()
            chunk_copy(index).wait_send()

        return carry

    lax.fori_loop(0, peers, arrive, 0)

    def accumulate(index, acc):
        return acc + gathered[index]

    summed = lax.fori_loop(0, peers, accumulate, jnp.zeros(gathered.shape[1:], jnp.float32))
    totals[grp] = summed[:, owned_width:]

    def total_copy(step):
        target = (grp + step) % n_grp
        return pltpu.make_async_remote_copy(
            src_ref=totals.at[grp],
            dst_ref=totals.at[grp],
            send_sem=total_send.at[target],
            recv_sem=total_recv.at[grp],
            device_id=(section, target, dy, dz),
            device_id_type=pl.DeviceIdType.MESH,
        )

    for step in range(1, n_grp):
        total_copy(step).start()
    for step in range(1, n_grp):
        source = (grp + step) % n_grp
        pltpu.make_async_remote_copy(
            src_ref=totals.at[source],
            dst_ref=totals.at[source],
            send_sem=total_send.at[source],
            recv_sem=total_recv.at[source],
            device_id=(section, source, dy, dz),
            device_id_type=pl.DeviceIdType.MESH,
        ).wait_recv()
        total_copy(step).wait_send()
    run_sum = totals[0]
    for index in range(1, n_grp):
        run_sum = run_sum + totals[index]
    own_total = summed[:, owned_width : owned_width + 1]
    factor = (run_sum[:, 0:1] / n_grp) / own_total
    out_ref[...] = summed[:, :owned_width] * factor


def reduce_owned(payload):
    sizes = (lax.axis_size("section"), lax.axis_size("grp"), lax.axis_size("dy"), lax.axis_size("dz"))
    n_section, n_grp, n_dy, n_dz = sizes
    peers = n_section * n_dy * n_dz
    rows, one, width = payload.shape
    owned_width = width - 128
    return pl.pallas_call(
        functools.partial(reduce_kernel, sizes),
        out_shape=jax.ShapeDtypeStruct((1, owned_width), jnp.float32),
        in_specs=[pl.BlockSpec(memory_space=pltpu.VMEM)],
        out_specs=pl.BlockSpec(memory_space=pltpu.VMEM),
        scratch_shapes=[
            pltpu.VMEM((peers, 1, width), jnp.float32),
            pltpu.VMEM((n_grp, 1, 128), jnp.float32),
            pltpu.SemaphoreType.DMA((peers,)),
            pltpu.SemaphoreType.DMA((peers,)),
            pltpu.SemaphoreType.DMA((n_grp,)),
            pltpu.SemaphoreType.DMA((n_grp,)),
        ],
        compiler_params=pltpu.CompilerParams(collective_id=0, has_side_effects=True),
    )(payload)


def frame_kernel(
    sizes,
    frames_ref,
    kernels_ref,
    half_ref,
    out_ref,
    wave_ref,
    halo_left,
    halo_right,
    own_scans,
    partner_scans,
    own_sem,
    z_send,
    z_recv,
    y_send,
    y_recv,
    halo_send,
    halo_recv,
    swap_send,
    swap_recv,
):
    n_section, n_dy, n_dz = sizes
    n_dev = n_dy * n_dz
    section = lax.axis_index("section")
    grp = lax.axis_index("grp")
    dy = lax.axis_index("dy")
    dz = lax.axis_index("dz")
    dev = dy * n_dz + dz
    partner_section = (section + 1) % n_section

    def dev_peer(index):
        return (section, grp, index // n_dz, index % n_dz)

    barrier = pltpu.get_barrier_semaphore()
    for step in range(1, n_dz):
        pl.semaphore_signal(
            barrier,
            inc=1,
            device_id=(section, grp, dy, (dz + step) % n_dz),
            device_id_type=pl.DeviceIdType.MESH,
        )
    up = (dy + 1) % n_dy
    down = (dy + n_dy - 1) % n_dy
    for row in (up, down):
        pl.semaphore_signal(
            barrier,
            inc=1,
            device_id=(section, grp, row, dz),
            device_id_type=pl.DeviceIdType.MESH,
        )
    pl.semaphore_signal(
        barrier,
        inc=1,
        device_id=(partner_section, grp, dy, dz),
        device_id_type=pl.DeviceIdType.MESH,
    )
    has_left = dev > 0
    has_right = dev < n_dev - 1
    far_left = jnp.logical_and(has_left, dz == 0)
    far_right = jnp.logical_and(has_right, dz == n_dz - 1)

    @pl.when(far_left)
    def _():
        pl.semaphore_signal(
            barrier, inc=1, device_id=dev_peer(dev - 1), device_id_type=pl.DeviceIdType.MESH
        )

    @pl.when(far_right)
    def _():
        pl.semaphore_signal(
            barrier, inc=1, device_id=dev_peer(dev + 1), device_id_type=pl.DeviceIdType.MESH
        )

    extra = far_left.astype(jnp.int32) + far_right.astype(jnp.int32)
    pl.semaphore_wait(barrier, n_dz - 1 + 2 + 1 + extra)

    own = pltpu.make_async_copy(half_ref, out_ref.at[dev], own_sem)
    own.start()

    def z_copy(target, source):
        return pltpu.make_async_remote_copy(
            src_ref=half_ref,
            dst_ref=out_ref.at[dy * n_dz + source],
            send_sem=z_send.at[target],
            recv_sem=z_recv.at[source],
            device_id=(section, grp, dy, target),
            device_id_type=pl.DeviceIdType.MESH,
        )

    for step in range(1, n_dz):
        z_copy((dz + step) % n_dz, dz).start()

    count_frames = frames_ref.shape[0]

    def to_left():
        return pltpu.make_async_remote_copy(
            src_ref=frames_ref.at[pl.ds(0, RAD)],
            dst_ref=halo_right,
            send_sem=halo_send.at[0],
            recv_sem=halo_recv.at[1],
            device_id=dev_peer(dev - 1),
            device_id_type=pl.DeviceIdType.MESH,
        )

    def to_right():
        return pltpu.make_async_remote_copy(
            src_ref=frames_ref.at[pl.ds(count_frames - RAD, RAD)],
            dst_ref=halo_left,
            send_sem=halo_send.at[1],
            recv_sem=halo_recv.at[0],
            device_id=dev_peer(dev + 1),
            device_id_type=pl.DeviceIdType.MESH,
        )

    @pl.when(has_left)
    def _():
        to_left().start()

    @pl.when(has_right)
    def _():
        to_right().start()

    @pl.when(jnp.logical_not(has_left))
    def _():
        halo_left[...] = jnp.zeros(halo_left.shape, halo_left.dtype)

    @pl.when(jnp.logical_not(has_right))
    def _():
        halo_right[...] = jnp.zeros(halo_right.shape, halo_right.dtype)

    def y_copy(direction, row, chunk):
        slot = row * n_dz + chunk
        target = up if direction == 0 else down
        return pltpu.make_async_remote_copy(
            src_ref=out_ref.at[slot],
            dst_ref=out_ref.at[slot],
            send_sem=y_send.at[direction * n_dy * n_dz + slot],
            recv_sem=y_recv.at[slot],
            device_id=(section, grp, target, dz),
            device_id_type=pl.DeviceIdType.MESH,
        )

    def y_own(direction):
        target = up if direction == 0 else down
        return pltpu.make_async_remote_copy(
            src_ref=half_ref,
            dst_ref=out_ref.at[dev],
            send_sem=y_send.at[direction * n_dy * n_dz + dev],
            recv_sem=y_recv.at[dev],
            device_id=(section, grp, target, dz),
            device_id_type=pl.DeviceIdType.MESH,
        )

    for direction in (0, 1):
        y_own(direction).start()
    for step in range(1, n_dz):
        source = (dz + n_dz - step) % n_dz
        z_copy(source, source).wait_recv()
        for direction in (0, 1):
            y_copy(direction, dy, source).start()
    own.wait()
    for step in range(1, n_dz):
        z_copy((dz + step) % n_dz, dz).wait_send()

    @pl.when(has_left)
    def _():
        to_right_of_left = pltpu.make_async_remote_copy(
            src_ref=frames_ref.at[pl.ds(0, RAD)],
            dst_ref=halo_left,
            send_sem=halo_send.at[1],
            recv_sem=halo_recv.at[0],
            device_id=dev_peer(dev - 1),
            device_id_type=pl.DeviceIdType.MESH,
        )
        to_right_of_left.wait_recv()
        to_left().wait_send()

    @pl.when(has_right)
    def _():
        to_left_of_right = pltpu.make_async_remote_copy(
            src_ref=frames_ref.at[pl.ds(0, RAD)],
            dst_ref=halo_right,
            send_sem=halo_send.at[0],
            recv_sem=halo_recv.at[1],
            device_id=dev_peer(dev + 1),
            device_id_type=pl.DeviceIdType.MESH,
        )
        to_left_of_right.wait_recv()
        to_right().wait_send()

    weights = retention_weights()

    row_block = 32

    def smooth_rows(block, carry):
        rows = pl.ds(pl.multiple_of(block * row_block, row_block), row_block)

        def padded_frame(place):
            if place < RAD:
                return halo_left[place, rows, :]
            if place < RAD + count_frames:
                return frames_ref[place - RAD, rows, :]
            return halo_right[place - RAD - count_frames, rows, :]

        for frame in range(count_frames):
            total = weights[0] * padded_frame(frame).astype(jnp.float32)
            for offset in range(1, 2 * RAD + 1):
                total = total + weights[offset] * padded_frame(frame + offset).astype(jnp.float32)
            own_scans[frame, rows, :] = total.astype(own_scans.dtype)
        return carry

    lax.fori_loop(0, own_scans.shape[1] // row_block, smooth_rows, 0)

    swap = pltpu.make_async_remote_copy(
        src_ref=own_scans,
        dst_ref=partner_scans,
        send_sem=swap_send,
        recv_sem=swap_recv,
        device_id=(partner_section, grp, dy, dz),
        device_id_type=pl.DeviceIdType.MESH,
    )
    swap.start()
    relay = n_dz // 2
    for chunk in range(n_dz):
        y_copy(0, down, chunk).wait_recv()
        if chunk < relay:
            y_copy(0, down, chunk).start()
        y_copy(1, up, chunk).wait_recv()
        if chunk >= relay:
            y_copy(1, up, chunk).start()
    swap.wait()

    half = own_scans.shape[1]

    def level_frame(frame, carry):
        for level in range(SCALES):
            table = kernels_ref[level]
            acc = jnp.dot(table[:, :half], own_scans[frame], preferred_element_type=jnp.float32)
            acc = acc + jnp.dot(
                table[:, half:], partner_scans[frame], preferred_element_type=jnp.float32
            )
            wave_ref[level, frame] = acc.astype(wave_ref.dtype)
        return carry

    lax.fori_loop(0, count_frames, level_frame, 0)

    opposite = (dy + 2) % n_dy
    for chunk in range(n_dz):
        y_copy(0, opposite, chunk).wait_recv()
    for direction in (0, 1):
        for chunk in range(n_dz):
            y_copy(direction, dy, chunk).wait_send()
    for chunk in range(relay):
        y_copy(0, down, chunk).wait_send()
    for chunk in range(relay, n_dz):
        y_copy(1, up, chunk).wait_send()


def frame_work(frames, kernels, half):
    sizes = (lax.axis_size("section"), lax.axis_size("dy"), lax.axis_size("dz"))
    n_section, n_dy, n_dz = sizes
    rows, channels = half.shape
    count_frames, mob_local, _ = frames.shape
    rows_out, wave = pl.pallas_call(
        functools.partial(frame_kernel, sizes),
        out_shape=(
            jax.ShapeDtypeStruct((n_dy * n_dz, rows, channels), half.dtype),
            jax.ShapeDtypeStruct((SCALES, count_frames, mob_local, channels), jnp.bfloat16),
        ),
        in_specs=[pl.BlockSpec(memory_space=pltpu.VMEM)] * 3,
        out_specs=(pl.BlockSpec(memory_space=pltpu.VMEM), pl.BlockSpec(memory_space=pltpu.VMEM)),
        scratch_shapes=[
            pltpu.VMEM((RAD, mob_local, channels), frames.dtype),
            pltpu.VMEM((RAD, mob_local, channels), frames.dtype),
            pltpu.VMEM((count_frames, mob_local, channels), jnp.bfloat16),
            pltpu.VMEM((count_frames, mob_local, channels), jnp.bfloat16),
            pltpu.SemaphoreType.DMA(()),
            pltpu.SemaphoreType.DMA((n_dz,)),
            pltpu.SemaphoreType.DMA((n_dz,)),
            pltpu.SemaphoreType.DMA((2 * n_dy * n_dz,)),
            pltpu.SemaphoreType.DMA((n_dy * n_dz,)),
            pltpu.SemaphoreType.DMA((2,)),
            pltpu.SemaphoreType.DMA((2,)),
            pltpu.SemaphoreType.DMA(()),
            pltpu.SemaphoreType.DMA(()),
        ],
        compiler_params=pltpu.CompilerParams(
            collective_id=1, has_side_effects=True, vmem_limit_bytes=56 * 1024 * 1024
        ),
    )(frames, kernels, half)
    return rows_out.reshape(n_dy * n_dz * rows, channels), wave


def score_kernel(
    order_ref, tile_ref, block_ref, count_ref, section_ref, wave_ref, mine_ref, other_ref, out_ref
):
    slot = order_ref[pl.program_id(0)]
    live = slot < count_ref[0]
    mine = block_ref[slot] % 2 == section_ref[0]

    def score(rows_ref):
        rows = rows_ref[...]
        acc = jnp.zeros((1, PB), jnp.float32)
        for level in range(SCALES):
            cells = wave_ref[level].reshape(-1, rows.shape[1])
            scores = lax.dot_general(
                cells, rows, (((1,), (1,)), ((), ())), preferred_element_type=jnp.float32
            )
            acc = acc + jnp.sum(jnp.maximum(scores, 0.0), axis=0, keepdims=True)
        cell_count = SCALES * wave_ref.shape[1] * wave_ref.shape[2]
        out_ref[0] = acc / cell_count

    @pl.when(jnp.logical_and(live, mine))
    def _():
        score(mine_ref)

    @pl.when(jnp.logical_and(live, jnp.logical_not(mine)))
    def _():
        score(other_ref)

    @pl.when(jnp.logical_not(live))
    def _():
        out_ref[0] = jnp.zeros((1, PB), jnp.float32)


def score_pairs(wavelet_stack, my_rows, other_rows, tile_ids, block_ids, live_pairs, section_index):
    slots = tile_ids.shape[0]
    scales, frames_local, mob_local, channels = wavelet_stack.shape
    slot_ids = jnp.arange(slots, dtype=jnp.int32)
    keys = jnp.where(slot_ids < live_pairs, tile_ids * slots + slot_ids, (mob_local // TM + 1) * slots + slot_ids)
    order = jnp.argsort(keys).astype(jnp.int32)

    def visited(k, o, c):
        return o[jnp.minimum(k, c[0] - 1)]

    grid_spec = pltpu.PrefetchScalarGridSpec(
        num_scalar_prefetch=5,
        grid=(slots,),
        in_specs=[
            pl.BlockSpec(
                (scales, frames_local, TM, channels),
                lambda k, o, t, b, c, s: (0, 0, t[visited(k, o, c)], 0),
            ),
            pl.BlockSpec((PB, channels), lambda k, o, t, b, c, s: (b[visited(k, o, c)] // 2, 0)),
            pl.BlockSpec((PB, channels), lambda k, o, t, b, c, s: (b[visited(k, o, c)] // 2, 0)),
        ],
        out_specs=pl.BlockSpec((1, 1, PB), lambda k, o, t, b, c, s: (o[k], 0, 0)),
    )
    out = pl.pallas_call(
        score_kernel,
        grid_spec=grid_spec,
        out_shape=jax.ShapeDtypeStruct((slots, 1, PB), jnp.float32),
    )(
        order,
        tile_ids,
        block_ids,
        live_pairs.reshape(1),
        section_index.astype(jnp.int32).reshape(1),
        wavelet_stack,
        my_rows,
        other_rows,
    )
    return out.reshape(slots, PB)


def solution(mesh):
    section_count, grp_count, dev_count = mesh.devices.shape
    dz_count = 8 if dev_count % 8 == 0 else dev_count
    split_mesh = jax.sharding.Mesh(
        mesh.devices.reshape(section_count, grp_count, dev_count // dz_count, dz_count),
        ("section", "grp", "dy", "dz"),
    )
    placed = (
        P("grp", DEV, "section", None),
        P(DEV, None),
        P("section", "grp", DEV),
        P("section", "grp", DEV),
        P("section", "grp", DEV),
        P(),
    )
    return jax.shard_map(
        on_device, mesh=split_mesh, in_specs=placed, out_specs=P("grp", DEV), check_vma=False
    )
```

```python
import functools
import math

import jax
import jax.numpy as jnp
from jax import lax
from jax.experimental import pallas as pl
from jax.experimental.pallas import tpu as pltpu
from jax.sharding import PartitionSpec as P

MOB = 512
SCALES = 6
RAD = 4
TM = 64
PB = 128
PREC = 8192
DEV = ("dy", "dz")


retention_spread = 2.0


def extended(cells, sides, width):
    for axis, dim in sides:
        count = lax.axis_size(axis)
        ends = count - 1
        head = lax.slice_in_dim(cells, 0, width, axis=dim)
        tail = lax.slice_in_dim(cells, cells.shape[dim] - width, cells.shape[dim], axis=dim)
        cells = jnp.concatenate(
            [
                lax.ppermute(tail, axis, [(i, (i + 1) % count) for i in range(ends)]),
                cells,
                lax.ppermute(head, axis, [((i + 1) % count, i) for i in range(ends)]),
            ],
            axis=dim,
        )
    return cells


def retention_weights():
    bell_values = [
        math.exp(-0.5 * (offset / retention_spread) ** 2) for offset in range(-RAD, RAD + 1)
    ]
    bell_total = sum(bell_values)
    return [weight_value / bell_total for weight_value in bell_values]


def mobility_kernels(row_start, row_count, col_start):
    row_place = (row_start + jnp.arange(row_count, dtype=jnp.int32)).astype(jnp.float32)
    col_place = ((col_start + jnp.arange(MOB, dtype=jnp.int32)) % MOB).astype(jnp.float32)
    distance = row_place[:, None] - col_place[None, :]
    tables = []
    for level in range(SCALES):
        spread_scans = 2.0**level
        scaled = distance / spread_scans
        tables.append(
            (1.0 - scaled * scaled)
            * jnp.exp(-0.5 * scaled * scaled)
            / math.sqrt(0.75 * math.sqrt(math.pi) * spread_scans)
        )
    return jnp.stack(tables).astype(jnp.bfloat16)


def on_device(frames, templates, pair_block, pair_tile, pair_count, owner_order):
    section_index = lax.axis_index("section")
    mob_local = frames.shape[2]
    section_count = lax.axis_size("section")
    kernels = mobility_kernels(section_index * mob_local, mob_local, section_index * mob_local)
    half_rows = templates.shape[0] // 2
    my_half = lax.dynamic_slice_in_dim(templates, section_index * half_rows, half_rows, 0)
    my_rows, other_rows, wavelet_stack = frame_work(frames[0], kernels, my_half)
    slots = pair_block.shape[2]
    live_pairs = pair_count[0, 0, 0]
    block_ids = pair_block[0, 0]
    tile_ids = pair_tile[0, 0]
    responses = score_pairs(
        wavelet_stack, my_rows, other_rows, tile_ids, block_ids, live_pairs, section_index
    )
    positions = jnp.take(owner_order.reshape(-1, PB), block_ids, axis=0).reshape(-1)
    groups = PREC // PB
    by_group = jnp.where(
        (positions // PB)[:, None] == jnp.arange(groups, dtype=jnp.int32)[None, :],
        responses.reshape(-1)[:, None],
        0.0,
    )
    by_lane = ((positions % PB)[:, None] == jnp.arange(PB, dtype=jnp.int32)[None, :]).astype(
        jnp.float32
    )
    placed = jnp.einsum(
        "ka,kb->ab",
        by_group,
        by_lane,
        precision=lax.Precision.HIGHEST,
        preferred_element_type=jnp.float32,
    ).reshape(-1)
    dev_count = lax.axis_size(DEV)
    local_total = jnp.sum(responses)
    payload = jnp.concatenate(
        [
            placed.reshape(dev_count, 1, PREC // dev_count),
            jnp.broadcast_to(local_total, (dev_count, 1, 128)),
        ],
        axis=2,
    )
    return reduce_owned(payload)


def reduce_kernel(sizes, payload_ref, out_ref, gathered, totals, send_sems, recv_sems, total_send, total_recv):
    n_section, n_grp, n_dy, n_dz = sizes
    n_dev = n_dy * n_dz
    section = lax.axis_index("section")
    grp = lax.axis_index("grp")
    dy = lax.axis_index("dy")
    dz = lax.axis_index("dz")
    dev = dy * n_dz + dz
    me = section * n_dev + dev
    peers = n_section * n_dev
    owned_width = out_ref.shape[1]

    barrier = pltpu.get_barrier_semaphore()

    def greet(index, carry):
        @pl.when(index != me)
        def _():
            pl.semaphore_signal(
                barrier,
                inc=1,
                device_id=(index // n_dev, grp, index % n_dev // n_dz, index % n_dz),
                device_id_type=pl.DeviceIdType.MESH,
            )

        return carry

    lax.fori_loop(0, peers, greet, 0)
    for step in range(1, n_grp):
        pl.semaphore_signal(
            barrier,
            inc=1,
            device_id=(section, (grp + step) % n_grp, dy, dz),
            device_id_type=pl.DeviceIdType.MESH,
        )
    pl.semaphore_wait(barrier, peers - 1 + n_grp - 1)

    def chunk_copy(index):
        return pltpu.make_async_remote_copy(
            src_ref=payload_ref.at[index % n_dev],
            dst_ref=gathered.at[me],
            send_sem=send_sems.at[index],
            recv_sem=recv_sems.at[me],
            device_id=(index // n_dev, grp, index % n_dev // n_dz, index % n_dz),
            device_id_type=pl.DeviceIdType.MESH,
        )

    def send(index, carry):
        @pl.when(index != me)
        def _():
            chunk_copy(index).start()

        return carry

    lax.fori_loop(0, peers, send, 0)
    gathered[me] = payload_ref[dev]

    def arrive(index, carry):
        @pl.when(index != me)
        def _():
            pltpu.make_async_remote_copy(
                src_ref=payload_ref.at[0],
                dst_ref=gathered.at[index],
                send_sem=send_sems.at[index],
                recv_sem=recv_sems.at[index],
                device_id=(index // n_dev, grp, index % n_dev // n_dz, index % n_dz),
                device_id_type=pl.DeviceIdType.MESH,
            ).wait_recv()
            chunk_copy(index).wait_send()

        return carry

    lax.fori_loop(0, peers, arrive, 0)

    def accumulate(index, acc):
        return acc + gathered[index]

    summed = lax.fori_loop(0, peers, accumulate, jnp.zeros(gathered.shape[1:], jnp.float32))
    totals[grp] = summed[:, owned_width:]

    def total_copy(step):
        target = (grp + step) % n_grp
        return pltpu.make_async_remote_copy(
            src_ref=totals.at[grp],
            dst_ref=totals.at[grp],
            send_sem=total_send.at[target],
            recv_sem=total_recv.at[grp],
            device_id=(section, target, dy, dz),
            device_id_type=pl.DeviceIdType.MESH,
        )

    for step in range(1, n_grp):
        total_copy(step).start()
    for step in range(1, n_grp):
        source = (grp + step) % n_grp
        pltpu.make_async_remote_copy(
            src_ref=totals.at[source],
            dst_ref=totals.at[source],
            send_sem=total_send.at[source],
            recv_sem=total_recv.at[source],
            device_id=(section, source, dy, dz),
            device_id_type=pl.DeviceIdType.MESH,
        ).wait_recv()
        total_copy(step).wait_send()
    run_sum = totals[0]
    for index in range(1, n_grp):
        run_sum = run_sum + totals[index]
    own_total = summed[:, owned_width : owned_width + 1]
    factor = (run_sum[:, 0:1] / n_grp) / own_total
    out_ref[...] = summed[:, :owned_width] * factor


def reduce_owned(payload):
    sizes = (lax.axis_size("section"), lax.axis_size("grp"), lax.axis_size("dy"), lax.axis_size("dz"))
    n_section, n_grp, n_dy, n_dz = sizes
    peers = n_section * n_dy * n_dz
    rows, one, width = payload.shape
    owned_width = width - 128
    return pl.pallas_call(
        functools.partial(reduce_kernel, sizes),
        out_shape=jax.ShapeDtypeStruct((1, owned_width), jnp.float32),
        in_specs=[pl.BlockSpec(memory_space=pltpu.VMEM)],
        out_specs=pl.BlockSpec(memory_space=pltpu.VMEM),
        scratch_shapes=[
            pltpu.VMEM((peers, 1, width), jnp.float32),
            pltpu.VMEM((n_grp, 1, 128), jnp.float32),
            pltpu.SemaphoreType.DMA((peers,)),
            pltpu.SemaphoreType.DMA((peers,)),
            pltpu.SemaphoreType.DMA((n_grp,)),
            pltpu.SemaphoreType.DMA((n_grp,)),
        ],
        compiler_params=pltpu.CompilerParams(collective_id=0, has_side_effects=True),
    )(payload)


def frame_kernel(
    sizes,
    frames_ref,
    kernels_ref,
    half_ref,
    out_ref,
    other_ref,
    wave_ref,
    halo_left,
    halo_right,
    own_scans,
    partner_scans,
    own_sem,
    z_send,
    z_recv,
    y_send,
    y_recv,
    halo_send,
    halo_recv,
    swap_send,
    swap_recv,
    pair_send,
    pair_recv,
):
    n_section, n_dy, n_dz = sizes
    n_dev = n_dy * n_dz
    section = lax.axis_index("section")
    grp = lax.axis_index("grp")
    dy = lax.axis_index("dy")
    dz = lax.axis_index("dz")
    dev = dy * n_dz + dz
    partner_section = (section + 1) % n_section

    def dev_peer(index):
        return (section, grp, index // n_dz, index % n_dz)

    barrier = pltpu.get_barrier_semaphore()
    for step in range(1, n_dz):
        pl.semaphore_signal(
            barrier,
            inc=1,
            device_id=(section, grp, dy, (dz + step) % n_dz),
            device_id_type=pl.DeviceIdType.MESH,
        )
    up = (dy + 1) % n_dy
    down = (dy + n_dy - 1) % n_dy
    for row in (up, down):
        pl.semaphore_signal(
            barrier,
            inc=1,
            device_id=(section, grp, row, dz),
            device_id_type=pl.DeviceIdType.MESH,
        )
    pl.semaphore_signal(
        barrier,
        inc=1,
        device_id=(partner_section, grp, dy, dz),
        device_id_type=pl.DeviceIdType.MESH,
    )
    has_left = dev > 0
    has_right = dev < n_dev - 1
    far_left = jnp.logical_and(has_left, dz == 0)
    far_right = jnp.logical_and(has_right, dz == n_dz - 1)

    @pl.when(far_left)
    def _():
        pl.semaphore_signal(
            barrier, inc=1, device_id=dev_peer(dev - 1), device_id_type=pl.DeviceIdType.MESH
        )

    @pl.when(far_right)
    def _():
        pl.semaphore_signal(
            barrier, inc=1, device_id=dev_peer(dev + 1), device_id_type=pl.DeviceIdType.MESH
        )

    extra = far_left.astype(jnp.int32) + far_right.astype(jnp.int32)
    pl.semaphore_wait(barrier, n_dz - 1 + 2 + 1 + extra)

    own = pltpu.make_async_copy(half_ref, out_ref.at[dev], own_sem)
    own.start()

    def pair_copy(slot, source_ref):
        return pltpu.make_async_remote_copy(
            src_ref=source_ref,
            dst_ref=other_ref.at[slot],
            send_sem=pair_send.at[slot],
            recv_sem=pair_recv.at[slot],
            device_id=(partner_section, grp, dy, dz),
            device_id_type=pl.DeviceIdType.MESH,
        )

    pair_copy(dev, half_ref).start()

    def z_copy(target, source):
        return pltpu.make_async_remote_copy(
            src_ref=half_ref,
            dst_ref=out_ref.at[dy * n_dz + source],
            send_sem=z_send.at[target],
            recv_sem=z_recv.at[source],
            device_id=(section, grp, dy, target),
            device_id_type=pl.DeviceIdType.MESH,
        )

    for step in range(1, n_dz):
        z_copy((dz + step) % n_dz, dz).start()

    count_frames = frames_ref.shape[0]

    def to_left():
        return pltpu.make_async_remote_copy(
            src_ref=frames_ref.at[pl.ds(0, RAD)],
            dst_ref=halo_right,
            send_sem=halo_send.at[0],
            recv_sem=halo_recv.at[1],
            device_id=dev_peer(dev - 1),
            device_id_type=pl.DeviceIdType.MESH,
        )

    def to_right():
        return pltpu.make_async_remote_copy(
            src_ref=frames_ref.at[pl.ds(count_frames - RAD, RAD)],
            dst_ref=halo_left,
            send_sem=halo_send.at[1],
            recv_sem=halo_recv.at[0],
            device_id=dev_peer(dev + 1),
            device_id_type=pl.DeviceIdType.MESH,
        )

    @pl.when(has_left)
    def _():
        to_left().start()

    @pl.when(has_right)
    def _():
        to_right().start()

    @pl.when(jnp.logical_not(has_left))
    def _():
        halo_left[...] = jnp.zeros(halo_left.shape, halo_left.dtype)

    @pl.when(jnp.logical_not(has_right))
    def _():
        halo_right[...] = jnp.zeros(halo_right.shape, halo_right.dtype)

    def y_copy(direction, row, chunk):
        slot = row * n_dz + chunk
        target = up if direction == 0 else down
        return pltpu.make_async_remote_copy(
            src_ref=out_ref.at[slot],
            dst_ref=out_ref.at[slot],
            send_sem=y_send.at[direction * n_dy * n_dz + slot],
            recv_sem=y_recv.at[slot],
            device_id=(section, grp, target, dz),
            device_id_type=pl.DeviceIdType.MESH,
        )

    def y_own(direction):
        target = up if direction == 0 else down
        return pltpu.make_async_remote_copy(
            src_ref=half_ref,
            dst_ref=out_ref.at[dev],
            send_sem=y_send.at[direction * n_dy * n_dz + dev],
            recv_sem=y_recv.at[dev],
            device_id=(section, grp, target, dz),
            device_id_type=pl.DeviceIdType.MESH,
        )

    for direction in (0, 1):
        y_own(direction).start()
    for step in range(1, n_dz):
        source = (dz + n_dz - step) % n_dz
        z_copy(source, source).wait_recv()
        for direction in (0, 1):
            y_copy(direction, dy, source).start()
        pair_copy(dy * n_dz + source, out_ref.at[dy * n_dz + source]).start()
    own.wait()
    for step in range(1, n_dz):
        z_copy((dz + step) % n_dz, dz).wait_send()

    @pl.when(has_left)
    def _():
        to_right_of_left = pltpu.make_async_remote_copy(
            src_ref=frames_ref.at[pl.ds(0, RAD)],
            dst_ref=halo_left,
            send_sem=halo_send.at[1],
            recv_sem=halo_recv.at[0],
            device_id=dev_peer(dev - 1),
            device_id_type=pl.DeviceIdType.MESH,
        )
        to_right_of_left.wait_recv()
        to_left().wait_send()

    @pl.when(has_right)
    def _():
        to_left_of_right = pltpu.make_async_remote_copy(
            src_ref=frames_ref.at[pl.ds(0, RAD)],
            dst_ref=halo_right,
            send_sem=halo_send.at[0],
            recv_sem=halo_recv.at[1],
            device_id=dev_peer(dev + 1),
            device_id_type=pl.DeviceIdType.MESH,
        )
        to_left_of_right.wait_recv()
        to_right().wait_send()

    weights = retention_weights()

    row_block = 32

    def smooth_rows(block, carry):
        rows = pl.ds(pl.multiple_of(block * row_block, row_block), row_block)

        def padded_frame(place):
            if place < RAD:
                return halo_left[place, rows, :]
            if place < RAD + count_frames:
                return frames_ref[place - RAD, rows, :]
            return halo_right[place - RAD - count_frames, rows, :]

        for frame in range(count_frames):
            total = weights[0] * padded_frame(frame).astype(jnp.float32)
            for offset in range(1, 2 * RAD + 1):
                total = total + weights[offset] * padded_frame(frame + offset).astype(jnp.float32)
            own_scans[frame, rows, :] = total.astype(own_scans.dtype)
        return carry

    lax.fori_loop(0, own_scans.shape[1] // row_block, smooth_rows, 0)

    swap = pltpu.make_async_remote_copy(
        src_ref=own_scans,
        dst_ref=partner_scans,
        send_sem=swap_send,
        recv_sem=swap_recv,
        device_id=(partner_section, grp, dy, dz),
        device_id_type=pl.DeviceIdType.MESH,
    )
    swap.start()
    relay = n_dz // 2
    for chunk in range(n_dz):
        y_copy(0, down, chunk).wait_recv()
        if chunk < relay:
            y_copy(0, down, chunk).start()
        pair_copy(down * n_dz + chunk, out_ref.at[down * n_dz + chunk]).start()
        y_copy(1, up, chunk).wait_recv()
        if chunk >= relay:
            y_copy(1, up, chunk).start()
        pair_copy(up * n_dz + chunk, out_ref.at[up * n_dz + chunk]).start()
    swap.wait()

    half = own_scans.shape[1]

    def level_frame(frame, carry):
        for level in range(SCALES):
            table = kernels_ref[level]
            acc = jnp.dot(table[:, :half], own_scans[frame], preferred_element_type=jnp.float32)
            acc = acc + jnp.dot(
                table[:, half:], partner_scans[frame], preferred_element_type=jnp.float32
            )
            wave_ref[level, frame] = acc.astype(wave_ref.dtype)
        return carry

    lax.fori_loop(0, count_frames, level_frame, 0)

    opposite = (dy + 2) % n_dy
    for chunk in range(n_dz):
        y_copy(0, opposite, chunk).wait_recv()
        pair_copy(opposite * n_dz + chunk, out_ref.at[opposite * n_dz + chunk]).start()
    for direction in (0, 1):
        for chunk in range(n_dz):
            y_copy(direction, dy, chunk).wait_send()
    for chunk in range(relay):
        y_copy(0, down, chunk).wait_send()
    for chunk in range(relay, n_dz):
        y_copy(1, up, chunk).wait_send()
    for slot in range(n_dev):
        pair_copy(slot, half_ref).wait_recv()
    for slot in range(n_dev):
        pair_copy(slot, half_ref).wait_send()


def frame_work(frames, kernels, half):
    sizes = (lax.axis_size("section"), lax.axis_size("dy"), lax.axis_size("dz"))
    n_section, n_dy, n_dz = sizes
    rows, channels = half.shape
    count_frames, mob_local, _ = frames.shape
    rows_out, other_out, wave = pl.pallas_call(
        functools.partial(frame_kernel, sizes),
        out_shape=(
            jax.ShapeDtypeStruct((n_dy * n_dz, rows, channels), half.dtype),
            jax.ShapeDtypeStruct((n_dy * n_dz, rows, channels), half.dtype),
            jax.ShapeDtypeStruct((SCALES, count_frames, mob_local, channels), jnp.bfloat16),
        ),
        in_specs=[pl.BlockSpec(memory_space=pltpu.VMEM)] * 3,
        out_specs=(pl.BlockSpec(memory_space=pltpu.VMEM),) * 3,
        scratch_shapes=[
            pltpu.VMEM((RAD, mob_local, channels), frames.dtype),
            pltpu.VMEM((RAD, mob_local, channels), frames.dtype),
            pltpu.VMEM((count_frames, mob_local, channels), jnp.bfloat16),
            pltpu.VMEM((count_frames, mob_local, channels), jnp.bfloat16),
            pltpu.SemaphoreType.DMA(()),
            pltpu.SemaphoreType.DMA((n_dz,)),
            pltpu.SemaphoreType.DMA((n_dz,)),
            pltpu.SemaphoreType.DMA((2 * n_dy * n_dz,)),
            pltpu.SemaphoreType.DMA((n_dy * n_dz,)),
            pltpu.SemaphoreType.DMA((2,)),
            pltpu.SemaphoreType.DMA((2,)),
            pltpu.SemaphoreType.DMA(()),
            pltpu.SemaphoreType.DMA(()),
            pltpu.SemaphoreType.DMA((n_dy * n_dz,)),
            pltpu.SemaphoreType.DMA((n_dy * n_dz,)),
        ],
        compiler_params=pltpu.CompilerParams(
            collective_id=1, has_side_effects=True, vmem_limit_bytes=56 * 1024 * 1024
        ),
    )(frames, kernels, half)
    return (
        rows_out.reshape(n_dy * n_dz * rows, channels),
        other_out.reshape(n_dy * n_dz * rows, channels),
        wave,
    )


def score_kernel(
    order_ref, tile_ref, block_ref, count_ref, section_ref, wave_ref, mine_ref, other_ref, out_ref
):
    slot = order_ref[pl.program_id(0)]
    live = slot < count_ref[0]
    mine = block_ref[slot] % 2 == section_ref[0]

    def score(rows_ref):
        rows = rows_ref[...]
        acc = jnp.zeros((1, PB), jnp.float32)
        for level in range(SCALES):
            cells = wave_ref[level].reshape(-1, rows.shape[1])
            scores = lax.dot_general(
                cells, rows, (((1,), (1,)), ((), ())), preferred_element_type=jnp.float32
            )
            acc = acc + jnp.sum(jnp.maximum(scores, 0.0), axis=0, keepdims=True)
        cell_count = SCALES * wave_ref.shape[1] * wave_ref.shape[2]
        out_ref[0] = acc / cell_count

    @pl.when(jnp.logical_and(live, mine))
    def _():
        score(mine_ref)

    @pl.when(jnp.logical_and(live, jnp.logical_not(mine)))
    def _():
        score(other_ref)

    @pl.when(jnp.logical_not(live))
    def _():
        out_ref[0] = jnp.zeros((1, PB), jnp.float32)


def score_pairs(wavelet_stack, my_rows, other_rows, tile_ids, block_ids, live_pairs, section_index):
    slots = tile_ids.shape[0]
    scales, frames_local, mob_local, channels = wavelet_stack.shape
    slot_ids = jnp.arange(slots, dtype=jnp.int32)
    keys = jnp.where(slot_ids < live_pairs, tile_ids * slots + slot_ids, (mob_local // TM + 1) * slots + slot_ids)
    order = jnp.argsort(keys).astype(jnp.int32)

    def visited(k, o, c):
        return o[jnp.minimum(k, c[0] - 1)]

    grid_spec = pltpu.PrefetchScalarGridSpec(
        num_scalar_prefetch=5,
        grid=(slots,),
        in_specs=[
            pl.BlockSpec(
                (scales, frames_local, TM, channels),
                lambda k, o, t, b, c, s: (0, 0, t[visited(k, o, c)], 0),
            ),
            pl.BlockSpec((PB, channels), lambda k, o, t, b, c, s: (b[visited(k, o, c)] // 2, 0)),
            pl.BlockSpec((PB, channels), lambda k, o, t, b, c, s: (b[visited(k, o, c)] // 2, 0)),
        ],
        out_specs=pl.BlockSpec((1, 1, PB), lambda k, o, t, b, c, s: (o[k], 0, 0)),
    )
    out = pl.pallas_call(
        score_kernel,
        grid_spec=grid_spec,
        out_shape=jax.ShapeDtypeStruct((slots, 1, PB), jnp.float32),
    )(
        order,
        tile_ids,
        block_ids,
        live_pairs.reshape(1),
        section_index.astype(jnp.int32).reshape(1),
        wavelet_stack,
        my_rows,
        other_rows,
    )
    return out.reshape(slots, PB)


def solution(mesh):
    section_count, grp_count, dev_count = mesh.devices.shape
    dz_count = 8 if dev_count % 8 == 0 else dev_count
    split_mesh = jax.sharding.Mesh(
        mesh.devices.reshape(section_count, grp_count, dev_count // dz_count, dz_count),
        ("section", "grp", "dy", "dz"),
    )
    placed = (
        P("grp", DEV, "section", None),
        P(DEV, None),
        P("section", "grp", DEV),
        P("section", "grp", DEV),
        P("section", "grp", DEV),
        P(),
    )
    return jax.shard_map(
        on_device, mesh=split_mesh, in_specs=placed, out_specs=P("grp", DEV), check_vma=False
    )
```

```python
import functools
import math

import jax
import jax.numpy as jnp
from jax import lax
from jax.experimental import pallas as pl
from jax.experimental.pallas import tpu as pltpu
from jax.sharding import PartitionSpec as P

MOB = 512
SCALES = 6
RAD = 4
TM = 64
PB = 128
PREC = 8192
DEV = ("dy", "dz")


retention_spread = 2.0


def extended(cells, sides, width):
    for axis, dim in sides:
        count = lax.axis_size(axis)
        ends = count - 1
        head = lax.slice_in_dim(cells, 0, width, axis=dim)
        tail = lax.slice_in_dim(cells, cells.shape[dim] - width, cells.shape[dim], axis=dim)
        cells = jnp.concatenate(
            [
                lax.ppermute(tail, axis, [(i, (i + 1) % count) for i in range(ends)]),
                cells,
                lax.ppermute(head, axis, [((i + 1) % count, i) for i in range(ends)]),
            ],
            axis=dim,
        )
    return cells


def retention_weights():
    bell_values = [
        math.exp(-0.5 * (offset / retention_spread) ** 2) for offset in range(-RAD, RAD + 1)
    ]
    bell_total = sum(bell_values)
    return [weight_value / bell_total for weight_value in bell_values]


def mobility_kernels(row_start, row_count, col_start):
    row_place = (row_start + jnp.arange(row_count, dtype=jnp.int32)).astype(jnp.float32)
    col_place = ((col_start + jnp.arange(MOB, dtype=jnp.int32)) % MOB).astype(jnp.float32)
    distance = row_place[:, None] - col_place[None, :]
    tables = []
    for level in range(SCALES):
        spread_scans = 2.0**level
        scaled = distance / spread_scans
        tables.append(
            (1.0 - scaled * scaled)
            * jnp.exp(-0.5 * scaled * scaled)
            / math.sqrt(0.75 * math.sqrt(math.pi) * spread_scans)
        )
    return jnp.stack(tables).astype(jnp.bfloat16)


def on_device(frames, templates, pair_block, pair_tile, pair_count, owner_order):
    section_index = lax.axis_index("section")
    mob_local = frames.shape[2]
    section_count = lax.axis_size("section")
    kernels = mobility_kernels(section_index * mob_local, mob_local, section_index * mob_local)
    half_rows = templates.shape[0] // 2
    my_half = lax.dynamic_slice_in_dim(templates, section_index * half_rows, half_rows, 0)
    my_rows, other_rows, wavelet_stack = frame_work(frames[0], kernels, my_half)
    slots = pair_block.shape[2]
    live_pairs = pair_count[0, 0, 0]
    block_ids = pair_block[0, 0]
    tile_ids = pair_tile[0, 0]
    responses = score_pairs(
        wavelet_stack, my_rows, other_rows, tile_ids, block_ids, live_pairs, section_index
    )
    positions = jnp.take(owner_order.reshape(-1, PB), block_ids, axis=0).reshape(-1)
    groups = PREC // PB
    by_group = jnp.where(
        (positions // PB)[:, None] == jnp.arange(groups, dtype=jnp.int32)[None, :],
        responses.reshape(-1)[:, None],
        0.0,
    )
    by_lane = ((positions % PB)[:, None] == jnp.arange(PB, dtype=jnp.int32)[None, :]).astype(
        jnp.float32
    )
    placed = jnp.einsum(
        "ka,kb->ab",
        by_group,
        by_lane,
        precision=lax.Precision.HIGHEST,
        preferred_element_type=jnp.float32,
    ).reshape(-1)
    dev_count = lax.axis_size(DEV)
    local_total = jnp.sum(responses)
    payload = jnp.concatenate(
        [
            placed.reshape(dev_count, 1, PREC // dev_count),
            jnp.broadcast_to(local_total, (dev_count, 1, 128)),
        ],
        axis=2,
    )
    return reduce_owned(payload)


def reduce_kernel(
    sizes,
    payload_ref,
    out_ref,
    mixed,
    line,
    line_in,
    column,
    column_in,
    totals,
    pair_send,
    pair_recv,
    z_send,
    z_recv,
    y_send,
    y_recv,
    total_send,
    total_recv,
):
    n_section, n_grp, n_dy, n_dz = sizes
    section = lax.axis_index("section")
    grp = lax.axis_index("grp")
    dy = lax.axis_index("dy")
    dz = lax.axis_index("dz")
    partner = (section + 1) % n_section
    owned_width = out_ref.shape[1]

    barrier = pltpu.get_barrier_semaphore()
    peers = [(partner, grp, dy, dz)]
    peers += [(section, grp, dy, (dz + step) % n_dz) for step in range(1, n_dz)]
    peers += [(section, grp, (dy + step) % n_dy, dz) for step in range(1, n_dy)]
    peers += [(section, (grp + step) % n_grp, dy, dz) for step in range(1, n_grp)]
    for peer in peers:
        pl.semaphore_signal(barrier, inc=1, device_id=peer, device_id_type=pl.DeviceIdType.MESH)
    pl.semaphore_wait(barrier, len(peers))

    swap = pltpu.make_async_remote_copy(
        src_ref=payload_ref,
        dst_ref=mixed,
        send_sem=pair_send,
        recv_sem=pair_recv,
        device_id=(partner, grp, dy, dz),
        device_id_type=pl.DeviceIdType.MESH,
    )
    swap.start()
    swap.wait()
    line[...] = payload_ref[...] + mixed[...]
    line_in[dz] = line[dz]

    def z_copy(target, source):
        return pltpu.make_async_remote_copy(
            src_ref=line.at[target],
            dst_ref=line_in.at[source],
            send_sem=z_send.at[target],
            recv_sem=z_recv.at[source],
            device_id=(section, grp, dy, target),
            device_id_type=pl.DeviceIdType.MESH,
        )

    for step in range(1, n_dz):
        z_copy((dz + step) % n_dz, dz).start()
    for step in range(1, n_dz):
        source = (dz + n_dz - step) % n_dz
        z_copy(source, source).wait_recv()
    partial = line_in[0]
    for index in range(1, n_dz):
        partial = partial + line_in[index]
    column[...] = partial
    column_in[dy] = column[dy]

    def y_copy(target, source):
        return pltpu.make_async_remote_copy(
            src_ref=column.at[target],
            dst_ref=column_in.at[source],
            send_sem=y_send.at[target],
            recv_sem=y_recv.at[source],
            device_id=(section, grp, target, dz),
            device_id_type=pl.DeviceIdType.MESH,
        )

    for step in range(1, n_dy):
        y_copy((dy + step) % n_dy, dy).start()
    for step in range(1, n_dy):
        source = (dy + n_dy - step) % n_dy
        y_copy(source, source).wait_recv()
    summed = column_in[0]
    for index in range(1, n_dy):
        summed = summed + column_in[index]
    summed = summed.reshape(summed.shape[-2:])
    totals[grp] = summed[:, owned_width:]

    def total_copy(step):
        target = (grp + step) % n_grp
        return pltpu.make_async_remote_copy(
            src_ref=totals.at[grp],
            dst_ref=totals.at[grp],
            send_sem=total_send.at[target],
            recv_sem=total_recv.at[grp],
            device_id=(section, target, dy, dz),
            device_id_type=pl.DeviceIdType.MESH,
        )

    for step in range(1, n_grp):
        total_copy(step).start()
    for step in range(1, n_grp):
        source = (grp + step) % n_grp
        pltpu.make_async_remote_copy(
            src_ref=totals.at[source],
            dst_ref=totals.at[source],
            send_sem=total_send.at[source],
            recv_sem=total_recv.at[source],
            device_id=(section, source, dy, dz),
            device_id_type=pl.DeviceIdType.MESH,
        ).wait_recv()
        total_copy(step).wait_send()
    for step in range(1, n_dz):
        z_copy((dz + step) % n_dz, dz).wait_send()
    for step in range(1, n_dy):
        y_copy((dy + step) % n_dy, dy).wait_send()
    run_sum = totals[0]
    for index in range(1, n_grp):
        run_sum = run_sum + totals[index]
    own_total = summed[:, owned_width : owned_width + 1]
    factor = (run_sum[:, 0:1] / n_grp) / own_total
    out_ref[...] = summed[:, :owned_width] * factor


def reduce_owned(payload):
    sizes = (lax.axis_size("section"), lax.axis_size("grp"), lax.axis_size("dy"), lax.axis_size("dz"))
    n_section, n_grp, n_dy, n_dz = sizes
    rows, one, width = payload.shape
    owned_width = width - 128
    lines = payload.reshape(n_dy, n_dz, one, width).transpose(1, 0, 2, 3)
    return pl.pallas_call(
        functools.partial(reduce_kernel, sizes),
        out_shape=jax.ShapeDtypeStruct((1, owned_width), jnp.float32),
        in_specs=[pl.BlockSpec(memory_space=pltpu.VMEM)],
        out_specs=pl.BlockSpec(memory_space=pltpu.VMEM),
        scratch_shapes=[
            pltpu.VMEM((n_dz, n_dy, one, width), jnp.float32),
            pltpu.VMEM((n_dz, n_dy, one, width), jnp.float32),
            pltpu.VMEM((n_dz, n_dy, one, width), jnp.float32),
            pltpu.VMEM((n_dy, one, width), jnp.float32),
            pltpu.VMEM((n_dy, one, width), jnp.float32),
            pltpu.VMEM((n_grp, 1, 128), jnp.float32),
            pltpu.SemaphoreType.DMA(()),
            pltpu.SemaphoreType.DMA(()),
            pltpu.SemaphoreType.DMA((n_dz,)),
            pltpu.SemaphoreType.DMA((n_dz,)),
            pltpu.SemaphoreType.DMA((n_dy,)),
            pltpu.SemaphoreType.DMA((n_dy,)),
            pltpu.SemaphoreType.DMA((n_grp,)),
            pltpu.SemaphoreType.DMA((n_grp,)),
        ],
        compiler_params=pltpu.CompilerParams(collective_id=0, has_side_effects=True),
    )(lines)


def frame_kernel(
    sizes,
    frames_ref,
    kernels_ref,
    half_ref,
    out_ref,
    other_ref,
    wave_ref,
    halo_left,
    halo_right,
    own_scans,
    partner_scans,
    own_sem,
    z_send,
    z_recv,
    y_send,
    y_recv,
    halo_send,
    halo_recv,
    swap_send,
    swap_recv,
    pair_send,
    pair_recv,
):
    n_section, n_dy, n_dz = sizes
    n_dev = n_dy * n_dz
    section = lax.axis_index("section")
    grp = lax.axis_index("grp")
    dy = lax.axis_index("dy")
    dz = lax.axis_index("dz")
    dev = dy * n_dz + dz
    partner_section = (section + 1) % n_section

    def dev_peer(index):
        return (section, grp, index // n_dz, index % n_dz)

    barrier = pltpu.get_barrier_semaphore()
    for step in range(1, n_dz):
        pl.semaphore_signal(
            barrier,
            inc=1,
            device_id=(section, grp, dy, (dz + step) % n_dz),
            device_id_type=pl.DeviceIdType.MESH,
        )
    up = (dy + 1) % n_dy
    down = (dy + n_dy - 1) % n_dy
    for row in (up, down):
        pl.semaphore_signal(
            barrier,
            inc=1,
            device_id=(section, grp, row, dz),
            device_id_type=pl.DeviceIdType.MESH,
        )
    pl.semaphore_signal(
        barrier,
        inc=1,
        device_id=(partner_section, grp, dy, dz),
        device_id_type=pl.DeviceIdType.MESH,
    )
    has_left = dev > 0
    has_right = dev < n_dev - 1
    far_left = jnp.logical_and(has_left, dz == 0)
    far_right = jnp.logical_and(has_right, dz == n_dz - 1)

    @pl.when(far_left)
    def _():
        pl.semaphore_signal(
            barrier, inc=1, device_id=dev_peer(dev - 1), device_id_type=pl.DeviceIdType.MESH
        )

    @pl.when(far_right)
    def _():
        pl.semaphore_signal(
            barrier, inc=1, device_id=dev_peer(dev + 1), device_id_type=pl.DeviceIdType.MESH
        )

    extra = far_left.astype(jnp.int32) + far_right.astype(jnp.int32)
    pl.semaphore_wait(barrier, n_dz - 1 + 2 + 1 + extra)

    own = pltpu.make_async_copy(half_ref, out_ref.at[dev], own_sem)
    own.start()

    def pair_copy(slot, source_ref):
        return pltpu.make_async_remote_copy(
            src_ref=source_ref,
            dst_ref=other_ref.at[slot],
            send_sem=pair_send.at[slot],
            recv_sem=pair_recv.at[slot],
            device_id=(partner_section, grp, dy, dz),
            device_id_type=pl.DeviceIdType.MESH,
        )

    pair_copy(dev, half_ref).start()

    def z_copy(target, source):
        return pltpu.make_async_remote_copy(
            src_ref=half_ref,
            dst_ref=out_ref.at[dy * n_dz + source],
            send_sem=z_send.at[target],
            recv_sem=z_recv.at[source],
            device_id=(section, grp, dy, target),
            device_id_type=pl.DeviceIdType.MESH,
        )

    for step in range(1, n_dz):
        z_copy((dz + step) % n_dz, dz).start()

    count_frames = frames_ref.shape[0]

    def to_left():
        return pltpu.make_async_remote_copy(
            src_ref=frames_ref.at[pl.ds(0, RAD)],
            dst_ref=halo_right,
            send_sem=halo_send.at[0],
            recv_sem=halo_recv.at[1],
            device_id=dev_peer(dev - 1),
            device_id_type=pl.DeviceIdType.MESH,
        )

    def to_right():
        return pltpu.make_async_remote_copy(
            src_ref=frames_ref.at[pl.ds(count_frames - RAD, RAD)],
            dst_ref=halo_left,
            send_sem=halo_send.at[1],
            recv_sem=halo_recv.at[0],
            device_id=dev_peer(dev + 1),
            device_id_type=pl.DeviceIdType.MESH,
        )

    @pl.when(has_left)
    def _():
        to_left().start()

    @pl.when(has_right)
    def _():
        to_right().start()

    @pl.when(jnp.logical_not(has_left))
    def _():
        halo_left[...] = jnp.zeros(halo_left.shape, halo_left.dtype)

    @pl.when(jnp.logical_not(has_right))
    def _():
        halo_right[...] = jnp.zeros(halo_right.shape, halo_right.dtype)

    def y_copy(direction, row, chunk):
        slot = row * n_dz + chunk
        target = up if direction == 0 else down
        return pltpu.make_async_remote_copy(
            src_ref=out_ref.at[slot],
            dst_ref=out_ref.at[slot],
            send_sem=y_send.at[direction * n_dy * n_dz + slot],
            recv_sem=y_recv.at[slot],
            device_id=(section, grp, target, dz),
            device_id_type=pl.DeviceIdType.MESH,
        )

    def y_own(direction):
        target = up if direction == 0 else down
        return pltpu.make_async_remote_copy(
            src_ref=half_ref,
            dst_ref=out_ref.at[dev],
            send_sem=y_send.at[direction * n_dy * n_dz + dev],
            recv_sem=y_recv.at[dev],
            device_id=(section, grp, target, dz),
            device_id_type=pl.DeviceIdType.MESH,
        )

    for direction in (0, 1):
        y_own(direction).start()
    for step in range(1, n_dz):
        source = (dz + n_dz - step) % n_dz
        z_copy(source, source).wait_recv()
        for direction in (0, 1):
            y_copy(direction, dy, source).start()
        pair_copy(dy * n_dz + source, out_ref.at[dy * n_dz + source]).start()
    own.wait()
    for step in range(1, n_dz):
        z_copy((dz + step) % n_dz, dz).wait_send()

    @pl.when(has_left)
    def _():
        to_right_of_left = pltpu.make_async_remote_copy(
            src_ref=frames_ref.at[pl.ds(0, RAD)],
            dst_ref=halo_left,
            send_sem=halo_send.at[1],
            recv_sem=halo_recv.at[0],
            device_id=dev_peer(dev - 1),
            device_id_type=pl.DeviceIdType.MESH,
        )
        to_right_of_left.wait_recv()
        to_left().wait_send()

    @pl.when(has_right)
    def _():
        to_left_of_right = pltpu.make_async_remote_copy(
            src_ref=frames_ref.at[pl.ds(0, RAD)],
            dst_ref=halo_right,
            send_sem=halo_send.at[0],
            recv_sem=halo_recv.at[1],
            device_id=dev_peer(dev + 1),
            device_id_type=pl.DeviceIdType.MESH,
        )
        to_left_of_right.wait_recv()
        to_right().wait_send()

    weights = retention_weights()

    row_block = 32

    def smooth_rows(block, carry):
        rows = pl.ds(pl.multiple_of(block * row_block, row_block), row_block)

        def padded_frame(place):
            if place < RAD:
                return halo_left[place, rows, :]
            if place < RAD + count_frames:
                return frames_ref[place - RAD, rows, :]
            return halo_right[place - RAD - count_frames, rows, :]

        for frame in range(count_frames):
            total = weights[0] * padded_frame(frame).astype(jnp.float32)
            for offset in range(1, 2 * RAD + 1):
                total = total + weights[offset] * padded_frame(frame + offset).astype(jnp.float32)
            own_scans[frame, rows, :] = total.astype(own_scans.dtype)
        return carry

    lax.fori_loop(0, own_scans.shape[1] // row_block, smooth_rows, 0)

    swap = pltpu.make_async_remote_copy(
        src_ref=own_scans,
        dst_ref=partner_scans,
        send_sem=swap_send,
        recv_sem=swap_recv,
        device_id=(partner_section, grp, dy, dz),
        device_id_type=pl.DeviceIdType.MESH,
    )
    swap.start()
    relay = n_dz // 2
    for chunk in range(n_dz):
        y_copy(0, down, chunk).wait_recv()
        if chunk < relay:
            y_copy(0, down, chunk).start()
        pair_copy(down * n_dz + chunk, out_ref.at[down * n_dz + chunk]).start()
        y_copy(1, up, chunk).wait_recv()
        if chunk >= relay:
            y_copy(1, up, chunk).start()
        pair_copy(up * n_dz + chunk, out_ref.at[up * n_dz + chunk]).start()
    swap.wait()

    half = own_scans.shape[1]

    def level_frame(frame, carry):
        for level in range(SCALES):
            table = kernels_ref[level]
            acc = jnp.dot(table[:, :half], own_scans[frame], preferred_element_type=jnp.float32)
            acc = acc + jnp.dot(
                table[:, half:], partner_scans[frame], preferred_element_type=jnp.float32
            )
            wave_ref[level, frame] = acc.astype(wave_ref.dtype)
        return carry

    lax.fori_loop(0, count_frames, level_frame, 0)

    opposite = (dy + 2) % n_dy
    for chunk in range(n_dz):
        y_copy(0, opposite, chunk).wait_recv()
        pair_copy(opposite * n_dz + chunk, out_ref.at[opposite * n_dz + chunk]).start()
    for direction in (0, 1):
        for chunk in range(n_dz):
            y_copy(direction, dy, chunk).wait_send()
    for chunk in range(relay):
        y_copy(0, down, chunk).wait_send()
    for chunk in range(relay, n_dz):
        y_copy(1, up, chunk).wait_send()
    for slot in range(n_dev):
        pair_copy(slot, half_ref).wait_recv()
    for slot in range(n_dev):
        pair_copy(slot, half_ref).wait_send()


def frame_work(frames, kernels, half):
    sizes = (lax.axis_size("section"), lax.axis_size("dy"), lax.axis_size("dz"))
    n_section, n_dy, n_dz = sizes
    rows, channels = half.shape
    count_frames, mob_local, _ = frames.shape
    rows_out, other_out, wave = pl.pallas_call(
        functools.partial(frame_kernel, sizes),
        out_shape=(
            jax.ShapeDtypeStruct((n_dy * n_dz, rows, channels), half.dtype),
            jax.ShapeDtypeStruct((n_dy * n_dz, rows, channels), half.dtype),
            jax.ShapeDtypeStruct((SCALES, count_frames, mob_local, channels), jnp.bfloat16),
        ),
        in_specs=[pl.BlockSpec(memory_space=pltpu.VMEM)] * 3,
        out_specs=(pl.BlockSpec(memory_space=pltpu.VMEM),) * 3,
        scratch_shapes=[
            pltpu.VMEM((RAD, mob_local, channels), frames.dtype),
            pltpu.VMEM((RAD, mob_local, channels), frames.dtype),
            pltpu.VMEM((count_frames, mob_local, channels), jnp.bfloat16),
            pltpu.VMEM((count_frames, mob_local, channels), jnp.bfloat16),
            pltpu.SemaphoreType.DMA(()),
            pltpu.SemaphoreType.DMA((n_dz,)),
            pltpu.SemaphoreType.DMA((n_dz,)),
            pltpu.SemaphoreType.DMA((2 * n_dy * n_dz,)),
            pltpu.SemaphoreType.DMA((n_dy * n_dz,)),
            pltpu.SemaphoreType.DMA((2,)),
            pltpu.SemaphoreType.DMA((2,)),
            pltpu.SemaphoreType.DMA(()),
            pltpu.SemaphoreType.DMA(()),
            pltpu.SemaphoreType.DMA((n_dy * n_dz,)),
            pltpu.SemaphoreType.DMA((n_dy * n_dz,)),
        ],
        compiler_params=pltpu.CompilerParams(
            collective_id=1, has_side_effects=True, vmem_limit_bytes=56 * 1024 * 1024
        ),
    )(frames, kernels, half)
    return (
        rows_out.reshape(n_dy * n_dz * rows, channels),
        other_out.reshape(n_dy * n_dz * rows, channels),
        wave,
    )


def score_kernel(
    order_ref, tile_ref, block_ref, count_ref, section_ref, wave_ref, mine_ref, other_ref, out_ref
):
    slot = order_ref[pl.program_id(0)]
    live = slot < count_ref[0]
    mine = block_ref[slot] % 2 == section_ref[0]

    def score(rows_ref):
        rows = rows_ref[...]
        acc = jnp.zeros((1, PB), jnp.float32)
        for level in range(SCALES):
            cells = wave_ref[level].reshape(-1, rows.shape[1])
            scores = lax.dot_general(
                cells, rows, (((1,), (1,)), ((), ())), preferred_element_type=jnp.float32
            )
            acc = acc + jnp.sum(jnp.maximum(scores, 0.0), axis=0, keepdims=True)
        cell_count = SCALES * wave_ref.shape[1] * wave_ref.shape[2]
        out_ref[0] = acc / cell_count

    @pl.when(jnp.logical_and(live, mine))
    def _():
        score(mine_ref)

    @pl.when(jnp.logical_and(live, jnp.logical_not(mine)))
    def _():
        score(other_ref)

    @pl.when(jnp.logical_not(live))
    def _():
        out_ref[0] = jnp.zeros((1, PB), jnp.float32)


def score_pairs(wavelet_stack, my_rows, other_rows, tile_ids, block_ids, live_pairs, section_index):
    slots = tile_ids.shape[0]
    scales, frames_local, mob_local, channels = wavelet_stack.shape
    slot_ids = jnp.arange(slots, dtype=jnp.int32)
    keys = jnp.where(slot_ids < live_pairs, tile_ids * slots + slot_ids, (mob_local // TM + 1) * slots + slot_ids)
    order = jnp.argsort(keys).astype(jnp.int32)

    def visited(k, o, c):
        return o[jnp.minimum(k, c[0] - 1)]

    grid_spec = pltpu.PrefetchScalarGridSpec(
        num_scalar_prefetch=5,
        grid=(slots,),
        in_specs=[
            pl.BlockSpec(
                (scales, frames_local, TM, channels),
                lambda k, o, t, b, c, s: (0, 0, t[visited(k, o, c)], 0),
            ),
            pl.BlockSpec((PB, channels), lambda k, o, t, b, c, s: (b[visited(k, o, c)] // 2, 0)),
            pl.BlockSpec((PB, channels), lambda k, o, t, b, c, s: (b[visited(k, o, c)] // 2, 0)),
        ],
        out_specs=pl.BlockSpec((1, 1, PB), lambda k, o, t, b, c, s: (o[k], 0, 0)),
    )
    out = pl.pallas_call(
        score_kernel,
        grid_spec=grid_spec,
        out_shape=jax.ShapeDtypeStruct((slots, 1, PB), jnp.float32),
    )(
        order,
        tile_ids,
        block_ids,
        live_pairs.reshape(1),
        section_index.astype(jnp.int32).reshape(1),
        wavelet_stack,
        my_rows,
        other_rows,
    )
    return out.reshape(slots, PB)


def solution(mesh):
    section_count, grp_count, dev_count = mesh.devices.shape
    dz_count = 8 if dev_count % 8 == 0 else dev_count
    split_mesh = jax.sharding.Mesh(
        mesh.devices.reshape(section_count, grp_count, dev_count // dz_count, dz_count),
        ("section", "grp", "dy", "dz"),
    )
    placed = (
        P("grp", DEV, "section", None),
        P(DEV, None),
        P("section", "grp", DEV),
        P("section", "grp", DEV),
        P("section", "grp", DEV),
        P(),
    )
    return jax.shard_map(
        on_device, mesh=split_mesh, in_specs=placed, out_specs=P("grp", DEV), check_vma=False
    )
```

```python
import functools
import math

import jax
import jax.numpy as jnp
from jax import lax
from jax.experimental import pallas as pl
from jax.experimental.pallas import tpu as pltpu
from jax.sharding import PartitionSpec as P

MOB = 512
SCALES = 6
RAD = 4
TM = 64
PB = 128
PREC = 8192
DEV = ("dy", "dz")


retention_spread = 2.0


def extended(cells, sides, width):
    for axis, dim in sides:
        count = lax.axis_size(axis)
        ends = count - 1
        head = lax.slice_in_dim(cells, 0, width, axis=dim)
        tail = lax.slice_in_dim(cells, cells.shape[dim] - width, cells.shape[dim], axis=dim)
        cells = jnp.concatenate(
            [
                lax.ppermute(tail, axis, [(i, (i + 1) % count) for i in range(ends)]),
                cells,
                lax.ppermute(head, axis, [((i + 1) % count, i) for i in range(ends)]),
            ],
            axis=dim,
        )
    return cells


def retention_weights():
    bell_values = [
        math.exp(-0.5 * (offset / retention_spread) ** 2) for offset in range(-RAD, RAD + 1)
    ]
    bell_total = sum(bell_values)
    return [weight_value / bell_total for weight_value in bell_values]


def mobility_kernels(row_start, row_count, col_start):
    row_place = (row_start + jnp.arange(row_count, dtype=jnp.int32)).astype(jnp.float32)
    col_place = ((col_start + jnp.arange(MOB, dtype=jnp.int32)) % MOB).astype(jnp.float32)
    distance = row_place[:, None] - col_place[None, :]
    tables = []
    for level in range(SCALES):
        spread_scans = 2.0**level
        scaled = distance / spread_scans
        tables.append(
            (1.0 - scaled * scaled)
            * jnp.exp(-0.5 * scaled * scaled)
            / math.sqrt(0.75 * math.sqrt(math.pi) * spread_scans)
        )
    return jnp.stack(tables).astype(jnp.bfloat16)


def on_device(frames, templates, pair_block, pair_tile, pair_count, owner_order):
    section_index = lax.axis_index("section")
    mob_local = frames.shape[2]
    section_count = lax.axis_size("section")
    kernels = mobility_kernels(section_index * mob_local, mob_local, section_index * mob_local)
    half_rows = templates.shape[0] // 2
    my_half = lax.dynamic_slice_in_dim(templates, section_index * half_rows, half_rows, 0)
    my_rows, other_rows, wavelet_stack = frame_work(frames[0], kernels, my_half)
    slots = pair_block.shape[2]
    live_pairs = pair_count[0, 0, 0]
    block_ids = pair_block[0, 0]
    tile_ids = pair_tile[0, 0]
    responses = score_pairs(
        wavelet_stack, my_rows, other_rows, tile_ids, block_ids, live_pairs, section_index
    )
    positions = jnp.take(owner_order.reshape(-1, PB), block_ids, axis=0).reshape(-1)
    groups = PREC // PB
    by_group = jnp.where(
        (positions // PB)[:, None] == jnp.arange(groups, dtype=jnp.int32)[None, :],
        responses.reshape(-1)[:, None],
        0.0,
    )
    by_lane = ((positions % PB)[:, None] == jnp.arange(PB, dtype=jnp.int32)[None, :]).astype(
        jnp.float32
    )
    placed = jnp.einsum(
        "ka,kb->ab",
        by_group,
        by_lane,
        precision=lax.Precision.HIGHEST,
        preferred_element_type=jnp.float32,
    ).reshape(-1)
    dev_count = lax.axis_size(DEV)
    return reduce_owned(placed.reshape(dev_count, 1, PREC // dev_count))


def reduce_kernel(
    sizes,
    payload_ref,
    out_ref,
    mixed,
    line,
    line_in,
    column,
    column_in,
    totals,
    pair_send,
    pair_recv,
    z_send,
    z_recv,
    y_send,
    y_recv,
    total_send,
    total_recv,
):
    n_section, n_grp, n_dy, n_dz = sizes
    section = lax.axis_index("section")
    grp = lax.axis_index("grp")
    dy = lax.axis_index("dy")
    dz = lax.axis_index("dz")
    partner = (section + 1) % n_section
    owned_width = out_ref.shape[1]

    barrier = pltpu.get_barrier_semaphore()
    peers = [(partner, grp, dy, dz)]
    peers += [(section, grp, dy, (dz + step) % n_dz) for step in range(1, n_dz)]
    peers += [(section, grp, (dy + step) % n_dy, dz) for step in range(1, n_dy)]
    peers += [(section, (grp + step) % n_grp, dy, dz) for step in range(1, n_grp)]
    for peer in peers:
        pl.semaphore_signal(barrier, inc=1, device_id=peer, device_id_type=pl.DeviceIdType.MESH)
    pl.semaphore_wait(barrier, len(peers))

    swap = pltpu.make_async_remote_copy(
        src_ref=payload_ref,
        dst_ref=mixed,
        send_sem=pair_send,
        recv_sem=pair_recv,
        device_id=(partner, grp, dy, dz),
        device_id_type=pl.DeviceIdType.MESH,
    )
    swap.start()
    swap.wait()
    combined = payload_ref[...] + mixed[...]
    line[:, :, :, :owned_width] = combined
    chip_total = jnp.sum(jnp.sum(jnp.sum(combined, axis=0), axis=0), axis=1, keepdims=True)
    line[:, :, :, owned_width:] = jnp.broadcast_to(
        chip_total[None, None], line.shape[:3] + (line.shape[3] - owned_width,)
    )
    line_in[dz] = line[dz]

    def z_copy(target, source):
        return pltpu.make_async_remote_copy(
            src_ref=line.at[target],
            dst_ref=line_in.at[source],
            send_sem=z_send.at[target],
            recv_sem=z_recv.at[source],
            device_id=(section, grp, dy, target),
            device_id_type=pl.DeviceIdType.MESH,
        )

    for step in range(1, n_dz):
        z_copy((dz + step) % n_dz, dz).start()
    for step in range(1, n_dz):
        source = (dz + n_dz - step) % n_dz
        z_copy(source, source).wait_recv()
    partial = line_in[0]
    for index in range(1, n_dz):
        partial = partial + line_in[index]
    column[...] = partial
    column_in[dy] = column[dy]

    def y_copy(target, source):
        return pltpu.make_async_remote_copy(
            src_ref=column.at[target],
            dst_ref=column_in.at[source],
            send_sem=y_send.at[target],
            recv_sem=y_recv.at[source],
            device_id=(section, grp, target, dz),
            device_id_type=pl.DeviceIdType.MESH,
        )

    for step in range(1, n_dy):
        y_copy((dy + step) % n_dy, dy).start()
    for step in range(1, n_dy):
        source = (dy + n_dy - step) % n_dy
        y_copy(source, source).wait_recv()
    summed = column_in[0]
    for index in range(1, n_dy):
        summed = summed + column_in[index]
    summed = summed.reshape(summed.shape[-2:])
    totals[grp] = summed[:, owned_width:]

    def total_copy(step):
        target = (grp + step) % n_grp
        return pltpu.make_async_remote_copy(
            src_ref=totals.at[grp],
            dst_ref=totals.at[grp],
            send_sem=total_send.at[target],
            recv_sem=total_recv.at[grp],
            device_id=(section, target, dy, dz),
            device_id_type=pl.DeviceIdType.MESH,
        )

    for step in range(1, n_grp):
        total_copy(step).start()
    for step in range(1, n_grp):
        source = (grp + step) % n_grp
        pltpu.make_async_remote_copy(
            src_ref=totals.at[source],
            dst_ref=totals.at[source],
            send_sem=total_send.at[source],
            recv_sem=total_recv.at[source],
            device_id=(section, source, dy, dz),
            device_id_type=pl.DeviceIdType.MESH,
        ).wait_recv()
        total_copy(step).wait_send()
    for step in range(1, n_dz):
        z_copy((dz + step) % n_dz, dz).wait_send()
    for step in range(1, n_dy):
        y_copy((dy + step) % n_dy, dy).wait_send()
    run_sum = totals[0]
    for index in range(1, n_grp):
        run_sum = run_sum + totals[index]
    own_total = summed[:, owned_width : owned_width + 1]
    factor = (run_sum[:, 0:1] / n_grp) / own_total
    out_ref[...] = summed[:, :owned_width] * factor


def reduce_owned(payload):
    sizes = (lax.axis_size("section"), lax.axis_size("grp"), lax.axis_size("dy"), lax.axis_size("dz"))
    n_section, n_grp, n_dy, n_dz = sizes
    rows, one, owned_width = payload.shape
    width = owned_width + 128
    lines = payload.reshape(n_dy, n_dz, one, owned_width).transpose(1, 0, 2, 3)
    return pl.pallas_call(
        functools.partial(reduce_kernel, sizes),
        out_shape=jax.ShapeDtypeStruct((1, owned_width), jnp.float32),
        in_specs=[pl.BlockSpec(memory_space=pltpu.VMEM)],
        out_specs=pl.BlockSpec(memory_space=pltpu.VMEM),
        scratch_shapes=[
            pltpu.VMEM((n_dz, n_dy, one, owned_width), jnp.float32),
            pltpu.VMEM((n_dz, n_dy, one, width), jnp.float32),
            pltpu.VMEM((n_dz, n_dy, one, width), jnp.float32),
            pltpu.VMEM((n_dy, one, width), jnp.float32),
            pltpu.VMEM((n_dy, one, width), jnp.float32),
            pltpu.VMEM((n_grp, 1, 128), jnp.float32),
            pltpu.SemaphoreType.DMA(()),
            pltpu.SemaphoreType.DMA(()),
            pltpu.SemaphoreType.DMA((n_dz,)),
            pltpu.SemaphoreType.DMA((n_dz,)),
            pltpu.SemaphoreType.DMA((n_dy,)),
            pltpu.SemaphoreType.DMA((n_dy,)),
            pltpu.SemaphoreType.DMA((n_grp,)),
            pltpu.SemaphoreType.DMA((n_grp,)),
        ],
        compiler_params=pltpu.CompilerParams(collective_id=0, has_side_effects=True),
    )(lines)


def frame_kernel(
    sizes,
    frames_ref,
    kernels_ref,
    half_ref,
    out_ref,
    other_ref,
    wave_ref,
    halo_left,
    halo_right,
    own_scans,
    partner_scans,
    own_sem,
    z_send,
    z_recv,
    y_send,
    y_recv,
    halo_send,
    halo_recv,
    swap_send,
    swap_recv,
    pair_send,
    pair_recv,
):
    n_section, n_dy, n_dz = sizes
    n_dev = n_dy * n_dz
    section = lax.axis_index("section")
    grp = lax.axis_index("grp")
    dy = lax.axis_index("dy")
    dz = lax.axis_index("dz")
    dev = dy * n_dz + dz
    partner_section = (section + 1) % n_section

    def dev_peer(index):
        return (section, grp, index // n_dz, index % n_dz)

    barrier = pltpu.get_barrier_semaphore()
    for step in range(1, n_dz):
        pl.semaphore_signal(
            barrier,
            inc=1,
            device_id=(section, grp, dy, (dz + step) % n_dz),
            device_id_type=pl.DeviceIdType.MESH,
        )
    up = (dy + 1) % n_dy
    down = (dy + n_dy - 1) % n_dy
    for row in (up, down):
        pl.semaphore_signal(
            barrier,
            inc=1,
            device_id=(section, grp, row, dz),
            device_id_type=pl.DeviceIdType.MESH,
        )
    pl.semaphore_signal(
        barrier,
        inc=1,
        device_id=(partner_section, grp, dy, dz),
        device_id_type=pl.DeviceIdType.MESH,
    )
    has_left = dev > 0
    has_right = dev < n_dev - 1
    far_left = jnp.logical_and(has_left, dz == 0)
    far_right = jnp.logical_and(has_right, dz == n_dz - 1)

    @pl.when(far_left)
    def _():
        pl.semaphore_signal(
            barrier, inc=1, device_id=dev_peer(dev - 1), device_id_type=pl.DeviceIdType.MESH
        )

    @pl.when(far_right)
    def _():
        pl.semaphore_signal(
            barrier, inc=1, device_id=dev_peer(dev + 1), device_id_type=pl.DeviceIdType.MESH
        )

    extra = far_left.astype(jnp.int32) + far_right.astype(jnp.int32)
    pl.semaphore_wait(barrier, n_dz - 1 + 2 + 1 + extra)

    own = pltpu.make_async_copy(half_ref, out_ref.at[dev], own_sem)
    own.start()

    def pair_copy(slot, source_ref):
        return pltpu.make_async_remote_copy(
            src_ref=source_ref,
            dst_ref=other_ref.at[slot],
            send_sem=pair_send.at[slot],
            recv_sem=pair_recv.at[slot],
            device_id=(partner_section, grp, dy, dz),
            device_id_type=pl.DeviceIdType.MESH,
        )

    pair_copy(dev, half_ref).start()

    def z_copy(target, source):
        return pltpu.make_async_remote_copy(
            src_ref=half_ref,
            dst_ref=out_ref.at[dy * n_dz + source],
            send_sem=z_send.at[target],
            recv_sem=z_recv.at[source],
            device_id=(section, grp, dy, target),
            device_id_type=pl.DeviceIdType.MESH,
        )

    for step in range(1, n_dz):
        z_copy((dz + step) % n_dz, dz).start()

    count_frames = frames_ref.shape[0]

    def to_left():
        return pltpu.make_async_remote_copy(
            src_ref=frames_ref.at[pl.ds(0, RAD)],
            dst_ref=halo_right,
            send_sem=halo_send.at[0],
            recv_sem=halo_recv.at[1],
            device_id=dev_peer(dev - 1),
            device_id_type=pl.DeviceIdType.MESH,
        )

    def to_right():
        return pltpu.make_async_remote_copy(
            src_ref=frames_ref.at[pl.ds(count_frames - RAD, RAD)],
            dst_ref=halo_left,
            send_sem=halo_send.at[1],
            recv_sem=halo_recv.at[0],
            device_id=dev_peer(dev + 1),
            device_id_type=pl.DeviceIdType.MESH,
        )

    @pl.when(has_left)
    def _():
        to_left().start()

    @pl.when(has_right)
    def _():
        to_right().start()

    @pl.when(jnp.logical_not(has_left))
    def _():
        halo_left[...] = jnp.zeros(halo_left.shape, halo_left.dtype)

    @pl.when(jnp.logical_not(has_right))
    def _():
        halo_right[...] = jnp.zeros(halo_right.shape, halo_right.dtype)

    def y_copy(direction, row, chunk):
        slot = row * n_dz + chunk
        target = up if direction == 0 else down
        return pltpu.make_async_remote_copy(
            src_ref=out_ref.at[slot],
            dst_ref=out_ref.at[slot],
            send_sem=y_send.at[direction * n_dy * n_dz + slot],
            recv_sem=y_recv.at[slot],
            device_id=(section, grp, target, dz),
            device_id_type=pl.DeviceIdType.MESH,
        )

    def y_own(direction):
        target = up if direction == 0 else down
        return pltpu.make_async_remote_copy(
            src_ref=half_ref,
            dst_ref=out_ref.at[dev],
            send_sem=y_send.at[direction * n_dy * n_dz + dev],
            recv_sem=y_recv.at[dev],
            device_id=(section, grp, target, dz),
            device_id_type=pl.DeviceIdType.MESH,
        )

    for direction in (0, 1):
        y_own(direction).start()
    for step in range(1, n_dz):
        source = (dz + n_dz - step) % n_dz
        z_copy(source, source).wait_recv()
        for direction in (0, 1):
            y_copy(direction, dy, source).start()
        pair_copy(dy * n_dz + source, out_ref.at[dy * n_dz + source]).start()
    own.wait()
    for step in range(1, n_dz):
        z_copy((dz + step) % n_dz, dz).wait_send()

    @pl.when(has_left)
    def _():
        to_right_of_left = pltpu.make_async_remote_copy(
            src_ref=frames_ref.at[pl.ds(0, RAD)],
            dst_ref=halo_left,
            send_sem=halo_send.at[1],
            recv_sem=halo_recv.at[0],
            device_id=dev_peer(dev - 1),
            device_id_type=pl.DeviceIdType.MESH,
        )
        to_right_of_left.wait_recv()
        to_left().wait_send()

    @pl.when(has_right)
    def _():
        to_left_of_right = pltpu.make_async_remote_copy(
            src_ref=frames_ref.at[pl.ds(0, RAD)],
            dst_ref=halo_right,
            send_sem=halo_send.at[0],
            recv_sem=halo_recv.at[1],
            device_id=dev_peer(dev + 1),
            device_id_type=pl.DeviceIdType.MESH,
        )
        to_left_of_right.wait_recv()
        to_right().wait_send()

    weights = retention_weights()

    row_block = 32

    def smooth_rows(block, carry):
        rows = pl.ds(pl.multiple_of(block * row_block, row_block), row_block)

        def padded_frame(place):
            if place < RAD:
                return halo_left[place, rows, :]
            if place < RAD + count_frames:
                return frames_ref[place - RAD, rows, :]
            return halo_right[place - RAD - count_frames, rows, :]

        for frame in range(count_frames):
            total = weights[0] * padded_frame(frame).astype(jnp.float32)
            for offset in range(1, 2 * RAD + 1):
                total = total + weights[offset] * padded_frame(frame + offset).astype(jnp.float32)
            own_scans[frame, rows, :] = total.astype(own_scans.dtype)
        return carry

    lax.fori_loop(0, own_scans.shape[1] // row_block, smooth_rows, 0)

    swap = pltpu.make_async_remote_copy(
        src_ref=own_scans,
        dst_ref=partner_scans,
        send_sem=swap_send,
        recv_sem=swap_recv,
        device_id=(partner_section, grp, dy, dz),
        device_id_type=pl.DeviceIdType.MESH,
    )
    swap.start()
    relay = n_dz // 2
    for chunk in range(n_dz):
        y_copy(0, down, chunk).wait_recv()
        if chunk < relay:
            y_copy(0, down, chunk).start()
        pair_copy(down * n_dz + chunk, out_ref.at[down * n_dz + chunk]).start()
        y_copy(1, up, chunk).wait_recv()
        if chunk >= relay:
            y_copy(1, up, chunk).start()
        pair_copy(up * n_dz + chunk, out_ref.at[up * n_dz + chunk]).start()
    swap.wait()

    half = own_scans.shape[1]

    def level_frame(frame, carry):
        for level in range(SCALES):
            table = kernels_ref[level]
            acc = jnp.dot(table[:, :half], own_scans[frame], preferred_element_type=jnp.float32)
            acc = acc + jnp.dot(
                table[:, half:], partner_scans[frame], preferred_element_type=jnp.float32
            )
            wave_ref[level, frame] = acc.astype(wave_ref.dtype)
        return carry

    lax.fori_loop(0, count_frames, level_frame, 0)

    opposite = (dy + 2) % n_dy
    for chunk in range(n_dz):
        y_copy(0, opposite, chunk).wait_recv()
        pair_copy(opposite * n_dz + chunk, out_ref.at[opposite * n_dz + chunk]).start()
    for direction in (0, 1):
        for chunk in range(n_dz):
            y_copy(direction, dy, chunk).wait_send()
    for chunk in range(relay):
        y_copy(0, down, chunk).wait_send()
    for chunk in range(relay, n_dz):
        y_copy(1, up, chunk).wait_send()
    for slot in range(n_dev):
        pair_copy(slot, half_ref).wait_recv()
    for slot in range(n_dev):
        pair_copy(slot, half_ref).wait_send()


def frame_work(frames, kernels, half):
    sizes = (lax.axis_size("section"), lax.axis_size("dy"), lax.axis_size("dz"))
    n_section, n_dy, n_dz = sizes
    rows, channels = half.shape
    count_frames, mob_local, _ = frames.shape
    rows_out, other_out, wave = pl.pallas_call(
        functools.partial(frame_kernel, sizes),
        out_shape=(
            jax.ShapeDtypeStruct((n_dy * n_dz, rows, channels), half.dtype),
            jax.ShapeDtypeStruct((n_dy * n_dz, rows, channels), half.dtype),
            jax.ShapeDtypeStruct((SCALES, count_frames, mob_local, channels), jnp.bfloat16),
        ),
        in_specs=[pl.BlockSpec(memory_space=pltpu.VMEM)] * 3,
        out_specs=(pl.BlockSpec(memory_space=pltpu.VMEM),) * 3,
        scratch_shapes=[
            pltpu.VMEM((RAD, mob_local, channels), frames.dtype),
            pltpu.VMEM((RAD, mob_local, channels), frames.dtype),
            pltpu.VMEM((count_frames, mob_local, channels), jnp.bfloat16),
            pltpu.VMEM((count_frames, mob_local, channels), jnp.bfloat16),
            pltpu.SemaphoreType.DMA(()),
            pltpu.SemaphoreType.DMA((n_dz,)),
            pltpu.SemaphoreType.DMA((n_dz,)),
            pltpu.SemaphoreType.DMA((2 * n_dy * n_dz,)),
            pltpu.SemaphoreType.DMA((n_dy * n_dz,)),
            pltpu.SemaphoreType.DMA((2,)),
            pltpu.SemaphoreType.DMA((2,)),
            pltpu.SemaphoreType.DMA(()),
            pltpu.SemaphoreType.DMA(()),
            pltpu.SemaphoreType.DMA((n_dy * n_dz,)),
            pltpu.SemaphoreType.DMA((n_dy * n_dz,)),
        ],
        compiler_params=pltpu.CompilerParams(
            collective_id=1, has_side_effects=True, vmem_limit_bytes=56 * 1024 * 1024
        ),
    )(frames, kernels, half)
    return (
        rows_out.reshape(n_dy * n_dz * rows, channels),
        other_out.reshape(n_dy * n_dz * rows, channels),
        wave,
    )


def score_kernel(
    order_ref, tile_ref, block_ref, count_ref, section_ref, wave_ref, mine_ref, other_ref, out_ref
):
    slot = order_ref[pl.program_id(0)]
    live = slot < count_ref[0]
    mine = block_ref[slot] % 2 == section_ref[0]

    def score(rows_ref):
        rows = rows_ref[...]
        acc = jnp.zeros((1, PB), jnp.float32)
        for level in range(SCALES):
            cells = wave_ref[level].reshape(-1, rows.shape[1])
            scores = lax.dot_general(
                cells, rows, (((1,), (1,)), ((), ())), preferred_element_type=jnp.float32
            )
            acc = acc + jnp.sum(jnp.maximum(scores, 0.0), axis=0, keepdims=True)
        cell_count = SCALES * wave_ref.shape[1] * wave_ref.shape[2]
        out_ref[0] = acc / cell_count

    @pl.when(jnp.logical_and(live, mine))
    def _():
        score(mine_ref)

    @pl.when(jnp.logical_and(live, jnp.logical_not(mine)))
    def _():
        score(other_ref)

    @pl.when(jnp.logical_not(live))
    def _():
        out_ref[0] = jnp.zeros((1, PB), jnp.float32)


def score_pairs(wavelet_stack, my_rows, other_rows, tile_ids, block_ids, live_pairs, section_index):
    slots = tile_ids.shape[0]
    scales, frames_local, mob_local, channels = wavelet_stack.shape
    slot_ids = jnp.arange(slots, dtype=jnp.int32)
    keys = jnp.where(slot_ids < live_pairs, tile_ids * slots + slot_ids, (mob_local // TM + 1) * slots + slot_ids)
    order = jnp.argsort(keys).astype(jnp.int32)

    def visited(k, o, c):
        return o[jnp.minimum(k, c[0] - 1)]

    grid_spec = pltpu.PrefetchScalarGridSpec(
        num_scalar_prefetch=5,
        grid=(slots,),
        in_specs=[
            pl.BlockSpec(
                (scales, frames_local, TM, channels),
                lambda k, o, t, b, c, s: (0, 0, t[visited(k, o, c)], 0),
            ),
            pl.BlockSpec((PB, channels), lambda k, o, t, b, c, s: (b[visited(k, o, c)] // 2, 0)),
            pl.BlockSpec((PB, channels), lambda k, o, t, b, c, s: (b[visited(k, o, c)] // 2, 0)),
        ],
        out_specs=pl.BlockSpec((1, 1, PB), lambda k, o, t, b, c, s: (o[k], 0, 0)),
    )
    out = pl.pallas_call(
        score_kernel,
        grid_spec=grid_spec,
        out_shape=jax.ShapeDtypeStruct((slots, 1, PB), jnp.float32),
    )(
        order,
        tile_ids,
        block_ids,
        live_pairs.reshape(1),
        section_index.astype(jnp.int32).reshape(1),
        wavelet_stack,
        my_rows,
        other_rows,
    )
    return out.reshape(slots, PB)


def solution(mesh):
    section_count, grp_count, dev_count = mesh.devices.shape
    dz_count = 8 if dev_count % 8 == 0 else dev_count
    split_mesh = jax.sharding.Mesh(
        mesh.devices.reshape(section_count, grp_count, dev_count // dz_count, dz_count),
        ("section", "grp", "dy", "dz"),
    )
    placed = (
        P("grp", DEV, "section", None),
        P(DEV, None),
        P("section", "grp", DEV),
        P("section", "grp", DEV),
        P("section", "grp", DEV),
        P(),
    )
    return jax.shard_map(
        on_device, mesh=split_mesh, in_specs=placed, out_specs=P("grp", DEV), check_vma=False
    )
```

```python
import functools
import math

import jax
import jax.numpy as jnp
from jax import lax
from jax.experimental import pallas as pl
from jax.experimental.pallas import tpu as pltpu
from jax.sharding import PartitionSpec as P

MOB = 512
SCALES = 6
RAD = 4
TM = 64
PB = 128
PREC = 8192
DEV = ("dy", "dz")


retention_spread = 2.0


def extended(cells, sides, width):
    for axis, dim in sides:
        count = lax.axis_size(axis)
        ends = count - 1
        head = lax.slice_in_dim(cells, 0, width, axis=dim)
        tail = lax.slice_in_dim(cells, cells.shape[dim] - width, cells.shape[dim], axis=dim)
        cells = jnp.concatenate(
            [
                lax.ppermute(tail, axis, [(i, (i + 1) % count) for i in range(ends)]),
                cells,
                lax.ppermute(head, axis, [((i + 1) % count, i) for i in range(ends)]),
            ],
            axis=dim,
        )
    return cells


def retention_weights():
    bell_values = [
        math.exp(-0.5 * (offset / retention_spread) ** 2) for offset in range(-RAD, RAD + 1)
    ]
    bell_total = sum(bell_values)
    return [weight_value / bell_total for weight_value in bell_values]


def mobility_kernels(row_start, row_count, col_start):
    row_place = (row_start + jnp.arange(row_count, dtype=jnp.int32)).astype(jnp.float32)
    col_place = ((col_start + jnp.arange(MOB, dtype=jnp.int32)) % MOB).astype(jnp.float32)
    distance = row_place[:, None] - col_place[None, :]
    tables = []
    for level in range(SCALES):
        spread_scans = 2.0**level
        scaled = distance / spread_scans
        tables.append(
            (1.0 - scaled * scaled)
            * jnp.exp(-0.5 * scaled * scaled)
            / math.sqrt(0.75 * math.sqrt(math.pi) * spread_scans)
        )
    return jnp.stack(tables).astype(jnp.bfloat16)


def on_device(frames, templates, pair_block, pair_tile, pair_count, owner_order):
    section_index = lax.axis_index("section")
    mob_local = frames.shape[2]
    section_count = lax.axis_size("section")
    kernels = mobility_kernels(section_index * mob_local, mob_local, section_index * mob_local)
    half_rows = templates.shape[0] // 2
    my_half = lax.dynamic_slice_in_dim(templates, section_index * half_rows, half_rows, 0)
    my_rows, other_rows, wavelet_stack = frame_work(frames[0], kernels, my_half)
    slots = pair_block.shape[2]
    live_pairs = pair_count[0, 0, 0]
    block_ids = pair_block[0, 0]
    tile_ids = pair_tile[0, 0]
    responses = score_pairs(
        wavelet_stack, my_rows, other_rows, tile_ids, block_ids, live_pairs, section_index
    )
    positions = jnp.take(owner_order.reshape(-1, PB), block_ids, axis=0).reshape(-1)
    groups = PREC // PB
    by_group = jnp.where(
        (positions // PB)[:, None] == jnp.arange(groups, dtype=jnp.int32)[None, :],
        responses.reshape(-1)[:, None],
        0.0,
    )
    by_lane = ((positions % PB)[:, None] == jnp.arange(PB, dtype=jnp.int32)[None, :]).astype(
        jnp.float32
    )
    placed = jnp.einsum(
        "ka,kb->ab",
        by_group,
        by_lane,
        precision=lax.Precision.HIGHEST,
        preferred_element_type=jnp.float32,
    ).reshape(-1)
    dev_count = lax.axis_size(DEV)
    return reduce_owned(placed.reshape(dev_count, 1, PREC // dev_count))


def reduce_kernel(
    sizes,
    payload_ref,
    out_ref,
    mixed,
    line,
    line_in,
    column,
    column_in,
    totals,
    pair_send,
    pair_recv,
    z_send,
    z_recv,
    y_send,
    y_recv,
    total_send,
    total_recv,
):
    n_section, n_grp, n_dy, n_dz = sizes
    section = lax.axis_index("section")
    grp = lax.axis_index("grp")
    dy = lax.axis_index("dy")
    dz = lax.axis_index("dz")
    partner = (section + 1) % n_section
    owned_width = out_ref.shape[1]

    barrier = pltpu.get_barrier_semaphore()
    peers = [(partner, grp, dy, dz)]
    peers += [(section, grp, dy, (dz + step) % n_dz) for step in range(1, n_dz)]
    peers += [(section, grp, (dy + step) % n_dy, dz) for step in range(1, n_dy)]
    peers += [(section, (grp + step) % n_grp, dy, dz) for step in range(1, n_grp)]
    for peer in peers:
        pl.semaphore_signal(barrier, inc=1, device_id=peer, device_id_type=pl.DeviceIdType.MESH)
    pl.semaphore_wait(barrier, len(peers))

    swap = pltpu.make_async_remote_copy(
        src_ref=payload_ref,
        dst_ref=mixed,
        send_sem=pair_send,
        recv_sem=pair_recv,
        device_id=(partner, grp, dy, dz),
        device_id_type=pl.DeviceIdType.MESH,
    )
    swap.start()
    swap.wait()
    combined = payload_ref[...] + mixed[...]
    line[:, :, :, :owned_width] = combined
    chip_total = jnp.sum(jnp.sum(jnp.sum(combined, axis=0), axis=0), axis=1, keepdims=True)
    line[:, :, :, owned_width:] = jnp.broadcast_to(
        chip_total[None, None], line.shape[:3] + (line.shape[3] - owned_width,)
    )
    line_in[dz] = line[dz]

    def z_copy(target, source):
        return pltpu.make_async_remote_copy(
            src_ref=line.at[target],
            dst_ref=line_in.at[source],
            send_sem=z_send.at[target],
            recv_sem=z_recv.at[source],
            device_id=(section, grp, dy, target),
            device_id_type=pl.DeviceIdType.MESH,
        )

    for step in range(1, n_dz):
        z_copy((dz + step) % n_dz, dz).start()
    for step in range(1, n_dz):
        source = (dz + n_dz - step) % n_dz
        z_copy(source, source).wait_recv()
    partial = line_in[0]
    for index in range(1, n_dz):
        partial = partial + line_in[index]
    column[...] = partial
    column_in[dy] = column[dy]

    def y_copy(target, source):
        return pltpu.make_async_remote_copy(
            src_ref=column.at[target],
            dst_ref=column_in.at[source],
            send_sem=y_send.at[target],
            recv_sem=y_recv.at[source],
            device_id=(section, grp, target, dz),
            device_id_type=pl.DeviceIdType.MESH,
        )

    for step in range(1, n_dy):
        y_copy((dy + step) % n_dy, dy).start()
    for step in range(1, n_dy):
        source = (dy + n_dy - step) % n_dy
        y_copy(source, source).wait_recv()
    summed = column_in[0]
    for index in range(1, n_dy):
        summed = summed + column_in[index]
    summed = summed.reshape(summed.shape[-2:])
    totals[grp] = summed[:, owned_width:]

    def total_copy(step):
        target = (grp + step) % n_grp
        return pltpu.make_async_remote_copy(
            src_ref=totals.at[grp],
            dst_ref=totals.at[grp],
            send_sem=total_send.at[target],
            recv_sem=total_recv.at[grp],
            device_id=(section, target, dy, dz),
            device_id_type=pl.DeviceIdType.MESH,
        )

    for step in range(1, n_grp):
        total_copy(step).start()
    for step in range(1, n_grp):
        source = (grp + step) % n_grp
        pltpu.make_async_remote_copy(
            src_ref=totals.at[source],
            dst_ref=totals.at[source],
            send_sem=total_send.at[source],
            recv_sem=total_recv.at[source],
            device_id=(section, source, dy, dz),
            device_id_type=pl.DeviceIdType.MESH,
        ).wait_recv()
        total_copy(step).wait_send()
    for step in range(1, n_dz):
        z_copy((dz + step) % n_dz, dz).wait_send()
    for step in range(1, n_dy):
        y_copy((dy + step) % n_dy, dy).wait_send()
    run_sum = totals[0]
    for index in range(1, n_grp):
        run_sum = run_sum + totals[index]
    own_total = summed[:, owned_width : owned_width + 1]
    factor = (run_sum[:, 0:1] / n_grp) / own_total
    out_ref[...] = summed[:, :owned_width] * factor


def reduce_owned(payload):
    sizes = (lax.axis_size("section"), lax.axis_size("grp"), lax.axis_size("dy"), lax.axis_size("dz"))
    n_section, n_grp, n_dy, n_dz = sizes
    rows, one, owned_width = payload.shape
    width = owned_width + 128
    lines = payload.reshape(n_dy, n_dz, one, owned_width).transpose(1, 0, 2, 3)
    return pl.pallas_call(
        functools.partial(reduce_kernel, sizes),
        out_shape=jax.ShapeDtypeStruct((1, owned_width), jnp.float32),
        in_specs=[pl.BlockSpec(memory_space=pltpu.VMEM)],
        out_specs=pl.BlockSpec(memory_space=pltpu.VMEM),
        scratch_shapes=[
            pltpu.VMEM((n_dz, n_dy, one, owned_width), jnp.float32),
            pltpu.VMEM((n_dz, n_dy, one, width), jnp.float32),
            pltpu.VMEM((n_dz, n_dy, one, width), jnp.float32),
            pltpu.VMEM((n_dy, one, width), jnp.float32),
            pltpu.VMEM((n_dy, one, width), jnp.float32),
            pltpu.VMEM((n_grp, 1, 128), jnp.float32),
            pltpu.SemaphoreType.DMA(()),
            pltpu.SemaphoreType.DMA(()),
            pltpu.SemaphoreType.DMA((n_dz,)),
            pltpu.SemaphoreType.DMA((n_dz,)),
            pltpu.SemaphoreType.DMA((n_dy,)),
            pltpu.SemaphoreType.DMA((n_dy,)),
            pltpu.SemaphoreType.DMA((n_grp,)),
            pltpu.SemaphoreType.DMA((n_grp,)),
        ],
        compiler_params=pltpu.CompilerParams(collective_id=0, has_side_effects=True),
    )(lines)


def frame_kernel(
    sizes,
    frames_ref,
    kernels_ref,
    half_ref,
    out_ref,
    other_ref,
    wave_ref,
    halo_left,
    halo_right,
    own_scans,
    partner_scans,
    own_sem,
    z_send,
    z_recv,
    y_send,
    y_recv,
    halo_send,
    halo_recv,
    swap_send,
    swap_recv,
    pair_send,
    pair_recv,
):
    n_section, n_dy, n_dz = sizes
    n_dev = n_dy * n_dz
    section = lax.axis_index("section")
    grp = lax.axis_index("grp")
    dy = lax.axis_index("dy")
    dz = lax.axis_index("dz")
    dev = dy * n_dz + dz
    partner_section = (section + 1) % n_section

    def dev_peer(index):
        return (section, grp, index // n_dz, index % n_dz)

    barrier = pltpu.get_barrier_semaphore()
    for step in range(1, n_dz):
        pl.semaphore_signal(
            barrier,
            inc=1,
            device_id=(section, grp, dy, (dz + step) % n_dz),
            device_id_type=pl.DeviceIdType.MESH,
        )
    up = (dy + 1) % n_dy
    down = (dy + n_dy - 1) % n_dy
    for row in (up, down):
        pl.semaphore_signal(
            barrier,
            inc=1,
            device_id=(section, grp, row, dz),
            device_id_type=pl.DeviceIdType.MESH,
        )
    pl.semaphore_signal(
        barrier,
        inc=1,
        device_id=(partner_section, grp, dy, dz),
        device_id_type=pl.DeviceIdType.MESH,
    )
    has_left = dev > 0
    has_right = dev < n_dev - 1
    far_left = jnp.logical_and(has_left, dz == 0)
    far_right = jnp.logical_and(has_right, dz == n_dz - 1)

    @pl.when(far_left)
    def _():
        pl.semaphore_signal(
            barrier, inc=1, device_id=dev_peer(dev - 1), device_id_type=pl.DeviceIdType.MESH
        )

    @pl.when(far_right)
    def _():
        pl.semaphore_signal(
            barrier, inc=1, device_id=dev_peer(dev + 1), device_id_type=pl.DeviceIdType.MESH
        )

    extra = far_left.astype(jnp.int32) + far_right.astype(jnp.int32)
    pl.semaphore_wait(barrier, n_dz - 1 + 2 + 1 + extra)

    own = pltpu.make_async_copy(half_ref, out_ref.at[dev], own_sem)
    own.start()

    def pair_copy(slot, source_ref):
        return pltpu.make_async_remote_copy(
            src_ref=source_ref,
            dst_ref=other_ref.at[slot],
            send_sem=pair_send.at[slot],
            recv_sem=pair_recv.at[slot],
            device_id=(partner_section, grp, dy, dz),
            device_id_type=pl.DeviceIdType.MESH,
        )

    pair_copy(dev, half_ref).start()

    def z_copy(target, source):
        return pltpu.make_async_remote_copy(
            src_ref=half_ref,
            dst_ref=out_ref.at[dy * n_dz + source],
            send_sem=z_send.at[target],
            recv_sem=z_recv.at[source],
            device_id=(section, grp, dy, target),
            device_id_type=pl.DeviceIdType.MESH,
        )

    for step in range(1, n_dz):
        z_copy((dz + step) % n_dz, dz).start()

    count_frames = frames_ref.shape[0]

    def to_left():
        return pltpu.make_async_remote_copy(
            src_ref=frames_ref.at[pl.ds(0, RAD)],
            dst_ref=halo_right,
            send_sem=halo_send.at[0],
            recv_sem=halo_recv.at[1],
            device_id=dev_peer(dev - 1),
            device_id_type=pl.DeviceIdType.MESH,
        )

    def to_right():
        return pltpu.make_async_remote_copy(
            src_ref=frames_ref.at[pl.ds(count_frames - RAD, RAD)],
            dst_ref=halo_left,
            send_sem=halo_send.at[1],
            recv_sem=halo_recv.at[0],
            device_id=dev_peer(dev + 1),
            device_id_type=pl.DeviceIdType.MESH,
        )

    @pl.when(has_left)
    def _():
        to_left().start()

    @pl.when(has_right)
    def _():
        to_right().start()

    @pl.when(jnp.logical_not(has_left))
    def _():
        halo_left[...] = jnp.zeros(halo_left.shape, halo_left.dtype)

    @pl.when(jnp.logical_not(has_right))
    def _():
        halo_right[...] = jnp.zeros(halo_right.shape, halo_right.dtype)

    def y_copy(direction, row, chunk):
        slot = row * n_dz + chunk
        target = up if direction == 0 else down
        return pltpu.make_async_remote_copy(
            src_ref=out_ref.at[slot],
            dst_ref=out_ref.at[slot],
            send_sem=y_send.at[direction * n_dy * n_dz + slot],
            recv_sem=y_recv.at[slot],
            device_id=(section, grp, target, dz),
            device_id_type=pl.DeviceIdType.MESH,
        )

    def y_own(direction):
        target = up if direction == 0 else down
        return pltpu.make_async_remote_copy(
            src_ref=half_ref,
            dst_ref=out_ref.at[dev],
            send_sem=y_send.at[direction * n_dy * n_dz + dev],
            recv_sem=y_recv.at[dev],
            device_id=(section, grp, target, dz),
            device_id_type=pl.DeviceIdType.MESH,
        )

    for direction in (0, 1):
        y_own(direction).start()
    for step in range(1, n_dz):
        source = (dz + n_dz - step) % n_dz
        z_copy(source, source).wait_recv()
        for direction in (0, 1):
            y_copy(direction, dy, source).start()
        pair_copy(dy * n_dz + source, out_ref.at[dy * n_dz + source]).start()
    own.wait()
    for step in range(1, n_dz):
        z_copy((dz + step) % n_dz, dz).wait_send()

    @pl.when(has_left)
    def _():
        to_right_of_left = pltpu.make_async_remote_copy(
            src_ref=frames_ref.at[pl.ds(0, RAD)],
            dst_ref=halo_left,
            send_sem=halo_send.at[1],
            recv_sem=halo_recv.at[0],
            device_id=dev_peer(dev - 1),
            device_id_type=pl.DeviceIdType.MESH,
        )
        to_right_of_left.wait_recv()
        to_left().wait_send()

    @pl.when(has_right)
    def _():
        to_left_of_right = pltpu.make_async_remote_copy(
            src_ref=frames_ref.at[pl.ds(0, RAD)],
            dst_ref=halo_right,
            send_sem=halo_send.at[0],
            recv_sem=halo_recv.at[1],
            device_id=dev_peer(dev + 1),
            device_id_type=pl.DeviceIdType.MESH,
        )
        to_left_of_right.wait_recv()
        to_right().wait_send()

    weights = retention_weights()

    row_block = 32

    def smooth_rows(block, carry):
        rows = pl.ds(pl.multiple_of(block * row_block, row_block), row_block)

        def padded_frame(place):
            if place < RAD:
                return halo_left[place, rows, :]
            if place < RAD + count_frames:
                return frames_ref[place - RAD, rows, :]
            return halo_right[place - RAD - count_frames, rows, :]

        for frame in range(count_frames):
            total = weights[0] * padded_frame(frame).astype(jnp.float32)
            for offset in range(1, 2 * RAD + 1):
                total = total + weights[offset] * padded_frame(frame + offset).astype(jnp.float32)
            own_scans[frame, rows, :] = total.astype(own_scans.dtype)
        return carry

    lax.fori_loop(0, own_scans.shape[1] // row_block, smooth_rows, 0)

    swap = pltpu.make_async_remote_copy(
        src_ref=own_scans,
        dst_ref=partner_scans,
        send_sem=swap_send,
        recv_sem=swap_recv,
        device_id=(partner_section, grp, dy, dz),
        device_id_type=pl.DeviceIdType.MESH,
    )
    swap.start()
    relay = n_dz // 2
    for chunk in range(n_dz):
        y_copy(0, down, chunk).wait_recv()
        if chunk < relay:
            y_copy(0, down, chunk).start()
        pair_copy(down * n_dz + chunk, out_ref.at[down * n_dz + chunk]).start()
        y_copy(1, up, chunk).wait_recv()
        if chunk >= relay:
            y_copy(1, up, chunk).start()
        pair_copy(up * n_dz + chunk, out_ref.at[up * n_dz + chunk]).start()
    swap.wait()

    half = own_scans.shape[1]

    def level_frame(frame, carry):
        scans = jnp.concatenate([own_scans[frame], partner_scans[frame]], axis=0)
        for level in range(SCALES):
            acc = jnp.dot(kernels_ref[level], scans, preferred_element_type=jnp.float32)
            wave_ref[level, frame] = acc.astype(wave_ref.dtype)
        return carry

    lax.fori_loop(0, count_frames, level_frame, 0)

    opposite = (dy + 2) % n_dy
    for chunk in range(n_dz):
        y_copy(0, opposite, chunk).wait_recv()
        pair_copy(opposite * n_dz + chunk, out_ref.at[opposite * n_dz + chunk]).start()
    for direction in (0, 1):
        for chunk in range(n_dz):
            y_copy(direction, dy, chunk).wait_send()
    for chunk in range(relay):
        y_copy(0, down, chunk).wait_send()
    for chunk in range(relay, n_dz):
        y_copy(1, up, chunk).wait_send()
    for slot in range(n_dev):
        pair_copy(slot, half_ref).wait_recv()
    for slot in range(n_dev):
        pair_copy(slot, half_ref).wait_send()


def frame_work(frames, kernels, half):
    sizes = (lax.axis_size("section"), lax.axis_size("dy"), lax.axis_size("dz"))
    n_section, n_dy, n_dz = sizes
    rows, channels = half.shape
    count_frames, mob_local, _ = frames.shape
    rows_out, other_out, wave = pl.pallas_call(
        functools.partial(frame_kernel, sizes),
        out_shape=(
            jax.ShapeDtypeStruct((n_dy * n_dz, rows, channels), half.dtype),
            jax.ShapeDtypeStruct((n_dy * n_dz, rows, channels), half.dtype),
            jax.ShapeDtypeStruct((SCALES, count_frames, mob_local, channels), jnp.bfloat16),
        ),
        in_specs=[pl.BlockSpec(memory_space=pltpu.VMEM)] * 3,
        out_specs=(pl.BlockSpec(memory_space=pltpu.VMEM),) * 3,
        scratch_shapes=[
            pltpu.VMEM((RAD, mob_local, channels), frames.dtype),
            pltpu.VMEM((RAD, mob_local, channels), frames.dtype),
            pltpu.VMEM((count_frames, mob_local, channels), jnp.bfloat16),
            pltpu.VMEM((count_frames, mob_local, channels), jnp.bfloat16),
            pltpu.SemaphoreType.DMA(()),
            pltpu.SemaphoreType.DMA((n_dz,)),
            pltpu.SemaphoreType.DMA((n_dz,)),
            pltpu.SemaphoreType.DMA((2 * n_dy * n_dz,)),
            pltpu.SemaphoreType.DMA((n_dy * n_dz,)),
            pltpu.SemaphoreType.DMA((2,)),
            pltpu.SemaphoreType.DMA((2,)),
            pltpu.SemaphoreType.DMA(()),
            pltpu.SemaphoreType.DMA(()),
            pltpu.SemaphoreType.DMA((n_dy * n_dz,)),
            pltpu.SemaphoreType.DMA((n_dy * n_dz,)),
        ],
        compiler_params=pltpu.CompilerParams(
            collective_id=1, has_side_effects=True, vmem_limit_bytes=56 * 1024 * 1024
        ),
    )(frames, kernels, half)
    return (
        rows_out.reshape(n_dy * n_dz * rows, channels),
        other_out.reshape(n_dy * n_dz * rows, channels),
        wave,
    )


def score_kernel(
    order_ref, tile_ref, block_ref, count_ref, section_ref, wave_ref, mine_ref, other_ref, out_ref
):
    slot = order_ref[pl.program_id(0)]
    live = slot < count_ref[0]
    mine = block_ref[slot] % 2 == section_ref[0]

    def score(rows_ref):
        rows = rows_ref[...]
        acc = jnp.zeros((1, PB), jnp.float32)
        for level in range(SCALES):
            cells = wave_ref[level].reshape(-1, rows.shape[1])
            scores = lax.dot_general(
                cells, rows, (((1,), (1,)), ((), ())), preferred_element_type=jnp.float32
            )
            acc = acc + jnp.sum(jnp.maximum(scores, 0.0), axis=0, keepdims=True)
        cell_count = SCALES * wave_ref.shape[1] * wave_ref.shape[2]
        out_ref[0] = acc / cell_count

    @pl.when(jnp.logical_and(live, mine))
    def _():
        score(mine_ref)

    @pl.when(jnp.logical_and(live, jnp.logical_not(mine)))
    def _():
        score(other_ref)

    @pl.when(jnp.logical_not(live))
    def _():
        out_ref[0] = jnp.zeros((1, PB), jnp.float32)


def score_pairs(wavelet_stack, my_rows, other_rows, tile_ids, block_ids, live_pairs, section_index):
    slots = tile_ids.shape[0]
    scales, frames_local, mob_local, channels = wavelet_stack.shape
    slot_ids = jnp.arange(slots, dtype=jnp.int32)
    keys = jnp.where(slot_ids < live_pairs, tile_ids * slots + slot_ids, (mob_local // TM + 1) * slots + slot_ids)
    order = jnp.argsort(keys).astype(jnp.int32)

    def visited(k, o, c):
        return o[jnp.minimum(k, c[0] - 1)]

    grid_spec = pltpu.PrefetchScalarGridSpec(
        num_scalar_prefetch=5,
        grid=(slots,),
        in_specs=[
            pl.BlockSpec(
                (scales, frames_local, TM, channels),
                lambda k, o, t, b, c, s: (0, 0, t[visited(k, o, c)], 0),
            ),
            pl.BlockSpec((PB, channels), lambda k, o, t, b, c, s: (b[visited(k, o, c)] // 2, 0)),
            pl.BlockSpec((PB, channels), lambda k, o, t, b, c, s: (b[visited(k, o, c)] // 2, 0)),
        ],
        out_specs=pl.BlockSpec((1, 1, PB), lambda k, o, t, b, c, s: (o[k], 0, 0)),
    )
    out = pl.pallas_call(
        score_kernel,
        grid_spec=grid_spec,
        out_shape=jax.ShapeDtypeStruct((slots, 1, PB), jnp.float32),
    )(
        order,
        tile_ids,
        block_ids,
        live_pairs.reshape(1),
        section_index.astype(jnp.int32).reshape(1),
        wavelet_stack,
        my_rows,
        other_rows,
    )
    return out.reshape(slots, PB)


def solution(mesh):
    section_count, grp_count, dev_count = mesh.devices.shape
    dz_count = 8 if dev_count % 8 == 0 else dev_count
    split_mesh = jax.sharding.Mesh(
        mesh.devices.reshape(section_count, grp_count, dev_count // dz_count, dz_count),
        ("section", "grp", "dy", "dz"),
    )
    placed = (
        P("grp", DEV, "section", None),
        P(DEV, None),
        P("section", "grp", DEV),
        P("section", "grp", DEV),
        P("section", "grp", DEV),
        P(),
    )
    return jax.shard_map(
        on_device, mesh=split_mesh, in_specs=placed, out_specs=P("grp", DEV), check_vma=False
    )
```

```python
import functools
import math

import jax
import jax.numpy as jnp
from jax import lax
from jax.experimental import pallas as pl
from jax.experimental.pallas import tpu as pltpu
from jax.sharding import PartitionSpec as P

MOB = 512
SCALES = 6
RAD = 4
TM = 64
PB = 128
PREC = 8192
DEV = ("dy", "dz")


retention_spread = 2.0


def extended(cells, sides, width):
    for axis, dim in sides:
        count = lax.axis_size(axis)
        ends = count - 1
        head = lax.slice_in_dim(cells, 0, width, axis=dim)
        tail = lax.slice_in_dim(cells, cells.shape[dim] - width, cells.shape[dim], axis=dim)
        cells = jnp.concatenate(
            [
                lax.ppermute(tail, axis, [(i, (i + 1) % count) for i in range(ends)]),
                cells,
                lax.ppermute(head, axis, [((i + 1) % count, i) for i in range(ends)]),
            ],
            axis=dim,
        )
    return cells


def retention_weights():
    bell_values = [
        math.exp(-0.5 * (offset / retention_spread) ** 2) for offset in range(-RAD, RAD + 1)
    ]
    bell_total = sum(bell_values)
    return [weight_value / bell_total for weight_value in bell_values]


def mobility_kernels(row_start, row_count, col_start):
    row_place = (row_start + jnp.arange(row_count, dtype=jnp.int32)).astype(jnp.float32)
    col_place = ((col_start + jnp.arange(MOB, dtype=jnp.int32)) % MOB).astype(jnp.float32)
    distance = row_place[:, None] - col_place[None, :]
    tables = []
    for level in range(SCALES):
        spread_scans = 2.0**level
        scaled = distance / spread_scans
        tables.append(
            (1.0 - scaled * scaled)
            * jnp.exp(-0.5 * scaled * scaled)
            / math.sqrt(0.75 * math.sqrt(math.pi) * spread_scans)
        )
    return jnp.stack(tables).astype(jnp.bfloat16)


def on_device(frames, templates, pair_block, pair_tile, pair_count, owner_order):
    section_index = lax.axis_index("section")
    mob_local = frames.shape[2]
    section_count = lax.axis_size("section")
    kernels = mobility_kernels(section_index * mob_local, mob_local, section_index * mob_local)
    half_rows = templates.shape[0] // 2
    my_half = lax.dynamic_slice_in_dim(templates, section_index * half_rows, half_rows, 0)
    my_rows, other_rows, wavelet_stack = frame_work(frames[0], kernels, my_half)
    slots = pair_block.shape[2]
    live_pairs = pair_count[0, 0, 0]
    block_ids = pair_block[0, 0]
    tile_ids = pair_tile[0, 0]
    responses = score_pairs(
        wavelet_stack, my_rows, other_rows, tile_ids, block_ids, live_pairs, section_index
    )
    positions = jnp.take(owner_order.reshape(-1, PB), block_ids, axis=0).reshape(-1)
    groups = PREC // PB
    by_group = jnp.where(
        (positions // PB)[:, None] == jnp.arange(groups, dtype=jnp.int32)[None, :],
        responses.reshape(-1)[:, None],
        0.0,
    )
    by_lane = ((positions % PB)[:, None] == jnp.arange(PB, dtype=jnp.int32)[None, :]).astype(
        jnp.float32
    )
    placed = jnp.einsum(
        "ka,kb->ab",
        by_group,
        by_lane,
        precision=lax.Precision.HIGHEST,
        preferred_element_type=jnp.float32,
    ).reshape(-1)
    dev_count = lax.axis_size(DEV)
    return reduce_owned(placed.reshape(dev_count, 1, PREC // dev_count))


def reduce_kernel(
    sizes,
    payload_ref,
    out_ref,
    mixed,
    line,
    line_in,
    column,
    column_in,
    totals,
    pair_send,
    pair_recv,
    z_send,
    z_recv,
    y_send,
    y_recv,
    total_send,
    total_recv,
):
    n_section, n_grp, n_dy, n_dz = sizes
    section = lax.axis_index("section")
    grp = lax.axis_index("grp")
    dy = lax.axis_index("dy")
    dz = lax.axis_index("dz")
    partner = (section + 1) % n_section
    owned_width = out_ref.shape[1]

    barrier = pltpu.get_barrier_semaphore()
    peers = [(partner, grp, dy, dz)]
    peers += [(section, grp, dy, (dz + step) % n_dz) for step in range(1, n_dz)]
    peers += [(section, grp, (dy + step) % n_dy, dz) for step in range(1, n_dy)]
    peers += [(section, (grp + step) % n_grp, dy, dz) for step in range(1, n_grp)]
    for peer in peers:
        pl.semaphore_signal(barrier, inc=1, device_id=peer, device_id_type=pl.DeviceIdType.MESH)
    pl.semaphore_wait(barrier, len(peers))

    swap = pltpu.make_async_remote_copy(
        src_ref=payload_ref,
        dst_ref=mixed,
        send_sem=pair_send,
        recv_sem=pair_recv,
        device_id=(partner, grp, dy, dz),
        device_id_type=pl.DeviceIdType.MESH,
    )
    swap.start()
    swap.wait()
    combined = payload_ref[...] + mixed[...]
    line[:, :, :, :owned_width] = combined
    chip_total = jnp.sum(jnp.sum(jnp.sum(combined, axis=0), axis=0), axis=1, keepdims=True)
    line[:, :, :, owned_width:] = jnp.broadcast_to(
        chip_total[None, None], line.shape[:3] + (line.shape[3] - owned_width,)
    )
    line_in[dz] = line[dz]

    def z_copy(target, source):
        return pltpu.make_async_remote_copy(
            src_ref=line.at[target],
            dst_ref=line_in.at[source],
            send_sem=z_send.at[target],
            recv_sem=z_recv.at[source],
            device_id=(section, grp, dy, target),
            device_id_type=pl.DeviceIdType.MESH,
        )

    for step in range(1, n_dz):
        z_copy((dz + step) % n_dz, dz).start()
    for step in range(1, n_dz):
        source = (dz + n_dz - step) % n_dz
        z_copy(source, source).wait_recv()
    partial = line_in[0]
    for index in range(1, n_dz):
        partial = partial + line_in[index]
    column[...] = partial
    column_in[dy] = column[dy]

    def y_copy(target, source):
        return pltpu.make_async_remote_copy(
            src_ref=column.at[target],
            dst_ref=column_in.at[source],
            send_sem=y_send.at[target],
            recv_sem=y_recv.at[source],
            device_id=(section, grp, target, dz),
            device_id_type=pl.DeviceIdType.MESH,
        )

    for step in range(1, n_dy):
        y_copy((dy + step) % n_dy, dy).start()
    for step in range(1, n_dy):
        source = (dy + n_dy - step) % n_dy
        y_copy(source, source).wait_recv()
    summed = column_in[0]
    for index in range(1, n_dy):
        summed = summed + column_in[index]
    summed = summed.reshape(summed.shape[-2:])
    totals[grp] = summed[:, owned_width:]

    def total_copy(step):
        target = (grp + step) % n_grp
        return pltpu.make_async_remote_copy(
            src_ref=totals.at[grp],
            dst_ref=totals.at[grp],
            send_sem=total_send.at[target],
            recv_sem=total_recv.at[grp],
            device_id=(section, target, dy, dz),
            device_id_type=pl.DeviceIdType.MESH,
        )

    for step in range(1, n_grp):
        total_copy(step).start()
    for step in range(1, n_grp):
        source = (grp + step) % n_grp
        pltpu.make_async_remote_copy(
            src_ref=totals.at[source],
            dst_ref=totals.at[source],
            send_sem=total_send.at[source],
            recv_sem=total_recv.at[source],
            device_id=(section, source, dy, dz),
            device_id_type=pl.DeviceIdType.MESH,
        ).wait_recv()
        total_copy(step).wait_send()
    for step in range(1, n_dz):
        z_copy((dz + step) % n_dz, dz).wait_send()
    for step in range(1, n_dy):
        y_copy((dy + step) % n_dy, dy).wait_send()
    run_sum = totals[0]
    for index in range(1, n_grp):
        run_sum = run_sum + totals[index]
    own_total = summed[:, owned_width : owned_width + 1]
    factor = (run_sum[:, 0:1] / n_grp) / own_total
    out_ref[...] = summed[:, :owned_width] * factor


def reduce_owned(payload):
    sizes = (lax.axis_size("section"), lax.axis_size("grp"), lax.axis_size("dy"), lax.axis_size("dz"))
    n_section, n_grp, n_dy, n_dz = sizes
    rows, one, owned_width = payload.shape
    width = owned_width + 128
    lines = payload.reshape(n_dy, n_dz, one, owned_width).transpose(1, 0, 2, 3)
    return pl.pallas_call(
        functools.partial(reduce_kernel, sizes),
        out_shape=jax.ShapeDtypeStruct((1, owned_width), jnp.float32),
        in_specs=[pl.BlockSpec(memory_space=pltpu.VMEM)],
        out_specs=pl.BlockSpec(memory_space=pltpu.VMEM),
        scratch_shapes=[
            pltpu.VMEM((n_dz, n_dy, one, owned_width), jnp.float32),
            pltpu.VMEM((n_dz, n_dy, one, width), jnp.float32),
            pltpu.VMEM((n_dz, n_dy, one, width), jnp.float32),
            pltpu.VMEM((n_dy, one, width), jnp.float32),
            pltpu.VMEM((n_dy, one, width), jnp.float32),
            pltpu.VMEM((n_grp, 1, 128), jnp.float32),
            pltpu.SemaphoreType.DMA(()),
            pltpu.SemaphoreType.DMA(()),
            pltpu.SemaphoreType.DMA((n_dz,)),
            pltpu.SemaphoreType.DMA((n_dz,)),
            pltpu.SemaphoreType.DMA((n_dy,)),
            pltpu.SemaphoreType.DMA((n_dy,)),
            pltpu.SemaphoreType.DMA((n_grp,)),
            pltpu.SemaphoreType.DMA((n_grp,)),
        ],
        compiler_params=pltpu.CompilerParams(collective_id=0, has_side_effects=True),
    )(lines)


def frame_kernel(
    sizes,
    frames_ref,
    kernels_ref,
    half_ref,
    out_ref,
    other_ref,
    wave_ref,
    halo_left,
    halo_right,
    own_scans,
    partner_scans,
    own_sem,
    z_send,
    z_recv,
    y_send,
    y_recv,
    halo_send,
    halo_recv,
    swap_send,
    swap_recv,
    pair_send,
    pair_recv,
):
    n_section, n_dy, n_dz = sizes
    n_dev = n_dy * n_dz
    section = lax.axis_index("section")
    grp = lax.axis_index("grp")
    dy = lax.axis_index("dy")
    dz = lax.axis_index("dz")
    dev = dy * n_dz + dz
    partner_section = (section + 1) % n_section

    def dev_peer(index):
        return (section, grp, index // n_dz, index % n_dz)

    barrier = pltpu.get_barrier_semaphore()
    for step in range(1, n_dz):
        pl.semaphore_signal(
            barrier,
            inc=1,
            device_id=(section, grp, dy, (dz + step) % n_dz),
            device_id_type=pl.DeviceIdType.MESH,
        )
    up = (dy + 1) % n_dy
    down = (dy + n_dy - 1) % n_dy
    for row in (up, down):
        pl.semaphore_signal(
            barrier,
            inc=1,
            device_id=(section, grp, row, dz),
            device_id_type=pl.DeviceIdType.MESH,
        )
    pl.semaphore_signal(
        barrier,
        inc=1,
        device_id=(partner_section, grp, dy, dz),
        device_id_type=pl.DeviceIdType.MESH,
    )
    has_left = dev > 0
    has_right = dev < n_dev - 1
    far_left = jnp.logical_and(has_left, dz == 0)
    far_right = jnp.logical_and(has_right, dz == n_dz - 1)

    @pl.when(far_left)
    def _():
        pl.semaphore_signal(
            barrier, inc=1, device_id=dev_peer(dev - 1), device_id_type=pl.DeviceIdType.MESH
        )

    @pl.when(far_right)
    def _():
        pl.semaphore_signal(
            barrier, inc=1, device_id=dev_peer(dev + 1), device_id_type=pl.DeviceIdType.MESH
        )

    extra = far_left.astype(jnp.int32) + far_right.astype(jnp.int32)
    pl.semaphore_wait(barrier, n_dz - 1 + 2 + 1 + extra)

    own = pltpu.make_async_copy(half_ref, out_ref.at[dev], own_sem)
    own.start()

    def pair_copy(slot, source_ref):
        return pltpu.make_async_remote_copy(
            src_ref=source_ref,
            dst_ref=other_ref.at[slot],
            send_sem=pair_send.at[slot],
            recv_sem=pair_recv.at[slot],
            device_id=(partner_section, grp, dy, dz),
            device_id_type=pl.DeviceIdType.MESH,
        )

    pair_copy(dev, half_ref).start()

    def z_copy(target, source):
        return pltpu.make_async_remote_copy(
            src_ref=half_ref,
            dst_ref=out_ref.at[dy * n_dz + source],
            send_sem=z_send.at[target],
            recv_sem=z_recv.at[source],
            device_id=(section, grp, dy, target),
            device_id_type=pl.DeviceIdType.MESH,
        )

    for step in range(1, n_dz):
        z_copy((dz + step) % n_dz, dz).start()

    count_frames = frames_ref.shape[0]

    def to_left():
        return pltpu.make_async_remote_copy(
            src_ref=frames_ref.at[pl.ds(0, RAD)],
            dst_ref=halo_right,
            send_sem=halo_send.at[0],
            recv_sem=halo_recv.at[1],
            device_id=dev_peer(dev - 1),
            device_id_type=pl.DeviceIdType.MESH,
        )

    def to_right():
        return pltpu.make_async_remote_copy(
            src_ref=frames_ref.at[pl.ds(count_frames - RAD, RAD)],
            dst_ref=halo_left,
            send_sem=halo_send.at[1],
            recv_sem=halo_recv.at[0],
            device_id=dev_peer(dev + 1),
            device_id_type=pl.DeviceIdType.MESH,
        )

    @pl.when(has_left)
    def _():
        to_left().start()

    @pl.when(has_right)
    def _():
        to_right().start()

    @pl.when(jnp.logical_not(has_left))
    def _():
        halo_left[...] = jnp.zeros(halo_left.shape, halo_left.dtype)

    @pl.when(jnp.logical_not(has_right))
    def _():
        halo_right[...] = jnp.zeros(halo_right.shape, halo_right.dtype)

    def y_copy(direction, row, chunk):
        slot = row * n_dz + chunk
        target = up if direction == 0 else down
        return pltpu.make_async_remote_copy(
            src_ref=out_ref.at[slot],
            dst_ref=out_ref.at[slot],
            send_sem=y_send.at[direction * n_dy * n_dz + slot],
            recv_sem=y_recv.at[slot],
            device_id=(section, grp, target, dz),
            device_id_type=pl.DeviceIdType.MESH,
        )

    def y_own(direction):
        target = up if direction == 0 else down
        return pltpu.make_async_remote_copy(
            src_ref=half_ref,
            dst_ref=out_ref.at[dev],
            send_sem=y_send.at[direction * n_dy * n_dz + dev],
            recv_sem=y_recv.at[dev],
            device_id=(section, grp, target, dz),
            device_id_type=pl.DeviceIdType.MESH,
        )

    for direction in (0, 1):
        y_own(direction).start()
    for step in range(1, n_dz):
        source = (dz + n_dz - step) % n_dz
        z_copy(source, source).wait_recv()
        for direction in (0, 1):
            y_copy(direction, dy, source).start()
        pair_copy(dy * n_dz + source, out_ref.at[dy * n_dz + source]).start()
    own.wait()
    for step in range(1, n_dz):
        z_copy((dz + step) % n_dz, dz).wait_send()

    @pl.when(has_left)
    def _():
        to_right_of_left = pltpu.make_async_remote_copy(
            src_ref=frames_ref.at[pl.ds(0, RAD)],
            dst_ref=halo_left,
            send_sem=halo_send.at[1],
            recv_sem=halo_recv.at[0],
            device_id=dev_peer(dev - 1),
            device_id_type=pl.DeviceIdType.MESH,
        )
        to_right_of_left.wait_recv()
        to_left().wait_send()

    @pl.when(has_right)
    def _():
        to_left_of_right = pltpu.make_async_remote_copy(
            src_ref=frames_ref.at[pl.ds(0, RAD)],
            dst_ref=halo_right,
            send_sem=halo_send.at[0],
            recv_sem=halo_recv.at[1],
            device_id=dev_peer(dev + 1),
            device_id_type=pl.DeviceIdType.MESH,
        )
        to_left_of_right.wait_recv()
        to_right().wait_send()

    weights = retention_weights()

    row_block = 32

    def smooth_rows(block, carry):
        rows = pl.ds(pl.multiple_of(block * row_block, row_block), row_block)

        def padded_frame(place):
            if place < RAD:
                return halo_left[place, rows, :]
            if place < RAD + count_frames:
                return frames_ref[place - RAD, rows, :]
            return halo_right[place - RAD - count_frames, rows, :]

        for frame in range(count_frames):
            total = weights[0] * padded_frame(frame).astype(jnp.float32)
            for offset in range(1, 2 * RAD + 1):
                total = total + weights[offset] * padded_frame(frame + offset).astype(jnp.float32)
            own_scans[frame, rows, :] = total.astype(own_scans.dtype)
        return carry

    lax.fori_loop(0, own_scans.shape[1] // row_block, smooth_rows, 0)

    swap = pltpu.make_async_remote_copy(
        src_ref=own_scans,
        dst_ref=partner_scans,
        send_sem=swap_send,
        recv_sem=swap_recv,
        device_id=(partner_section, grp, dy, dz),
        device_id_type=pl.DeviceIdType.MESH,
    )
    swap.start()
    relay = n_dz // 2
    for chunk in range(n_dz):
        y_copy(0, down, chunk).wait_recv()
        if chunk < relay:
            y_copy(0, down, chunk).start()
        pair_copy(down * n_dz + chunk, out_ref.at[down * n_dz + chunk]).start()
        y_copy(1, up, chunk).wait_recv()
        if chunk >= relay:
            y_copy(1, up, chunk).start()
        pair_copy(up * n_dz + chunk, out_ref.at[up * n_dz + chunk]).start()
    swap.wait()

    half = own_scans.shape[1]

    def level_frame(frame, carry):
        for level in range(SCALES):
            table = kernels_ref[level]
            acc = jnp.dot(table[:, :half], own_scans[frame], preferred_element_type=jnp.float32)
            acc = acc + jnp.dot(
                table[:, half:], partner_scans[frame], preferred_element_type=jnp.float32
            )
            wave_ref[level, frame] = acc.astype(wave_ref.dtype)
        return carry

    lax.fori_loop(0, count_frames, level_frame, 0)

    opposite = (dy + 2) % n_dy
    for chunk in range(n_dz):
        y_copy(0, opposite, chunk).wait_recv()
        pair_copy(opposite * n_dz + chunk, out_ref.at[opposite * n_dz + chunk]).start()
    for direction in (0, 1):
        for chunk in range(n_dz):
            y_copy(direction, dy, chunk).wait_send()
    for chunk in range(relay):
        y_copy(0, down, chunk).wait_send()
    for chunk in range(relay, n_dz):
        y_copy(1, up, chunk).wait_send()
    for slot in range(n_dev):
        pair_copy(slot, half_ref).wait_recv()
    for slot in range(n_dev):
        pair_copy(slot, half_ref).wait_send()


def frame_work(frames, kernels, half):
    sizes = (lax.axis_size("section"), lax.axis_size("dy"), lax.axis_size("dz"))
    n_section, n_dy, n_dz = sizes
    rows, channels = half.shape
    count_frames, mob_local, _ = frames.shape
    rows_out, other_out, wave = pl.pallas_call(
        functools.partial(frame_kernel, sizes),
        out_shape=(
            jax.ShapeDtypeStruct((n_dy * n_dz, rows, channels), half.dtype),
            jax.ShapeDtypeStruct((n_dy * n_dz, rows, channels), half.dtype),
            jax.ShapeDtypeStruct((SCALES, count_frames, mob_local, channels), jnp.bfloat16),
        ),
        in_specs=[pl.BlockSpec(memory_space=pltpu.VMEM)] * 3,
        out_specs=(pl.BlockSpec(memory_space=pltpu.VMEM),) * 3,
        scratch_shapes=[
            pltpu.VMEM((RAD, mob_local, channels), frames.dtype),
            pltpu.VMEM((RAD, mob_local, channels), frames.dtype),
            pltpu.VMEM((count_frames, mob_local, channels), jnp.bfloat16),
            pltpu.VMEM((count_frames, mob_local, channels), jnp.bfloat16),
            pltpu.SemaphoreType.DMA(()),
            pltpu.SemaphoreType.DMA((n_dz,)),
            pltpu.SemaphoreType.DMA((n_dz,)),
            pltpu.SemaphoreType.DMA((2 * n_dy * n_dz,)),
            pltpu.SemaphoreType.DMA((n_dy * n_dz,)),
            pltpu.SemaphoreType.DMA((2,)),
            pltpu.SemaphoreType.DMA((2,)),
            pltpu.SemaphoreType.DMA(()),
            pltpu.SemaphoreType.DMA(()),
            pltpu.SemaphoreType.DMA((n_dy * n_dz,)),
            pltpu.SemaphoreType.DMA((n_dy * n_dz,)),
        ],
        compiler_params=pltpu.CompilerParams(
            collective_id=1, has_side_effects=True, vmem_limit_bytes=56 * 1024 * 1024
        ),
    )(frames, kernels, half)
    return (
        rows_out.reshape(n_dy * n_dz * rows, channels),
        other_out.reshape(n_dy * n_dz * rows, channels),
        wave,
    )


def score_kernel(
    order_ref, tile_ref, block_ref, count_ref, section_ref, wave_ref, mine_ref, other_ref, out_ref
):
    slot = order_ref[pl.program_id(0)]
    live = slot < count_ref[0]
    mine = block_ref[slot] % 2 == section_ref[0]

    def score(rows_ref):
        rows = rows_ref[...]
        acc = jnp.zeros((1, PB), jnp.float32)
        for level in range(SCALES):
            cells = wave_ref[level].reshape(-1, rows.shape[1])
            scores = lax.dot_general(
                cells, rows, (((1,), (1,)), ((), ())), preferred_element_type=jnp.float32
            )
            acc = acc + jnp.sum(jnp.maximum(scores, 0.0), axis=0, keepdims=True)
        cell_count = SCALES * wave_ref.shape[1] * wave_ref.shape[2]
        out_ref[0] = acc / cell_count

    @pl.when(jnp.logical_and(live, mine))
    def _():
        score(mine_ref)

    @pl.when(jnp.logical_and(live, jnp.logical_not(mine)))
    def _():
        score(other_ref)

    @pl.when(jnp.logical_not(live))
    def _():
        out_ref[0] = jnp.zeros((1, PB), jnp.float32)


def score_pairs(wavelet_stack, my_rows, other_rows, tile_ids, block_ids, live_pairs, section_index):
    slots = tile_ids.shape[0]
    scales, frames_local, mob_local, channels = wavelet_stack.shape
    slot_ids = jnp.arange(slots, dtype=jnp.int32)
    keys = jnp.where(slot_ids < live_pairs, tile_ids * slots + slot_ids, (mob_local // TM + 1) * slots + slot_ids)
    ranks = jnp.sum((keys[None, :] < keys[:, None]).astype(jnp.int32), axis=1)
    order = jnp.sum(
        jnp.where(ranks[None, :] == slot_ids[:, None], slot_ids[None, :], 0), axis=1
    ).astype(jnp.int32)

    def visited(k, o, c):
        return o[jnp.minimum(k, c[0] - 1)]

    grid_spec = pltpu.PrefetchScalarGridSpec(
        num_scalar_prefetch=5,
        grid=(slots,),
        in_specs=[
            pl.BlockSpec(
                (scales, frames_local, TM, channels),
                lambda k, o, t, b, c, s: (0, 0, t[visited(k, o, c)], 0),
            ),
            pl.BlockSpec((PB, channels), lambda k, o, t, b, c, s: (b[visited(k, o, c)] // 2, 0)),
            pl.BlockSpec((PB, channels), lambda k, o, t, b, c, s: (b[visited(k, o, c)] // 2, 0)),
        ],
        out_specs=pl.BlockSpec((1, 1, PB), lambda k, o, t, b, c, s: (o[k], 0, 0)),
    )
    out = pl.pallas_call(
        score_kernel,
        grid_spec=grid_spec,
        out_shape=jax.ShapeDtypeStruct((slots, 1, PB), jnp.float32),
    )(
        order,
        tile_ids,
        block_ids,
        live_pairs.reshape(1),
        section_index.astype(jnp.int32).reshape(1),
        wavelet_stack,
        my_rows,
        other_rows,
    )
    return out.reshape(slots, PB)


def solution(mesh):
    section_count, grp_count, dev_count = mesh.devices.shape
    dz_count = 8 if dev_count % 8 == 0 else dev_count
    split_mesh = jax.sharding.Mesh(
        mesh.devices.reshape(section_count, grp_count, dev_count // dz_count, dz_count),
        ("section", "grp", "dy", "dz"),
    )
    placed = (
        P("grp", DEV, "section", None),
        P(DEV, None),
        P("section", "grp", DEV),
        P("section", "grp", DEV),
        P("section", "grp", DEV),
        P(),
    )
    return jax.shard_map(
        on_device, mesh=split_mesh, in_specs=placed, out_specs=P("grp", DEV), check_vma=False
    )
```

```python
import functools
import math

import jax
import jax.numpy as jnp
from jax import lax
from jax.experimental import pallas as pl
from jax.experimental.pallas import tpu as pltpu
from jax.sharding import PartitionSpec as P

MOB = 512
SCALES = 6
RAD = 4
TM = 64
PB = 128
PREC = 8192
DEV = ("dy", "dz")


retention_spread = 2.0


def extended(cells, sides, width):
    for axis, dim in sides:
        count = lax.axis_size(axis)
        ends = count - 1
        head = lax.slice_in_dim(cells, 0, width, axis=dim)
        tail = lax.slice_in_dim(cells, cells.shape[dim] - width, cells.shape[dim], axis=dim)
        cells = jnp.concatenate(
            [
                lax.ppermute(tail, axis, [(i, (i + 1) % count) for i in range(ends)]),
                cells,
                lax.ppermute(head, axis, [((i + 1) % count, i) for i in range(ends)]),
            ],
            axis=dim,
        )
    return cells


def retention_weights():
    bell_values = [
        math.exp(-0.5 * (offset / retention_spread) ** 2) for offset in range(-RAD, RAD + 1)
    ]
    bell_total = sum(bell_values)
    return [weight_value / bell_total for weight_value in bell_values]


def mobility_kernels(row_start, row_count, col_start):
    row_place = (row_start + jnp.arange(row_count, dtype=jnp.int32)).astype(jnp.float32)
    col_place = ((col_start + jnp.arange(MOB, dtype=jnp.int32)) % MOB).astype(jnp.float32)
    distance = row_place[:, None] - col_place[None, :]
    tables = []
    for level in range(SCALES):
        spread_scans = 2.0**level
        scaled = distance / spread_scans
        tables.append(
            (1.0 - scaled * scaled)
            * jnp.exp(-0.5 * scaled * scaled)
            / math.sqrt(0.75 * math.sqrt(math.pi) * spread_scans)
        )
    return jnp.stack(tables).astype(jnp.bfloat16)


def on_device(frames, templates, pair_block, pair_tile, pair_count, owner_order):
    section_index = lax.axis_index("section")
    mob_local = frames.shape[2]
    section_count = lax.axis_size("section")
    kernels = mobility_kernels(section_index * mob_local, mob_local, section_index * mob_local)
    half_rows = templates.shape[0] // 2
    my_half = lax.dynamic_slice_in_dim(templates, section_index * half_rows, half_rows, 0)
    my_rows, other_rows, wavelet_stack = frame_work(frames[0], kernels, my_half)
    slots = pair_block.shape[2]
    live_pairs = pair_count[0, 0, 0]
    block_ids = pair_block[0, 0]
    tile_ids = pair_tile[0, 0]
    responses = score_pairs(
        wavelet_stack, my_rows, other_rows, tile_ids, block_ids, live_pairs, section_index
    )
    positions = jnp.take(owner_order.reshape(-1, PB), block_ids, axis=0).reshape(-1)
    groups = PREC // PB
    by_group = jnp.where(
        (positions // PB)[:, None] == jnp.arange(groups, dtype=jnp.int32)[None, :],
        responses.reshape(-1)[:, None],
        0.0,
    )
    by_lane = ((positions % PB)[:, None] == jnp.arange(PB, dtype=jnp.int32)[None, :]).astype(
        jnp.float32
    )
    placed = jnp.einsum(
        "ka,kb->ab",
        by_group,
        by_lane,
        precision=lax.Precision.HIGHEST,
        preferred_element_type=jnp.float32,
    ).reshape(-1)
    dev_count = lax.axis_size(DEV)
    return reduce_owned(placed.reshape(dev_count, 1, PREC // dev_count))


def reduce_kernel(
    sizes,
    payload_ref,
    out_ref,
    mixed,
    line,
    line_in,
    column,
    column_in,
    totals,
    pair_send,
    pair_recv,
    z_send,
    z_recv,
    y_send,
    y_recv,
    total_send,
    total_recv,
):
    n_section, n_grp, n_dy, n_dz = sizes
    cores = totals
    section = lax.axis_index("section")
    grp = lax.axis_index("grp")
    dy = lax.axis_index("dy")
    dz = lax.axis_index("dz")
    partner = (section + 1) % n_section
    owned_width = out_ref.shape[1]

    barrier = pltpu.get_barrier_semaphore()
    peers = [(partner, grp, dy, dz)]
    peers += [(section, grp, dy, (dz + step) % n_dz) for step in range(1, n_dz)]
    peers += [(section, grp, (dy + step) % n_dy, dz) for step in range(1, n_dy)]
    peers += [
        (side, (grp + step) % n_grp, dy, dz) for side in range(n_section) for step in range(1, n_grp)
    ]
    for peer in peers:
        pl.semaphore_signal(barrier, inc=1, device_id=peer, device_id_type=pl.DeviceIdType.MESH)
    pl.semaphore_wait(barrier, len(peers))

    swap = pltpu.make_async_remote_copy(
        src_ref=payload_ref,
        dst_ref=mixed,
        send_sem=pair_send,
        recv_sem=pair_recv,
        device_id=(partner, grp, dy, dz),
        device_id_type=pl.DeviceIdType.MESH,
    )
    swap.start()
    own_slot = section * n_grp + grp
    own_sum = jnp.sum(jnp.sum(jnp.sum(payload_ref[...], axis=0), axis=0), axis=1, keepdims=True)
    cores[own_slot] = jnp.broadcast_to(own_sum, (1, 128))
    cores[partner * n_grp + grp] = jnp.zeros((1, 128), jnp.float32)

    def core_copy(side, other):
        return pltpu.make_async_remote_copy(
            src_ref=cores.at[own_slot],
            dst_ref=cores.at[own_slot],
            send_sem=total_send.at[side * n_grp + other],
            recv_sem=total_recv.at[own_slot],
            device_id=(side, other, dy, dz),
            device_id_type=pl.DeviceIdType.MESH,
        )

    def core_arrival(side, other):
        slot = side * n_grp + other
        return pltpu.make_async_remote_copy(
            src_ref=cores.at[slot],
            dst_ref=cores.at[slot],
            send_sem=total_send.at[slot],
            recv_sem=total_recv.at[slot],
            device_id=(side, other, dy, dz),
            device_id_type=pl.DeviceIdType.MESH,
        )

    for side in range(n_section):
        for step in range(1, n_grp):
            core_copy(side, (grp + step) % n_grp).start()
    swap.wait()
    combined = payload_ref[...] + mixed[...]
    line[:, :, :, :owned_width] = combined
    chip_total = jnp.sum(jnp.sum(jnp.sum(combined, axis=0), axis=0), axis=1, keepdims=True)
    for side in range(n_section):
        for step in range(1, n_grp):
            core_arrival(side, (grp + step) % n_grp).wait_recv()
    lanes = lax.broadcasted_iota(jnp.int32, (1, line.shape[3] - owned_width), 1)
    spread = jnp.where(lanes == grp, chip_total, 0.0)
    for other in range(n_grp):
        other_total = cores[other] + cores[n_grp + other]
        spread = jnp.where(jnp.logical_and(lanes == other, other != grp), other_total, spread)
    line[:, :, :, owned_width:] = jnp.broadcast_to(spread[None, None], line.shape[:3] + spread.shape[1:])
    line_in[dz] = line[dz]

    def z_copy(target, source):
        return pltpu.make_async_remote_copy(
            src_ref=line.at[target],
            dst_ref=line_in.at[source],
            send_sem=z_send.at[target],
            recv_sem=z_recv.at[source],
            device_id=(section, grp, dy, target),
            device_id_type=pl.DeviceIdType.MESH,
        )

    for step in range(1, n_dz):
        z_copy((dz + step) % n_dz, dz).start()
    for step in range(1, n_dz):
        source = (dz + n_dz - step) % n_dz
        z_copy(source, source).wait_recv()
    partial = line_in[0]
    for index in range(1, n_dz):
        partial = partial + line_in[index]
    column[...] = partial
    column_in[dy] = column[dy]

    def y_copy(target, source):
        return pltpu.make_async_remote_copy(
            src_ref=column.at[target],
            dst_ref=column_in.at[source],
            send_sem=y_send.at[target],
            recv_sem=y_recv.at[source],
            device_id=(section, grp, target, dz),
            device_id_type=pl.DeviceIdType.MESH,
        )

    for step in range(1, n_dy):
        y_copy((dy + step) % n_dy, dy).start()
    for step in range(1, n_dy):
        source = (dy + n_dy - step) % n_dy
        y_copy(source, source).wait_recv()
    summed = column_in[0]
    for index in range(1, n_dy):
        summed = summed + column_in[index]
    summed = summed.reshape(summed.shape[-2:])
    for step in range(1, n_dz):
        z_copy((dz + step) % n_dz, dz).wait_send()
    for step in range(1, n_dy):
        y_copy((dy + step) % n_dy, dy).wait_send()
    for side in range(n_section):
        for step in range(1, n_grp):
            core_copy(side, (grp + step) % n_grp).wait_send()
    run_totals = summed[:, owned_width:]
    run_sum = jnp.sum(run_totals, axis=1, keepdims=True)
    own_total = jnp.sum(jnp.where(lanes == grp, run_totals, 0.0), axis=1, keepdims=True)
    factor = (run_sum / n_grp) / own_total
    out_ref[...] = summed[:, :owned_width] * factor


def reduce_owned(payload):
    sizes = (lax.axis_size("section"), lax.axis_size("grp"), lax.axis_size("dy"), lax.axis_size("dz"))
    n_section, n_grp, n_dy, n_dz = sizes
    rows, one, owned_width = payload.shape
    width = owned_width + 128
    lines = payload.reshape(n_dy, n_dz, one, owned_width).transpose(1, 0, 2, 3)
    return pl.pallas_call(
        functools.partial(reduce_kernel, sizes),
        out_shape=jax.ShapeDtypeStruct((1, owned_width), jnp.float32),
        in_specs=[pl.BlockSpec(memory_space=pltpu.VMEM)],
        out_specs=pl.BlockSpec(memory_space=pltpu.VMEM),
        scratch_shapes=[
            pltpu.VMEM((n_dz, n_dy, one, owned_width), jnp.float32),
            pltpu.VMEM((n_dz, n_dy, one, width), jnp.float32),
            pltpu.VMEM((n_dz, n_dy, one, width), jnp.float32),
            pltpu.VMEM((n_dy, one, width), jnp.float32),
            pltpu.VMEM((n_dy, one, width), jnp.float32),
            pltpu.VMEM((n_section * n_grp, 1, 128), jnp.float32),
            pltpu.SemaphoreType.DMA(()),
            pltpu.SemaphoreType.DMA(()),
            pltpu.SemaphoreType.DMA((n_dz,)),
            pltpu.SemaphoreType.DMA((n_dz,)),
            pltpu.SemaphoreType.DMA((n_dy,)),
            pltpu.SemaphoreType.DMA((n_dy,)),
            pltpu.SemaphoreType.DMA((n_section * n_grp,)),
            pltpu.SemaphoreType.DMA((n_section * n_grp,)),
        ],
        compiler_params=pltpu.CompilerParams(collective_id=0, has_side_effects=True),
    )(lines)


def frame_kernel(
    sizes,
    frames_ref,
    kernels_ref,
    half_ref,
    out_ref,
    other_ref,
    wave_ref,
    halo_left,
    halo_right,
    own_scans,
    partner_scans,
    own_sem,
    z_send,
    z_recv,
    y_send,
    y_recv,
    halo_send,
    halo_recv,
    swap_send,
    swap_recv,
    pair_send,
    pair_recv,
):
    n_section, n_dy, n_dz = sizes
    n_dev = n_dy * n_dz
    section = lax.axis_index("section")
    grp = lax.axis_index("grp")
    dy = lax.axis_index("dy")
    dz = lax.axis_index("dz")
    dev = dy * n_dz + dz
    partner_section = (section + 1) % n_section

    def dev_peer(index):
        return (section, grp, index // n_dz, index % n_dz)

    barrier = pltpu.get_barrier_semaphore()
    for step in range(1, n_dz):
        pl.semaphore_signal(
            barrier,
            inc=1,
            device_id=(section, grp, dy, (dz + step) % n_dz),
            device_id_type=pl.DeviceIdType.MESH,
        )
    up = (dy + 1) % n_dy
    down = (dy + n_dy - 1) % n_dy
    for row in (up, down):
        pl.semaphore_signal(
            barrier,
            inc=1,
            device_id=(section, grp, row, dz),
            device_id_type=pl.DeviceIdType.MESH,
        )
    pl.semaphore_signal(
        barrier,
        inc=1,
        device_id=(partner_section, grp, dy, dz),
        device_id_type=pl.DeviceIdType.MESH,
    )
    has_left = dev > 0
    has_right = dev < n_dev - 1
    far_left = jnp.logical_and(has_left, dz == 0)
    far_right = jnp.logical_and(has_right, dz == n_dz - 1)

    @pl.when(far_left)
    def _():
        pl.semaphore_signal(
            barrier, inc=1, device_id=dev_peer(dev - 1), device_id_type=pl.DeviceIdType.MESH
        )

    @pl.when(far_right)
    def _():
        pl.semaphore_signal(
            barrier, inc=1, device_id=dev_peer(dev + 1), device_id_type=pl.DeviceIdType.MESH
        )

    extra = far_left.astype(jnp.int32) + far_right.astype(jnp.int32)
    pl.semaphore_wait(barrier, n_dz - 1 + 2 + 1 + extra)

    own = pltpu.make_async_copy(half_ref, out_ref.at[dev], own_sem)
    own.start()

    def pair_copy(slot, source_ref):
        return pltpu.make_async_remote_copy(
            src_ref=source_ref,
            dst_ref=other_ref.at[slot],
            send_sem=pair_send.at[slot],
            recv_sem=pair_recv.at[slot],
            device_id=(partner_section, grp, dy, dz),
            device_id_type=pl.DeviceIdType.MESH,
        )

    pair_copy(dev, half_ref).start()

    def z_copy(target, source):
        return pltpu.make_async_remote_copy(
            src_ref=half_ref,
            dst_ref=out_ref.at[dy * n_dz + source],
            send_sem=z_send.at[target],
            recv_sem=z_recv.at[source],
            device_id=(section, grp, dy, target),
            device_id_type=pl.DeviceIdType.MESH,
        )

    for step in range(1, n_dz):
        z_copy((dz + step) % n_dz, dz).start()

    count_frames = frames_ref.shape[0]

    def to_left():
        return pltpu.make_async_remote_copy(
            src_ref=frames_ref.at[pl.ds(0, RAD)],
            dst_ref=halo_right,
            send_sem=halo_send.at[0],
            recv_sem=halo_recv.at[1],
            device_id=dev_peer(dev - 1),
            device_id_type=pl.DeviceIdType.MESH,
        )

    def to_right():
        return pltpu.make_async_remote_copy(
            src_ref=frames_ref.at[pl.ds(count_frames - RAD, RAD)],
            dst_ref=halo_left,
            send_sem=halo_send.at[1],
            recv_sem=halo_recv.at[0],
            device_id=dev_peer(dev + 1),
            device_id_type=pl.DeviceIdType.MESH,
        )

    @pl.when(has_left)
    def _():
        to_left().start()

    @pl.when(has_right)
    def _():
        to_right().start()

    @pl.when(jnp.logical_not(has_left))
    def _():
        halo_left[...] = jnp.zeros(halo_left.shape, halo_left.dtype)

    @pl.when(jnp.logical_not(has_right))
    def _():
        halo_right[...] = jnp.zeros(halo_right.shape, halo_right.dtype)

    def y_copy(direction, row, chunk):
        slot = row * n_dz + chunk
        target = up if direction == 0 else down
        return pltpu.make_async_remote_copy(
            src_ref=out_ref.at[slot],
            dst_ref=out_ref.at[slot],
            send_sem=y_send.at[direction * n_dy * n_dz + slot],
            recv_sem=y_recv.at[slot],
            device_id=(section, grp, target, dz),
            device_id_type=pl.DeviceIdType.MESH,
        )

    def y_own(direction):
        target = up if direction == 0 else down
        return pltpu.make_async_remote_copy(
            src_ref=half_ref,
            dst_ref=out_ref.at[dev],
            send_sem=y_send.at[direction * n_dy * n_dz + dev],
            recv_sem=y_recv.at[dev],
            device_id=(section, grp, target, dz),
            device_id_type=pl.DeviceIdType.MESH,
        )

    for direction in (0, 1):
        y_own(direction).start()
    for step in range(1, n_dz):
        source = (dz + n_dz - step) % n_dz
        z_copy(source, source).wait_recv()
        for direction in (0, 1):
            y_copy(direction, dy, source).start()
        pair_copy(dy * n_dz + source, out_ref.at[dy * n_dz + source]).start()
    own.wait()
    for step in range(1, n_dz):
        z_copy((dz + step) % n_dz, dz).wait_send()

    @pl.when(has_left)
    def _():
        to_right_of_left = pltpu.make_async_remote_copy(
            src_ref=frames_ref.at[pl.ds(0, RAD)],
            dst_ref=halo_left,
            send_sem=halo_send.at[1],
            recv_sem=halo_recv.at[0],
            device_id=dev_peer(dev - 1),
            device_id_type=pl.DeviceIdType.MESH,
        )
        to_right_of_left.wait_recv()
        to_left().wait_send()

    @pl.when(has_right)
    def _():
        to_left_of_right = pltpu.make_async_remote_copy(
            src_ref=frames_ref.at[pl.ds(0, RAD)],
            dst_ref=halo_right,
            send_sem=halo_send.at[0],
            recv_sem=halo_recv.at[1],
            device_id=dev_peer(dev + 1),
            device_id_type=pl.DeviceIdType.MESH,
        )
        to_left_of_right.wait_recv()
        to_right().wait_send()

    weights = retention_weights()

    row_block = 32

    def smooth_rows(block, carry):
        rows = pl.ds(pl.multiple_of(block * row_block, row_block), row_block)

        def padded_frame(place):
            if place < RAD:
                return halo_left[place, rows, :]
            if place < RAD + count_frames:
                return frames_ref[place - RAD, rows, :]
            return halo_right[place - RAD - count_frames, rows, :]

        for frame in range(count_frames):
            total = weights[0] * padded_frame(frame).astype(jnp.float32)
            for offset in range(1, 2 * RAD + 1):
                total = total + weights[offset] * padded_frame(frame + offset).astype(jnp.float32)
            own_scans[frame, rows, :] = total.astype(own_scans.dtype)
        return carry

    lax.fori_loop(0, own_scans.shape[1] // row_block, smooth_rows, 0)

    swap = pltpu.make_async_remote_copy(
        src_ref=own_scans,
        dst_ref=partner_scans,
        send_sem=swap_send,
        recv_sem=swap_recv,
        device_id=(partner_section, grp, dy, dz),
        device_id_type=pl.DeviceIdType.MESH,
    )
    swap.start()
    relay = n_dz // 2
    for chunk in range(n_dz):
        y_copy(0, down, chunk).wait_recv()
        if chunk < relay:
            y_copy(0, down, chunk).start()
        pair_copy(down * n_dz + chunk, out_ref.at[down * n_dz + chunk]).start()
        y_copy(1, up, chunk).wait_recv()
        if chunk >= relay:
            y_copy(1, up, chunk).start()
        pair_copy(up * n_dz + chunk, out_ref.at[up * n_dz + chunk]).start()
    swap.wait()

    half = own_scans.shape[1]

    def level_frame(frame, carry):
        for level in range(SCALES):
            table = kernels_ref[level]
            acc = jnp.dot(table[:, :half], own_scans[frame], preferred_element_type=jnp.float32)
            acc = acc + jnp.dot(
                table[:, half:], partner_scans[frame], preferred_element_type=jnp.float32
            )
            wave_ref[level, frame] = acc.astype(wave_ref.dtype)
        return carry

    lax.fori_loop(0, count_frames, level_frame, 0)

    opposite = (dy + 2) % n_dy
    for chunk in range(n_dz):
        y_copy(0, opposite, chunk).wait_recv()
        pair_copy(opposite * n_dz + chunk, out_ref.at[opposite * n_dz + chunk]).start()
    for direction in (0, 1):
        for chunk in range(n_dz):
            y_copy(direction, dy, chunk).wait_send()
    for chunk in range(relay):
        y_copy(0, down, chunk).wait_send()
    for chunk in range(relay, n_dz):
        y_copy(1, up, chunk).wait_send()
    for slot in range(n_dev):
        pair_copy(slot, half_ref).wait_recv()
    for slot in range(n_dev):
        pair_copy(slot, half_ref).wait_send()


def frame_work(frames, kernels, half):
    sizes = (lax.axis_size("section"), lax.axis_size("dy"), lax.axis_size("dz"))
    n_section, n_dy, n_dz = sizes
    rows, channels = half.shape
    count_frames, mob_local, _ = frames.shape
    rows_out, other_out, wave = pl.pallas_call(
        functools.partial(frame_kernel, sizes),
        out_shape=(
            jax.ShapeDtypeStruct((n_dy * n_dz, rows, channels), half.dtype),
            jax.ShapeDtypeStruct((n_dy * n_dz, rows, channels), half.dtype),
            jax.ShapeDtypeStruct((SCALES, count_frames, mob_local, channels), jnp.bfloat16),
        ),
        in_specs=[pl.BlockSpec(memory_space=pltpu.VMEM)] * 3,
        out_specs=(pl.BlockSpec(memory_space=pltpu.VMEM),) * 3,
        scratch_shapes=[
            pltpu.VMEM((RAD, mob_local, channels), frames.dtype),
            pltpu.VMEM((RAD, mob_local, channels), frames.dtype),
            pltpu.VMEM((count_frames, mob_local, channels), jnp.bfloat16),
            pltpu.VMEM((count_frames, mob_local, channels), jnp.bfloat16),
            pltpu.SemaphoreType.DMA(()),
            pltpu.SemaphoreType.DMA((n_dz,)),
            pltpu.SemaphoreType.DMA((n_dz,)),
            pltpu.SemaphoreType.DMA((2 * n_dy * n_dz,)),
            pltpu.SemaphoreType.DMA((n_dy * n_dz,)),
            pltpu.SemaphoreType.DMA((2,)),
            pltpu.SemaphoreType.DMA((2,)),
            pltpu.SemaphoreType.DMA(()),
            pltpu.SemaphoreType.DMA(()),
            pltpu.SemaphoreType.DMA((n_dy * n_dz,)),
            pltpu.SemaphoreType.DMA((n_dy * n_dz,)),
        ],
        compiler_params=pltpu.CompilerParams(
            collective_id=1, has_side_effects=True, vmem_limit_bytes=56 * 1024 * 1024
        ),
    )(frames, kernels, half)
    return (
        rows_out.reshape(n_dy * n_dz * rows, channels),
        other_out.reshape(n_dy * n_dz * rows, channels),
        wave,
    )


def score_kernel(
    order_ref, tile_ref, block_ref, count_ref, section_ref, wave_ref, mine_ref, other_ref, out_ref
):
    slot = order_ref[pl.program_id(0)]
    live = slot < count_ref[0]
    mine = block_ref[slot] % 2 == section_ref[0]

    def score(rows_ref):
        rows = rows_ref[...]
        acc = jnp.zeros((1, PB), jnp.float32)
        for level in range(SCALES):
            cells = wave_ref[level].reshape(-1, rows.shape[1])
            scores = lax.dot_general(
                cells, rows, (((1,), (1,)), ((), ())), preferred_element_type=jnp.float32
            )
            acc = acc + jnp.sum(jnp.maximum(scores, 0.0), axis=0, keepdims=True)
        cell_count = SCALES * wave_ref.shape[1] * wave_ref.shape[2]
        out_ref[0] = acc / cell_count

    @pl.when(jnp.logical_and(live, mine))
    def _():
        score(mine_ref)

    @pl.when(jnp.logical_and(live, jnp.logical_not(mine)))
    def _():
        score(other_ref)

    @pl.when(jnp.logical_not(live))
    def _():
        out_ref[0] = jnp.zeros((1, PB), jnp.float32)


def score_pairs(wavelet_stack, my_rows, other_rows, tile_ids, block_ids, live_pairs, section_index):
    slots = tile_ids.shape[0]
    scales, frames_local, mob_local, channels = wavelet_stack.shape
    slot_ids = jnp.arange(slots, dtype=jnp.int32)
    keys = jnp.where(slot_ids < live_pairs, tile_ids * slots + slot_ids, (mob_local // TM + 1) * slots + slot_ids)
    order = jnp.argsort(keys).astype(jnp.int32)

    def visited(k, o, c):
        return o[jnp.minimum(k, c[0] - 1)]

    grid_spec = pltpu.PrefetchScalarGridSpec(
        num_scalar_prefetch=5,
        grid=(slots,),
        in_specs=[
            pl.BlockSpec(
                (scales, frames_local, TM, channels),
                lambda k, o, t, b, c, s: (0, 0, t[visited(k, o, c)], 0),
            ),
            pl.BlockSpec((PB, channels), lambda k, o, t, b, c, s: (b[visited(k, o, c)] // 2, 0)),
            pl.BlockSpec((PB, channels), lambda k, o, t, b, c, s: (b[visited(k, o, c)] // 2, 0)),
        ],
        out_specs=pl.BlockSpec((1, 1, PB), lambda k, o, t, b, c, s: (o[k], 0, 0)),
    )
    out = pl.pallas_call(
        score_kernel,
        grid_spec=grid_spec,
        out_shape=jax.ShapeDtypeStruct((slots, 1, PB), jnp.float32),
    )(
        order,
        tile_ids,
        block_ids,
        live_pairs.reshape(1),
        section_index.astype(jnp.int32).reshape(1),
        wavelet_stack,
        my_rows,
        other_rows,
    )
    return out.reshape(slots, PB)


def solution(mesh):
    section_count, grp_count, dev_count = mesh.devices.shape
    dz_count = 8 if dev_count % 8 == 0 else dev_count
    split_mesh = jax.sharding.Mesh(
        mesh.devices.reshape(section_count, grp_count, dev_count // dz_count, dz_count),
        ("section", "grp", "dy", "dz"),
    )
    placed = (
        P("grp", DEV, "section", None),
        P(DEV, None),
        P("section", "grp", DEV),
        P("section", "grp", DEV),
        P("section", "grp", DEV),
        P(),
    )
    return jax.shard_map(
        on_device, mesh=split_mesh, in_specs=placed, out_specs=P("grp", DEV), check_vma=False
    )
```

```python
import functools
import math

import jax
import jax.numpy as jnp
from jax import lax
from jax.experimental import pallas as pl
from jax.experimental.pallas import tpu as pltpu
from jax.sharding import PartitionSpec as P

MOB = 512
SCALES = 6
RAD = 4
TM = 64
PB = 128
PREC = 8192
DEV = ("dy", "dz")


retention_spread = 2.0


def extended(cells, sides, width):
    for axis, dim in sides:
        count = lax.axis_size(axis)
        ends = count - 1
        head = lax.slice_in_dim(cells, 0, width, axis=dim)
        tail = lax.slice_in_dim(cells, cells.shape[dim] - width, cells.shape[dim], axis=dim)
        cells = jnp.concatenate(
            [
                lax.ppermute(tail, axis, [(i, (i + 1) % count) for i in range(ends)]),
                cells,
                lax.ppermute(head, axis, [((i + 1) % count, i) for i in range(ends)]),
            ],
            axis=dim,
        )
    return cells


def retention_weights():
    bell_values = [
        math.exp(-0.5 * (offset / retention_spread) ** 2) for offset in range(-RAD, RAD + 1)
    ]
    bell_total = sum(bell_values)
    return [weight_value / bell_total for weight_value in bell_values]


def mobility_kernels(row_start, row_count, col_start):
    row_place = (row_start + jnp.arange(row_count, dtype=jnp.int32)).astype(jnp.float32)
    col_place = ((col_start + jnp.arange(MOB, dtype=jnp.int32)) % MOB).astype(jnp.float32)
    distance = row_place[:, None] - col_place[None, :]
    tables = []
    for level in range(SCALES):
        spread_scans = 2.0**level
        scaled = distance / spread_scans
        tables.append(
            (1.0 - scaled * scaled)
            * jnp.exp(-0.5 * scaled * scaled)
            / math.sqrt(0.75 * math.sqrt(math.pi) * spread_scans)
        )
    return jnp.stack(tables).astype(jnp.bfloat16)


def on_device(frames, templates, pair_block, pair_tile, pair_count, owner_order):
    section_index = lax.axis_index("section")
    mob_local = frames.shape[2]
    section_count = lax.axis_size("section")
    half_rows = templates.shape[0] // 2
    my_half = lax.dynamic_slice_in_dim(templates, section_index * half_rows, half_rows, 0)
    my_rows, other_rows, wavelet_stack = frame_work(frames[0], my_half)
    slots = pair_block.shape[2]
    live_pairs = pair_count[0, 0, 0]
    block_ids = pair_block[0, 0]
    tile_ids = pair_tile[0, 0]
    responses = score_pairs(
        wavelet_stack, my_rows, other_rows, tile_ids, block_ids, live_pairs, section_index
    )
    positions = jnp.take(owner_order.reshape(-1, PB), block_ids, axis=0).reshape(-1)
    groups = PREC // PB
    by_group = jnp.where(
        (positions // PB)[:, None] == jnp.arange(groups, dtype=jnp.int32)[None, :],
        responses.reshape(-1)[:, None],
        0.0,
    )
    by_lane = ((positions % PB)[:, None] == jnp.arange(PB, dtype=jnp.int32)[None, :]).astype(
        jnp.float32
    )
    placed = jnp.einsum(
        "ka,kb->ab",
        by_group,
        by_lane,
        precision=lax.Precision.HIGHEST,
        preferred_element_type=jnp.float32,
    ).reshape(-1)
    dev_count = lax.axis_size(DEV)
    return reduce_owned(placed.reshape(dev_count, 1, PREC // dev_count))


def reduce_kernel(
    sizes,
    payload_ref,
    out_ref,
    mixed,
    line,
    line_in,
    column,
    column_in,
    totals,
    pair_send,
    pair_recv,
    z_send,
    z_recv,
    y_send,
    y_recv,
    total_send,
    total_recv,
):
    n_section, n_grp, n_dy, n_dz = sizes
    cores = totals
    section = lax.axis_index("section")
    grp = lax.axis_index("grp")
    dy = lax.axis_index("dy")
    dz = lax.axis_index("dz")
    partner = (section + 1) % n_section
    owned_width = out_ref.shape[1]

    barrier = pltpu.get_barrier_semaphore()
    peers = [(partner, grp, dy, dz)]
    peers += [(section, grp, dy, (dz + step) % n_dz) for step in range(1, n_dz)]
    peers += [(section, grp, (dy + step) % n_dy, dz) for step in range(1, n_dy)]
    peers += [
        (side, (grp + step) % n_grp, dy, dz) for side in range(n_section) for step in range(1, n_grp)
    ]
    for peer in peers:
        pl.semaphore_signal(barrier, inc=1, device_id=peer, device_id_type=pl.DeviceIdType.MESH)
    pl.semaphore_wait(barrier, len(peers))

    swap = pltpu.make_async_remote_copy(
        src_ref=payload_ref,
        dst_ref=mixed,
        send_sem=pair_send,
        recv_sem=pair_recv,
        device_id=(partner, grp, dy, dz),
        device_id_type=pl.DeviceIdType.MESH,
    )
    swap.start()
    own_slot = section * n_grp + grp
    own_sum = jnp.sum(jnp.sum(jnp.sum(payload_ref[...], axis=0), axis=0), axis=1, keepdims=True)
    cores[own_slot] = jnp.broadcast_to(own_sum, (1, 128))
    cores[partner * n_grp + grp] = jnp.zeros((1, 128), jnp.float32)

    def core_copy(side, other):
        return pltpu.make_async_remote_copy(
            src_ref=cores.at[own_slot],
            dst_ref=cores.at[own_slot],
            send_sem=total_send.at[side * n_grp + other],
            recv_sem=total_recv.at[own_slot],
            device_id=(side, other, dy, dz),
            device_id_type=pl.DeviceIdType.MESH,
        )

    def core_arrival(side, other):
        slot = side * n_grp + other
        return pltpu.make_async_remote_copy(
            src_ref=cores.at[slot],
            dst_ref=cores.at[slot],
            send_sem=total_send.at[slot],
            recv_sem=total_recv.at[slot],
            device_id=(side, other, dy, dz),
            device_id_type=pl.DeviceIdType.MESH,
        )

    for side in range(n_section):
        for step in range(1, n_grp):
            core_copy(side, (grp + step) % n_grp).start()
    swap.wait()
    combined = payload_ref[...] + mixed[...]
    line[:, :, :, :owned_width] = combined
    chip_total = jnp.sum(jnp.sum(jnp.sum(combined, axis=0), axis=0), axis=1, keepdims=True)
    for side in range(n_section):
        for step in range(1, n_grp):
            core_arrival(side, (grp + step) % n_grp).wait_recv()
    lanes = lax.broadcasted_iota(jnp.int32, (1, line.shape[3] - owned_width), 1)
    spread = jnp.where(lanes == grp, chip_total, 0.0)
    for other in range(n_grp):
        other_total = cores[other] + cores[n_grp + other]
        spread = jnp.where(jnp.logical_and(lanes == other, other != grp), other_total, spread)
    line[:, :, :, owned_width:] = jnp.broadcast_to(spread[None, None], line.shape[:3] + spread.shape[1:])
    line_in[dz] = line[dz]

    def z_copy(target, source):
        return pltpu.make_async_remote_copy(
            src_ref=line.at[target],
            dst_ref=line_in.at[source],
            send_sem=z_send.at[target],
            recv_sem=z_recv.at[source],
            device_id=(section, grp, dy, target),
            device_id_type=pl.DeviceIdType.MESH,
        )

    for step in range(1, n_dz):
        z_copy((dz + step) % n_dz, dz).start()
    for step in range(1, n_dz):
        source = (dz + n_dz - step) % n_dz
        z_copy(source, source).wait_recv()
    partial = line_in[0]
    for index in range(1, n_dz):
        partial = partial + line_in[index]
    column[...] = partial
    column_in[dy] = column[dy]

    def y_copy(target, source):
        return pltpu.make_async_remote_copy(
            src_ref=column.at[target],
            dst_ref=column_in.at[source],
            send_sem=y_send.at[target],
            recv_sem=y_recv.at[source],
            device_id=(section, grp, target, dz),
            device_id_type=pl.DeviceIdType.MESH,
        )

    for step in range(1, n_dy):
        y_copy((dy + step) % n_dy, dy).start()
    for step in range(1, n_dy):
        source = (dy + n_dy - step) % n_dy
        y_copy(source, source).wait_recv()
    summed = column_in[0]
    for index in range(1, n_dy):
        summed = summed + column_in[index]
    summed = summed.reshape(summed.shape[-2:])
    for step in range(1, n_dz):
        z_copy((dz + step) % n_dz, dz).wait_send()
    for step in range(1, n_dy):
        y_copy((dy + step) % n_dy, dy).wait_send()
    for side in range(n_section):
        for step in range(1, n_grp):
            core_copy(side, (grp + step) % n_grp).wait_send()
    run_totals = summed[:, owned_width:]
    run_sum = jnp.sum(run_totals, axis=1, keepdims=True)
    own_total = jnp.sum(jnp.where(lanes == grp, run_totals, 0.0), axis=1, keepdims=True)
    factor = (run_sum / n_grp) / own_total
    out_ref[...] = summed[:, :owned_width] * factor


def reduce_owned(payload):
    sizes = (lax.axis_size("section"), lax.axis_size("grp"), lax.axis_size("dy"), lax.axis_size("dz"))
    n_section, n_grp, n_dy, n_dz = sizes
    rows, one, owned_width = payload.shape
    width = owned_width + 128
    lines = payload.reshape(n_dy, n_dz, one, owned_width).transpose(1, 0, 2, 3)
    return pl.pallas_call(
        functools.partial(reduce_kernel, sizes),
        out_shape=jax.ShapeDtypeStruct((1, owned_width), jnp.float32),
        in_specs=[pl.BlockSpec(memory_space=pltpu.VMEM)],
        out_specs=pl.BlockSpec(memory_space=pltpu.VMEM),
        scratch_shapes=[
            pltpu.VMEM((n_dz, n_dy, one, owned_width), jnp.float32),
            pltpu.VMEM((n_dz, n_dy, one, width), jnp.float32),
            pltpu.VMEM((n_dz, n_dy, one, width), jnp.float32),
            pltpu.VMEM((n_dy, one, width), jnp.float32),
            pltpu.VMEM((n_dy, one, width), jnp.float32),
            pltpu.VMEM((n_section * n_grp, 1, 128), jnp.float32),
            pltpu.SemaphoreType.DMA(()),
            pltpu.SemaphoreType.DMA(()),
            pltpu.SemaphoreType.DMA((n_dz,)),
            pltpu.SemaphoreType.DMA((n_dz,)),
            pltpu.SemaphoreType.DMA((n_dy,)),
            pltpu.SemaphoreType.DMA((n_dy,)),
            pltpu.SemaphoreType.DMA((n_section * n_grp,)),
            pltpu.SemaphoreType.DMA((n_section * n_grp,)),
        ],
        compiler_params=pltpu.CompilerParams(collective_id=0, has_side_effects=True),
    )(lines)


def frame_kernel(
    sizes,
    frames_ref,
    half_ref,
    out_ref,
    other_ref,
    wave_ref,
    kernels_ref,
    halo_left,
    halo_right,
    own_scans,
    partner_scans,
    own_sem,
    z_send,
    z_recv,
    y_send,
    y_recv,
    halo_send,
    halo_recv,
    swap_send,
    swap_recv,
    pair_send,
    pair_recv,
):
    n_section, n_dy, n_dz = sizes
    n_dev = n_dy * n_dz
    section = lax.axis_index("section")
    grp = lax.axis_index("grp")
    dy = lax.axis_index("dy")
    dz = lax.axis_index("dz")
    dev = dy * n_dz + dz
    partner_section = (section + 1) % n_section

    def dev_peer(index):
        return (section, grp, index // n_dz, index % n_dz)

    barrier = pltpu.get_barrier_semaphore()
    for step in range(1, n_dz):
        pl.semaphore_signal(
            barrier,
            inc=1,
            device_id=(section, grp, dy, (dz + step) % n_dz),
            device_id_type=pl.DeviceIdType.MESH,
        )
    up = (dy + 1) % n_dy
    down = (dy + n_dy - 1) % n_dy
    for row in (up, down):
        pl.semaphore_signal(
            barrier,
            inc=1,
            device_id=(section, grp, row, dz),
            device_id_type=pl.DeviceIdType.MESH,
        )
    pl.semaphore_signal(
        barrier,
        inc=1,
        device_id=(partner_section, grp, dy, dz),
        device_id_type=pl.DeviceIdType.MESH,
    )
    has_left = dev > 0
    has_right = dev < n_dev - 1
    far_left = jnp.logical_and(has_left, dz == 0)
    far_right = jnp.logical_and(has_right, dz == n_dz - 1)

    @pl.when(far_left)
    def _():
        pl.semaphore_signal(
            barrier, inc=1, device_id=dev_peer(dev - 1), device_id_type=pl.DeviceIdType.MESH
        )

    @pl.when(far_right)
    def _():
        pl.semaphore_signal(
            barrier, inc=1, device_id=dev_peer(dev + 1), device_id_type=pl.DeviceIdType.MESH
        )

    extra = far_left.astype(jnp.int32) + far_right.astype(jnp.int32)
    pl.semaphore_wait(barrier, n_dz - 1 + 2 + 1 + extra)

    own = pltpu.make_async_copy(half_ref, out_ref.at[dev], own_sem)
    own.start()

    def pair_copy(slot, source_ref):
        return pltpu.make_async_remote_copy(
            src_ref=source_ref,
            dst_ref=other_ref.at[slot],
            send_sem=pair_send.at[slot],
            recv_sem=pair_recv.at[slot],
            device_id=(partner_section, grp, dy, dz),
            device_id_type=pl.DeviceIdType.MESH,
        )

    pair_copy(dev, half_ref).start()

    def z_copy(target, source):
        return pltpu.make_async_remote_copy(
            src_ref=half_ref,
            dst_ref=out_ref.at[dy * n_dz + source],
            send_sem=z_send.at[target],
            recv_sem=z_recv.at[source],
            device_id=(section, grp, dy, target),
            device_id_type=pl.DeviceIdType.MESH,
        )

    for step in range(1, n_dz):
        z_copy((dz + step) % n_dz, dz).start()

    count_frames = frames_ref.shape[0]

    def to_left():
        return pltpu.make_async_remote_copy(
            src_ref=frames_ref.at[pl.ds(0, RAD)],
            dst_ref=halo_right,
            send_sem=halo_send.at[0],
            recv_sem=halo_recv.at[1],
            device_id=dev_peer(dev - 1),
            device_id_type=pl.DeviceIdType.MESH,
        )

    def to_right():
        return pltpu.make_async_remote_copy(
            src_ref=frames_ref.at[pl.ds(count_frames - RAD, RAD)],
            dst_ref=halo_left,
            send_sem=halo_send.at[1],
            recv_sem=halo_recv.at[0],
            device_id=dev_peer(dev + 1),
            device_id_type=pl.DeviceIdType.MESH,
        )

    @pl.when(has_left)
    def _():
        to_left().start()

    @pl.when(has_right)
    def _():
        to_right().start()

    @pl.when(jnp.logical_not(has_left))
    def _():
        halo_left[...] = jnp.zeros(halo_left.shape, halo_left.dtype)

    @pl.when(jnp.logical_not(has_right))
    def _():
        halo_right[...] = jnp.zeros(halo_right.shape, halo_right.dtype)

    def y_copy(direction, row, chunk):
        slot = row * n_dz + chunk
        target = up if direction == 0 else down
        return pltpu.make_async_remote_copy(
            src_ref=out_ref.at[slot],
            dst_ref=out_ref.at[slot],
            send_sem=y_send.at[direction * n_dy * n_dz + slot],
            recv_sem=y_recv.at[slot],
            device_id=(section, grp, target, dz),
            device_id_type=pl.DeviceIdType.MESH,
        )

    def y_own(direction):
        target = up if direction == 0 else down
        return pltpu.make_async_remote_copy(
            src_ref=half_ref,
            dst_ref=out_ref.at[dev],
            send_sem=y_send.at[direction * n_dy * n_dz + dev],
            recv_sem=y_recv.at[dev],
            device_id=(section, grp, target, dz),
            device_id_type=pl.DeviceIdType.MESH,
        )

    for direction in (0, 1):
        y_own(direction).start()
    for step in range(1, n_dz):
        source = (dz + n_dz - step) % n_dz
        z_copy(source, source).wait_recv()
        for direction in (0, 1):
            y_copy(direction, dy, source).start()
        pair_copy(dy * n_dz + source, out_ref.at[dy * n_dz + source]).start()
    own.wait()
    for step in range(1, n_dz):
        z_copy((dz + step) % n_dz, dz).wait_send()

    @pl.when(has_left)
    def _():
        to_right_of_left = pltpu.make_async_remote_copy(
            src_ref=frames_ref.at[pl.ds(0, RAD)],
            dst_ref=halo_left,
            send_sem=halo_send.at[1],
            recv_sem=halo_recv.at[0],
            device_id=dev_peer(dev - 1),
            device_id_type=pl.DeviceIdType.MESH,
        )
        to_right_of_left.wait_recv()
        to_left().wait_send()

    @pl.when(has_right)
    def _():
        to_left_of_right = pltpu.make_async_remote_copy(
            src_ref=frames_ref.at[pl.ds(0, RAD)],
            dst_ref=halo_right,
            send_sem=halo_send.at[0],
            recv_sem=halo_recv.at[1],
            device_id=dev_peer(dev + 1),
            device_id_type=pl.DeviceIdType.MESH,
        )
        to_left_of_right.wait_recv()
        to_right().wait_send()

    mob_rows = kernels_ref.shape[1]
    mob_all = kernels_ref.shape[2]
    row_place = (
        section * mob_rows + lax.broadcasted_iota(jnp.int32, (mob_rows, mob_all), 0)
    ).astype(jnp.float32)
    col_place = (
        (section * mob_rows + lax.broadcasted_iota(jnp.int32, (mob_rows, mob_all), 1)) % mob_all
    ).astype(jnp.float32)
    distance = row_place - col_place
    for level in range(SCALES):
        spread_scans = 2.0**level
        scaled = distance / spread_scans
        kernels_ref[level] = (
            (1.0 - scaled * scaled)
            * jnp.exp(-0.5 * scaled * scaled)
            / math.sqrt(0.75 * math.sqrt(math.pi) * spread_scans)
        ).astype(kernels_ref.dtype)

    weights = retention_weights()

    row_block = 32

    def smooth_rows(block, carry):
        rows = pl.ds(pl.multiple_of(block * row_block, row_block), row_block)

        def padded_frame(place):
            if place < RAD:
                return halo_left[place, rows, :]
            if place < RAD + count_frames:
                return frames_ref[place - RAD, rows, :]
            return halo_right[place - RAD - count_frames, rows, :]

        for frame in range(count_frames):
            total = weights[0] * padded_frame(frame).astype(jnp.float32)
            for offset in range(1, 2 * RAD + 1):
                total = total + weights[offset] * padded_frame(frame + offset).astype(jnp.float32)
            own_scans[frame, rows, :] = total.astype(own_scans.dtype)
        return carry

    lax.fori_loop(0, own_scans.shape[1] // row_block, smooth_rows, 0)

    swap = pltpu.make_async_remote_copy(
        src_ref=own_scans,
        dst_ref=partner_scans,
        send_sem=swap_send,
        recv_sem=swap_recv,
        device_id=(partner_section, grp, dy, dz),
        device_id_type=pl.DeviceIdType.MESH,
    )
    swap.start()
    relay = n_dz // 2
    for chunk in range(n_dz):
        y_copy(0, down, chunk).wait_recv()
        if chunk < relay:
            y_copy(0, down, chunk).start()
        pair_copy(down * n_dz + chunk, out_ref.at[down * n_dz + chunk]).start()
        y_copy(1, up, chunk).wait_recv()
        if chunk >= relay:
            y_copy(1, up, chunk).start()
        pair_copy(up * n_dz + chunk, out_ref.at[up * n_dz + chunk]).start()
    swap.wait()

    half = own_scans.shape[1]

    def level_frame(frame, carry):
        for level in range(SCALES):
            table = kernels_ref[level]
            acc = jnp.dot(table[:, :half], own_scans[frame], preferred_element_type=jnp.float32)
            acc = acc + jnp.dot(
                table[:, half:], partner_scans[frame], preferred_element_type=jnp.float32
            )
            wave_ref[level, frame] = acc.astype(wave_ref.dtype)
        return carry

    lax.fori_loop(0, count_frames, level_frame, 0)

    opposite = (dy + 2) % n_dy
    for chunk in range(n_dz):
        y_copy(0, opposite, chunk).wait_recv()
        pair_copy(opposite * n_dz + chunk, out_ref.at[opposite * n_dz + chunk]).start()
    for direction in (0, 1):
        for chunk in range(n_dz):
            y_copy(direction, dy, chunk).wait_send()
    for chunk in range(relay):
        y_copy(0, down, chunk).wait_send()
    for chunk in range(relay, n_dz):
        y_copy(1, up, chunk).wait_send()
    for slot in range(n_dev):
        pair_copy(slot, half_ref).wait_recv()
    for slot in range(n_dev):
        pair_copy(slot, half_ref).wait_send()


def frame_work(frames, half):
    sizes = (lax.axis_size("section"), lax.axis_size("dy"), lax.axis_size("dz"))
    n_section, n_dy, n_dz = sizes
    rows, channels = half.shape
    count_frames, mob_local, _ = frames.shape
    rows_out, other_out, wave = pl.pallas_call(
        functools.partial(frame_kernel, sizes),
        out_shape=(
            jax.ShapeDtypeStruct((n_dy * n_dz, rows, channels), half.dtype),
            jax.ShapeDtypeStruct((n_dy * n_dz, rows, channels), half.dtype),
            jax.ShapeDtypeStruct((SCALES, count_frames, mob_local, channels), jnp.bfloat16),
        ),
        in_specs=[pl.BlockSpec(memory_space=pltpu.VMEM)] * 2,
        out_specs=(pl.BlockSpec(memory_space=pltpu.VMEM),) * 3,
        scratch_shapes=[
            pltpu.VMEM((SCALES, mob_local, 2 * mob_local), jnp.bfloat16),
            pltpu.VMEM((RAD, mob_local, channels), frames.dtype),
            pltpu.VMEM((RAD, mob_local, channels), frames.dtype),
            pltpu.VMEM((count_frames, mob_local, channels), jnp.bfloat16),
            pltpu.VMEM((count_frames, mob_local, channels), jnp.bfloat16),
            pltpu.SemaphoreType.DMA(()),
            pltpu.SemaphoreType.DMA((n_dz,)),
            pltpu.SemaphoreType.DMA((n_dz,)),
            pltpu.SemaphoreType.DMA((2 * n_dy * n_dz,)),
            pltpu.SemaphoreType.DMA((n_dy * n_dz,)),
            pltpu.SemaphoreType.DMA((2,)),
            pltpu.SemaphoreType.DMA((2,)),
            pltpu.SemaphoreType.DMA(()),
            pltpu.SemaphoreType.DMA(()),
            pltpu.SemaphoreType.DMA((n_dy * n_dz,)),
            pltpu.SemaphoreType.DMA((n_dy * n_dz,)),
        ],
        compiler_params=pltpu.CompilerParams(
            collective_id=1, has_side_effects=True, vmem_limit_bytes=56 * 1024 * 1024
        ),
    )(frames, half)
    return (
        rows_out.reshape(n_dy * n_dz * rows, channels),
        other_out.reshape(n_dy * n_dz * rows, channels),
        wave,
    )


def score_kernel(
    order_ref, tile_ref, block_ref, count_ref, section_ref, wave_ref, mine_ref, other_ref, out_ref
):
    slot = order_ref[pl.program_id(0)]
    live = slot < count_ref[0]
    mine = block_ref[slot] % 2 == section_ref[0]

    def score(rows_ref):
        rows = rows_ref[...]
        acc = jnp.zeros((1, PB), jnp.float32)
        for level in range(SCALES):
            cells = wave_ref[level].reshape(-1, rows.shape[1])
            scores = lax.dot_general(
                cells, rows, (((1,), (1,)), ((), ())), preferred_element_type=jnp.float32
            )
            acc = acc + jnp.sum(jnp.maximum(scores, 0.0), axis=0, keepdims=True)
        cell_count = SCALES * wave_ref.shape[1] * wave_ref.shape[2]
        out_ref[0] = acc / cell_count

    @pl.when(jnp.logical_and(live, mine))
    def _():
        score(mine_ref)

    @pl.when(jnp.logical_and(live, jnp.logical_not(mine)))
    def _():
        score(other_ref)

    @pl.when(jnp.logical_not(live))
    def _():
        out_ref[0] = jnp.zeros((1, PB), jnp.float32)


def score_pairs(wavelet_stack, my_rows, other_rows, tile_ids, block_ids, live_pairs, section_index):
    slots = tile_ids.shape[0]
    scales, frames_local, mob_local, channels = wavelet_stack.shape
    slot_ids = jnp.arange(slots, dtype=jnp.int32)
    keys = jnp.where(slot_ids < live_pairs, tile_ids * slots + slot_ids, (mob_local // TM + 1) * slots + slot_ids)
    order = jnp.argsort(keys).astype(jnp.int32)

    def visited(k, o, c):
        return o[jnp.minimum(k, c[0] - 1)]

    grid_spec = pltpu.PrefetchScalarGridSpec(
        num_scalar_prefetch=5,
        grid=(slots,),
        in_specs=[
            pl.BlockSpec(
                (scales, frames_local, TM, channels),
                lambda k, o, t, b, c, s: (0, 0, t[visited(k, o, c)], 0),
            ),
            pl.BlockSpec((PB, channels), lambda k, o, t, b, c, s: (b[visited(k, o, c)] // 2, 0)),
            pl.BlockSpec((PB, channels), lambda k, o, t, b, c, s: (b[visited(k, o, c)] // 2, 0)),
        ],
        out_specs=pl.BlockSpec((1, 1, PB), lambda k, o, t, b, c, s: (o[k], 0, 0)),
    )
    out = pl.pallas_call(
        score_kernel,
        grid_spec=grid_spec,
        out_shape=jax.ShapeDtypeStruct((slots, 1, PB), jnp.float32),
    )(
        order,
        tile_ids,
        block_ids,
        live_pairs.reshape(1),
        section_index.astype(jnp.int32).reshape(1),
        wavelet_stack,
        my_rows,
        other_rows,
    )
    return out.reshape(slots, PB)


def solution(mesh):
    section_count, grp_count, dev_count = mesh.devices.shape
    dz_count = 8 if dev_count % 8 == 0 else dev_count
    split_mesh = jax.sharding.Mesh(
        mesh.devices.reshape(section_count, grp_count, dev_count // dz_count, dz_count),
        ("section", "grp", "dy", "dz"),
    )
    placed = (
        P("grp", DEV, "section", None),
        P(DEV, None),
        P("section", "grp", DEV),
        P("section", "grp", DEV),
        P("section", "grp", DEV),
        P(),
    )
    return jax.shard_map(
        on_device, mesh=split_mesh, in_specs=placed, out_specs=P("grp", DEV), check_vma=False
    )
```

```python
import functools
import math

import jax
import jax.numpy as jnp
from jax import lax
from jax.experimental import pallas as pl
from jax.experimental.pallas import tpu as pltpu
from jax.sharding import PartitionSpec as P

MOB = 512
SCALES = 6
RAD = 4
TM = 64
PB = 128
PREC = 8192
DEV = ("dy", "dz")


retention_spread = 2.0


def extended(cells, sides, width):
    for axis, dim in sides:
        count = lax.axis_size(axis)
        ends = count - 1
        head = lax.slice_in_dim(cells, 0, width, axis=dim)
        tail = lax.slice_in_dim(cells, cells.shape[dim] - width, cells.shape[dim], axis=dim)
        cells = jnp.concatenate(
            [
                lax.ppermute(tail, axis, [(i, (i + 1) % count) for i in range(ends)]),
                cells,
                lax.ppermute(head, axis, [((i + 1) % count, i) for i in range(ends)]),
            ],
            axis=dim,
        )
    return cells


def retention_weights():
    bell_values = [
        math.exp(-0.5 * (offset / retention_spread) ** 2) for offset in range(-RAD, RAD + 1)
    ]
    bell_total = sum(bell_values)
    return [weight_value / bell_total for weight_value in bell_values]


def mobility_kernels(row_start, row_count, col_start):
    row_place = (row_start + jnp.arange(row_count, dtype=jnp.int32)).astype(jnp.float32)
    col_place = ((col_start + jnp.arange(MOB, dtype=jnp.int32)) % MOB).astype(jnp.float32)
    distance = row_place[:, None] - col_place[None, :]
    tables = []
    for level in range(SCALES):
        spread_scans = 2.0**level
        scaled = distance / spread_scans
        tables.append(
            (1.0 - scaled * scaled)
            * jnp.exp(-0.5 * scaled * scaled)
            / math.sqrt(0.75 * math.sqrt(math.pi) * spread_scans)
        )
    return jnp.stack(tables).astype(jnp.bfloat16)


def on_device(frames, templates, pair_block, pair_tile, pair_count, owner_order):
    section_index = lax.axis_index("section")
    mob_local = frames.shape[2]
    section_count = lax.axis_size("section")
    my_rows, other_rows, wavelet_stack = frame_work(frames[0], templates)
    slots = pair_block.shape[2]
    live_pairs = pair_count[0, 0, 0]
    block_ids = pair_block[0, 0]
    tile_ids = pair_tile[0, 0]
    responses = score_pairs(
        wavelet_stack, my_rows, other_rows, tile_ids, block_ids, live_pairs, section_index
    )
    positions = jnp.take(owner_order.reshape(-1, PB), block_ids, axis=0).reshape(-1)
    groups = PREC // PB
    by_group = jnp.where(
        (positions // PB)[:, None] == jnp.arange(groups, dtype=jnp.int32)[None, :],
        responses.reshape(-1)[:, None],
        0.0,
    )
    by_lane = ((positions % PB)[:, None] == jnp.arange(PB, dtype=jnp.int32)[None, :]).astype(
        jnp.float32
    )
    placed = jnp.einsum(
        "ka,kb->ab",
        by_group,
        by_lane,
        precision=lax.Precision.HIGHEST,
        preferred_element_type=jnp.float32,
    ).reshape(-1)
    dev_count = lax.axis_size(DEV)
    return reduce_owned(placed.reshape(dev_count, 1, PREC // dev_count))


def reduce_kernel(
    sizes,
    payload_ref,
    out_ref,
    mixed,
    line,
    line_in,
    column,
    column_in,
    totals,
    pair_send,
    pair_recv,
    z_send,
    z_recv,
    y_send,
    y_recv,
    total_send,
    total_recv,
):
    n_section, n_grp, n_dy, n_dz = sizes
    cores = totals
    section = lax.axis_index("section")
    grp = lax.axis_index("grp")
    dy = lax.axis_index("dy")
    dz = lax.axis_index("dz")
    partner = (section + 1) % n_section
    owned_width = out_ref.shape[1]

    barrier = pltpu.get_barrier_semaphore()
    peers = [(partner, grp, dy, dz)]
    peers += [(section, grp, dy, (dz + step) % n_dz) for step in range(1, n_dz)]
    peers += [(section, grp, (dy + step) % n_dy, dz) for step in range(1, n_dy)]
    peers += [
        (side, (grp + step) % n_grp, dy, dz) for side in range(n_section) for step in range(1, n_grp)
    ]
    for peer in peers:
        pl.semaphore_signal(barrier, inc=1, device_id=peer, device_id_type=pl.DeviceIdType.MESH)
    pl.semaphore_wait(barrier, len(peers))

    swap = pltpu.make_async_remote_copy(
        src_ref=payload_ref,
        dst_ref=mixed,
        send_sem=pair_send,
        recv_sem=pair_recv,
        device_id=(partner, grp, dy, dz),
        device_id_type=pl.DeviceIdType.MESH,
    )
    swap.start()
    own_slot = section * n_grp + grp
    own_sum = jnp.sum(jnp.sum(jnp.sum(payload_ref[...], axis=0), axis=0), axis=1, keepdims=True)
    cores[own_slot] = jnp.broadcast_to(own_sum, (1, 128))
    cores[partner * n_grp + grp] = jnp.zeros((1, 128), jnp.float32)

    def core_copy(side, other):
        return pltpu.make_async_remote_copy(
            src_ref=cores.at[own_slot],
            dst_ref=cores.at[own_slot],
            send_sem=total_send.at[side * n_grp + other],
            recv_sem=total_recv.at[own_slot],
            device_id=(side, other, dy, dz),
            device_id_type=pl.DeviceIdType.MESH,
        )

    def core_arrival(side, other):
        slot = side * n_grp + other
        return pltpu.make_async_remote_copy(
            src_ref=cores.at[slot],
            dst_ref=cores.at[slot],
            send_sem=total_send.at[slot],
            recv_sem=total_recv.at[slot],
            device_id=(side, other, dy, dz),
            device_id_type=pl.DeviceIdType.MESH,
        )

    for side in range(n_section):
        for step in range(1, n_grp):
            core_copy(side, (grp + step) % n_grp).start()
    swap.wait()
    combined = payload_ref[...] + mixed[...]
    line[:, :, :, :owned_width] = combined
    chip_total = jnp.sum(jnp.sum(jnp.sum(combined, axis=0), axis=0), axis=1, keepdims=True)
    for side in range(n_section):
        for step in range(1, n_grp):
            core_arrival(side, (grp + step) % n_grp).wait_recv()
    lanes = lax.broadcasted_iota(jnp.int32, (1, line.shape[3] - owned_width), 1)
    spread = jnp.where(lanes == grp, chip_total, 0.0)
    for other in range(n_grp):
        other_total = cores[other] + cores[n_grp + other]
        spread = jnp.where(jnp.logical_and(lanes == other, other != grp), other_total, spread)
    line[:, :, :, owned_width:] = jnp.broadcast_to(spread[None, None], line.shape[:3] + spread.shape[1:])
    line_in[dz] = line[dz]

    def z_copy(target, source):
        return pltpu.make_async_remote_copy(
            src_ref=line.at[target],
            dst_ref=line_in.at[source],
            send_sem=z_send.at[target],
            recv_sem=z_recv.at[source],
            device_id=(section, grp, dy, target),
            device_id_type=pl.DeviceIdType.MESH,
        )

    for step in range(1, n_dz):
        z_copy((dz + step) % n_dz, dz).start()
    for step in range(1, n_dz):
        source = (dz + n_dz - step) % n_dz
        z_copy(source, source).wait_recv()
    partial = line_in[0]
    for index in range(1, n_dz):
        partial = partial + line_in[index]
    column[...] = partial
    column_in[dy] = column[dy]

    def y_copy(target, source):
        return pltpu.make_async_remote_copy(
            src_ref=column.at[target],
            dst_ref=column_in.at[source],
            send_sem=y_send.at[target],
            recv_sem=y_recv.at[source],
            device_id=(section, grp, target, dz),
            device_id_type=pl.DeviceIdType.MESH,
        )

    for step in range(1, n_dy):
        y_copy((dy + step) % n_dy, dy).start()
    for step in range(1, n_dy):
        source = (dy + n_dy - step) % n_dy
        y_copy(source, source).wait_recv()
    summed = column_in[0]
    for index in range(1, n_dy):
        summed = summed + column_in[index]
    summed = summed.reshape(summed.shape[-2:])
    for step in range(1, n_dz):
        z_copy((dz + step) % n_dz, dz).wait_send()
    for step in range(1, n_dy):
        y_copy((dy + step) % n_dy, dy).wait_send()
    for side in range(n_section):
        for step in range(1, n_grp):
            core_copy(side, (grp + step) % n_grp).wait_send()
    run_totals = summed[:, owned_width:]
    run_sum = jnp.sum(run_totals, axis=1, keepdims=True)
    own_total = jnp.sum(jnp.where(lanes == grp, run_totals, 0.0), axis=1, keepdims=True)
    factor = (run_sum / n_grp) / own_total
    out_ref[...] = summed[:, :owned_width] * factor


def reduce_owned(payload):
    sizes = (lax.axis_size("section"), lax.axis_size("grp"), lax.axis_size("dy"), lax.axis_size("dz"))
    n_section, n_grp, n_dy, n_dz = sizes
    rows, one, owned_width = payload.shape
    width = owned_width + 128
    lines = payload.reshape(n_dy, n_dz, one, owned_width).transpose(1, 0, 2, 3)
    return pl.pallas_call(
        functools.partial(reduce_kernel, sizes),
        out_shape=jax.ShapeDtypeStruct((1, owned_width), jnp.float32),
        in_specs=[pl.BlockSpec(memory_space=pltpu.VMEM)],
        out_specs=pl.BlockSpec(memory_space=pltpu.VMEM),
        scratch_shapes=[
            pltpu.VMEM((n_dz, n_dy, one, owned_width), jnp.float32),
            pltpu.VMEM((n_dz, n_dy, one, width), jnp.float32),
            pltpu.VMEM((n_dz, n_dy, one, width), jnp.float32),
            pltpu.VMEM((n_dy, one, width), jnp.float32),
            pltpu.VMEM((n_dy, one, width), jnp.float32),
            pltpu.VMEM((n_section * n_grp, 1, 128), jnp.float32),
            pltpu.SemaphoreType.DMA(()),
            pltpu.SemaphoreType.DMA(()),
            pltpu.SemaphoreType.DMA((n_dz,)),
            pltpu.SemaphoreType.DMA((n_dz,)),
            pltpu.SemaphoreType.DMA((n_dy,)),
            pltpu.SemaphoreType.DMA((n_dy,)),
            pltpu.SemaphoreType.DMA((n_section * n_grp,)),
            pltpu.SemaphoreType.DMA((n_section * n_grp,)),
        ],
        compiler_params=pltpu.CompilerParams(collective_id=0, has_side_effects=True),
    )(lines)


def frame_kernel(
    sizes,
    frames_ref,
    templates_ref,
    out_ref,
    other_ref,
    wave_ref,
    kernels_ref,
    halo_left,
    halo_right,
    own_scans,
    partner_scans,
    own_sem,
    z_send,
    z_recv,
    y_send,
    y_recv,
    halo_send,
    halo_recv,
    swap_send,
    swap_recv,
    pair_send,
    pair_recv,
):
    n_section, n_dy, n_dz = sizes
    n_dev = n_dy * n_dz
    section = lax.axis_index("section")
    grp = lax.axis_index("grp")
    dy = lax.axis_index("dy")
    dz = lax.axis_index("dz")
    dev = dy * n_dz + dz
    partner_section = (section + 1) % n_section
    half_rows = out_ref.shape[1]
    half_src = templates_ref.at[pl.ds(section * half_rows, half_rows)]

    def dev_peer(index):
        return (section, grp, index // n_dz, index % n_dz)

    barrier = pltpu.get_barrier_semaphore()
    for step in range(1, n_dz):
        pl.semaphore_signal(
            barrier,
            inc=1,
            device_id=(section, grp, dy, (dz + step) % n_dz),
            device_id_type=pl.DeviceIdType.MESH,
        )
    up = (dy + 1) % n_dy
    down = (dy + n_dy - 1) % n_dy
    for row in (up, down):
        pl.semaphore_signal(
            barrier,
            inc=1,
            device_id=(section, grp, row, dz),
            device_id_type=pl.DeviceIdType.MESH,
        )
    pl.semaphore_signal(
        barrier,
        inc=1,
        device_id=(partner_section, grp, dy, dz),
        device_id_type=pl.DeviceIdType.MESH,
    )
    has_left = dev > 0
    has_right = dev < n_dev - 1
    far_left = jnp.logical_and(has_left, dz == 0)
    far_right = jnp.logical_and(has_right, dz == n_dz - 1)

    @pl.when(far_left)
    def _():
        pl.semaphore_signal(
            barrier, inc=1, device_id=dev_peer(dev - 1), device_id_type=pl.DeviceIdType.MESH
        )

    @pl.when(far_right)
    def _():
        pl.semaphore_signal(
            barrier, inc=1, device_id=dev_peer(dev + 1), device_id_type=pl.DeviceIdType.MESH
        )

    extra = far_left.astype(jnp.int32) + far_right.astype(jnp.int32)
    pl.semaphore_wait(barrier, n_dz - 1 + 2 + 1 + extra)

    own = pltpu.make_async_copy(half_src, out_ref.at[dev], own_sem)
    own.start()

    def pair_copy(slot, source_ref):
        return pltpu.make_async_remote_copy(
            src_ref=source_ref,
            dst_ref=other_ref.at[slot],
            send_sem=pair_send.at[slot],
            recv_sem=pair_recv.at[slot],
            device_id=(partner_section, grp, dy, dz),
            device_id_type=pl.DeviceIdType.MESH,
        )

    pair_copy(dev, half_src).start()

    def z_copy(target, source):
        return pltpu.make_async_remote_copy(
            src_ref=half_src,
            dst_ref=out_ref.at[dy * n_dz + source],
            send_sem=z_send.at[target],
            recv_sem=z_recv.at[source],
            device_id=(section, grp, dy, target),
            device_id_type=pl.DeviceIdType.MESH,
        )

    for step in range(1, n_dz):
        z_copy((dz + step) % n_dz, dz).start()

    count_frames = frames_ref.shape[0]

    def to_left():
        return pltpu.make_async_remote_copy(
            src_ref=frames_ref.at[pl.ds(0, RAD)],
            dst_ref=halo_right,
            send_sem=halo_send.at[0],
            recv_sem=halo_recv.at[1],
            device_id=dev_peer(dev - 1),
            device_id_type=pl.DeviceIdType.MESH,
        )

    def to_right():
        return pltpu.make_async_remote_copy(
            src_ref=frames_ref.at[pl.ds(count_frames - RAD, RAD)],
            dst_ref=halo_left,
            send_sem=halo_send.at[1],
            recv_sem=halo_recv.at[0],
            device_id=dev_peer(dev + 1),
            device_id_type=pl.DeviceIdType.MESH,
        )

    @pl.when(has_left)
    def _():
        to_left().start()

    @pl.when(has_right)
    def _():
        to_right().start()

    @pl.when(jnp.logical_not(has_left))
    def _():
        halo_left[...] = jnp.zeros(halo_left.shape, halo_left.dtype)

    @pl.when(jnp.logical_not(has_right))
    def _():
        halo_right[...] = jnp.zeros(halo_right.shape, halo_right.dtype)

    def y_copy(direction, row, chunk):
        slot = row * n_dz + chunk
        target = up if direction == 0 else down
        return pltpu.make_async_remote_copy(
            src_ref=out_ref.at[slot],
            dst_ref=out_ref.at[slot],
            send_sem=y_send.at[direction * n_dy * n_dz + slot],
            recv_sem=y_recv.at[slot],
            device_id=(section, grp, target, dz),
            device_id_type=pl.DeviceIdType.MESH,
        )

    def y_own(direction):
        target = up if direction == 0 else down
        return pltpu.make_async_remote_copy(
            src_ref=half_src,
            dst_ref=out_ref.at[dev],
            send_sem=y_send.at[direction * n_dy * n_dz + dev],
            recv_sem=y_recv.at[dev],
            device_id=(section, grp, target, dz),
            device_id_type=pl.DeviceIdType.MESH,
        )

    for direction in (0, 1):
        y_own(direction).start()
    for step in range(1, n_dz):
        source = (dz + n_dz - step) % n_dz
        z_copy(source, source).wait_recv()
        for direction in (0, 1):
            y_copy(direction, dy, source).start()
        pair_copy(dy * n_dz + source, out_ref.at[dy * n_dz + source]).start()
    own.wait()
    for step in range(1, n_dz):
        z_copy((dz + step) % n_dz, dz).wait_send()

    @pl.when(has_left)
    def _():
        to_right_of_left = pltpu.make_async_remote_copy(
            src_ref=frames_ref.at[pl.ds(0, RAD)],
            dst_ref=halo_left,
            send_sem=halo_send.at[1],
            recv_sem=halo_recv.at[0],
            device_id=dev_peer(dev - 1),
            device_id_type=pl.DeviceIdType.MESH,
        )
        to_right_of_left.wait_recv()
        to_left().wait_send()

    @pl.when(has_right)
    def _():
        to_left_of_right = pltpu.make_async_remote_copy(
            src_ref=frames_ref.at[pl.ds(0, RAD)],
            dst_ref=halo_right,
            send_sem=halo_send.at[0],
            recv_sem=halo_recv.at[1],
            device_id=dev_peer(dev + 1),
            device_id_type=pl.DeviceIdType.MESH,
        )
        to_left_of_right.wait_recv()
        to_right().wait_send()

    mob_rows = kernels_ref.shape[1]
    mob_all = kernels_ref.shape[2]
    row_place = (
        section * mob_rows + lax.broadcasted_iota(jnp.int32, (mob_rows, mob_all), 0)
    ).astype(jnp.float32)
    col_place = (
        (section * mob_rows + lax.broadcasted_iota(jnp.int32, (mob_rows, mob_all), 1)) % mob_all
    ).astype(jnp.float32)
    distance = row_place - col_place
    for level in range(SCALES):
        spread_scans = 2.0**level
        scaled = distance / spread_scans
        kernels_ref[level] = (
            (1.0 - scaled * scaled)
            * jnp.exp(-0.5 * scaled * scaled)
            / math.sqrt(0.75 * math.sqrt(math.pi) * spread_scans)
        ).astype(kernels_ref.dtype)

    weights = retention_weights()

    row_block = 32

    def smooth_rows(block, carry):
        rows = pl.ds(pl.multiple_of(block * row_block, row_block), row_block)

        def padded_frame(place):
            if place < RAD:
                return halo_left[place, rows, :]
            if place < RAD + count_frames:
                return frames_ref[place - RAD, rows, :]
            return halo_right[place - RAD - count_frames, rows, :]

        for frame in range(count_frames):
            total = weights[0] * padded_frame(frame).astype(jnp.float32)
            for offset in range(1, 2 * RAD + 1):
                total = total + weights[offset] * padded_frame(frame + offset).astype(jnp.float32)
            own_scans[frame, rows, :] = total.astype(own_scans.dtype)
        return carry

    lax.fori_loop(0, own_scans.shape[1] // row_block, smooth_rows, 0)

    swap = pltpu.make_async_remote_copy(
        src_ref=own_scans,
        dst_ref=partner_scans,
        send_sem=swap_send,
        recv_sem=swap_recv,
        device_id=(partner_section, grp, dy, dz),
        device_id_type=pl.DeviceIdType.MESH,
    )
    swap.start()
    relay = n_dz // 2
    for chunk in range(n_dz):
        y_copy(0, down, chunk).wait_recv()
        if chunk < relay:
            y_copy(0, down, chunk).start()
        pair_copy(down * n_dz + chunk, out_ref.at[down * n_dz + chunk]).start()
        y_copy(1, up, chunk).wait_recv()
        if chunk >= relay:
            y_copy(1, up, chunk).start()
        pair_copy(up * n_dz + chunk, out_ref.at[up * n_dz + chunk]).start()
    swap.wait()

    half = own_scans.shape[1]

    def level_frame(frame, carry):
        for level in range(SCALES):
            table = kernels_ref[level]
            acc = jnp.dot(table[:, :half], own_scans[frame], preferred_element_type=jnp.float32)
            acc = acc + jnp.dot(
                table[:, half:], partner_scans[frame], preferred_element_type=jnp.float32
            )
            wave_ref[level, frame] = acc.astype(wave_ref.dtype)
        return carry

    lax.fori_loop(0, count_frames, level_frame, 0)

    opposite = (dy + 2) % n_dy
    for chunk in range(n_dz):
        y_copy(0, opposite, chunk).wait_recv()
        pair_copy(opposite * n_dz + chunk, out_ref.at[opposite * n_dz + chunk]).start()
    for direction in (0, 1):
        for chunk in range(n_dz):
            y_copy(direction, dy, chunk).wait_send()
    for chunk in range(relay):
        y_copy(0, down, chunk).wait_send()
    for chunk in range(relay, n_dz):
        y_copy(1, up, chunk).wait_send()
    for slot in range(n_dev):
        pair_copy(slot, half_src).wait_recv()
    for slot in range(n_dev):
        pair_copy(slot, half_src).wait_send()


def frame_work(frames, templates):
    sizes = (lax.axis_size("section"), lax.axis_size("dy"), lax.axis_size("dz"))
    n_section, n_dy, n_dz = sizes
    rows, channels = templates.shape[0] // 2, templates.shape[1]
    half = templates
    count_frames, mob_local, _ = frames.shape
    rows_out, other_out, wave = pl.pallas_call(
        functools.partial(frame_kernel, sizes),
        out_shape=(
            jax.ShapeDtypeStruct((n_dy * n_dz, rows, channels), half.dtype),
            jax.ShapeDtypeStruct((n_dy * n_dz, rows, channels), half.dtype),
            jax.ShapeDtypeStruct((SCALES, count_frames, mob_local, channels), jnp.bfloat16),
        ),
        in_specs=[pl.BlockSpec(memory_space=pltpu.VMEM)] * 2,
        out_specs=(pl.BlockSpec(memory_space=pltpu.VMEM),) * 3,
        scratch_shapes=[
            pltpu.VMEM((SCALES, mob_local, 2 * mob_local), jnp.bfloat16),
            pltpu.VMEM((RAD, mob_local, channels), frames.dtype),
            pltpu.VMEM((RAD, mob_local, channels), frames.dtype),
            pltpu.VMEM((count_frames, mob_local, channels), jnp.bfloat16),
            pltpu.VMEM((count_frames, mob_local, channels), jnp.bfloat16),
            pltpu.SemaphoreType.DMA(()),
            pltpu.SemaphoreType.DMA((n_dz,)),
            pltpu.SemaphoreType.DMA((n_dz,)),
            pltpu.SemaphoreType.DMA((2 * n_dy * n_dz,)),
            pltpu.SemaphoreType.DMA((n_dy * n_dz,)),
            pltpu.SemaphoreType.DMA((2,)),
            pltpu.SemaphoreType.DMA((2,)),
            pltpu.SemaphoreType.DMA(()),
            pltpu.SemaphoreType.DMA(()),
            pltpu.SemaphoreType.DMA((n_dy * n_dz,)),
            pltpu.SemaphoreType.DMA((n_dy * n_dz,)),
        ],
        compiler_params=pltpu.CompilerParams(
            collective_id=1, has_side_effects=True, vmem_limit_bytes=56 * 1024 * 1024
        ),
    )(frames, templates)
    return (
        rows_out.reshape(n_dy * n_dz * rows, channels),
        other_out.reshape(n_dy * n_dz * rows, channels),
        wave,
    )


def score_kernel(
    order_ref, tile_ref, block_ref, count_ref, section_ref, wave_ref, mine_ref, other_ref, out_ref
):
    slot = order_ref[pl.program_id(0)]
    live = slot < count_ref[0]
    mine = block_ref[slot] % 2 == section_ref[0]

    def score(rows_ref):
        rows = rows_ref[...]
        acc = jnp.zeros((1, PB), jnp.float32)
        for level in range(SCALES):
            cells = wave_ref[level].reshape(-1, rows.shape[1])
            scores = lax.dot_general(
                cells, rows, (((1,), (1,)), ((), ())), preferred_element_type=jnp.float32
            )
            acc = acc + jnp.sum(jnp.maximum(scores, 0.0), axis=0, keepdims=True)
        cell_count = SCALES * wave_ref.shape[1] * wave_ref.shape[2]
        out_ref[0] = acc / cell_count

    @pl.when(jnp.logical_and(live, mine))
    def _():
        score(mine_ref)

    @pl.when(jnp.logical_and(live, jnp.logical_not(mine)))
    def _():
        score(other_ref)

    @pl.when(jnp.logical_not(live))
    def _():
        out_ref[0] = jnp.zeros((1, PB), jnp.float32)


def score_pairs(wavelet_stack, my_rows, other_rows, tile_ids, block_ids, live_pairs, section_index):
    slots = tile_ids.shape[0]
    scales, frames_local, mob_local, channels = wavelet_stack.shape
    slot_ids = jnp.arange(slots, dtype=jnp.int32)
    keys = jnp.where(slot_ids < live_pairs, tile_ids * slots + slot_ids, (mob_local // TM + 1) * slots + slot_ids)
    order = jnp.argsort(keys).astype(jnp.int32)

    def visited(k, o, c):
        return o[jnp.minimum(k, c[0] - 1)]

    grid_spec = pltpu.PrefetchScalarGridSpec(
        num_scalar_prefetch=5,
        grid=(slots,),
        in_specs=[
            pl.BlockSpec(
                (scales, frames_local, TM, channels),
                lambda k, o, t, b, c, s: (0, 0, t[visited(k, o, c)], 0),
            ),
            pl.BlockSpec((PB, channels), lambda k, o, t, b, c, s: (b[visited(k, o, c)] // 2, 0)),
            pl.BlockSpec((PB, channels), lambda k, o, t, b, c, s: (b[visited(k, o, c)] // 2, 0)),
        ],
        out_specs=pl.BlockSpec((1, 1, PB), lambda k, o, t, b, c, s: (o[k], 0, 0)),
    )
    out = pl.pallas_call(
        score_kernel,
        grid_spec=grid_spec,
        out_shape=jax.ShapeDtypeStruct((slots, 1, PB), jnp.float32),
    )(
        order,
        tile_ids,
        block_ids,
        live_pairs.reshape(1),
        section_index.astype(jnp.int32).reshape(1),
        wavelet_stack,
        my_rows,
        other_rows,
    )
    return out.reshape(slots, PB)


def solution(mesh):
    section_count, grp_count, dev_count = mesh.devices.shape
    dz_count = 8 if dev_count % 8 == 0 else dev_count
    split_mesh = jax.sharding.Mesh(
        mesh.devices.reshape(section_count, grp_count, dev_count // dz_count, dz_count),
        ("section", "grp", "dy", "dz"),
    )
    placed = (
        P("grp", DEV, "section", None),
        P(DEV, None),
        P("section", "grp", DEV),
        P("section", "grp", DEV),
        P("section", "grp", DEV),
        P(),
    )
    return jax.shard_map(
        on_device, mesh=split_mesh, in_specs=placed, out_specs=P("grp", DEV), check_vma=False
    )
```

```python
import functools
import math

import jax
import jax.numpy as jnp
from jax import lax
from jax.experimental import pallas as pl
from jax.experimental.pallas import tpu as pltpu
from jax.sharding import PartitionSpec as P

MOB = 512
SCALES = 6
RAD = 4
TM = 64
PB = 128
PREC = 8192
DEV = ("dy", "dz")


retention_spread = 2.0


def extended(cells, sides, width):
    for axis, dim in sides:
        count = lax.axis_size(axis)
        ends = count - 1
        head = lax.slice_in_dim(cells, 0, width, axis=dim)
        tail = lax.slice_in_dim(cells, cells.shape[dim] - width, cells.shape[dim], axis=dim)
        cells = jnp.concatenate(
            [
                lax.ppermute(tail, axis, [(i, (i + 1) % count) for i in range(ends)]),
                cells,
                lax.ppermute(head, axis, [((i + 1) % count, i) for i in range(ends)]),
            ],
            axis=dim,
        )
    return cells


def retention_weights():
    bell_values = [
        math.exp(-0.5 * (offset / retention_spread) ** 2) for offset in range(-RAD, RAD + 1)
    ]
    bell_total = sum(bell_values)
    return [weight_value / bell_total for weight_value in bell_values]


def mobility_kernels(row_start, row_count, col_start):
    row_place = (row_start + jnp.arange(row_count, dtype=jnp.int32)).astype(jnp.float32)
    col_place = ((col_start + jnp.arange(MOB, dtype=jnp.int32)) % MOB).astype(jnp.float32)
    distance = row_place[:, None] - col_place[None, :]
    tables = []
    for level in range(SCALES):
        spread_scans = 2.0**level
        scaled = distance / spread_scans
        tables.append(
            (1.0 - scaled * scaled)
            * jnp.exp(-0.5 * scaled * scaled)
            / math.sqrt(0.75 * math.sqrt(math.pi) * spread_scans)
        )
    return jnp.stack(tables).astype(jnp.bfloat16)


def on_device(frames, templates, pair_block, pair_tile, pair_count, owner_order):
    section_index = lax.axis_index("section")
    mob_local = frames.shape[2]
    section_count = lax.axis_size("section")
    my_rows, other_rows, wavelet_stack = frame_work(frames[0], templates)
    slots = pair_block.shape[2]
    live_pairs = pair_count[0, 0, 0]
    block_ids = pair_block[0, 0]
    tile_ids = pair_tile[0, 0]
    responses = score_pairs(
        wavelet_stack, my_rows, other_rows, tile_ids, block_ids, live_pairs, section_index
    )
    positions = jnp.take(owner_order.reshape(-1, PB), block_ids, axis=0).reshape(-1)
    groups = PREC // PB
    n_dy, n_dz = lax.axis_size("dy"), lax.axis_size("dz")
    shard = PREC // (n_dy * n_dz)
    owner = positions // shard
    line_group = ((owner % n_dz) * n_dy + owner // n_dz) * (shard // PB) + positions % shard // PB
    by_group = jnp.where(
        line_group[:, None] == jnp.arange(groups, dtype=jnp.int32)[None, :],
        responses.reshape(-1)[:, None],
        0.0,
    )
    by_lane = ((positions % PB)[:, None] == jnp.arange(PB, dtype=jnp.int32)[None, :]).astype(
        jnp.float32
    )
    placed = jnp.einsum(
        "ka,kb->ab",
        by_group,
        by_lane,
        precision=lax.Precision.HIGHEST,
        preferred_element_type=jnp.float32,
    ).reshape(-1)
    return reduce_owned(placed.reshape(n_dz, n_dy, 1, shard))


def reduce_kernel(
    sizes,
    payload_ref,
    out_ref,
    mixed,
    line,
    line_in,
    column,
    column_in,
    totals,
    pair_send,
    pair_recv,
    z_send,
    z_recv,
    y_send,
    y_recv,
    total_send,
    total_recv,
):
    n_section, n_grp, n_dy, n_dz = sizes
    cores = totals
    section = lax.axis_index("section")
    grp = lax.axis_index("grp")
    dy = lax.axis_index("dy")
    dz = lax.axis_index("dz")
    partner = (section + 1) % n_section
    owned_width = out_ref.shape[1]

    barrier = pltpu.get_barrier_semaphore()
    peers = [(partner, grp, dy, dz)]
    peers += [(section, grp, dy, (dz + step) % n_dz) for step in range(1, n_dz)]
    peers += [(section, grp, (dy + step) % n_dy, dz) for step in range(1, n_dy)]
    peers += [
        (side, (grp + step) % n_grp, dy, dz) for side in range(n_section) for step in range(1, n_grp)
    ]
    for peer in peers:
        pl.semaphore_signal(barrier, inc=1, device_id=peer, device_id_type=pl.DeviceIdType.MESH)
    pl.semaphore_wait(barrier, len(peers))

    swap = pltpu.make_async_remote_copy(
        src_ref=payload_ref,
        dst_ref=mixed,
        send_sem=pair_send,
        recv_sem=pair_recv,
        device_id=(partner, grp, dy, dz),
        device_id_type=pl.DeviceIdType.MESH,
    )
    swap.start()
    own_slot = section * n_grp + grp
    own_sum = jnp.sum(jnp.sum(jnp.sum(payload_ref[...], axis=0), axis=0), axis=1, keepdims=True)
    cores[own_slot] = jnp.broadcast_to(own_sum, (1, 128))
    cores[partner * n_grp + grp] = jnp.zeros((1, 128), jnp.float32)

    def core_copy(side, other):
        return pltpu.make_async_remote_copy(
            src_ref=cores.at[own_slot],
            dst_ref=cores.at[own_slot],
            send_sem=total_send.at[side * n_grp + other],
            recv_sem=total_recv.at[own_slot],
            device_id=(side, other, dy, dz),
            device_id_type=pl.DeviceIdType.MESH,
        )

    def core_arrival(side, other):
        slot = side * n_grp + other
        return pltpu.make_async_remote_copy(
            src_ref=cores.at[slot],
            dst_ref=cores.at[slot],
            send_sem=total_send.at[slot],
            recv_sem=total_recv.at[slot],
            device_id=(side, other, dy, dz),
            device_id_type=pl.DeviceIdType.MESH,
        )

    for side in range(n_section):
        for step in range(1, n_grp):
            core_copy(side, (grp + step) % n_grp).start()
    swap.wait()
    combined = payload_ref[...] + mixed[...]
    line[:, :, :, :owned_width] = combined
    chip_total = jnp.sum(jnp.sum(jnp.sum(combined, axis=0), axis=0), axis=1, keepdims=True)
    for side in range(n_section):
        for step in range(1, n_grp):
            core_arrival(side, (grp + step) % n_grp).wait_recv()
    lanes = lax.broadcasted_iota(jnp.int32, (1, line.shape[3] - owned_width), 1)
    spread = jnp.where(lanes == grp, chip_total, 0.0)
    for other in range(n_grp):
        other_total = cores[other] + cores[n_grp + other]
        spread = jnp.where(jnp.logical_and(lanes == other, other != grp), other_total, spread)
    line[:, :, :, owned_width:] = jnp.broadcast_to(spread[None, None], line.shape[:3] + spread.shape[1:])
    line_in[dz] = line[dz]

    def z_copy(target, source):
        return pltpu.make_async_remote_copy(
            src_ref=line.at[target],
            dst_ref=line_in.at[source],
            send_sem=z_send.at[target],
            recv_sem=z_recv.at[source],
            device_id=(section, grp, dy, target),
            device_id_type=pl.DeviceIdType.MESH,
        )

    for step in range(1, n_dz):
        z_copy((dz + step) % n_dz, dz).start()
    for step in range(1, n_dz):
        source = (dz + n_dz - step) % n_dz
        z_copy(source, source).wait_recv()
    partial = line_in[0]
    for index in range(1, n_dz):
        partial = partial + line_in[index]
    column[...] = partial
    column_in[dy] = column[dy]

    def y_copy(target, source):
        return pltpu.make_async_remote_copy(
            src_ref=column.at[target],
            dst_ref=column_in.at[source],
            send_sem=y_send.at[target],
            recv_sem=y_recv.at[source],
            device_id=(section, grp, target, dz),
            device_id_type=pl.DeviceIdType.MESH,
        )

    for step in range(1, n_dy):
        y_copy((dy + step) % n_dy, dy).start()
    for step in range(1, n_dy):
        source = (dy + n_dy - step) % n_dy
        y_copy(source, source).wait_recv()
    summed = column_in[0]
    for index in range(1, n_dy):
        summed = summed + column_in[index]
    summed = summed.reshape(summed.shape[-2:])
    for step in range(1, n_dz):
        z_copy((dz + step) % n_dz, dz).wait_send()
    for step in range(1, n_dy):
        y_copy((dy + step) % n_dy, dy).wait_send()
    for side in range(n_section):
        for step in range(1, n_grp):
            core_copy(side, (grp + step) % n_grp).wait_send()
    run_totals = summed[:, owned_width:]
    run_sum = jnp.sum(run_totals, axis=1, keepdims=True)
    own_total = jnp.sum(jnp.where(lanes == grp, run_totals, 0.0), axis=1, keepdims=True)
    factor = (run_sum / n_grp) / own_total
    out_ref[...] = summed[:, :owned_width] * factor


def reduce_owned(payload):
    sizes = (lax.axis_size("section"), lax.axis_size("grp"), lax.axis_size("dy"), lax.axis_size("dz"))
    n_section, n_grp, n_dy, n_dz = sizes
    lines = payload
    one, owned_width = payload.shape[2:]
    width = owned_width + 128
    return pl.pallas_call(
        functools.partial(reduce_kernel, sizes),
        out_shape=jax.ShapeDtypeStruct((1, owned_width), jnp.float32),
        in_specs=[pl.BlockSpec(memory_space=pltpu.VMEM)],
        out_specs=pl.BlockSpec(memory_space=pltpu.VMEM),
        scratch_shapes=[
            pltpu.VMEM((n_dz, n_dy, one, owned_width), jnp.float32),
            pltpu.VMEM((n_dz, n_dy, one, width), jnp.float32),
            pltpu.VMEM((n_dz, n_dy, one, width), jnp.float32),
            pltpu.VMEM((n_dy, one, width), jnp.float32),
            pltpu.VMEM((n_dy, one, width), jnp.float32),
            pltpu.VMEM((n_section * n_grp, 1, 128), jnp.float32),
            pltpu.SemaphoreType.DMA(()),
            pltpu.SemaphoreType.DMA(()),
            pltpu.SemaphoreType.DMA((n_dz,)),
            pltpu.SemaphoreType.DMA((n_dz,)),
            pltpu.SemaphoreType.DMA((n_dy,)),
            pltpu.SemaphoreType.DMA((n_dy,)),
            pltpu.SemaphoreType.DMA((n_section * n_grp,)),
            pltpu.SemaphoreType.DMA((n_section * n_grp,)),
        ],
        compiler_params=pltpu.CompilerParams(collective_id=0, has_side_effects=True),
    )(lines)


def frame_kernel(
    sizes,
    frames_ref,
    templates_ref,
    out_ref,
    other_ref,
    wave_ref,
    kernels_ref,
    halo_left,
    halo_right,
    own_scans,
    partner_scans,
    own_sem,
    z_send,
    z_recv,
    y_send,
    y_recv,
    halo_send,
    halo_recv,
    swap_send,
    swap_recv,
    pair_send,
    pair_recv,
):
    n_section, n_dy, n_dz = sizes
    n_dev = n_dy * n_dz
    section = lax.axis_index("section")
    grp = lax.axis_index("grp")
    dy = lax.axis_index("dy")
    dz = lax.axis_index("dz")
    dev = dy * n_dz + dz
    partner_section = (section + 1) % n_section
    half_rows = out_ref.shape[1]
    half_src = templates_ref.at[pl.ds(section * half_rows, half_rows)]

    def dev_peer(index):
        return (section, grp, index // n_dz, index % n_dz)

    barrier = pltpu.get_barrier_semaphore()
    for step in range(1, n_dz):
        pl.semaphore_signal(
            barrier,
            inc=1,
            device_id=(section, grp, dy, (dz + step) % n_dz),
            device_id_type=pl.DeviceIdType.MESH,
        )
    up = (dy + 1) % n_dy
    down = (dy + n_dy - 1) % n_dy
    for row in (up, down):
        pl.semaphore_signal(
            barrier,
            inc=1,
            device_id=(section, grp, row, dz),
            device_id_type=pl.DeviceIdType.MESH,
        )
    pl.semaphore_signal(
        barrier,
        inc=1,
        device_id=(partner_section, grp, dy, dz),
        device_id_type=pl.DeviceIdType.MESH,
    )
    has_left = dev > 0
    has_right = dev < n_dev - 1
    far_left = jnp.logical_and(has_left, dz == 0)
    far_right = jnp.logical_and(has_right, dz == n_dz - 1)

    @pl.when(far_left)
    def _():
        pl.semaphore_signal(
            barrier, inc=1, device_id=dev_peer(dev - 1), device_id_type=pl.DeviceIdType.MESH
        )

    @pl.when(far_right)
    def _():
        pl.semaphore_signal(
            barrier, inc=1, device_id=dev_peer(dev + 1), device_id_type=pl.DeviceIdType.MESH
        )

    extra = far_left.astype(jnp.int32) + far_right.astype(jnp.int32)
    pl.semaphore_wait(barrier, n_dz - 1 + 2 + 1 + extra)

    own = pltpu.make_async_copy(half_src, out_ref.at[dev], own_sem)
    own.start()

    def pair_copy(slot, source_ref):
        return pltpu.make_async_remote_copy(
            src_ref=source_ref,
            dst_ref=other_ref.at[slot],
            send_sem=pair_send.at[slot],
            recv_sem=pair_recv.at[slot],
            device_id=(partner_section, grp, dy, dz),
            device_id_type=pl.DeviceIdType.MESH,
        )

    pair_copy(dev, half_src).start()

    def z_copy(target, source):
        return pltpu.make_async_remote_copy(
            src_ref=half_src,
            dst_ref=out_ref.at[dy * n_dz + source],
            send_sem=z_send.at[target],
            recv_sem=z_recv.at[source],
            device_id=(section, grp, dy, target),
            device_id_type=pl.DeviceIdType.MESH,
        )

    for step in range(1, n_dz):
        z_copy((dz + step) % n_dz, dz).start()

    count_frames = frames_ref.shape[0]

    def to_left():
        return pltpu.make_async_remote_copy(
            src_ref=frames_ref.at[pl.ds(0, RAD)],
            dst_ref=halo_right,
            send_sem=halo_send.at[0],
            recv_sem=halo_recv.at[1],
            device_id=dev_peer(dev - 1),
            device_id_type=pl.DeviceIdType.MESH,
        )

    def to_right():
        return pltpu.make_async_remote_copy(
            src_ref=frames_ref.at[pl.ds(count_frames - RAD, RAD)],
            dst_ref=halo_left,
            send_sem=halo_send.at[1],
            recv_sem=halo_recv.at[0],
            device_id=dev_peer(dev + 1),
            device_id_type=pl.DeviceIdType.MESH,
        )

    @pl.when(has_left)
    def _():
        to_left().start()

    @pl.when(has_right)
    def _():
        to_right().start()

    @pl.when(jnp.logical_not(has_left))
    def _():
        halo_left[...] = jnp.zeros(halo_left.shape, halo_left.dtype)

    @pl.when(jnp.logical_not(has_right))
    def _():
        halo_right[...] = jnp.zeros(halo_right.shape, halo_right.dtype)

    def y_copy(direction, row, chunk):
        slot = row * n_dz + chunk
        target = up if direction == 0 else down
        return pltpu.make_async_remote_copy(
            src_ref=out_ref.at[slot],
            dst_ref=out_ref.at[slot],
            send_sem=y_send.at[direction * n_dy * n_dz + slot],
            recv_sem=y_recv.at[slot],
            device_id=(section, grp, target, dz),
            device_id_type=pl.DeviceIdType.MESH,
        )

    def y_own(direction):
        target = up if direction == 0 else down
        return pltpu.make_async_remote_copy(
            src_ref=half_src,
            dst_ref=out_ref.at[dev],
            send_sem=y_send.at[direction * n_dy * n_dz + dev],
            recv_sem=y_recv.at[dev],
            device_id=(section, grp, target, dz),
            device_id_type=pl.DeviceIdType.MESH,
        )

    for direction in (0, 1):
        y_own(direction).start()
    for step in range(1, n_dz):
        source = (dz + n_dz - step) % n_dz
        z_copy(source, source).wait_recv()
        for direction in (0, 1):
            y_copy(direction, dy, source).start()
        pair_copy(dy * n_dz + source, out_ref.at[dy * n_dz + source]).start()
    own.wait()
    for step in range(1, n_dz):
        z_copy((dz + step) % n_dz, dz).wait_send()

    @pl.when(has_left)
    def _():
        to_right_of_left = pltpu.make_async_remote_copy(
            src_ref=frames_ref.at[pl.ds(0, RAD)],
            dst_ref=halo_left,
            send_sem=halo_send.at[1],
            recv_sem=halo_recv.at[0],
            device_id=dev_peer(dev - 1),
            device_id_type=pl.DeviceIdType.MESH,
        )
        to_right_of_left.wait_recv()
        to_left().wait_send()

    @pl.when(has_right)
    def _():
        to_left_of_right = pltpu.make_async_remote_copy(
            src_ref=frames_ref.at[pl.ds(0, RAD)],
            dst_ref=halo_right,
            send_sem=halo_send.at[0],
            recv_sem=halo_recv.at[1],
            device_id=dev_peer(dev + 1),
            device_id_type=pl.DeviceIdType.MESH,
        )
        to_left_of_right.wait_recv()
        to_right().wait_send()

    mob_rows = kernels_ref.shape[1]
    mob_all = kernels_ref.shape[2]
    row_place = (
        section * mob_rows + lax.broadcasted_iota(jnp.int32, (mob_rows, mob_all), 0)
    ).astype(jnp.float32)
    col_place = (
        (section * mob_rows + lax.broadcasted_iota(jnp.int32, (mob_rows, mob_all), 1)) % mob_all
    ).astype(jnp.float32)
    distance = row_place - col_place
    for level in range(SCALES):
        spread_scans = 2.0**level
        scaled = distance / spread_scans
        kernels_ref[level] = (
            (1.0 - scaled * scaled)
            * jnp.exp(-0.5 * scaled * scaled)
            / math.sqrt(0.75 * math.sqrt(math.pi) * spread_scans)
        ).astype(kernels_ref.dtype)

    weights = retention_weights()

    row_block = 32

    def smooth_rows(block, carry):
        rows = pl.ds(pl.multiple_of(block * row_block, row_block), row_block)

        def padded_frame(place):
            if place < RAD:
                return halo_left[place, rows, :]
            if place < RAD + count_frames:
                return frames_ref[place - RAD, rows, :]
            return halo_right[place - RAD - count_frames, rows, :]

        for frame in range(count_frames):
            total = weights[0] * padded_frame(frame).astype(jnp.float32)
            for offset in range(1, 2 * RAD + 1):
                total = total + weights[offset] * padded_frame(frame + offset).astype(jnp.float32)
            own_scans[frame, rows, :] = total.astype(own_scans.dtype)
        return carry

    lax.fori_loop(0, own_scans.shape[1] // row_block, smooth_rows, 0)

    swap = pltpu.make_async_remote_copy(
        src_ref=own_scans,
        dst_ref=partner_scans,
        send_sem=swap_send,
        recv_sem=swap_recv,
        device_id=(partner_section, grp, dy, dz),
        device_id_type=pl.DeviceIdType.MESH,
    )
    swap.start()
    relay = n_dz // 2
    for chunk in range(n_dz):
        y_copy(0, down, chunk).wait_recv()
        if chunk < relay:
            y_copy(0, down, chunk).start()
        pair_copy(down * n_dz + chunk, out_ref.at[down * n_dz + chunk]).start()
        y_copy(1, up, chunk).wait_recv()
        if chunk >= relay:
            y_copy(1, up, chunk).start()
        pair_copy(up * n_dz + chunk, out_ref.at[up * n_dz + chunk]).start()
    swap.wait()

    half = own_scans.shape[1]

    def level_frame(frame, carry):
        for level in range(SCALES):
            table = kernels_ref[level]
            acc = jnp.dot(table[:, :half], own_scans[frame], preferred_element_type=jnp.float32)
            acc = acc + jnp.dot(
                table[:, half:], partner_scans[frame], preferred_element_type=jnp.float32
            )
            wave_ref[level, frame] = acc.astype(wave_ref.dtype)
        return carry

    lax.fori_loop(0, count_frames, level_frame, 0)

    opposite = (dy + 2) % n_dy
    for chunk in range(n_dz):
        y_copy(0, opposite, chunk).wait_recv()
        pair_copy(opposite * n_dz + chunk, out_ref.at[opposite * n_dz + chunk]).start()
    for direction in (0, 1):
        for chunk in range(n_dz):
            y_copy(direction, dy, chunk).wait_send()
    for chunk in range(relay):
        y_copy(0, down, chunk).wait_send()
    for chunk in range(relay, n_dz):
        y_copy(1, up, chunk).wait_send()
    for slot in range(n_dev):
        pair_copy(slot, half_src).wait_recv()
    for slot in range(n_dev):
        pair_copy(slot, half_src).wait_send()


def frame_work(frames, templates):
    sizes = (lax.axis_size("section"), lax.axis_size("dy"), lax.axis_size("dz"))
    n_section, n_dy, n_dz = sizes
    rows, channels = templates.shape[0] // 2, templates.shape[1]
    half = templates
    count_frames, mob_local, _ = frames.shape
    rows_out, other_out, wave = pl.pallas_call(
        functools.partial(frame_kernel, sizes),
        out_shape=(
            jax.ShapeDtypeStruct((n_dy * n_dz, rows, channels), half.dtype),
            jax.ShapeDtypeStruct((n_dy * n_dz, rows, channels), half.dtype),
            jax.ShapeDtypeStruct((SCALES, count_frames, mob_local, channels), jnp.bfloat16),
        ),
        in_specs=[pl.BlockSpec(memory_space=pltpu.VMEM)] * 2,
        out_specs=(pl.BlockSpec(memory_space=pltpu.VMEM),) * 3,
        scratch_shapes=[
            pltpu.VMEM((SCALES, mob_local, 2 * mob_local), jnp.bfloat16),
            pltpu.VMEM((RAD, mob_local, channels), frames.dtype),
            pltpu.VMEM((RAD, mob_local, channels), frames.dtype),
            pltpu.VMEM((count_frames, mob_local, channels), jnp.bfloat16),
            pltpu.VMEM((count_frames, mob_local, channels), jnp.bfloat16),
            pltpu.SemaphoreType.DMA(()),
            pltpu.SemaphoreType.DMA((n_dz,)),
            pltpu.SemaphoreType.DMA((n_dz,)),
            pltpu.SemaphoreType.DMA((2 * n_dy * n_dz,)),
            pltpu.SemaphoreType.DMA((n_dy * n_dz,)),
            pltpu.SemaphoreType.DMA((2,)),
            pltpu.SemaphoreType.DMA((2,)),
            pltpu.SemaphoreType.DMA(()),
            pltpu.SemaphoreType.DMA(()),
            pltpu.SemaphoreType.DMA((n_dy * n_dz,)),
            pltpu.SemaphoreType.DMA((n_dy * n_dz,)),
        ],
        compiler_params=pltpu.CompilerParams(
            collective_id=1, has_side_effects=True, vmem_limit_bytes=56 * 1024 * 1024
        ),
    )(frames, templates)
    return (
        rows_out.reshape(n_dy * n_dz * rows, channels),
        other_out.reshape(n_dy * n_dz * rows, channels),
        wave,
    )


def score_kernel(
    order_ref, tile_ref, block_ref, count_ref, section_ref, wave_ref, mine_ref, other_ref, out_ref
):
    slot = order_ref[pl.program_id(0)]
    live = slot < count_ref[0]
    mine = block_ref[slot] % 2 == section_ref[0]

    def score(rows_ref):
        rows = rows_ref[...]
        acc = jnp.zeros((1, PB), jnp.float32)
        for level in range(SCALES):
            cells = wave_ref[level].reshape(-1, rows.shape[1])
            scores = lax.dot_general(
                cells, rows, (((1,), (1,)), ((), ())), preferred_element_type=jnp.float32
            )
            acc = acc + jnp.sum(jnp.maximum(scores, 0.0), axis=0, keepdims=True)
        cell_count = SCALES * wave_ref.shape[1] * wave_ref.shape[2]
        out_ref[0] = acc / cell_count

    @pl.when(jnp.logical_and(live, mine))
    def _():
        score(mine_ref)

    @pl.when(jnp.logical_and(live, jnp.logical_not(mine)))
    def _():
        score(other_ref)

    @pl.when(jnp.logical_not(live))
    def _():
        out_ref[0] = jnp.zeros((1, PB), jnp.float32)


def score_pairs(wavelet_stack, my_rows, other_rows, tile_ids, block_ids, live_pairs, section_index):
    slots = tile_ids.shape[0]
    scales, frames_local, mob_local, channels = wavelet_stack.shape
    slot_ids = jnp.arange(slots, dtype=jnp.int32)
    keys = jnp.where(slot_ids < live_pairs, tile_ids * slots + slot_ids, (mob_local // TM + 1) * slots + slot_ids)
    order = jnp.argsort(keys).astype(jnp.int32)

    def visited(k, o, c):
        return o[jnp.minimum(k, c[0] - 1)]

    grid_spec = pltpu.PrefetchScalarGridSpec(
        num_scalar_prefetch=5,
        grid=(slots,),
        in_specs=[
            pl.BlockSpec(
                (scales, frames_local, TM, channels),
                lambda k, o, t, b, c, s: (0, 0, t[visited(k, o, c)], 0),
            ),
            pl.BlockSpec((PB, channels), lambda k, o, t, b, c, s: (b[visited(k, o, c)] // 2, 0)),
            pl.BlockSpec((PB, channels), lambda k, o, t, b, c, s: (b[visited(k, o, c)] // 2, 0)),
        ],
        out_specs=pl.BlockSpec((1, 1, PB), lambda k, o, t, b, c, s: (o[k], 0, 0)),
    )
    out = pl.pallas_call(
        score_kernel,
        grid_spec=grid_spec,
        out_shape=jax.ShapeDtypeStruct((slots, 1, PB), jnp.float32),
    )(
        order,
        tile_ids,
        block_ids,
        live_pairs.reshape(1),
        section_index.astype(jnp.int32).reshape(1),
        wavelet_stack,
        my_rows,
        other_rows,
    )
    return out.reshape(slots, PB)


def solution(mesh):
    section_count, grp_count, dev_count = mesh.devices.shape
    dz_count = 8 if dev_count % 8 == 0 else dev_count
    split_mesh = jax.sharding.Mesh(
        mesh.devices.reshape(section_count, grp_count, dev_count // dz_count, dz_count),
        ("section", "grp", "dy", "dz"),
    )
    placed = (
        P("grp", DEV, "section", None),
        P(DEV, None),
        P("section", "grp", DEV),
        P("section", "grp", DEV),
        P("section", "grp", DEV),
        P(),
    )
    return jax.shard_map(
        on_device, mesh=split_mesh, in_specs=placed, out_specs=P("grp", DEV), check_vma=False
    )
```

```python
import functools
import math

import jax
import jax.numpy as jnp
from jax import lax
from jax.experimental import pallas as pl
from jax.experimental.pallas import tpu as pltpu
from jax.sharding import PartitionSpec as P

MOB = 512
SCALES = 6
RAD = 4
TM = 64
PB = 128
PREC = 8192
DEV = ("dy", "dz")


retention_spread = 2.0


def extended(cells, sides, width):
    for axis, dim in sides:
        count = lax.axis_size(axis)
        ends = count - 1
        head = lax.slice_in_dim(cells, 0, width, axis=dim)
        tail = lax.slice_in_dim(cells, cells.shape[dim] - width, cells.shape[dim], axis=dim)
        cells = jnp.concatenate(
            [
                lax.ppermute(tail, axis, [(i, (i + 1) % count) for i in range(ends)]),
                cells,
                lax.ppermute(head, axis, [((i + 1) % count, i) for i in range(ends)]),
            ],
            axis=dim,
        )
    return cells


def retention_weights():
    bell_values = [
        math.exp(-0.5 * (offset / retention_spread) ** 2) for offset in range(-RAD, RAD + 1)
    ]
    bell_total = sum(bell_values)
    return [weight_value / bell_total for weight_value in bell_values]


def mobility_kernels(row_start, row_count, col_start):
    row_place = (row_start + jnp.arange(row_count, dtype=jnp.int32)).astype(jnp.float32)
    col_place = ((col_start + jnp.arange(MOB, dtype=jnp.int32)) % MOB).astype(jnp.float32)
    distance = row_place[:, None] - col_place[None, :]
    tables = []
    for level in range(SCALES):
        spread_scans = 2.0**level
        scaled = distance / spread_scans
        tables.append(
            (1.0 - scaled * scaled)
            * jnp.exp(-0.5 * scaled * scaled)
            / math.sqrt(0.75 * math.sqrt(math.pi) * spread_scans)
        )
    return jnp.stack(tables).astype(jnp.bfloat16)


def on_device(frames, templates, pair_block, pair_tile, pair_count, owner_order):
    section_index = lax.axis_index("section")
    mob_local = frames.shape[2]
    section_count = lax.axis_size("section")
    my_rows, other_rows, wavelet_stack = frame_work(frames[0], templates)
    slots = pair_block.shape[2]
    live_pairs = pair_count[0, 0, 0]
    block_ids = pair_block[0, 0]
    tile_ids = pair_tile[0, 0]
    responses = score_pairs(
        wavelet_stack, my_rows, other_rows, tile_ids, block_ids, live_pairs, section_index
    )
    positions = jnp.take(owner_order.reshape(-1, PB), block_ids, axis=0).reshape(-1)
    groups = PREC // PB
    by_group = jnp.where(
        (positions // PB)[:, None] == jnp.arange(groups, dtype=jnp.int32)[None, :],
        responses.reshape(-1)[:, None],
        0.0,
    )
    by_lane = ((positions % PB)[:, None] == jnp.arange(PB, dtype=jnp.int32)[None, :]).astype(
        jnp.float32
    )
    placed = jnp.einsum(
        "ka,kb->ab",
        by_group,
        by_lane,
        precision=lax.Precision.HIGHEST,
        preferred_element_type=jnp.float32,
    ).reshape(-1)
    dev_count = lax.axis_size(DEV)
    return reduce_owned(placed.reshape(dev_count, 1, PREC // dev_count))


def reduce_kernel(
    sizes,
    payload_ref,
    out_ref,
    mixed,
    line,
    line_in,
    column,
    column_in,
    totals,
    pair_send,
    pair_recv,
    z_send,
    z_recv,
    y_send,
    y_recv,
    total_send,
    total_recv,
):
    n_section, n_grp, n_dy, n_dz = sizes
    cores = totals
    section = lax.axis_index("section")
    grp = lax.axis_index("grp")
    dy = lax.axis_index("dy")
    dz = lax.axis_index("dz")
    partner = (section + 1) % n_section
    owned_width = out_ref.shape[1]

    barrier = pltpu.get_barrier_semaphore()
    peers = [(partner, grp, dy, dz)]
    peers += [(section, grp, dy, (dz + step) % n_dz) for step in range(1, n_dz)]
    peers += [(section, grp, (dy + step) % n_dy, dz) for step in range(1, n_dy)]
    peers += [
        (side, (grp + step) % n_grp, dy, dz) for side in range(n_section) for step in range(1, n_grp)
    ]
    for peer in peers:
        pl.semaphore_signal(barrier, inc=1, device_id=peer, device_id_type=pl.DeviceIdType.MESH)
    pl.semaphore_wait(barrier, len(peers))

    swap = pltpu.make_async_remote_copy(
        src_ref=payload_ref,
        dst_ref=mixed,
        send_sem=pair_send,
        recv_sem=pair_recv,
        device_id=(partner, grp, dy, dz),
        device_id_type=pl.DeviceIdType.MESH,
    )
    swap.start()
    own_slot = section * n_grp + grp
    own_sum = jnp.sum(jnp.sum(jnp.sum(payload_ref[...], axis=0), axis=0), axis=1, keepdims=True)
    cores[own_slot] = jnp.broadcast_to(own_sum, (1, 128))
    cores[partner * n_grp + grp] = jnp.zeros((1, 128), jnp.float32)

    def core_copy(side, other):
        return pltpu.make_async_remote_copy(
            src_ref=cores.at[own_slot],
            dst_ref=cores.at[own_slot],
            send_sem=total_send.at[side * n_grp + other],
            recv_sem=total_recv.at[own_slot],
            device_id=(side, other, dy, dz),
            device_id_type=pl.DeviceIdType.MESH,
        )

    def core_arrival(side, other):
        slot = side * n_grp + other
        return pltpu.make_async_remote_copy(
            src_ref=cores.at[slot],
            dst_ref=cores.at[slot],
            send_sem=total_send.at[slot],
            recv_sem=total_recv.at[slot],
            device_id=(side, other, dy, dz),
            device_id_type=pl.DeviceIdType.MESH,
        )

    for side in range(n_section):
        for step in range(1, n_grp):
            core_copy(side, (grp + step) % n_grp).start()
    swap.wait()
    combined = payload_ref[...] + mixed[...]
    line[:, :, :, :owned_width] = combined
    chip_total = jnp.sum(jnp.sum(jnp.sum(combined, axis=0), axis=0), axis=1, keepdims=True)
    for side in range(n_section):
        for step in range(1, n_grp):
            core_arrival(side, (grp + step) % n_grp).wait_recv()
    lanes = lax.broadcasted_iota(jnp.int32, (1, line.shape[3] - owned_width), 1)
    spread = jnp.where(lanes == grp, chip_total, 0.0)
    for other in range(n_grp):
        other_total = cores[other] + cores[n_grp + other]
        spread = jnp.where(jnp.logical_and(lanes == other, other != grp), other_total, spread)
    line[:, :, :, owned_width:] = jnp.broadcast_to(spread[None, None], line.shape[:3] + spread.shape[1:])
    line_in[dz] = line[dz]

    def z_copy(target, source):
        return pltpu.make_async_remote_copy(
            src_ref=line.at[target],
            dst_ref=line_in.at[source],
            send_sem=z_send.at[target],
            recv_sem=z_recv.at[source],
            device_id=(section, grp, dy, target),
            device_id_type=pl.DeviceIdType.MESH,
        )

    for step in range(1, n_dz):
        z_copy((dz + step) % n_dz, dz).start()
    for step in range(1, n_dz):
        source = (dz + n_dz - step) % n_dz
        z_copy(source, source).wait_recv()
    partial = line_in[0]
    for index in range(1, n_dz):
        partial = partial + line_in[index]
    column[...] = partial
    column_in[dy] = column[dy]

    def y_copy(target, source):
        return pltpu.make_async_remote_copy(
            src_ref=column.at[target],
            dst_ref=column_in.at[source],
            send_sem=y_send.at[target],
            recv_sem=y_recv.at[source],
            device_id=(section, grp, target, dz),
            device_id_type=pl.DeviceIdType.MESH,
        )

    for step in range(1, n_dy):
        y_copy((dy + step) % n_dy, dy).start()
    for step in range(1, n_dy):
        source = (dy + n_dy - step) % n_dy
        y_copy(source, source).wait_recv()
    summed = column_in[0]
    for index in range(1, n_dy):
        summed = summed + column_in[index]
    summed = summed.reshape(summed.shape[-2:])
    for step in range(1, n_dz):
        z_copy((dz + step) % n_dz, dz).wait_send()
    for step in range(1, n_dy):
        y_copy((dy + step) % n_dy, dy).wait_send()
    for side in range(n_section):
        for step in range(1, n_grp):
            core_copy(side, (grp + step) % n_grp).wait_send()
    run_totals = summed[:, owned_width:]
    run_sum = jnp.sum(run_totals, axis=1, keepdims=True)
    own_total = jnp.sum(jnp.where(lanes == grp, run_totals, 0.0), axis=1, keepdims=True)
    factor = (run_sum / n_grp) / own_total
    out_ref[...] = summed[:, :owned_width] * factor


def reduce_owned(payload):
    sizes = (lax.axis_size("section"), lax.axis_size("grp"), lax.axis_size("dy"), lax.axis_size("dz"))
    n_section, n_grp, n_dy, n_dz = sizes
    rows, one, owned_width = payload.shape
    width = owned_width + 128
    lines = payload.reshape(n_dy, n_dz, one, owned_width).transpose(1, 0, 2, 3)
    return pl.pallas_call(
        functools.partial(reduce_kernel, sizes),
        out_shape=jax.ShapeDtypeStruct((1, owned_width), jnp.float32),
        in_specs=[pl.BlockSpec(memory_space=pltpu.VMEM)],
        out_specs=pl.BlockSpec(memory_space=pltpu.VMEM),
        scratch_shapes=[
            pltpu.VMEM((n_dz, n_dy, one, owned_width), jnp.float32),
            pltpu.VMEM((n_dz, n_dy, one, width), jnp.float32),
            pltpu.VMEM((n_dz, n_dy, one, width), jnp.float32),
            pltpu.VMEM((n_dy, one, width), jnp.float32),
            pltpu.VMEM((n_dy, one, width), jnp.float32),
            pltpu.VMEM((n_section * n_grp, 1, 128), jnp.float32),
            pltpu.SemaphoreType.DMA(()),
            pltpu.SemaphoreType.DMA(()),
            pltpu.SemaphoreType.DMA((n_dz,)),
            pltpu.SemaphoreType.DMA((n_dz,)),
            pltpu.SemaphoreType.DMA((n_dy,)),
            pltpu.SemaphoreType.DMA((n_dy,)),
            pltpu.SemaphoreType.DMA((n_section * n_grp,)),
            pltpu.SemaphoreType.DMA((n_section * n_grp,)),
        ],
        compiler_params=pltpu.CompilerParams(collective_id=0, has_side_effects=True),
    )(lines)


def frame_kernel(
    sizes,
    frames_ref,
    templates_ref,
    out_ref,
    other_ref,
    wave_ref,
    kernels_ref,
    halo_left,
    halo_right,
    own_scans,
    partner_scans,
    own_sem,
    z_send,
    z_recv,
    y_send,
    y_recv,
    halo_send,
    halo_recv,
    swap_send,
    swap_recv,
    pair_send,
    pair_recv,
):
    n_section, n_dy, n_dz = sizes
    n_dev = n_dy * n_dz
    section = lax.axis_index("section")
    grp = lax.axis_index("grp")
    dy = lax.axis_index("dy")
    dz = lax.axis_index("dz")
    dev = dy * n_dz + dz
    partner_section = (section + 1) % n_section
    half_rows = out_ref.shape[1]
    half_src = templates_ref.at[pl.ds(section * half_rows, half_rows)]

    def dev_peer(index):
        return (section, grp, index // n_dz, index % n_dz)

    barrier = pltpu.get_barrier_semaphore()
    for step in range(1, n_dz):
        pl.semaphore_signal(
            barrier,
            inc=1,
            device_id=(section, grp, dy, (dz + step) % n_dz),
            device_id_type=pl.DeviceIdType.MESH,
        )
    up = (dy + 1) % n_dy
    down = (dy + n_dy - 1) % n_dy
    for row in (up, down):
        pl.semaphore_signal(
            barrier,
            inc=1,
            device_id=(section, grp, row, dz),
            device_id_type=pl.DeviceIdType.MESH,
        )
    pl.semaphore_signal(
        barrier,
        inc=1,
        device_id=(partner_section, grp, dy, dz),
        device_id_type=pl.DeviceIdType.MESH,
    )
    has_left = dev > 0
    has_right = dev < n_dev - 1
    far_left = jnp.logical_and(has_left, dz == 0)
    far_right = jnp.logical_and(has_right, dz == n_dz - 1)

    @pl.when(far_left)
    def _():
        pl.semaphore_signal(
            barrier, inc=1, device_id=dev_peer(dev - 1), device_id_type=pl.DeviceIdType.MESH
        )

    @pl.when(far_right)
    def _():
        pl.semaphore_signal(
            barrier, inc=1, device_id=dev_peer(dev + 1), device_id_type=pl.DeviceIdType.MESH
        )

    extra = far_left.astype(jnp.int32) + far_right.astype(jnp.int32)
    pl.semaphore_wait(barrier, n_dz - 1 + 2 + 1 + extra)

    own = pltpu.make_async_copy(half_src, out_ref.at[dev], own_sem)
    own.start()

    def pair_copy(slot, source_ref):
        return pltpu.make_async_remote_copy(
            src_ref=source_ref,
            dst_ref=other_ref.at[slot],
            send_sem=pair_send.at[slot],
            recv_sem=pair_recv.at[slot],
            device_id=(partner_section, grp, dy, dz),
            device_id_type=pl.DeviceIdType.MESH,
        )

    pair_copy(dev, half_src).start()

    def z_copy(target, source):
        return pltpu.make_async_remote_copy(
            src_ref=half_src,
            dst_ref=out_ref.at[dy * n_dz + source],
            send_sem=z_send.at[target],
            recv_sem=z_recv.at[source],
            device_id=(section, grp, dy, target),
            device_id_type=pl.DeviceIdType.MESH,
        )

    for step in range(1, n_dz):
        z_copy((dz + step) % n_dz, dz).start()

    count_frames = frames_ref.shape[0]

    def to_left():
        return pltpu.make_async_remote_copy(
            src_ref=frames_ref.at[pl.ds(0, RAD)],
            dst_ref=halo_right,
            send_sem=halo_send.at[0],
            recv_sem=halo_recv.at[1],
            device_id=dev_peer(dev - 1),
            device_id_type=pl.DeviceIdType.MESH,
        )

    def to_right():
        return pltpu.make_async_remote_copy(
            src_ref=frames_ref.at[pl.ds(count_frames - RAD, RAD)],
            dst_ref=halo_left,
            send_sem=halo_send.at[1],
            recv_sem=halo_recv.at[0],
            device_id=dev_peer(dev + 1),
            device_id_type=pl.DeviceIdType.MESH,
        )

    @pl.when(has_left)
    def _():
        to_left().start()

    @pl.when(has_right)
    def _():
        to_right().start()

    @pl.when(jnp.logical_not(has_left))
    def _():
        halo_left[...] = jnp.zeros(halo_left.shape, halo_left.dtype)

    @pl.when(jnp.logical_not(has_right))
    def _():
        halo_right[...] = jnp.zeros(halo_right.shape, halo_right.dtype)

    def y_copy(direction, row, chunk):
        slot = row * n_dz + chunk
        target = up if direction == 0 else down
        return pltpu.make_async_remote_copy(
            src_ref=out_ref.at[slot],
            dst_ref=out_ref.at[slot],
            send_sem=y_send.at[direction * n_dy * n_dz + slot],
            recv_sem=y_recv.at[slot],
            device_id=(section, grp, target, dz),
            device_id_type=pl.DeviceIdType.MESH,
        )

    def y_own(direction):
        target = up if direction == 0 else down
        return pltpu.make_async_remote_copy(
            src_ref=half_src,
            dst_ref=out_ref.at[dev],
            send_sem=y_send.at[direction * n_dy * n_dz + dev],
            recv_sem=y_recv.at[dev],
            device_id=(section, grp, target, dz),
            device_id_type=pl.DeviceIdType.MESH,
        )

    for direction in (0, 1):
        y_own(direction).start()
    for step in range(1, n_dz):
        source = (dz + n_dz - step) % n_dz
        z_copy(source, source).wait_recv()
        for direction in (0, 1):
            y_copy(direction, dy, source).start()
        pair_copy(dy * n_dz + source, out_ref.at[dy * n_dz + source]).start()
    own.wait()
    for step in range(1, n_dz):
        z_copy((dz + step) % n_dz, dz).wait_send()

    @pl.when(has_left)
    def _():
        to_right_of_left = pltpu.make_async_remote_copy(
            src_ref=frames_ref.at[pl.ds(0, RAD)],
            dst_ref=halo_left,
            send_sem=halo_send.at[1],
            recv_sem=halo_recv.at[0],
            device_id=dev_peer(dev - 1),
            device_id_type=pl.DeviceIdType.MESH,
        )
        to_right_of_left.wait_recv()
        to_left().wait_send()

    @pl.when(has_right)
    def _():
        to_left_of_right = pltpu.make_async_remote_copy(
            src_ref=frames_ref.at[pl.ds(0, RAD)],
            dst_ref=halo_right,
            send_sem=halo_send.at[0],
            recv_sem=halo_recv.at[1],
            device_id=dev_peer(dev + 1),
            device_id_type=pl.DeviceIdType.MESH,
        )
        to_left_of_right.wait_recv()
        to_right().wait_send()

    mob_rows = kernels_ref.shape[1]
    mob_all = kernels_ref.shape[2]
    row_place = (
        section * mob_rows + lax.broadcasted_iota(jnp.int32, (mob_rows, mob_all), 0)
    ).astype(jnp.float32)
    col_place = (
        (section * mob_rows + lax.broadcasted_iota(jnp.int32, (mob_rows, mob_all), 1)) % mob_all
    ).astype(jnp.float32)
    distance = row_place - col_place
    for level in range(SCALES):
        spread_scans = 2.0**level
        scaled = distance / spread_scans
        kernels_ref[level] = (
            (1.0 - scaled * scaled)
            * jnp.exp(-0.5 * scaled * scaled)
            / math.sqrt(0.75 * math.sqrt(math.pi) * spread_scans)
        ).astype(kernels_ref.dtype)

    weights = retention_weights()

    row_block = 32

    def smooth_rows(block, carry):
        rows = pl.ds(pl.multiple_of(block * row_block, row_block), row_block)

        def padded_frame(place):
            if place < RAD:
                return halo_left[place, rows, :]
            if place < RAD + count_frames:
                return frames_ref[place - RAD, rows, :]
            return halo_right[place - RAD - count_frames, rows, :]

        for frame in range(count_frames):
            total = weights[0] * padded_frame(frame).astype(jnp.float32)
            for offset in range(1, 2 * RAD + 1):
                total = total + weights[offset] * padded_frame(frame + offset).astype(jnp.float32)
            own_scans[frame, rows, :] = total.astype(own_scans.dtype)
        return carry

    lax.fori_loop(0, own_scans.shape[1] // row_block, smooth_rows, 0)

    swap = pltpu.make_async_remote_copy(
        src_ref=own_scans,
        dst_ref=partner_scans,
        send_sem=swap_send,
        recv_sem=swap_recv,
        device_id=(partner_section, grp, dy, dz),
        device_id_type=pl.DeviceIdType.MESH,
    )
    swap.start()
    relay = n_dz // 2
    for chunk in range(n_dz):
        y_copy(0, down, chunk).wait_recv()
        if chunk < relay:
            y_copy(0, down, chunk).start()
        pair_copy(down * n_dz + chunk, out_ref.at[down * n_dz + chunk]).start()
        y_copy(1, up, chunk).wait_recv()
        if chunk >= relay:
            y_copy(1, up, chunk).start()
        pair_copy(up * n_dz + chunk, out_ref.at[up * n_dz + chunk]).start()
    swap.wait()

    half = own_scans.shape[1]

    def level_frame(frame, carry):
        for level in range(SCALES):
            table = kernels_ref[level]
            acc = jnp.dot(table[:, :half], own_scans[frame], preferred_element_type=jnp.float32)
            acc = acc + jnp.dot(
                table[:, half:], partner_scans[frame], preferred_element_type=jnp.float32
            )
            wave_ref[level, frame] = acc.astype(wave_ref.dtype)
        return carry

    lax.fori_loop(0, count_frames, level_frame, 0)

    opposite = (dy + 2) % n_dy
    for chunk in range(n_dz):
        y_copy(0, opposite, chunk).wait_recv()
        pair_copy(opposite * n_dz + chunk, out_ref.at[opposite * n_dz + chunk]).start()
    for direction in (0, 1):
        for chunk in range(n_dz):
            y_copy(direction, dy, chunk).wait_send()
    for chunk in range(relay):
        y_copy(0, down, chunk).wait_send()
    for chunk in range(relay, n_dz):
        y_copy(1, up, chunk).wait_send()
    for slot in range(n_dev):
        pair_copy(slot, half_src).wait_recv()
    for slot in range(n_dev):
        pair_copy(slot, half_src).wait_send()


def frame_work(frames, templates):
    sizes = (lax.axis_size("section"), lax.axis_size("dy"), lax.axis_size("dz"))
    n_section, n_dy, n_dz = sizes
    rows, channels = templates.shape[0] // 2, templates.shape[1]
    half = templates
    count_frames, mob_local, _ = frames.shape
    rows_out, other_out, wave = pl.pallas_call(
        functools.partial(frame_kernel, sizes),
        out_shape=(
            jax.ShapeDtypeStruct((n_dy * n_dz, rows, channels), half.dtype),
            jax.ShapeDtypeStruct((n_dy * n_dz, rows, channels), half.dtype),
            jax.ShapeDtypeStruct((SCALES, count_frames, mob_local, channels), jnp.bfloat16),
        ),
        in_specs=[pl.BlockSpec(memory_space=pltpu.VMEM)] * 2,
        out_specs=(pl.BlockSpec(memory_space=pltpu.VMEM),) * 3,
        scratch_shapes=[
            pltpu.VMEM((SCALES, mob_local, 2 * mob_local), jnp.bfloat16),
            pltpu.VMEM((RAD, mob_local, channels), frames.dtype),
            pltpu.VMEM((RAD, mob_local, channels), frames.dtype),
            pltpu.VMEM((count_frames, mob_local, channels), jnp.bfloat16),
            pltpu.VMEM((count_frames, mob_local, channels), jnp.bfloat16),
            pltpu.SemaphoreType.DMA(()),
            pltpu.SemaphoreType.DMA((n_dz,)),
            pltpu.SemaphoreType.DMA((n_dz,)),
            pltpu.SemaphoreType.DMA((2 * n_dy * n_dz,)),
            pltpu.SemaphoreType.DMA((n_dy * n_dz,)),
            pltpu.SemaphoreType.DMA((2,)),
            pltpu.SemaphoreType.DMA((2,)),
            pltpu.SemaphoreType.DMA(()),
            pltpu.SemaphoreType.DMA(()),
            pltpu.SemaphoreType.DMA((n_dy * n_dz,)),
            pltpu.SemaphoreType.DMA((n_dy * n_dz,)),
        ],
        compiler_params=pltpu.CompilerParams(
            collective_id=1, has_side_effects=True, vmem_limit_bytes=56 * 1024 * 1024
        ),
    )(frames, templates)
    return (
        rows_out.reshape(n_dy * n_dz * rows, channels),
        other_out.reshape(n_dy * n_dz * rows, channels),
        wave,
    )


def score_kernel(
    order_ref, tile_ref, block_ref, count_ref, section_ref, wave_ref, mine_ref, other_ref, out_ref
):
    slot = order_ref[pl.program_id(0)]
    live = slot < count_ref[0]
    mine = block_ref[slot] % 2 == section_ref[0]

    def score(rows_ref):
        rows = rows_ref[...]
        acc = jnp.zeros((8, PB), jnp.float32)
        for level in range(SCALES):
            cells = wave_ref[level].reshape(-1, rows.shape[1])
            scores = lax.dot_general(
                cells, rows, (((1,), (1,)), ((), ())), preferred_element_type=jnp.float32
            )
            acc = acc + jnp.sum(jnp.maximum(scores, 0.0).reshape(-1, 8, PB), axis=0)
        cell_count = SCALES * wave_ref.shape[1] * wave_ref.shape[2]
        out_ref[0] = jnp.sum(acc, axis=0, keepdims=True) / cell_count

    @pl.when(jnp.logical_and(live, mine))
    def _():
        score(mine_ref)

    @pl.when(jnp.logical_and(live, jnp.logical_not(mine)))
    def _():
        score(other_ref)

    @pl.when(jnp.logical_not(live))
    def _():
        out_ref[0] = jnp.zeros((1, PB), jnp.float32)


def score_pairs(wavelet_stack, my_rows, other_rows, tile_ids, block_ids, live_pairs, section_index):
    slots = tile_ids.shape[0]
    scales, frames_local, mob_local, channels = wavelet_stack.shape
    slot_ids = jnp.arange(slots, dtype=jnp.int32)
    keys = jnp.where(slot_ids < live_pairs, tile_ids * slots + slot_ids, (mob_local // TM + 1) * slots + slot_ids)
    order = jnp.argsort(keys).astype(jnp.int32)

    def visited(k, o, c):
        return o[jnp.minimum(k, c[0] - 1)]

    grid_spec = pltpu.PrefetchScalarGridSpec(
        num_scalar_prefetch=5,
        grid=(slots,),
        in_specs=[
            pl.BlockSpec(
                (scales, frames_local, TM, channels),
                lambda k, o, t, b, c, s: (0, 0, t[visited(k, o, c)], 0),
            ),
            pl.BlockSpec((PB, channels), lambda k, o, t, b, c, s: (b[visited(k, o, c)] // 2, 0)),
            pl.BlockSpec((PB, channels), lambda k, o, t, b, c, s: (b[visited(k, o, c)] // 2, 0)),
        ],
        out_specs=pl.BlockSpec((1, 1, PB), lambda k, o, t, b, c, s: (o[k], 0, 0)),
    )
    out = pl.pallas_call(
        score_kernel,
        grid_spec=grid_spec,
        out_shape=jax.ShapeDtypeStruct((slots, 1, PB), jnp.float32),
    )(
        order,
        tile_ids,
        block_ids,
        live_pairs.reshape(1),
        section_index.astype(jnp.int32).reshape(1),
        wavelet_stack,
        my_rows,
        other_rows,
    )
    return out.reshape(slots, PB)


def solution(mesh):
    section_count, grp_count, dev_count = mesh.devices.shape
    dz_count = 8 if dev_count % 8 == 0 else dev_count
    split_mesh = jax.sharding.Mesh(
        mesh.devices.reshape(section_count, grp_count, dev_count // dz_count, dz_count),
        ("section", "grp", "dy", "dz"),
    )
    placed = (
        P("grp", DEV, "section", None),
        P(DEV, None),
        P("section", "grp", DEV),
        P("section", "grp", DEV),
        P("section", "grp", DEV),
        P(),
    )
    return jax.shard_map(
        on_device, mesh=split_mesh, in_specs=placed, out_specs=P("grp", DEV), check_vma=False
    )
```

```python
import functools
import math

import jax
import jax.numpy as jnp
from jax import lax
from jax.experimental import pallas as pl
from jax.experimental.pallas import tpu as pltpu
from jax.sharding import PartitionSpec as P

MOB = 512
SCALES = 6
RAD = 4
TM = 64
PB = 128
PREC = 8192
DEV = ("dy", "dz")


retention_spread = 2.0


def extended(cells, sides, width):
    for axis, dim in sides:
        count = lax.axis_size(axis)
        ends = count - 1
        head = lax.slice_in_dim(cells, 0, width, axis=dim)
        tail = lax.slice_in_dim(cells, cells.shape[dim] - width, cells.shape[dim], axis=dim)
        cells = jnp.concatenate(
            [
                lax.ppermute(tail, axis, [(i, (i + 1) % count) for i in range(ends)]),
                cells,
                lax.ppermute(head, axis, [((i + 1) % count, i) for i in range(ends)]),
            ],
            axis=dim,
        )
    return cells


def retention_weights():
    bell_values = [
        math.exp(-0.5 * (offset / retention_spread) ** 2) for offset in range(-RAD, RAD + 1)
    ]
    bell_total = sum(bell_values)
    return [weight_value / bell_total for weight_value in bell_values]


def mobility_kernels(row_start, row_count, col_start):
    row_place = (row_start + jnp.arange(row_count, dtype=jnp.int32)).astype(jnp.float32)
    col_place = ((col_start + jnp.arange(MOB, dtype=jnp.int32)) % MOB).astype(jnp.float32)
    distance = row_place[:, None] - col_place[None, :]
    tables = []
    for level in range(SCALES):
        spread_scans = 2.0**level
        scaled = distance / spread_scans
        tables.append(
            (1.0 - scaled * scaled)
            * jnp.exp(-0.5 * scaled * scaled)
            / math.sqrt(0.75 * math.sqrt(math.pi) * spread_scans)
        )
    return jnp.stack(tables).astype(jnp.bfloat16)


def on_device(frames, templates, pair_block, pair_tile, pair_count, owner_order):
    section_index = lax.axis_index("section")
    mob_local = frames.shape[2]
    section_count = lax.axis_size("section")
    my_rows, other_rows, wavelet_stack = frame_work(frames[0], templates)
    slots = pair_block.shape[2]
    live_pairs = pair_count[0, 0, 0]
    block_ids = pair_block[0, 0]
    tile_ids = pair_tile[0, 0]
    responses = score_pairs(
        wavelet_stack, my_rows, other_rows, tile_ids, block_ids, live_pairs, section_index
    )
    positions = jnp.take(owner_order.reshape(-1, PB), block_ids, axis=0).reshape(-1)
    groups = PREC // PB
    by_group = jnp.where(
        (positions // PB)[:, None] == jnp.arange(groups, dtype=jnp.int32)[None, :],
        responses.reshape(-1)[:, None],
        0.0,
    )
    by_lane = ((positions % PB)[:, None] == jnp.arange(PB, dtype=jnp.int32)[None, :]).astype(
        jnp.float32
    )
    placed = jnp.einsum(
        "ka,kb->ab",
        by_group,
        by_lane,
        precision=lax.Precision.HIGHEST,
        preferred_element_type=jnp.float32,
    ).reshape(-1)
    dev_count = lax.axis_size(DEV)
    summed = reduce_owned(placed.reshape(dev_count, 1, PREC // dev_count))
    owned_width = PREC // dev_count
    run_totals = summed[:, owned_width:]
    lanes = jnp.arange(run_totals.shape[1], dtype=jnp.int32)[None, :]
    run_sum = jnp.sum(run_totals, axis=1, keepdims=True)
    own_total = jnp.sum(
        jnp.where(lanes == lax.axis_index("grp"), run_totals, 0.0), axis=1, keepdims=True
    )
    factor = (run_sum / lax.axis_size("grp")) / own_total
    return summed[:, :owned_width] * factor


def reduce_kernel(
    sizes,
    payload_ref,
    out_ref,
    mixed,
    line,
    line_in,
    column,
    column_in,
    totals,
    pair_send,
    pair_recv,
    z_send,
    z_recv,
    y_send,
    y_recv,
    total_send,
    total_recv,
):
    n_section, n_grp, n_dy, n_dz = sizes
    cores = totals
    section = lax.axis_index("section")
    grp = lax.axis_index("grp")
    dy = lax.axis_index("dy")
    dz = lax.axis_index("dz")
    partner = (section + 1) % n_section
    owned_width = mixed.shape[3]

    barrier = pltpu.get_barrier_semaphore()
    peers = [(partner, grp, dy, dz)]
    peers += [(section, grp, dy, (dz + step) % n_dz) for step in range(1, n_dz)]
    peers += [(section, grp, (dy + step) % n_dy, dz) for step in range(1, n_dy)]
    peers += [
        (side, (grp + step) % n_grp, dy, dz) for side in range(n_section) for step in range(1, n_grp)
    ]
    for peer in peers:
        pl.semaphore_signal(barrier, inc=1, device_id=peer, device_id_type=pl.DeviceIdType.MESH)
    pl.semaphore_wait(barrier, len(peers))

    swap = pltpu.make_async_remote_copy(
        src_ref=payload_ref,
        dst_ref=mixed,
        send_sem=pair_send,
        recv_sem=pair_recv,
        device_id=(partner, grp, dy, dz),
        device_id_type=pl.DeviceIdType.MESH,
    )
    swap.start()
    own_slot = section * n_grp + grp
    own_sum = jnp.sum(jnp.sum(jnp.sum(payload_ref[...], axis=0), axis=0), axis=1, keepdims=True)
    cores[own_slot] = jnp.broadcast_to(own_sum, (1, 128))
    cores[partner * n_grp + grp] = jnp.zeros((1, 128), jnp.float32)

    def core_copy(side, other):
        return pltpu.make_async_remote_copy(
            src_ref=cores.at[own_slot],
            dst_ref=cores.at[own_slot],
            send_sem=total_send.at[side * n_grp + other],
            recv_sem=total_recv.at[own_slot],
            device_id=(side, other, dy, dz),
            device_id_type=pl.DeviceIdType.MESH,
        )

    def core_arrival(side, other):
        slot = side * n_grp + other
        return pltpu.make_async_remote_copy(
            src_ref=cores.at[slot],
            dst_ref=cores.at[slot],
            send_sem=total_send.at[slot],
            recv_sem=total_recv.at[slot],
            device_id=(side, other, dy, dz),
            device_id_type=pl.DeviceIdType.MESH,
        )

    for side in range(n_section):
        for step in range(1, n_grp):
            core_copy(side, (grp + step) % n_grp).start()
    swap.wait()
    combined = payload_ref[...] + mixed[...]
    line[:, :, :, :owned_width] = combined
    chip_total = jnp.sum(jnp.sum(jnp.sum(combined, axis=0), axis=0), axis=1, keepdims=True)
    for side in range(n_section):
        for step in range(1, n_grp):
            core_arrival(side, (grp + step) % n_grp).wait_recv()
    lanes = lax.broadcasted_iota(jnp.int32, (1, line.shape[3] - owned_width), 1)
    spread = jnp.where(lanes == grp, chip_total, 0.0)
    for other in range(n_grp):
        other_total = cores[other] + cores[n_grp + other]
        spread = jnp.where(jnp.logical_and(lanes == other, other != grp), other_total, spread)
    line[:, :, :, owned_width:] = jnp.broadcast_to(spread[None, None], line.shape[:3] + spread.shape[1:])
    line_in[dz] = line[dz]

    def z_copy(target, source):
        return pltpu.make_async_remote_copy(
            src_ref=line.at[target],
            dst_ref=line_in.at[source],
            send_sem=z_send.at[target],
            recv_sem=z_recv.at[source],
            device_id=(section, grp, dy, target),
            device_id_type=pl.DeviceIdType.MESH,
        )

    for step in range(1, n_dz):
        z_copy((dz + step) % n_dz, dz).start()
    for step in range(1, n_dz):
        source = (dz + n_dz - step) % n_dz
        z_copy(source, source).wait_recv()
    partial = line_in[0]
    for index in range(1, n_dz):
        partial = partial + line_in[index]
    column[...] = partial
    column_in[dy] = column[dy]

    def y_copy(target, source):
        return pltpu.make_async_remote_copy(
            src_ref=column.at[target],
            dst_ref=column_in.at[source],
            send_sem=y_send.at[target],
            recv_sem=y_recv.at[source],
            device_id=(section, grp, target, dz),
            device_id_type=pl.DeviceIdType.MESH,
        )

    for step in range(1, n_dy):
        y_copy((dy + step) % n_dy, dy).start()
    for step in range(1, n_dy):
        source = (dy + n_dy - step) % n_dy
        y_copy(source, source).wait_recv()
    summed = column_in[0]
    for index in range(1, n_dy):
        summed = summed + column_in[index]
    summed = summed.reshape(summed.shape[-2:])
    for step in range(1, n_dz):
        z_copy((dz + step) % n_dz, dz).wait_send()
    for step in range(1, n_dy):
        y_copy((dy + step) % n_dy, dy).wait_send()
    for side in range(n_section):
        for step in range(1, n_grp):
            core_copy(side, (grp + step) % n_grp).wait_send()
    out_ref[...] = summed


def reduce_owned(payload):
    sizes = (lax.axis_size("section"), lax.axis_size("grp"), lax.axis_size("dy"), lax.axis_size("dz"))
    n_section, n_grp, n_dy, n_dz = sizes
    rows, one, owned_width = payload.shape
    width = owned_width + 128
    lines = payload.reshape(n_dy, n_dz, one, owned_width).transpose(1, 0, 2, 3)
    return pl.pallas_call(
        functools.partial(reduce_kernel, sizes),
        out_shape=jax.ShapeDtypeStruct((1, width), jnp.float32),
        in_specs=[pl.BlockSpec(memory_space=pltpu.VMEM)],
        out_specs=pl.BlockSpec(memory_space=pltpu.VMEM),
        scratch_shapes=[
            pltpu.VMEM((n_dz, n_dy, one, owned_width), jnp.float32),
            pltpu.VMEM((n_dz, n_dy, one, width), jnp.float32),
            pltpu.VMEM((n_dz, n_dy, one, width), jnp.float32),
            pltpu.VMEM((n_dy, one, width), jnp.float32),
            pltpu.VMEM((n_dy, one, width), jnp.float32),
            pltpu.VMEM((n_section * n_grp, 1, 128), jnp.float32),
            pltpu.SemaphoreType.DMA(()),
            pltpu.SemaphoreType.DMA(()),
            pltpu.SemaphoreType.DMA((n_dz,)),
            pltpu.SemaphoreType.DMA((n_dz,)),
            pltpu.SemaphoreType.DMA((n_dy,)),
            pltpu.SemaphoreType.DMA((n_dy,)),
            pltpu.SemaphoreType.DMA((n_section * n_grp,)),
            pltpu.SemaphoreType.DMA((n_section * n_grp,)),
        ],
        compiler_params=pltpu.CompilerParams(collective_id=0, has_side_effects=True),
    )(lines)


def frame_kernel(
    sizes,
    frames_ref,
    templates_ref,
    out_ref,
    other_ref,
    wave_ref,
    kernels_ref,
    halo_left,
    halo_right,
    own_scans,
    partner_scans,
    own_sem,
    z_send,
    z_recv,
    y_send,
    y_recv,
    halo_send,
    halo_recv,
    swap_send,
    swap_recv,
    pair_send,
    pair_recv,
):
    n_section, n_dy, n_dz = sizes
    n_dev = n_dy * n_dz
    section = lax.axis_index("section")
    grp = lax.axis_index("grp")
    dy = lax.axis_index("dy")
    dz = lax.axis_index("dz")
    dev = dy * n_dz + dz
    partner_section = (section + 1) % n_section
    half_rows = out_ref.shape[1]
    half_src = templates_ref.at[pl.ds(section * half_rows, half_rows)]

    def dev_peer(index):
        return (section, grp, index // n_dz, index % n_dz)

    barrier = pltpu.get_barrier_semaphore()
    for step in range(1, n_dz):
        pl.semaphore_signal(
            barrier,
            inc=1,
            device_id=(section, grp, dy, (dz + step) % n_dz),
            device_id_type=pl.DeviceIdType.MESH,
        )
    up = (dy + 1) % n_dy
    down = (dy + n_dy - 1) % n_dy
    for row in (up, down):
        pl.semaphore_signal(
            barrier,
            inc=1,
            device_id=(section, grp, row, dz),
            device_id_type=pl.DeviceIdType.MESH,
        )
    pl.semaphore_signal(
        barrier,
        inc=1,
        device_id=(partner_section, grp, dy, dz),
        device_id_type=pl.DeviceIdType.MESH,
    )
    has_left = dev > 0
    has_right = dev < n_dev - 1
    far_left = jnp.logical_and(has_left, dz == 0)
    far_right = jnp.logical_and(has_right, dz == n_dz - 1)

    @pl.when(far_left)
    def _():
        pl.semaphore_signal(
            barrier, inc=1, device_id=dev_peer(dev - 1), device_id_type=pl.DeviceIdType.MESH
        )

    @pl.when(far_right)
    def _():
        pl.semaphore_signal(
            barrier, inc=1, device_id=dev_peer(dev + 1), device_id_type=pl.DeviceIdType.MESH
        )

    extra = far_left.astype(jnp.int32) + far_right.astype(jnp.int32)
    pl.semaphore_wait(barrier, n_dz - 1 + 2 + 1 + extra)

    own = pltpu.make_async_copy(half_src, out_ref.at[dev], own_sem)
    own.start()

    def pair_copy(slot, source_ref):
        return pltpu.make_async_remote_copy(
            src_ref=source_ref,
            dst_ref=other_ref.at[slot],
            send_sem=pair_send.at[slot],
            recv_sem=pair_recv.at[slot],
            device_id=(partner_section, grp, dy, dz),
            device_id_type=pl.DeviceIdType.MESH,
        )

    pair_copy(dev, half_src).start()

    def z_copy(target, source):
        return pltpu.make_async_remote_copy(
            src_ref=half_src,
            dst_ref=out_ref.at[dy * n_dz + source],
            send_sem=z_send.at[target],
            recv_sem=z_recv.at[source],
            device_id=(section, grp, dy, target),
            device_id_type=pl.DeviceIdType.MESH,
        )

    for step in range(1, n_dz):
        z_copy((dz + step) % n_dz, dz).start()

    count_frames = frames_ref.shape[0]

    def to_left():
        return pltpu.make_async_remote_copy(
            src_ref=frames_ref.at[pl.ds(0, RAD)],
            dst_ref=halo_right,
            send_sem=halo_send.at[0],
            recv_sem=halo_recv.at[1],
            device_id=dev_peer(dev - 1),
            device_id_type=pl.DeviceIdType.MESH,
        )

    def to_right():
        return pltpu.make_async_remote_copy(
            src_ref=frames_ref.at[pl.ds(count_frames - RAD, RAD)],
            dst_ref=halo_left,
            send_sem=halo_send.at[1],
            recv_sem=halo_recv.at[0],
            device_id=dev_peer(dev + 1),
            device_id_type=pl.DeviceIdType.MESH,
        )

    @pl.when(has_left)
    def _():
        to_left().start()

    @pl.when(has_right)
    def _():
        to_right().start()

    @pl.when(jnp.logical_not(has_left))
    def _():
        halo_left[...] = jnp.zeros(halo_left.shape, halo_left.dtype)

    @pl.when(jnp.logical_not(has_right))
    def _():
        halo_right[...] = jnp.zeros(halo_right.shape, halo_right.dtype)

    def y_copy(direction, row, chunk):
        slot = row * n_dz + chunk
        target = up if direction == 0 else down
        return pltpu.make_async_remote_copy(
            src_ref=out_ref.at[slot],
            dst_ref=out_ref.at[slot],
            send_sem=y_send.at[direction * n_dy * n_dz + slot],
            recv_sem=y_recv.at[slot],
            device_id=(section, grp, target, dz),
            device_id_type=pl.DeviceIdType.MESH,
        )

    def y_own(direction):
        target = up if direction == 0 else down
        return pltpu.make_async_remote_copy(
            src_ref=half_src,
            dst_ref=out_ref.at[dev],
            send_sem=y_send.at[direction * n_dy * n_dz + dev],
            recv_sem=y_recv.at[dev],
            device_id=(section, grp, target, dz),
            device_id_type=pl.DeviceIdType.MESH,
        )

    for direction in (0, 1):
        y_own(direction).start()
    for step in range(1, n_dz):
        source = (dz + n_dz - step) % n_dz
        z_copy(source, source).wait_recv()
        for direction in (0, 1):
            y_copy(direction, dy, source).start()
        pair_copy(dy * n_dz + source, out_ref.at[dy * n_dz + source]).start()
    own.wait()
    for step in range(1, n_dz):
        z_copy((dz + step) % n_dz, dz).wait_send()

    @pl.when(has_left)
    def _():
        to_right_of_left = pltpu.make_async_remote_copy(
            src_ref=frames_ref.at[pl.ds(0, RAD)],
            dst_ref=halo_left,
            send_sem=halo_send.at[1],
            recv_sem=halo_recv.at[0],
            device_id=dev_peer(dev - 1),
            device_id_type=pl.DeviceIdType.MESH,
        )
        to_right_of_left.wait_recv()
        to_left().wait_send()

    @pl.when(has_right)
    def _():
        to_left_of_right = pltpu.make_async_remote_copy(
            src_ref=frames_ref.at[pl.ds(0, RAD)],
            dst_ref=halo_right,
            send_sem=halo_send.at[0],
            recv_sem=halo_recv.at[1],
            device_id=dev_peer(dev + 1),
            device_id_type=pl.DeviceIdType.MESH,
        )
        to_left_of_right.wait_recv()
        to_right().wait_send()

    mob_rows = kernels_ref.shape[1]
    mob_all = kernels_ref.shape[2]
    row_place = (
        section * mob_rows + lax.broadcasted_iota(jnp.int32, (mob_rows, mob_all), 0)
    ).astype(jnp.float32)
    col_place = (
        (section * mob_rows + lax.broadcasted_iota(jnp.int32, (mob_rows, mob_all), 1)) % mob_all
    ).astype(jnp.float32)
    distance = row_place - col_place
    for level in range(SCALES):
        spread_scans = 2.0**level
        scaled = distance / spread_scans
        kernels_ref[level] = (
            (1.0 - scaled * scaled)
            * jnp.exp(-0.5 * scaled * scaled)
            / math.sqrt(0.75 * math.sqrt(math.pi) * spread_scans)
        ).astype(kernels_ref.dtype)

    weights = retention_weights()

    row_block = 32

    def smooth_rows(block, carry):
        rows = pl.ds(pl.multiple_of(block * row_block, row_block), row_block)

        def padded_frame(place):
            if place < RAD:
                return halo_left[place, rows, :]
            if place < RAD + count_frames:
                return frames_ref[place - RAD, rows, :]
            return halo_right[place - RAD - count_frames, rows, :]

        for frame in range(count_frames):
            total = weights[0] * padded_frame(frame).astype(jnp.float32)
            for offset in range(1, 2 * RAD + 1):
                total = total + weights[offset] * padded_frame(frame + offset).astype(jnp.float32)
            own_scans[frame, rows, :] = total.astype(own_scans.dtype)
        return carry

    lax.fori_loop(0, own_scans.shape[1] // row_block, smooth_rows, 0)

    swap = pltpu.make_async_remote_copy(
        src_ref=own_scans,
        dst_ref=partner_scans,
        send_sem=swap_send,
        recv_sem=swap_recv,
        device_id=(partner_section, grp, dy, dz),
        device_id_type=pl.DeviceIdType.MESH,
    )
    swap.start()
    relay = n_dz // 2
    for chunk in range(n_dz):
        y_copy(0, down, chunk).wait_recv()
        if chunk < relay:
            y_copy(0, down, chunk).start()
        pair_copy(down * n_dz + chunk, out_ref.at[down * n_dz + chunk]).start()
        y_copy(1, up, chunk).wait_recv()
        if chunk >= relay:
            y_copy(1, up, chunk).start()
        pair_copy(up * n_dz + chunk, out_ref.at[up * n_dz + chunk]).start()
    swap.wait()

    half = own_scans.shape[1]

    def level_frame(frame, carry):
        for level in range(SCALES):
            table = kernels_ref[level]
            acc = jnp.dot(table[:, :half], own_scans[frame], preferred_element_type=jnp.float32)
            acc = acc + jnp.dot(
                table[:, half:], partner_scans[frame], preferred_element_type=jnp.float32
            )
            wave_ref[level, frame] = acc.astype(wave_ref.dtype)
        return carry

    lax.fori_loop(0, count_frames, level_frame, 0)

    opposite = (dy + 2) % n_dy
    for chunk in range(n_dz):
        y_copy(0, opposite, chunk).wait_recv()
        pair_copy(opposite * n_dz + chunk, out_ref.at[opposite * n_dz + chunk]).start()
    for direction in (0, 1):
        for chunk in range(n_dz):
            y_copy(direction, dy, chunk).wait_send()
    for chunk in range(relay):
        y_copy(0, down, chunk).wait_send()
    for chunk in range(relay, n_dz):
        y_copy(1, up, chunk).wait_send()
    for slot in range(n_dev):
        pair_copy(slot, half_src).wait_recv()
    for slot in range(n_dev):
        pair_copy(slot, half_src).wait_send()


def frame_work(frames, templates):
    sizes = (lax.axis_size("section"), lax.axis_size("dy"), lax.axis_size("dz"))
    n_section, n_dy, n_dz = sizes
    rows, channels = templates.shape[0] // 2, templates.shape[1]
    half = templates
    count_frames, mob_local, _ = frames.shape
    rows_out, other_out, wave = pl.pallas_call(
        functools.partial(frame_kernel, sizes),
        out_shape=(
            jax.ShapeDtypeStruct((n_dy * n_dz, rows, channels), half.dtype),
            jax.ShapeDtypeStruct((n_dy * n_dz, rows, channels), half.dtype),
            jax.ShapeDtypeStruct((SCALES, count_frames, mob_local, channels), jnp.bfloat16),
        ),
        in_specs=[pl.BlockSpec(memory_space=pltpu.VMEM)] * 2,
        out_specs=(pl.BlockSpec(memory_space=pltpu.VMEM),) * 3,
        scratch_shapes=[
            pltpu.VMEM((SCALES, mob_local, 2 * mob_local), jnp.bfloat16),
            pltpu.VMEM((RAD, mob_local, channels), frames.dtype),
            pltpu.VMEM((RAD, mob_local, channels), frames.dtype),
            pltpu.VMEM((count_frames, mob_local, channels), jnp.bfloat16),
            pltpu.VMEM((count_frames, mob_local, channels), jnp.bfloat16),
            pltpu.SemaphoreType.DMA(()),
            pltpu.SemaphoreType.DMA((n_dz,)),
            pltpu.SemaphoreType.DMA((n_dz,)),
            pltpu.SemaphoreType.DMA((2 * n_dy * n_dz,)),
            pltpu.SemaphoreType.DMA((n_dy * n_dz,)),
            pltpu.SemaphoreType.DMA((2,)),
            pltpu.SemaphoreType.DMA((2,)),
            pltpu.SemaphoreType.DMA(()),
            pltpu.SemaphoreType.DMA(()),
            pltpu.SemaphoreType.DMA((n_dy * n_dz,)),
            pltpu.SemaphoreType.DMA((n_dy * n_dz,)),
        ],
        compiler_params=pltpu.CompilerParams(
            collective_id=1, has_side_effects=True, vmem_limit_bytes=56 * 1024 * 1024
        ),
    )(frames, templates)
    return (
        rows_out.reshape(n_dy * n_dz * rows, channels),
        other_out.reshape(n_dy * n_dz * rows, channels),
        wave,
    )


def score_kernel(
    order_ref, tile_ref, block_ref, count_ref, section_ref, wave_ref, mine_ref, other_ref, out_ref
):
    slot = order_ref[pl.program_id(0)]
    live = slot < count_ref[0]
    mine = block_ref[slot] % 2 == section_ref[0]

    def score(rows_ref):
        rows = rows_ref[...]
        acc = jnp.zeros((1, PB), jnp.float32)
        for level in range(SCALES):
            cells = wave_ref[level].reshape(-1, rows.shape[1])
            scores = lax.dot_general(
                cells, rows, (((1,), (1,)), ((), ())), preferred_element_type=jnp.float32
            )
            acc = acc + jnp.sum(jnp.maximum(scores, 0.0), axis=0, keepdims=True)
        cell_count = SCALES * wave_ref.shape[1] * wave_ref.shape[2]
        out_ref[0] = acc / cell_count

    @pl.when(jnp.logical_and(live, mine))
    def _():
        score(mine_ref)

    @pl.when(jnp.logical_and(live, jnp.logical_not(mine)))
    def _():
        score(other_ref)

    @pl.when(jnp.logical_not(live))
    def _():
        out_ref[0] = jnp.zeros((1, PB), jnp.float32)


def score_pairs(wavelet_stack, my_rows, other_rows, tile_ids, block_ids, live_pairs, section_index):
    slots = tile_ids.shape[0]
    scales, frames_local, mob_local, channels = wavelet_stack.shape
    slot_ids = jnp.arange(slots, dtype=jnp.int32)
    keys = jnp.where(slot_ids < live_pairs, tile_ids * slots + slot_ids, (mob_local // TM + 1) * slots + slot_ids)
    order = jnp.argsort(keys).astype(jnp.int32)

    def visited(k, o, c):
        return o[jnp.minimum(k, c[0] - 1)]

    grid_spec = pltpu.PrefetchScalarGridSpec(
        num_scalar_prefetch=5,
        grid=(slots,),
        in_specs=[
            pl.BlockSpec(
                (scales, frames_local, TM, channels),
                lambda k, o, t, b, c, s: (0, 0, t[visited(k, o, c)], 0),
            ),
            pl.BlockSpec((PB, channels), lambda k, o, t, b, c, s: (b[visited(k, o, c)] // 2, 0)),
            pl.BlockSpec((PB, channels), lambda k, o, t, b, c, s: (b[visited(k, o, c)] // 2, 0)),
        ],
        out_specs=pl.BlockSpec((1, 1, PB), lambda k, o, t, b, c, s: (o[k], 0, 0)),
    )
    out = pl.pallas_call(
        score_kernel,
        grid_spec=grid_spec,
        out_shape=jax.ShapeDtypeStruct((slots, 1, PB), jnp.float32),
    )(
        order,
        tile_ids,
        block_ids,
        live_pairs.reshape(1),
        section_index.astype(jnp.int32).reshape(1),
        wavelet_stack,
        my_rows,
        other_rows,
    )
    return out.reshape(slots, PB)


def solution(mesh):
    section_count, grp_count, dev_count = mesh.devices.shape
    dz_count = 8 if dev_count % 8 == 0 else dev_count
    split_mesh = jax.sharding.Mesh(
        mesh.devices.reshape(section_count, grp_count, dev_count // dz_count, dz_count),
        ("section", "grp", "dy", "dz"),
    )
    placed = (
        P("grp", DEV, "section", None),
        P(DEV, None),
        P("section", "grp", DEV),
        P("section", "grp", DEV),
        P("section", "grp", DEV),
        P(),
    )
    return jax.shard_map(
        on_device, mesh=split_mesh, in_specs=placed, out_specs=P("grp", DEV), check_vma=False
    )
```

```python
import functools
import math

import jax
import jax.numpy as jnp
from jax import lax
from jax.experimental import pallas as pl
from jax.experimental.pallas import tpu as pltpu
from jax.sharding import PartitionSpec as P

MOB = 512
SCALES = 6
RAD = 4
TM = 64
PB = 128
PREC = 8192
DEV = ("dy", "dz")


retention_spread = 2.0


def extended(cells, sides, width):
    for axis, dim in sides:
        count = lax.axis_size(axis)
        ends = count - 1
        head = lax.slice_in_dim(cells, 0, width, axis=dim)
        tail = lax.slice_in_dim(cells, cells.shape[dim] - width, cells.shape[dim], axis=dim)
        cells = jnp.concatenate(
            [
                lax.ppermute(tail, axis, [(i, (i + 1) % count) for i in range(ends)]),
                cells,
                lax.ppermute(head, axis, [((i + 1) % count, i) for i in range(ends)]),
            ],
            axis=dim,
        )
    return cells


def retention_weights():
    bell_values = [
        math.exp(-0.5 * (offset / retention_spread) ** 2) for offset in range(-RAD, RAD + 1)
    ]
    bell_total = sum(bell_values)
    return [weight_value / bell_total for weight_value in bell_values]


def mobility_kernels(row_start, row_count, col_start):
    row_place = (row_start + jnp.arange(row_count, dtype=jnp.int32)).astype(jnp.float32)
    col_place = ((col_start + jnp.arange(MOB, dtype=jnp.int32)) % MOB).astype(jnp.float32)
    distance = row_place[:, None] - col_place[None, :]
    tables = []
    for level in range(SCALES):
        spread_scans = 2.0**level
        scaled = distance / spread_scans
        tables.append(
            (1.0 - scaled * scaled)
            * jnp.exp(-0.5 * scaled * scaled)
            / math.sqrt(0.75 * math.sqrt(math.pi) * spread_scans)
        )
    return jnp.stack(tables).astype(jnp.bfloat16)


def on_device(frames, templates, pair_block, pair_tile, pair_count, owner_order):
    section_index = lax.axis_index("section")
    mob_local = frames.shape[2]
    section_count = lax.axis_size("section")
    my_rows, other_rows, wavelet_stack = frame_work(frames[0], templates)
    slots = pair_block.shape[2]
    live_pairs = pair_count[0, 0, 0]
    block_ids = pair_block[0, 0]
    tile_ids = pair_tile[0, 0]
    responses = score_pairs(
        wavelet_stack, my_rows, other_rows, tile_ids, block_ids, live_pairs, section_index
    )
    positions = jnp.take(owner_order.reshape(-1, PB), block_ids, axis=0).reshape(-1)
    groups = PREC // PB
    by_group = jnp.where(
        (positions // PB)[:, None] == jnp.arange(groups, dtype=jnp.int32)[None, :],
        responses.reshape(-1)[:, None],
        0.0,
    )
    by_lane = ((positions % PB)[:, None] == jnp.arange(PB, dtype=jnp.int32)[None, :]).astype(
        jnp.float32
    )
    placed = jnp.einsum(
        "ka,kb->ab",
        by_group,
        by_lane,
        precision=lax.Precision.HIGHEST,
        preferred_element_type=jnp.float32,
    ).reshape(-1)
    dev_count = lax.axis_size(DEV)
    return reduce_owned(placed.reshape(dev_count, 1, PREC // dev_count))


def reduce_kernel(
    sizes,
    payload_ref,
    out_ref,
    mixed,
    line,
    line_in,
    column,
    column_in,
    totals,
    pair_send,
    pair_recv,
    z_send,
    z_recv,
    y_send,
    y_recv,
    total_send,
    total_recv,
):
    n_section, n_grp, n_dy, n_dz = sizes
    cores = totals
    section = lax.axis_index("section")
    grp = lax.axis_index("grp")
    dy = lax.axis_index("dy")
    dz = lax.axis_index("dz")
    partner = (section + 1) % n_section
    owned_width = out_ref.shape[1]

    barrier = pltpu.get_barrier_semaphore()
    peers = [(partner, grp, dy, dz)]
    peers += [(section, grp, dy, (dz + step) % n_dz) for step in range(1, n_dz)]
    peers += [(section, grp, (dy + step) % n_dy, dz) for step in range(1, n_dy)]
    peers += [
        (side, (grp + step) % n_grp, dy, dz) for side in range(n_section) for step in range(1, n_grp)
    ]
    for peer in peers:
        pl.semaphore_signal(barrier, inc=1, device_id=peer, device_id_type=pl.DeviceIdType.MESH)
    pl.semaphore_wait(barrier, len(peers))

    swap = pltpu.make_async_remote_copy(
        src_ref=payload_ref,
        dst_ref=mixed,
        send_sem=pair_send,
        recv_sem=pair_recv,
        device_id=(partner, grp, dy, dz),
        device_id_type=pl.DeviceIdType.MESH,
    )
    swap.start()
    own_slot = section * n_grp + grp
    own_sum = jnp.sum(jnp.sum(jnp.sum(payload_ref[...], axis=0), axis=0), axis=1, keepdims=True)
    cores[own_slot] = jnp.broadcast_to(own_sum, (1, 128))
    cores[partner * n_grp + grp] = jnp.zeros((1, 128), jnp.float32)

    def core_copy(side, other):
        return pltpu.make_async_remote_copy(
            src_ref=cores.at[own_slot],
            dst_ref=cores.at[own_slot],
            send_sem=total_send.at[side * n_grp + other],
            recv_sem=total_recv.at[own_slot],
            device_id=(side, other, dy, dz),
            device_id_type=pl.DeviceIdType.MESH,
        )

    def core_arrival(side, other):
        slot = side * n_grp + other
        return pltpu.make_async_remote_copy(
            src_ref=cores.at[slot],
            dst_ref=cores.at[slot],
            send_sem=total_send.at[slot],
            recv_sem=total_recv.at[slot],
            device_id=(side, other, dy, dz),
            device_id_type=pl.DeviceIdType.MESH,
        )

    for side in range(n_section):
        for step in range(1, n_grp):
            core_copy(side, (grp + step) % n_grp).start()
    swap.wait()
    combined = payload_ref[...] + mixed[...]
    line[:, :, :, :owned_width] = combined
    chip_total = jnp.sum(jnp.sum(jnp.sum(combined, axis=0), axis=0), axis=1, keepdims=True)
    for side in range(n_section):
        for step in range(1, n_grp):
            core_arrival(side, (grp + step) % n_grp).wait_recv()
    lanes = lax.broadcasted_iota(jnp.int32, (1, line.shape[3] - owned_width), 1)
    spread = jnp.where(lanes == grp, chip_total, 0.0)
    for other in range(n_grp):
        other_total = cores[other] + cores[n_grp + other]
        spread = jnp.where(jnp.logical_and(lanes == other, other != grp), other_total, spread)
    line[:, :, :, owned_width:] = jnp.broadcast_to(spread[None, None], line.shape[:3] + spread.shape[1:])
    line_in[dz] = line[dz]

    def z_copy(target, source):
        return pltpu.make_async_remote_copy(
            src_ref=line.at[target],
            dst_ref=line_in.at[source],
            send_sem=z_send.at[target],
            recv_sem=z_recv.at[source],
            device_id=(section, grp, dy, target),
            device_id_type=pl.DeviceIdType.MESH,
        )

    for step in range(1, n_dz):
        z_copy((dz + step) % n_dz, dz).start()
    for step in range(1, n_dz):
        source = (dz + n_dz - step) % n_dz
        z_copy(source, source).wait_recv()
    partial = line_in[0]
    for index in range(1, n_dz):
        partial = partial + line_in[index]
    column[...] = partial
    column_in[dy] = column[dy]

    def y_copy(target, source):
        return pltpu.make_async_remote_copy(
            src_ref=column.at[target],
            dst_ref=column_in.at[source],
            send_sem=y_send.at[target],
            recv_sem=y_recv.at[source],
            device_id=(section, grp, target, dz),
            device_id_type=pl.DeviceIdType.MESH,
        )

    for step in range(1, n_dy):
        y_copy((dy + step) % n_dy, dy).start()
    for step in range(1, n_dy):
        source = (dy + n_dy - step) % n_dy
        y_copy(source, source).wait_recv()
    summed = column_in[0]
    for index in range(1, n_dy):
        summed = summed + column_in[index]
    summed = summed.reshape(summed.shape[-2:])
    for step in range(1, n_dz):
        z_copy((dz + step) % n_dz, dz).wait_send()
    for step in range(1, n_dy):
        y_copy((dy + step) % n_dy, dy).wait_send()
    for side in range(n_section):
        for step in range(1, n_grp):
            core_copy(side, (grp + step) % n_grp).wait_send()
    run_totals = summed[:, owned_width:]
    run_sum = jnp.sum(run_totals, axis=1, keepdims=True)
    own_total = jnp.sum(jnp.where(lanes == grp, run_totals, 0.0), axis=1, keepdims=True)
    factor = (run_sum / n_grp) / own_total
    out_ref[...] = summed[:, :owned_width] * factor


def reduce_owned(payload):
    sizes = (lax.axis_size("section"), lax.axis_size("grp"), lax.axis_size("dy"), lax.axis_size("dz"))
    n_section, n_grp, n_dy, n_dz = sizes
    rows, one, owned_width = payload.shape
    width = owned_width + 128
    lines = payload.reshape(n_dy, n_dz, one, owned_width).transpose(1, 0, 2, 3)
    return pl.pallas_call(
        functools.partial(reduce_kernel, sizes),
        out_shape=jax.ShapeDtypeStruct((1, owned_width), jnp.float32),
        in_specs=[pl.BlockSpec(memory_space=pltpu.VMEM)],
        out_specs=pl.BlockSpec(memory_space=pltpu.VMEM),
        scratch_shapes=[
            pltpu.VMEM((n_dz, n_dy, one, owned_width), jnp.float32),
            pltpu.VMEM((n_dz, n_dy, one, width), jnp.float32),
            pltpu.VMEM((n_dz, n_dy, one, width), jnp.float32),
            pltpu.VMEM((n_dy, one, width), jnp.float32),
            pltpu.VMEM((n_dy, one, width), jnp.float32),
            pltpu.VMEM((n_section * n_grp, 1, 128), jnp.float32),
            pltpu.SemaphoreType.DMA(()),
            pltpu.SemaphoreType.DMA(()),
            pltpu.SemaphoreType.DMA((n_dz,)),
            pltpu.SemaphoreType.DMA((n_dz,)),
            pltpu.SemaphoreType.DMA((n_dy,)),
            pltpu.SemaphoreType.DMA((n_dy,)),
            pltpu.SemaphoreType.DMA((n_section * n_grp,)),
            pltpu.SemaphoreType.DMA((n_section * n_grp,)),
        ],
        compiler_params=pltpu.CompilerParams(collective_id=0, has_side_effects=True),
    )(lines)


def frame_kernel(
    sizes,
    frames_ref,
    templates_ref,
    out_ref,
    other_ref,
    wave_ref,
    kernels_ref,
    halo_left,
    halo_right,
    own_scans,
    partner_scans,
    own_sem,
    z_send,
    z_recv,
    y_send,
    y_recv,
    halo_send,
    halo_recv,
    swap_send,
    swap_recv,
    pair_send,
    pair_recv,
):
    n_section, n_dy, n_dz = sizes
    n_dev = n_dy * n_dz
    section = lax.axis_index("section")
    grp = lax.axis_index("grp")
    dy = lax.axis_index("dy")
    dz = lax.axis_index("dz")
    dev = dy * n_dz + dz
    partner_section = (section + 1) % n_section
    half_rows = out_ref.shape[1]
    half_src = templates_ref.at[pl.ds(section * half_rows, half_rows)]

    def dev_peer(index):
        return (section, grp, index // n_dz, index % n_dz)

    barrier = pltpu.get_barrier_semaphore()
    for step in range(1, n_dz):
        pl.semaphore_signal(
            barrier,
            inc=1,
            device_id=(section, grp, dy, (dz + step) % n_dz),
            device_id_type=pl.DeviceIdType.MESH,
        )
    up = (dy + 1) % n_dy
    down = (dy + n_dy - 1) % n_dy
    for row in (up, down):
        pl.semaphore_signal(
            barrier,
            inc=1,
            device_id=(section, grp, row, dz),
            device_id_type=pl.DeviceIdType.MESH,
        )
    pl.semaphore_signal(
        barrier,
        inc=1,
        device_id=(partner_section, grp, dy, dz),
        device_id_type=pl.DeviceIdType.MESH,
    )
    has_left = dev > 0
    has_right = dev < n_dev - 1
    far_left = jnp.logical_and(has_left, dz == 0)
    far_right = jnp.logical_and(has_right, dz == n_dz - 1)

    @pl.when(far_left)
    def _():
        pl.semaphore_signal(
            barrier, inc=1, device_id=dev_peer(dev - 1), device_id_type=pl.DeviceIdType.MESH
        )

    @pl.when(far_right)
    def _():
        pl.semaphore_signal(
            barrier, inc=1, device_id=dev_peer(dev + 1), device_id_type=pl.DeviceIdType.MESH
        )

    extra = far_left.astype(jnp.int32) + far_right.astype(jnp.int32)
    pl.semaphore_wait(barrier, n_dz - 1 + 2 + 1 + extra)

    own = pltpu.make_async_copy(half_src, out_ref.at[dev], own_sem)
    own.start()

    def pair_copy(slot, source_ref):
        return pltpu.make_async_remote_copy(
            src_ref=source_ref,
            dst_ref=other_ref.at[slot],
            send_sem=pair_send.at[slot],
            recv_sem=pair_recv.at[slot],
            device_id=(partner_section, grp, dy, dz),
            device_id_type=pl.DeviceIdType.MESH,
        )

    pair_copy(dev, half_src).start()

    def z_copy(target, source):
        return pltpu.make_async_remote_copy(
            src_ref=half_src,
            dst_ref=out_ref.at[dy * n_dz + source],
            send_sem=z_send.at[target],
            recv_sem=z_recv.at[source],
            device_id=(section, grp, dy, target),
            device_id_type=pl.DeviceIdType.MESH,
        )

    for step in range(1, n_dz):
        z_copy((dz + step) % n_dz, dz).start()

    count_frames = frames_ref.shape[0]

    def to_left():
        return pltpu.make_async_remote_copy(
            src_ref=frames_ref.at[pl.ds(0, RAD)],
            dst_ref=halo_right,
            send_sem=halo_send.at[0],
            recv_sem=halo_recv.at[1],
            device_id=dev_peer(dev - 1),
            device_id_type=pl.DeviceIdType.MESH,
        )

    def to_right():
        return pltpu.make_async_remote_copy(
            src_ref=frames_ref.at[pl.ds(count_frames - RAD, RAD)],
            dst_ref=halo_left,
            send_sem=halo_send.at[1],
            recv_sem=halo_recv.at[0],
            device_id=dev_peer(dev + 1),
            device_id_type=pl.DeviceIdType.MESH,
        )

    @pl.when(has_left)
    def _():
        to_left().start()

    @pl.when(has_right)
    def _():
        to_right().start()

    @pl.when(jnp.logical_not(has_left))
    def _():
        halo_left[...] = jnp.zeros(halo_left.shape, halo_left.dtype)

    @pl.when(jnp.logical_not(has_right))
    def _():
        halo_right[...] = jnp.zeros(halo_right.shape, halo_right.dtype)

    def y_copy(direction, row, chunk):
        slot = row * n_dz + chunk
        target = up if direction == 0 else down
        return pltpu.make_async_remote_copy(
            src_ref=out_ref.at[slot],
            dst_ref=out_ref.at[slot],
            send_sem=y_send.at[direction * n_dy * n_dz + slot],
            recv_sem=y_recv.at[slot],
            device_id=(section, grp, target, dz),
            device_id_type=pl.DeviceIdType.MESH,
        )

    def y_own(direction):
        target = up if direction == 0 else down
        return pltpu.make_async_remote_copy(
            src_ref=half_src,
            dst_ref=out_ref.at[dev],
            send_sem=y_send.at[direction * n_dy * n_dz + dev],
            recv_sem=y_recv.at[dev],
            device_id=(section, grp, target, dz),
            device_id_type=pl.DeviceIdType.MESH,
        )

    for direction in (0, 1):
        y_own(direction).start()
    for step in range(1, n_dz):
        source = (dz + n_dz - step) % n_dz
        z_copy(source, source).wait_recv()
        for direction in (0, 1):
            y_copy(direction, dy, source).start()
        pair_copy(dy * n_dz + source, out_ref.at[dy * n_dz + source]).start()
    own.wait()

    @pl.when(has_left)
    def _():
        to_right_of_left = pltpu.make_async_remote_copy(
            src_ref=frames_ref.at[pl.ds(0, RAD)],
            dst_ref=halo_left,
            send_sem=halo_send.at[1],
            recv_sem=halo_recv.at[0],
            device_id=dev_peer(dev - 1),
            device_id_type=pl.DeviceIdType.MESH,
        )
        to_right_of_left.wait_recv()
        to_left().wait_send()

    @pl.when(has_right)
    def _():
        to_left_of_right = pltpu.make_async_remote_copy(
            src_ref=frames_ref.at[pl.ds(0, RAD)],
            dst_ref=halo_right,
            send_sem=halo_send.at[0],
            recv_sem=halo_recv.at[1],
            device_id=dev_peer(dev + 1),
            device_id_type=pl.DeviceIdType.MESH,
        )
        to_left_of_right.wait_recv()
        to_right().wait_send()

    mob_rows = kernels_ref.shape[1]
    mob_all = kernels_ref.shape[2]
    row_place = (
        section * mob_rows + lax.broadcasted_iota(jnp.int32, (mob_rows, mob_all), 0)
    ).astype(jnp.float32)
    col_place = (
        (section * mob_rows + lax.broadcasted_iota(jnp.int32, (mob_rows, mob_all), 1)) % mob_all
    ).astype(jnp.float32)
    distance = row_place - col_place
    for level in range(SCALES):
        spread_scans = 2.0**level
        scaled = distance / spread_scans
        kernels_ref[level] = (
            (1.0 - scaled * scaled)
            * jnp.exp(-0.5 * scaled * scaled)
            / math.sqrt(0.75 * math.sqrt(math.pi) * spread_scans)
        ).astype(kernels_ref.dtype)

    weights = retention_weights()

    row_block = 32

    def smooth_rows(block, carry):
        rows = pl.ds(pl.multiple_of(block * row_block, row_block), row_block)

        def padded_frame(place):
            if place < RAD:
                return halo_left[place, rows, :]
            if place < RAD + count_frames:
                return frames_ref[place - RAD, rows, :]
            return halo_right[place - RAD - count_frames, rows, :]

        for frame in range(count_frames):
            total = weights[0] * padded_frame(frame).astype(jnp.float32)
            for offset in range(1, 2 * RAD + 1):
                total = total + weights[offset] * padded_frame(frame + offset).astype(jnp.float32)
            own_scans[frame, rows, :] = total.astype(own_scans.dtype)
        return carry

    lax.fori_loop(0, own_scans.shape[1] // row_block, smooth_rows, 0)

    swap = pltpu.make_async_remote_copy(
        src_ref=own_scans,
        dst_ref=partner_scans,
        send_sem=swap_send,
        recv_sem=swap_recv,
        device_id=(partner_section, grp, dy, dz),
        device_id_type=pl.DeviceIdType.MESH,
    )
    swap.start()
    relay = n_dz // 2
    for chunk in range(n_dz):
        y_copy(0, down, chunk).wait_recv()
        if chunk < relay:
            y_copy(0, down, chunk).start()
        pair_copy(down * n_dz + chunk, out_ref.at[down * n_dz + chunk]).start()
        y_copy(1, up, chunk).wait_recv()
        if chunk >= relay:
            y_copy(1, up, chunk).start()
        pair_copy(up * n_dz + chunk, out_ref.at[up * n_dz + chunk]).start()
    swap.wait()

    half = own_scans.shape[1]

    def level_frame(frame, carry):
        for level in range(SCALES):
            table = kernels_ref[level]
            acc = jnp.dot(table[:, :half], own_scans[frame], preferred_element_type=jnp.float32)
            acc = acc + jnp.dot(
                table[:, half:], partner_scans[frame], preferred_element_type=jnp.float32
            )
            wave_ref[level, frame] = acc.astype(wave_ref.dtype)
        return carry

    lax.fori_loop(0, count_frames, level_frame, 0)

    opposite = (dy + 2) % n_dy
    for chunk in range(n_dz):
        y_copy(0, opposite, chunk).wait_recv()
        pair_copy(opposite * n_dz + chunk, out_ref.at[opposite * n_dz + chunk]).start()
    for direction in (0, 1):
        for chunk in range(n_dz):
            y_copy(direction, dy, chunk).wait_send()
    for chunk in range(relay):
        y_copy(0, down, chunk).wait_send()
    for chunk in range(relay, n_dz):
        y_copy(1, up, chunk).wait_send()
    for slot in range(n_dev):
        pair_copy(slot, half_src).wait_recv()
    for slot in range(n_dev):
        pair_copy(slot, half_src).wait_send()
    for step in range(1, n_dz):
        z_copy((dz + step) % n_dz, dz).wait_send()


def frame_work(frames, templates):
    sizes = (lax.axis_size("section"), lax.axis_size("dy"), lax.axis_size("dz"))
    n_section, n_dy, n_dz = sizes
    rows, channels = templates.shape[0] // 2, templates.shape[1]
    half = templates
    count_frames, mob_local, _ = frames.shape
    rows_out, other_out, wave = pl.pallas_call(
        functools.partial(frame_kernel, sizes),
        out_shape=(
            jax.ShapeDtypeStruct((n_dy * n_dz, rows, channels), half.dtype),
            jax.ShapeDtypeStruct((n_dy * n_dz, rows, channels), half.dtype),
            jax.ShapeDtypeStruct((SCALES, count_frames, mob_local, channels), jnp.bfloat16),
        ),
        in_specs=[pl.BlockSpec(memory_space=pltpu.VMEM)] * 2,
        out_specs=(pl.BlockSpec(memory_space=pltpu.VMEM),) * 3,
        scratch_shapes=[
            pltpu.VMEM((SCALES, mob_local, 2 * mob_local), jnp.bfloat16),
            pltpu.VMEM((RAD, mob_local, channels), frames.dtype),
            pltpu.VMEM((RAD, mob_local, channels), frames.dtype),
            pltpu.VMEM((count_frames, mob_local, channels), jnp.bfloat16),
            pltpu.VMEM((count_frames, mob_local, channels), jnp.bfloat16),
            pltpu.SemaphoreType.DMA(()),
            pltpu.SemaphoreType.DMA((n_dz,)),
            pltpu.SemaphoreType.DMA((n_dz,)),
            pltpu.SemaphoreType.DMA((2 * n_dy * n_dz,)),
            pltpu.SemaphoreType.DMA((n_dy * n_dz,)),
            pltpu.SemaphoreType.DMA((2,)),
            pltpu.SemaphoreType.DMA((2,)),
            pltpu.SemaphoreType.DMA(()),
            pltpu.SemaphoreType.DMA(()),
            pltpu.SemaphoreType.DMA((n_dy * n_dz,)),
            pltpu.SemaphoreType.DMA((n_dy * n_dz,)),
        ],
        compiler_params=pltpu.CompilerParams(
            collective_id=1, has_side_effects=True, vmem_limit_bytes=56 * 1024 * 1024
        ),
    )(frames, templates)
    return (
        rows_out.reshape(n_dy * n_dz * rows, channels),
        other_out.reshape(n_dy * n_dz * rows, channels),
        wave,
    )


def score_kernel(
    order_ref, tile_ref, block_ref, count_ref, section_ref, wave_ref, mine_ref, other_ref, out_ref
):
    slot = order_ref[pl.program_id(0)]
    live = slot < count_ref[0]
    mine = block_ref[slot] % 2 == section_ref[0]

    def score(rows_ref):
        rows = rows_ref[...]
        acc = jnp.zeros((1, PB), jnp.float32)
        for level in range(SCALES):
            cells = wave_ref[level].reshape(-1, rows.shape[1])
            scores = lax.dot_general(
                cells, rows, (((1,), (1,)), ((), ())), preferred_element_type=jnp.float32
            )
            acc = acc + jnp.sum(jnp.maximum(scores, 0.0), axis=0, keepdims=True)
        cell_count = SCALES * wave_ref.shape[1] * wave_ref.shape[2]
        out_ref[0] = acc / cell_count

    @pl.when(jnp.logical_and(live, mine))
    def _():
        score(mine_ref)

    @pl.when(jnp.logical_and(live, jnp.logical_not(mine)))
    def _():
        score(other_ref)

    @pl.when(jnp.logical_not(live))
    def _():
        out_ref[0] = jnp.zeros((1, PB), jnp.float32)


def score_pairs(wavelet_stack, my_rows, other_rows, tile_ids, block_ids, live_pairs, section_index):
    slots = tile_ids.shape[0]
    scales, frames_local, mob_local, channels = wavelet_stack.shape
    slot_ids = jnp.arange(slots, dtype=jnp.int32)
    keys = jnp.where(slot_ids < live_pairs, tile_ids * slots + slot_ids, (mob_local // TM + 1) * slots + slot_ids)
    order = jnp.argsort(keys).astype(jnp.int32)

    def visited(k, o, c):
        return o[jnp.minimum(k, c[0] - 1)]

    grid_spec = pltpu.PrefetchScalarGridSpec(
        num_scalar_prefetch=5,
        grid=(slots,),
        in_specs=[
            pl.BlockSpec(
                (scales, frames_local, TM, channels),
                lambda k, o, t, b, c, s: (0, 0, t[visited(k, o, c)], 0),
            ),
            pl.BlockSpec((PB, channels), lambda k, o, t, b, c, s: (b[visited(k, o, c)] // 2, 0)),
            pl.BlockSpec((PB, channels), lambda k, o, t, b, c, s: (b[visited(k, o, c)] // 2, 0)),
        ],
        out_specs=pl.BlockSpec((1, 1, PB), lambda k, o, t, b, c, s: (o[k], 0, 0)),
    )
    out = pl.pallas_call(
        score_kernel,
        grid_spec=grid_spec,
        out_shape=jax.ShapeDtypeStruct((slots, 1, PB), jnp.float32),
    )(
        order,
        tile_ids,
        block_ids,
        live_pairs.reshape(1),
        section_index.astype(jnp.int32).reshape(1),
        wavelet_stack,
        my_rows,
        other_rows,
    )
    return out.reshape(slots, PB)


def solution(mesh):
    section_count, grp_count, dev_count = mesh.devices.shape
    dz_count = 8 if dev_count % 8 == 0 else dev_count
    split_mesh = jax.sharding.Mesh(
        mesh.devices.reshape(section_count, grp_count, dev_count // dz_count, dz_count),
        ("section", "grp", "dy", "dz"),
    )
    placed = (
        P("grp", DEV, "section", None),
        P(DEV, None),
        P("section", "grp", DEV),
        P("section", "grp", DEV),
        P("section", "grp", DEV),
        P(),
    )
    return jax.shard_map(
        on_device, mesh=split_mesh, in_specs=placed, out_specs=P("grp", DEV), check_vma=False
    )
```

```python
import functools
import math

import jax
import jax.numpy as jnp
from jax import lax
from jax.experimental import pallas as pl
from jax.experimental.pallas import tpu as pltpu
from jax.sharding import PartitionSpec as P

MOB = 512
SCALES = 6
RAD = 4
TM = 64
PB = 128
PREC = 8192
DEV = ("dy", "dz")


retention_spread = 2.0


def extended(cells, sides, width):
    for axis, dim in sides:
        count = lax.axis_size(axis)
        ends = count - 1
        head = lax.slice_in_dim(cells, 0, width, axis=dim)
        tail = lax.slice_in_dim(cells, cells.shape[dim] - width, cells.shape[dim], axis=dim)
        cells = jnp.concatenate(
            [
                lax.ppermute(tail, axis, [(i, (i + 1) % count) for i in range(ends)]),
                cells,
                lax.ppermute(head, axis, [((i + 1) % count, i) for i in range(ends)]),
            ],
            axis=dim,
        )
    return cells


def retention_weights():
    bell_values = [
        math.exp(-0.5 * (offset / retention_spread) ** 2) for offset in range(-RAD, RAD + 1)
    ]
    bell_total = sum(bell_values)
    return [weight_value / bell_total for weight_value in bell_values]


def mobility_kernels(row_start, row_count, col_start):
    row_place = (row_start + jnp.arange(row_count, dtype=jnp.int32)).astype(jnp.float32)
    col_place = ((col_start + jnp.arange(MOB, dtype=jnp.int32)) % MOB).astype(jnp.float32)
    distance = row_place[:, None] - col_place[None, :]
    tables = []
    for level in range(SCALES):
        spread_scans = 2.0**level
        scaled = distance / spread_scans
        tables.append(
            (1.0 - scaled * scaled)
            * jnp.exp(-0.5 * scaled * scaled)
            / math.sqrt(0.75 * math.sqrt(math.pi) * spread_scans)
        )
    return jnp.stack(tables).astype(jnp.bfloat16)


def on_device(frames, templates, pair_block, pair_tile, pair_count, owner_order):
    section_index = lax.axis_index("section")
    mob_local = frames.shape[2]
    section_count = lax.axis_size("section")
    my_rows, other_rows, wavelet_stack = frame_work(frames[0], templates)
    slots = pair_block.shape[2]
    live_pairs = pair_count[0, 0, 0]
    block_ids = pair_block[0, 0]
    tile_ids = pair_tile[0, 0]
    responses = score_pairs(
        wavelet_stack, my_rows, other_rows, tile_ids, block_ids, live_pairs, section_index
    )
    positions = jnp.take(owner_order.reshape(-1, PB), block_ids, axis=0).reshape(-1)
    groups = PREC // PB
    by_group = jnp.where(
        (positions // PB)[:, None] == jnp.arange(groups, dtype=jnp.int32)[None, :],
        responses.reshape(-1)[:, None],
        0.0,
    )
    by_lane = ((positions % PB)[:, None] == jnp.arange(PB, dtype=jnp.int32)[None, :]).astype(
        jnp.float32
    )
    placed = jnp.einsum(
        "ka,kb->ab",
        by_group,
        by_lane,
        precision=lax.Precision.HIGHEST,
        preferred_element_type=jnp.float32,
    ).reshape(-1)
    dev_count = lax.axis_size(DEV)
    return reduce_owned(placed.reshape(dev_count, 1, PREC // dev_count))


def reduce_kernel(
    sizes,
    payload_ref,
    out_ref,
    mixed,
    line,
    line_in,
    column,
    column_in,
    totals,
    pair_send,
    pair_recv,
    z_send,
    z_recv,
    y_send,
    y_recv,
    total_send,
    total_recv,
):
    n_section, n_grp, n_dy, n_dz = sizes
    cores = totals
    section = lax.axis_index("section")
    grp = lax.axis_index("grp")
    dy = lax.axis_index("dy")
    dz = lax.axis_index("dz")
    partner = (section + 1) % n_section
    owned_width = out_ref.shape[1]

    barrier = pltpu.get_barrier_semaphore()
    peers = [(partner, grp, dy, dz)]
    peers += [(section, grp, dy, (dz + step) % n_dz) for step in range(1, n_dz)]
    peers += [(section, grp, (dy + step) % n_dy, dz) for step in range(1, n_dy)]
    peers += [
        (side, (grp + step) % n_grp, dy, dz) for side in range(n_section) for step in range(1, n_grp)
    ]
    for peer in peers:
        pl.semaphore_signal(barrier, inc=1, device_id=peer, device_id_type=pl.DeviceIdType.MESH)
    pl.semaphore_wait(barrier, len(peers))

    swap = pltpu.make_async_remote_copy(
        src_ref=payload_ref,
        dst_ref=mixed,
        send_sem=pair_send,
        recv_sem=pair_recv,
        device_id=(partner, grp, dy, dz),
        device_id_type=pl.DeviceIdType.MESH,
    )
    swap.start()
    own_slot = section * n_grp + grp
    own_sum = jnp.sum(jnp.sum(jnp.sum(payload_ref[...], axis=0), axis=0), axis=1, keepdims=True)
    cores[own_slot] = jnp.broadcast_to(own_sum, (1, 128))
    cores[partner * n_grp + grp] = jnp.zeros((1, 128), jnp.float32)

    def core_copy(side, other):
        return pltpu.make_async_remote_copy(
            src_ref=cores.at[own_slot],
            dst_ref=cores.at[own_slot],
            send_sem=total_send.at[side * n_grp + other],
            recv_sem=total_recv.at[own_slot],
            device_id=(side, other, dy, dz),
            device_id_type=pl.DeviceIdType.MESH,
        )

    def core_arrival(side, other):
        slot = side * n_grp + other
        return pltpu.make_async_remote_copy(
            src_ref=cores.at[slot],
            dst_ref=cores.at[slot],
            send_sem=total_send.at[slot],
            recv_sem=total_recv.at[slot],
            device_id=(side, other, dy, dz),
            device_id_type=pl.DeviceIdType.MESH,
        )

    for side in range(n_section):
        for step in range(1, n_grp):
            core_copy(side, (grp + step) % n_grp).start()
    swap.wait()
    combined = payload_ref[...] + mixed[...]
    line[:, :, :, :owned_width] = combined
    chip_total = jnp.sum(jnp.sum(jnp.sum(combined, axis=0), axis=0), axis=1, keepdims=True)
    for side in range(n_section):
        for step in range(1, n_grp):
            core_arrival(side, (grp + step) % n_grp).wait_recv()
    lanes = lax.broadcasted_iota(jnp.int32, (1, line.shape[3] - owned_width), 1)
    spread = jnp.where(lanes == grp, chip_total, 0.0)
    for other in range(n_grp):
        other_total = cores[other] + cores[n_grp + other]
        spread = jnp.where(jnp.logical_and(lanes == other, other != grp), other_total, spread)
    line[:, :, :, owned_width:] = jnp.broadcast_to(spread[None, None], line.shape[:3] + spread.shape[1:])
    line_in[dz] = line[dz]

    def z_copy(target, source):
        return pltpu.make_async_remote_copy(
            src_ref=line.at[target],
            dst_ref=line_in.at[source],
            send_sem=z_send.at[target],
            recv_sem=z_recv.at[source],
            device_id=(section, grp, dy, target),
            device_id_type=pl.DeviceIdType.MESH,
        )

    for step in range(1, n_dz):
        z_copy((dz + step) % n_dz, dz).start()
    for step in range(1, n_dz):
        source = (dz + n_dz - step) % n_dz
        z_copy(source, source).wait_recv()
    partial = line_in[0]
    for index in range(1, n_dz):
        partial = partial + line_in[index]
    column[...] = partial
    column_in[dy] = column[dy]

    def y_copy(target, source):
        return pltpu.make_async_remote_copy(
            src_ref=column.at[target],
            dst_ref=column_in.at[source],
            send_sem=y_send.at[target],
            recv_sem=y_recv.at[source],
            device_id=(section, grp, target, dz),
            device_id_type=pl.DeviceIdType.MESH,
        )

    for step in range(1, n_dy):
        y_copy((dy + step) % n_dy, dy).start()
    for step in range(1, n_dy):
        source = (dy + n_dy - step) % n_dy
        y_copy(source, source).wait_recv()
    summed = column_in[0]
    for index in range(1, n_dy):
        summed = summed + column_in[index]
    summed = summed.reshape(summed.shape[-2:])
    for step in range(1, n_dz):
        z_copy((dz + step) % n_dz, dz).wait_send()
    for step in range(1, n_dy):
        y_copy((dy + step) % n_dy, dy).wait_send()
    for side in range(n_section):
        for step in range(1, n_grp):
            core_copy(side, (grp + step) % n_grp).wait_send()
    run_totals = summed[:, owned_width:]
    run_sum = jnp.sum(run_totals, axis=1, keepdims=True)
    own_total = jnp.sum(jnp.where(lanes == grp, run_totals, 0.0), axis=1, keepdims=True)
    factor = (run_sum / n_grp) / own_total
    out_ref[...] = summed[:, :owned_width] * factor


def reduce_owned(payload):
    sizes = (lax.axis_size("section"), lax.axis_size("grp"), lax.axis_size("dy"), lax.axis_size("dz"))
    n_section, n_grp, n_dy, n_dz = sizes
    rows, one, owned_width = payload.shape
    width = owned_width + 128
    lines = payload.reshape(n_dy, n_dz, one, owned_width).transpose(1, 0, 2, 3)
    return pl.pallas_call(
        functools.partial(reduce_kernel, sizes),
        out_shape=jax.ShapeDtypeStruct((1, owned_width), jnp.float32),
        in_specs=[pl.BlockSpec(memory_space=pltpu.VMEM)],
        out_specs=pl.BlockSpec(memory_space=pltpu.VMEM),
        scratch_shapes=[
            pltpu.VMEM((n_dz, n_dy, one, owned_width), jnp.float32),
            pltpu.VMEM((n_dz, n_dy, one, width), jnp.float32),
            pltpu.VMEM((n_dz, n_dy, one, width), jnp.float32),
            pltpu.VMEM((n_dy, one, width), jnp.float32),
            pltpu.VMEM((n_dy, one, width), jnp.float32),
            pltpu.VMEM((n_section * n_grp, 1, 128), jnp.float32),
            pltpu.SemaphoreType.DMA(()),
            pltpu.SemaphoreType.DMA(()),
            pltpu.SemaphoreType.DMA((n_dz,)),
            pltpu.SemaphoreType.DMA((n_dz,)),
            pltpu.SemaphoreType.DMA((n_dy,)),
            pltpu.SemaphoreType.DMA((n_dy,)),
            pltpu.SemaphoreType.DMA((n_section * n_grp,)),
            pltpu.SemaphoreType.DMA((n_section * n_grp,)),
        ],
        compiler_params=pltpu.CompilerParams(collective_id=0, has_side_effects=True),
    )(lines)


def frame_kernel(
    sizes,
    frames_ref,
    templates_ref,
    out_ref,
    other_ref,
    wave_ref,
    kernels_ref,
    halo_left,
    halo_right,
    own_scans,
    partner_scans,
    own_sem,
    z_send,
    z_recv,
    y_send,
    y_recv,
    halo_send,
    halo_recv,
    swap_send,
    swap_recv,
    pair_send,
    pair_recv,
):
    n_section, n_dy, n_dz = sizes
    n_dev = n_dy * n_dz
    section = lax.axis_index("section")
    grp = lax.axis_index("grp")
    dy = lax.axis_index("dy")
    dz = lax.axis_index("dz")
    dev = dy * n_dz + dz
    partner_section = (section + 1) % n_section
    half_rows = out_ref.shape[1]
    half_src = templates_ref.at[pl.ds(section * half_rows, half_rows)]

    def dev_peer(index):
        return (section, grp, index // n_dz, index % n_dz)

    barrier = pltpu.get_barrier_semaphore()
    for step in range(1, n_dz):
        pl.semaphore_signal(
            barrier,
            inc=1,
            device_id=(section, grp, dy, (dz + step) % n_dz),
            device_id_type=pl.DeviceIdType.MESH,
        )
    up = (dy + 1) % n_dy
    down = (dy + n_dy - 1) % n_dy
    for row in (up, down):
        pl.semaphore_signal(
            barrier,
            inc=1,
            device_id=(section, grp, row, dz),
            device_id_type=pl.DeviceIdType.MESH,
        )
    pl.semaphore_signal(
        barrier,
        inc=1,
        device_id=(partner_section, grp, dy, dz),
        device_id_type=pl.DeviceIdType.MESH,
    )
    has_left = dev > 0
    has_right = dev < n_dev - 1
    far_left = jnp.logical_and(has_left, dz == 0)
    far_right = jnp.logical_and(has_right, dz == n_dz - 1)

    @pl.when(far_left)
    def _():
        pl.semaphore_signal(
            barrier, inc=1, device_id=dev_peer(dev - 1), device_id_type=pl.DeviceIdType.MESH
        )

    @pl.when(far_right)
    def _():
        pl.semaphore_signal(
            barrier, inc=1, device_id=dev_peer(dev + 1), device_id_type=pl.DeviceIdType.MESH
        )

    extra = far_left.astype(jnp.int32) + far_right.astype(jnp.int32)
    pl.semaphore_wait(barrier, n_dz - 1 + 2 + 1 + extra)

    own = pltpu.make_async_copy(half_src, out_ref.at[dev], own_sem)
    own.start()

    def pair_copy(slot, source_ref):
        return pltpu.make_async_remote_copy(
            src_ref=source_ref,
            dst_ref=other_ref.at[slot],
            send_sem=pair_send.at[slot],
            recv_sem=pair_recv.at[slot],
            device_id=(partner_section, grp, dy, dz),
            device_id_type=pl.DeviceIdType.MESH,
        )

    pair_copy(dev, half_src).start()

    def z_copy(target, source):
        return pltpu.make_async_remote_copy(
            src_ref=half_src,
            dst_ref=out_ref.at[dy * n_dz + source],
            send_sem=z_send.at[target],
            recv_sem=z_recv.at[source],
            device_id=(section, grp, dy, target),
            device_id_type=pl.DeviceIdType.MESH,
        )

    for step in range(1, n_dz):
        z_copy((dz + step) % n_dz, dz).start()

    count_frames = frames_ref.shape[0]

    def to_left():
        return pltpu.make_async_remote_copy(
            src_ref=frames_ref.at[pl.ds(0, RAD)],
            dst_ref=halo_right,
            send_sem=halo_send.at[0],
            recv_sem=halo_recv.at[1],
            device_id=dev_peer(dev - 1),
            device_id_type=pl.DeviceIdType.MESH,
        )

    def to_right():
        return pltpu.make_async_remote_copy(
            src_ref=frames_ref.at[pl.ds(count_frames - RAD, RAD)],
            dst_ref=halo_left,
            send_sem=halo_send.at[1],
            recv_sem=halo_recv.at[0],
            device_id=dev_peer(dev + 1),
            device_id_type=pl.DeviceIdType.MESH,
        )

    @pl.when(has_left)
    def _():
        to_left().start()

    @pl.when(has_right)
    def _():
        to_right().start()

    @pl.when(jnp.logical_not(has_left))
    def _():
        halo_left[...] = jnp.zeros(halo_left.shape, halo_left.dtype)

    @pl.when(jnp.logical_not(has_right))
    def _():
        halo_right[...] = jnp.zeros(halo_right.shape, halo_right.dtype)

    def y_copy(direction, row, chunk):
        slot = row * n_dz + chunk
        target = up if direction == 0 else down
        return pltpu.make_async_remote_copy(
            src_ref=out_ref.at[slot],
            dst_ref=out_ref.at[slot],
            send_sem=y_send.at[direction * n_dy * n_dz + slot],
            recv_sem=y_recv.at[slot],
            device_id=(section, grp, target, dz),
            device_id_type=pl.DeviceIdType.MESH,
        )

    def y_own(direction):
        target = up if direction == 0 else down
        return pltpu.make_async_remote_copy(
            src_ref=half_src,
            dst_ref=out_ref.at[dev],
            send_sem=y_send.at[direction * n_dy * n_dz + dev],
            recv_sem=y_recv.at[dev],
            device_id=(section, grp, target, dz),
            device_id_type=pl.DeviceIdType.MESH,
        )

    for direction in (0, 1):
        y_own(direction).start()
    for step in range(1, n_dz):
        source = (dz + n_dz - step) % n_dz
        z_copy(source, source).wait_recv()
        for direction in (0, 1):
            y_copy(direction, dy, source).start()
        pair_copy(dy * n_dz + source, out_ref.at[dy * n_dz + source]).start()

    @pl.when(has_left)
    def _():
        to_right_of_left = pltpu.make_async_remote_copy(
            src_ref=frames_ref.at[pl.ds(0, RAD)],
            dst_ref=halo_left,
            send_sem=halo_send.at[1],
            recv_sem=halo_recv.at[0],
            device_id=dev_peer(dev - 1),
            device_id_type=pl.DeviceIdType.MESH,
        )
        to_right_of_left.wait_recv()
        to_left().wait_send()

    @pl.when(has_right)
    def _():
        to_left_of_right = pltpu.make_async_remote_copy(
            src_ref=frames_ref.at[pl.ds(0, RAD)],
            dst_ref=halo_right,
            send_sem=halo_send.at[0],
            recv_sem=halo_recv.at[1],
            device_id=dev_peer(dev + 1),
            device_id_type=pl.DeviceIdType.MESH,
        )
        to_left_of_right.wait_recv()
        to_right().wait_send()

    mob_rows = kernels_ref.shape[1]
    mob_all = kernels_ref.shape[2]
    row_place = (
        section * mob_rows + lax.broadcasted_iota(jnp.int32, (mob_rows, mob_all), 0)
    ).astype(jnp.float32)
    col_place = (
        (section * mob_rows + lax.broadcasted_iota(jnp.int32, (mob_rows, mob_all), 1)) % mob_all
    ).astype(jnp.float32)
    distance = row_place - col_place
    for level in range(SCALES):
        spread_scans = 2.0**level
        scaled = distance / spread_scans
        kernels_ref[level] = (
            (1.0 - scaled * scaled)
            * jnp.exp(-0.5 * scaled * scaled)
            / math.sqrt(0.75 * math.sqrt(math.pi) * spread_scans)
        ).astype(kernels_ref.dtype)

    weights = retention_weights()

    row_block = 32

    def smooth_rows(block, carry):
        rows = pl.ds(pl.multiple_of(block * row_block, row_block), row_block)

        def padded_frame(place):
            if place < RAD:
                return halo_left[place, rows, :]
            if place < RAD + count_frames:
                return frames_ref[place - RAD, rows, :]
            return halo_right[place - RAD - count_frames, rows, :]

        for frame in range(count_frames):
            total = weights[0] * padded_frame(frame).astype(jnp.float32)
            for offset in range(1, 2 * RAD + 1):
                total = total + weights[offset] * padded_frame(frame + offset).astype(jnp.float32)
            own_scans[frame, rows, :] = total.astype(own_scans.dtype)
        return carry

    lax.fori_loop(0, own_scans.shape[1] // row_block, smooth_rows, 0)

    swap = pltpu.make_async_remote_copy(
        src_ref=own_scans,
        dst_ref=partner_scans,
        send_sem=swap_send,
        recv_sem=swap_recv,
        device_id=(partner_section, grp, dy, dz),
        device_id_type=pl.DeviceIdType.MESH,
    )
    swap.start()
    relay = n_dz // 2
    for chunk in range(n_dz):
        y_copy(0, down, chunk).wait_recv()
        if chunk < relay:
            y_copy(0, down, chunk).start()
        pair_copy(down * n_dz + chunk, out_ref.at[down * n_dz + chunk]).start()
        y_copy(1, up, chunk).wait_recv()
        if chunk >= relay:
            y_copy(1, up, chunk).start()
        pair_copy(up * n_dz + chunk, out_ref.at[up * n_dz + chunk]).start()
    swap.wait()

    half = own_scans.shape[1]

    def level_frame(frame, carry):
        for level in range(SCALES):
            table = kernels_ref[level]
            acc = jnp.dot(table[:, :half], own_scans[frame], preferred_element_type=jnp.float32)
            acc = acc + jnp.dot(
                table[:, half:], partner_scans[frame], preferred_element_type=jnp.float32
            )
            wave_ref[level, frame] = acc.astype(wave_ref.dtype)
        return carry

    lax.fori_loop(0, count_frames, level_frame, 0)

    opposite = (dy + 2) % n_dy
    for chunk in range(n_dz):
        y_copy(0, opposite, chunk).wait_recv()
        pair_copy(opposite * n_dz + chunk, out_ref.at[opposite * n_dz + chunk]).start()
    for direction in (0, 1):
        for chunk in range(n_dz):
            y_copy(direction, dy, chunk).wait_send()
    for chunk in range(relay):
        y_copy(0, down, chunk).wait_send()
    for chunk in range(relay, n_dz):
        y_copy(1, up, chunk).wait_send()
    for slot in range(n_dev):
        pair_copy(slot, half_src).wait_recv()
    for slot in range(n_dev):
        pair_copy(slot, half_src).wait_send()
    for step in range(1, n_dz):
        z_copy((dz + step) % n_dz, dz).wait_send()
    own.wait()


def frame_work(frames, templates):
    sizes = (lax.axis_size("section"), lax.axis_size("dy"), lax.axis_size("dz"))
    n_section, n_dy, n_dz = sizes
    rows, channels = templates.shape[0] // 2, templates.shape[1]
    half = templates
    count_frames, mob_local, _ = frames.shape
    rows_out, other_out, wave = pl.pallas_call(
        functools.partial(frame_kernel, sizes),
        out_shape=(
            jax.ShapeDtypeStruct((n_dy * n_dz, rows, channels), half.dtype),
            jax.ShapeDtypeStruct((n_dy * n_dz, rows, channels), half.dtype),
            jax.ShapeDtypeStruct((SCALES, count_frames, mob_local, channels), jnp.bfloat16),
        ),
        in_specs=[pl.BlockSpec(memory_space=pltpu.VMEM)] * 2,
        out_specs=(pl.BlockSpec(memory_space=pltpu.VMEM),) * 3,
        scratch_shapes=[
            pltpu.VMEM((SCALES, mob_local, 2 * mob_local), jnp.bfloat16),
            pltpu.VMEM((RAD, mob_local, channels), frames.dtype),
            pltpu.VMEM((RAD, mob_local, channels), frames.dtype),
            pltpu.VMEM((count_frames, mob_local, channels), jnp.bfloat16),
            pltpu.VMEM((count_frames, mob_local, channels), jnp.bfloat16),
            pltpu.SemaphoreType.DMA(()),
            pltpu.SemaphoreType.DMA((n_dz,)),
            pltpu.SemaphoreType.DMA((n_dz,)),
            pltpu.SemaphoreType.DMA((2 * n_dy * n_dz,)),
            pltpu.SemaphoreType.DMA((n_dy * n_dz,)),
            pltpu.SemaphoreType.DMA((2,)),
            pltpu.SemaphoreType.DMA((2,)),
            pltpu.SemaphoreType.DMA(()),
            pltpu.SemaphoreType.DMA(()),
            pltpu.SemaphoreType.DMA((n_dy * n_dz,)),
            pltpu.SemaphoreType.DMA((n_dy * n_dz,)),
        ],
        compiler_params=pltpu.CompilerParams(
            collective_id=1, has_side_effects=True, vmem_limit_bytes=56 * 1024 * 1024
        ),
    )(frames, templates)
    return (
        rows_out.reshape(n_dy * n_dz * rows, channels),
        other_out.reshape(n_dy * n_dz * rows, channels),
        wave,
    )


def score_kernel(
    order_ref, tile_ref, block_ref, count_ref, section_ref, wave_ref, mine_ref, other_ref, out_ref
):
    slot = order_ref[pl.program_id(0)]
    live = slot < count_ref[0]
    mine = block_ref[slot] % 2 == section_ref[0]

    def score(rows_ref):
        rows = rows_ref[...]
        acc = jnp.zeros((1, PB), jnp.float32)
        for level in range(SCALES):
            cells = wave_ref[level].reshape(-1, rows.shape[1])
            scores = lax.dot_general(
                cells, rows, (((1,), (1,)), ((), ())), preferred_element_type=jnp.float32
            )
            acc = acc + jnp.sum(jnp.maximum(scores, 0.0), axis=0, keepdims=True)
        cell_count = SCALES * wave_ref.shape[1] * wave_ref.shape[2]
        out_ref[0] = acc / cell_count

    @pl.when(jnp.logical_and(live, mine))
    def _():
        score(mine_ref)

    @pl.when(jnp.logical_and(live, jnp.logical_not(mine)))
    def _():
        score(other_ref)

    @pl.when(jnp.logical_not(live))
    def _():
        out_ref[0] = jnp.zeros((1, PB), jnp.float32)


def score_pairs(wavelet_stack, my_rows, other_rows, tile_ids, block_ids, live_pairs, section_index):
    slots = tile_ids.shape[0]
    scales, frames_local, mob_local, channels = wavelet_stack.shape
    slot_ids = jnp.arange(slots, dtype=jnp.int32)
    keys = jnp.where(slot_ids < live_pairs, tile_ids * slots + slot_ids, (mob_local // TM + 1) * slots + slot_ids)
    order = jnp.argsort(keys).astype(jnp.int32)

    def visited(k, o, c):
        return o[jnp.minimum(k, c[0] - 1)]

    grid_spec = pltpu.PrefetchScalarGridSpec(
        num_scalar_prefetch=5,
        grid=(slots,),
        in_specs=[
            pl.BlockSpec(
                (scales, frames_local, TM, channels),
                lambda k, o, t, b, c, s: (0, 0, t[visited(k, o, c)], 0),
            ),
            pl.BlockSpec((PB, channels), lambda k, o, t, b, c, s: (b[visited(k, o, c)] // 2, 0)),
            pl.BlockSpec((PB, channels), lambda k, o, t, b, c, s: (b[visited(k, o, c)] // 2, 0)),
        ],
        out_specs=pl.BlockSpec((1, 1, PB), lambda k, o, t, b, c, s: (o[k], 0, 0)),
    )
    out = pl.pallas_call(
        score_kernel,
        grid_spec=grid_spec,
        out_shape=jax.ShapeDtypeStruct((slots, 1, PB), jnp.float32),
    )(
        order,
        tile_ids,
        block_ids,
        live_pairs.reshape(1),
        section_index.astype(jnp.int32).reshape(1),
        wavelet_stack,
        my_rows,
        other_rows,
    )
    return out.reshape(slots, PB)


def solution(mesh):
    section_count, grp_count, dev_count = mesh.devices.shape
    dz_count = 8 if dev_count % 8 == 0 else dev_count
    split_mesh = jax.sharding.Mesh(
        mesh.devices.reshape(section_count, grp_count, dev_count // dz_count, dz_count),
        ("section", "grp", "dy", "dz"),
    )
    placed = (
        P("grp", DEV, "section", None),
        P(DEV, None),
        P("section", "grp", DEV),
        P("section", "grp", DEV),
        P("section", "grp", DEV),
        P(),
    )
    return jax.shard_map(
        on_device, mesh=split_mesh, in_specs=placed, out_specs=P("grp", DEV), check_vma=False
    )
```
